32 devices in a mesh: dp: 8 (over z, x), fsdp: 4 (over y, core).
Axes of the slice: x: 2, y: 2, z: 4, core: 2. Of those that a mesh axis runs over, the one named last changes fastest.
Arguments:
- tokens: float32 [16, 1024, 512], P('dp', 'fsdp'), may hold values from -12 to 12
- segments: int32 [16, 1024], P('dp', 'fsdp'), may hold values from 0 to 15, never falling along the last dimension, each value on 1 to 512 neighbouring positions
- cotangent: float32 [16, 1024, 512], P('dp', 'fsdp'), may hold values from -6 to 6
- ln1_gain: float32 [512], P('dp'), may hold values from 0.5 to 1.5
- ln1_bias: float32 [512], P('dp'), may hold values from -2.5 to 2.5
- w_qkv: float32 [512, 1536], P('fsdp', 'dp'), may hold values from -0.25 to 0.25
- w_out: float32 [512, 512], P('fsdp', 'dp'), may hold values from -1.5 to 1.5
- ln2_gain: float32 [512], P('dp'), may hold values from 0.5 to 1.5
- ln2_bias: float32 [512], P('dp'), may hold values from -2.5 to 2.5
- w_up: float32 [512, 2048], P('fsdp', 'dp'), may hold values from -0.25 to 0.25
- w_down: float32 [2048, 512], P('fsdp', 'dp'), may hold values from -0.125 to 0.125
Outputs:
- output: float32 [16, 1024, 512], P('dp', 'fsdp')
- grad_tokens: float32 [16, 1024, 512], P('dp', 'fsdp')
- grad_ln1_gain: float32 [512], P('dp')
- grad_ln1_bias: float32 [512], P('dp')
- grad_w_qkv: float32 [512, 1536], P('fsdp', 'dp')
- grad_w_out: float32 [512, 512], P('fsdp', 'dp')
- grad_ln2_gain: float32 [512], P('dp')
- grad_ln2_bias: float32 [512], P('dp')
- grad_w_up: float32 [512, 2048], P('fsdp', 'dp')
- grad_w_down: float32 [2048, 512], P('fsdp', 'dp')
The draws below stay inside these ranges and needn't reach their ends.
Inputs may be any that keep to these rules, and one draw needn't show every extreme that they name: `segments`: in each sequence the numbers never fall; each document runs for 1 to 512 tokens, and one runs for exactly 512.
All inputs are finite; a program needn't handle non-finite values.
Results may differ from the reference program's by a relative error of at most 0.0003.
Values sent between devices are 32-bit elements; how exact they have to be, the bound alone decides.
No kernel may reach another device: no remote copies, remote signals or barrier semaphores. Data moves between devices by JAX's collectives and lax.ppermute only.
A program may use at most 256 MiB of HBM per device.

```python
import math
import jax
import jax.numpy as jnp
import numpy as np
from jax import lax

D = 512
HEADS = 8
FF = 2048
NR = 16
LEVELS = 6
LENGTH = 1024
SEQS = 16


def draw_tokens(key, part):
    key_rows, key_cols, key_base = jax.random.split(key, 3)
    row_scale = jnp.exp(jax.random.uniform(key_rows, (SEQS, LENGTH, 1), jnp.float32, math.log(0.3), math.log(3.0)))
    col_scale = jnp.exp(jax.random.uniform(key_cols, (D,), jnp.float32, math.log(0.3), math.log(3.0)))
    base_values = jnp.clip(jax.random.normal(key_base, (SEQS, LENGTH, D), jnp.float32), -4.0, 4.0)
    return jnp.clip(base_values * row_scale * col_scale, -12.0, 12.0)


def block_scale(own_key, dims, cuts, smallest, high):
    loudness, own = 1.0, jax.random.fold_in(own_key, 6)
    for position, parts in cuts:
        steps = jnp.exp(jax.random.uniform(jax.random.fold_in(own, position), (parts,), jnp.float32, smallest / len(cuts), high / len(cuts)))
        loudness = loudness * jnp.repeat(steps, dims[position] // parts).reshape([-1 if axis == position else 1 for axis in range(len(dims))])
    return loudness


def profile(amount, total, most, lean):
    weights = [(1 << 20) // math.isqrt(rank ** lean) + 1 for rank in range(2, amount + 1)]
    spare, holding = total - most - (amount - 1), [1] * (amount - 1)
    while spare > 0:
        candidates = [i for i in range(amount - 1) if holding[i] < most]
        mass, budget = sum([weights[i] for i in candidates]), spare
        for i in candidates:
            more = min(most - holding[i], max(1, budget * weights[i] // mass), spare)
            holding[i] = holding[i] + more
            spare = spare - more
    return np.array([most] + holding)


def uneven(stream_key, number_of, total, bound, skew):
    if number_of == 2:
        one = jax.random.randint(stream_key, (), max(1, total - bound), min(bound, total - 1) + 1)
        return jnp.stack([one, total - one])
    lengths = jnp.asarray(profile(number_of, total, bound, skew), jnp.int32)
    couples = (number_of - 1) // 2
    giver, taker = lengths[1:1 + 2 * couples:2], lengths[2:2 + 2 * couples:2]
    room = jnp.minimum(giver - 1, bound - taker)
    moved = jax.random.randint(jax.random.fold_in(stream_key, 1), (couples,), 0, 1 << 20) % (room + 1)
    lengths = lengths.at[1:1 + 2 * couples:2].set(giver - moved).at[2:2 + 2 * couples:2].set(taker + moved)
    return lengths[jax.random.permutation(jax.random.fold_in(stream_key, 2), number_of)]


def noise(key, extent, width, most, cuts=(), held_as=jnp.bfloat16):
    drawn = jax.random.normal(key, extent, jnp.float32) * width
    if len(cuts) > 0:
        drawn = block_scale(key, extent, cuts, -0.22, 0.18) * drawn
    return jnp.clip(drawn, min=-most, max=most).astype(held_as)


def setup_inputs(seed: int = 0) -> dict:
    key_list = jax.random.split(jax.random.key(seed), 12)
    tokens = draw_tokens(jax.random.fold_in(key_list[11], 71), 0)
    segments = jax.vmap(lambda own: jnp.searchsorted(jnp.cumsum(uneven(own, LENGTH // 64, LENGTH, LENGTH // 2, 2)), jnp.arange(LENGTH), side="right"))(jax.random.split(key_list[1], SEQS)).reshape((SEQS, LENGTH)).astype(jnp.int32)
    cotangent = noise(key_list[2], (SEQS, LENGTH, D), 1.0, 6.0, ((0, 8), (1, 4)), jnp.float32)
    ln1_gain = jnp.clip(1.0 + 0.1 * jax.random.normal(key_list[3], (D,), jnp.float32), 0.5, 1.5)
    ln1_bias = noise(key_list[4], (D,), 0.5, 2.5, ((0, 8),), jnp.float32)
    w_qkv = noise(key_list[5], (D, 3 * D), D ** -0.5, 0.25, ((0, 4), (1, 8)), jnp.float32)
    w_out = noise(key_list[6], (D, D), (D // 32) ** -0.5, 1.5, ((0, 4), (1, 8)), jnp.float32)
    ln2_gain = jnp.clip(1.0 + 0.1 * jax.random.normal(key_list[7], (D,), jnp.float32), 0.5, 1.5)
    ln2_bias = noise(key_list[8], (D,), 0.5, 2.5, ((0, 8),), jnp.float32)
    w_up = noise(key_list[9], (D, FF), D ** -0.5, 0.25, ((0, 4), (1, 8)), jnp.float32)
    w_down = noise(key_list[10], (FF, D), FF ** -0.5, 0.125, ((0, 4), (1, 8)), jnp.float32)
    return dict(tokens=tokens, segments=segments, cotangent=cotangent, ln1_gain=ln1_gain, ln1_bias=ln1_bias, w_qkv=w_qkv, w_out=w_out, ln2_gain=ln2_gain, ln2_bias=ln2_bias, w_up=w_up, w_down=w_down)


EPSILON = 1e-05
MASKED = -1e+30
HIGHEST = lax.Precision.HIGHEST

@jax.custom_vjp
def low(v):
    return lax.optimization_barrier(v.astype(jnp.bfloat16)).astype(jnp.float32)

@jax.custom_vjp
def low_back(v):
    return v

def low_keep(v):
    return (low(v), None)

def low_pass(kept, grad):
    return (grad,)

def back_keep(v):
    return (v, None)

def back_low(kept, grad):
    return (low(grad),)
low.defvjp(low_keep, low_pass)
low_back.defvjp(back_keep, back_low)

def layer_norm(values, gain_vec, shift_vec):
    centre = values - lax.optimization_barrier(jnp.mean(values, axis=-1, keepdims=True))
    spread = lax.optimization_barrier(jnp.mean(centre * centre, axis=-1, keepdims=True))
    return centre * lax.rsqrt(spread + EPSILON) * gain_vec + shift_vec

def coarsen(values, group_ratio):
    batch_size, item_count, head_count, head_width = values.shape
    return lax.optimization_barrier(jnp.mean(values.reshape(batch_size, item_count // group_ratio, group_ratio, head_count, head_width), axis=2))

def seg_range(seg_block, group_ratio):
    batch_size, item_count = seg_block.shape
    grouped = seg_block.reshape(batch_size, item_count // group_ratio, group_ratio)
    return (lax.optimization_barrier(jnp.min(grouped, axis=2)), lax.optimization_barrier(jnp.max(grouped, axis=2)))

def sibling(values):
    full_shape = values.shape
    paired = values.reshape((full_shape[0], full_shape[1] // 2, 2) + full_shape[2:])
    return jnp.flip(paired, axis=2).reshape(full_shape)

def expand(values, group_ratio):
    return jnp.repeat(values, group_ratio, axis=1)

def block_part(queries, key_heads, val_heads, low_query, high_query, low_key, high_key, swapped):
    batch_size, item_count, head_count, head_width = queries.shape
    blocks = item_count // NR
    query_b = queries.reshape(batch_size, blocks, NR, head_count, head_width)
    key_b = key_heads.reshape(batch_size, blocks, NR, head_count, head_width)
    val_b = val_heads.reshape(batch_size, blocks, NR, head_count, head_width)
    low_qb = low_query.reshape(batch_size, blocks, NR)
    high_qb = high_query.reshape(batch_size, blocks, NR)
    low_kb = low_key.reshape(batch_size, blocks, NR)
    high_kb = high_key.reshape(batch_size, blocks, NR)
    if swapped:
        key_b = sibling(key_b)
        val_b = sibling(val_b)
        low_kb = sibling(low_kb)
        high_kb = sibling(high_kb)
    scores = jnp.einsum('gbihd,gbjhd->gbhij', query_b, key_b, precision=HIGHEST) * head_width ** (-0.5)
    allowed = (low_qb[..., :, None] <= high_kb[..., None, :]) & (low_kb[..., None, :] <= high_qb[..., :, None])
    scores = jnp.where(allowed[:, :, None], scores, MASKED)
    peak_score = lax.optimization_barrier(jnp.max(scores, axis=-1))
    probabilities = jnp.exp(scores - peak_score[..., None])
    weight_sum = lax.optimization_barrier(jnp.sum(probabilities, axis=-1))
    mixture = jnp.einsum('gbhij,gbjhd->gbihd', probabilities, val_b, precision=HIGHEST)
    peak_score = jnp.swapaxes(peak_score, 2, 3).reshape(batch_size, item_count, head_count)
    weight_sum = jnp.swapaxes(weight_sum, 2, 3).reshape(batch_size, item_count, head_count)
    return (peak_score, weight_sum, mixture.reshape(batch_size, item_count, head_count, head_width))

def combine(part_list):
    overall = part_list[0][0]
    for part_item in part_list[1:]:
        overall = jnp.maximum(overall, part_item[0])
    denominator = jnp.zeros_like(overall)
    numerator = jnp.zeros_like(part_list[0][2])
    for peak_score, weight_sum, mixture, group_ratio in part_list:
        factor = group_ratio * jnp.exp(peak_score - overall)
        denominator = denominator + factor * weight_sum
        numerator = numerator + factor[..., None] * mixture
    return numerator / denominator[..., None]

def attention(queries, key_heads, val_heads, seg_block):
    part_list = [block_part(queries, key_heads, val_heads, seg_block, seg_block, seg_block, seg_block, False) + (1.0,)]
    for level_index in range(LEVELS):
        group_ratio = 2 ** level_index
        low_group, high_group = seg_range(seg_block, group_ratio)
        peak_score, weight_sum, mixture = block_part(coarsen(queries, group_ratio), coarsen(key_heads, group_ratio), coarsen(val_heads, group_ratio), low_group, high_group, low_group, high_group, True)
        part_list.append((expand(peak_score, group_ratio), expand(weight_sum, group_ratio), expand(mixture, group_ratio), float(group_ratio)))
    return combine(part_list)

def block_layer(seq_block, seg_block, ln1_gain, ln1_bias, w_qkv, w_out, ln2_gain, ln2_bias, w_up, w_down):
    batch_size, seq_len, model_width = seq_block.shape
    normed = layer_norm(seq_block, ln1_gain, ln1_bias).reshape(batch_size * seq_len, model_width)
    packed = jnp.dot(normed, w_qkv, precision=HIGHEST).reshape(batch_size, seq_len, 3, HEADS, model_width // HEADS)
    attended = attention(packed[:, :, 0], packed[:, :, 1], packed[:, :, 2], seg_block).reshape(batch_size * seq_len, model_width)
    middle = seq_block + jnp.dot(attended, w_out, precision=HIGHEST).reshape(batch_size, seq_len, model_width)
    normed_two = layer_norm(middle, ln2_gain, ln2_bias).reshape(batch_size * seq_len, model_width)
    hidden = jax.nn.gelu(jnp.dot(normed_two, w_up, precision=HIGHEST))
    return middle + jnp.dot(hidden, w_down, precision=HIGHEST).reshape(batch_size, seq_len, model_width)

def reference(tokens, segments, cotangent, ln1_gain, ln1_bias, w_qkv, w_out, ln2_gain, ln2_bias, w_up, w_down):
    group_size = math.gcd(SEQS, max(1, 4096 // LENGTH))
    step_count = SEQS // group_size
    params = (ln1_gain, ln1_bias, w_qkv, w_out, ln2_gain, ln2_bias, w_up, w_down)
    token_steps = tokens.reshape(step_count, group_size, LENGTH, D)
    seg_steps = segments.reshape(step_count, group_size, LENGTH)
    cot_steps = cotangent.reshape(step_count, group_size, LENGTH, D)

    def scan_step(carry, inputs):
        seq_block, seg_block, cot_block = inputs

        def forward(block_in, gain_one, bias_one, full_qkv, full_out, gain_two, bias_two, full_up, full_down):
            return block_layer(block_in, seg_block, gain_one, bias_one, full_qkv, full_out, gain_two, bias_two, full_up, full_down)
        output, pullback = jax.vjp(forward, seq_block, *params)
        gradients = pullback(cot_block)
        return (tuple((left + right for left, right in zip(carry, gradients[1:]))), (output, gradients[0]))
    zero_sums = tuple((jnp.zeros_like(param) for param in params))
    totals, (outputs, input_grads) = lax.scan(scan_step, zero_sums, (token_steps, seg_steps, cot_steps))
    return (outputs.reshape(SEQS, LENGTH, D), input_grads.reshape(SEQS, LENGTH, D), totals[0], totals[1], totals[2], totals[3], totals[4], totals[5], totals[6], totals[7])
```

```python
import jax
import jax.numpy as jnp
import numpy as np
from jax import lax
from jax.experimental import pallas as pl
from jax.experimental.pallas import tpu as pltpu
from jax.sharding import PartitionSpec as P

HEADS = 8
NR = 16
LEVELS = 6
EPSILON = 1e-05
MASKED = -1e30
F32 = jnp.float32
BF16 = jnp.bfloat16
LN_ROWS = 16


def split(x):
    high = x.astype(BF16)
    return high, (x - high.astype(F32)).astype(BF16)


def mm(a, b, ca, cb):
    return lax.dot_general(a, b, (((ca,), (cb,)), ((), ())), preferred_element_type=F32)


def mm3(a, b, ca, cb):
    return mm(a[0], b[0], ca, cb) + mm(a[0], b[1], ca, cb) + mm(a[1], b[0], ca, cb)


def mm2(a, b, ca, cb):
    return mm(a, b[0], ca, cb) + mm(a, b[1], ca, cb)


def level_layout(length):
    rows, start = [], 0
    for level in range(1, LEVELS):
        count = length >> level
        rows.append((level, start, count))
        start += count
    return rows, start


def pooling(length):
    spread = np.zeros((length, length), np.float32)
    pool = np.zeros((length, length), np.float32)
    same = np.zeros((length, length), np.float32)
    layout, _ = level_layout(length)
    bounds = [first for _, first, _ in layout] + [length]
    for index, (level, first, count) in enumerate(layout):
        token = np.arange(length)
        spread[token, first + (token >> level)] = 1.0
        pool[first + (token >> level), token] = 0.5**level
        same[bounds[index] : bounds[index + 1], bounds[index] : bounds[index + 1]] = 1.0
    return spread, pool, same


def score_bias(seg, near, far_a, far_b):
    count, length = seg.shape
    token = np.arange(length)
    pair = (token[:, None] >> 5) == (token[None, :] >> 5)
    ok = pair[None] & (seg[:, :, None] == seg[:, None, :])
    parts = [jnp.where(ok, 0.0, MASKED)]
    for level in range(1, LEVELS):
        ratio = 1 << level

        def ends(values):
            grouped = values.reshape(count, length // ratio, ratio)
            return grouped[:, :, 0], grouped[:, :, -1]

        low_q, high_q = ends(seg)
        low_q = jnp.repeat(low_q, ratio, axis=1)
        high_q = jnp.repeat(high_q, ratio, axis=1)
        if 2 * NR * ratio <= length:
            low_k, high_k = ends(seg)
            block_q = (token >> level) >> 4
            block_k = np.arange(length >> level) >> 4
            where = (block_q[:, None] ^ 1) == block_k[None, :]
        else:
            if NR * ratio <= length:
                low_k, high_k = ends(near)
            else:
                pieces = [ends(far_a), ends(far_b)]
                low_k = jnp.concatenate([pieces[0][0], pieces[1][0]], axis=1)
                high_k = jnp.concatenate([pieces[0][1], pieces[1][1]], axis=1)
            where = np.ones((length, low_k.shape[1]), bool)
        ok = (
            where[None]
            & (low_q[:, :, None] <= high_k[:, None, :])
            & (low_k[:, None, :] <= high_q[:, :, None])
        )
        parts.append(jnp.where(ok, np.float32(level * np.log(2.0)), MASKED))
    return jnp.concatenate(parts, axis=2).astype(F32)


class Plan:
    def __init__(self, dp, fsdp):
        self.dp, self.fsdp = dp, fsdp

    def slots(self):
        return [(d, f) for d in range(self.dp) for f in range(self.fsdp)]


def assemble(scratch, refs, plan, me_d, me_f, rows, lanes):
    for d, f in plan.slots():
        row = pl.multiple_of((me_d ^ d) * rows, 8)
        col = pl.multiple_of((me_f ^ f) * lanes, 128)
        scratch[pl.ds(row, rows), pl.ds(col, lanes)] = refs[0][d, f, :rows, :]


def norm_rows(refs, plan, rows):
    total = refs[0][0, 0, rows:, :]
    for d in range(1, plan.dp):
        total = total + refs[0][d, 0, rows:, :]
    return jnp.concatenate([total[4 * i : 4 * i + 4] for i in range(4)], axis=1)


def whole(shape=None):
    return pl.BlockSpec(memory_space=pltpu.VMEM)


SMEM = pl.BlockSpec(memory_space=pltpu.SMEM)


def call(body, outs, scratch=(), **kw):
    return pl.pallas_call(
        body,
        out_shape=[jax.ShapeDtypeStruct(s, t) for s, t in outs],
        scratch_shapes=list(scratch),
        **kw,
    )


def qkv_stage(me, tokens, slots, plan, pool, seqs):
    rows_all, width = tokens.shape
    length = rows_all // seqs
    triple = 3 * width
    rows = triple // plan.dp
    lanes = width // plan.fsdp
    n4, n5 = length >> 4, length >> 5

    def body(me_ref, tok, pool_ref, *rest):
        refs = rest[: len(slots)]
        packed, wh, wl, xhat, inv, ln, s4, s5, full = rest[len(slots) :]
        assemble(full, refs, plan, me_ref[0], me_ref[1], rows, lanes)
        params = norm_rows(refs, plan, rows)
        ln[0:4, :] = params
        w = split(full[...])
        wh[...] = w[0]
        wl[...] = w[1]
        x = tok[...]
        centre = x - jnp.mean(x, axis=1, keepdims=True)
        scale = lax.rsqrt(jnp.mean(centre * centre, axis=1, keepdims=True) + EPSILON)
        xh = centre * scale
        xhat[...] = xh
        inv[...] = jnp.broadcast_to(scale, inv.shape)
        normed = xh * params[0:1, :] + params[1:2, :]
        packed[...] = mm3(split(normed), w, 1, 1)
        a24 = pool_ref[...]
        for s in range(seqs):
            for j in range(2):
                kv = packed[
                    s * length : (s + 1) * length, (j + 1) * width : (j + 2) * width
                ]
                means = mm2(a24, split(kv), 1, 0)
                s4[s, j] = means[:n4]
                s5[s, j] = means[n4 : n4 + n5]

    return call(
        body,
        [
            ((rows_all, triple), F32),
            ((triple, width), BF16),
            ((triple, width), BF16),
            ((rows_all, width), F32),
            ((rows_all, 128), F32),
            ((8, width), F32),
            ((seqs, 2, n4, width), F32),
            ((seqs, 2, n5, width), F32),
        ],
        [pltpu.VMEM((triple, width), F32)],
        in_specs=[SMEM, whole(), whole()] + [whole()] * len(slots),
        out_specs=[whole()] * 8,
    )(me, tokens, pool, *slots)


def head_tools(q, k, v, fk, fv, pool, same, local):
    length = q.shape[0]
    lane = lax.broadcasted_iota(jnp.int32, (length, 128), 1) < 64
    pooled = mm2(pool, split(jnp.concatenate([q, k, v], axis=1)), 1, 0)
    qc = pooled[:, :128]
    kc = jnp.concatenate([pooled[:local, 128:256], fk], axis=0)
    vc = jnp.concatenate([pooled[:local, 256:], fv], axis=0)

    def both(x):
        zero = jnp.zeros_like(x)
        return jnp.concatenate([jnp.where(lane, x, zero), jnp.where(lane, zero, x)], axis=0)

    return lane, both, split(both(q)), split(k), split(v), split(both(qc)), split(kc), split(vc)


def pair_scores(q2, ks, qc2, kcs, spread, same, bias):
    length = spread.shape[0]
    s0 = mm3(q2, ks, 1, 1)
    sc = mm3(qc2, kcs, 1, 1) * jnp.concatenate([same, same], axis=0)
    sch, scl = split(sc)
    st = jnp.concatenate(
        [
            mm2(spread, (sch[:length], scl[:length]), 1, 0),
            mm2(spread, (sch[length:], scl[length:]), 1, 0),
        ],
        axis=0,
    )
    b0 = bias[:, :length]
    bc = bias[:, length:]
    return s0 + jnp.concatenate([b0, b0], axis=0), st + jnp.concatenate([bc, bc], axis=0)


def attention_specs(length, width):
    pairs = width // 128
    block = lambda off: pl.BlockSpec((length, 128), lambda s, h: (s, off * pairs + h))
    far = lambda j: pl.BlockSpec((1, 1, 32, 128), lambda s, h: (s, j, 0, h))
    fixed = pl.BlockSpec((length, length), lambda s, h: (0, 0))
    bias = pl.BlockSpec((1, length, 2 * length), lambda s, h: (s, 0, 0))
    return block, far, fixed, bias


def attention_forward(packed, far, bias, spread, pool, same, seqs, local):
    rows_all, triple = packed.shape
    width = triple // 3
    length = rows_all // seqs
    block, far_spec, fixed, bias_spec = attention_specs(length, width)

    def body(q_ref, k_ref, v_ref, fk, fv, bias_ref, spread_ref, pool_ref, same_ref, out, lse):
        lane, both, q2, ks, vs, qc2, kcs, vcs = head_tools(
            q_ref[...] * 0.125,
            k_ref[...],
            v_ref[...],
            fk[0, 0],
            fv[0, 0],
            pool_ref[...],
            same_ref[...],
            local,
        )
        s0, st = pair_scores(q2, ks, qc2, kcs, spread_ref[...], same_ref[...], bias_ref[0])
        peak = jnp.maximum(
            jnp.max(s0, axis=1, keepdims=True), jnp.max(st, axis=1, keepdims=True)
        )
        p0 = jnp.exp(s0 - peak)
        pc = jnp.exp(st - peak)
        total = jnp.sum(p0, axis=1, keepdims=True) + jnp.sum(pc, axis=1, keepdims=True)
        mixed = (mm3(split(p0), vs, 1, 0) + mm3(split(pc), vcs, 1, 0)) / total
        out[...] = jnp.where(lane, mixed[:length], mixed[length:])
        logs = peak + jnp.log(total)
        lse[...] = jnp.where(lane, logs[:length], logs[length:])

    return pl.pallas_call(
        body,
        grid=(seqs, width // 128),
        out_shape=[jax.ShapeDtypeStruct((rows_all, width), F32)] * 2,
        in_specs=[
            block(0),
            block(1),
            block(2),
            far_spec(0),
            far_spec(1),
            bias_spec,
            fixed,
            fixed,
            fixed,
        ],
        out_specs=[block(0), block(0)],
    )(packed, packed, packed, far, far, bias, spread, pool, same)


def attention_backward(packed, far, bias, spread, pool, same, attended, lse, grad, seqs, local):
    rows_all, triple = packed.shape
    width = triple // 3
    length = rows_all // seqs
    block, far_spec, fixed, bias_spec = attention_specs(length, width)
    n4, n5 = length >> 4, length >> 5

    def body(
        q_ref,
        k_ref,
        v_ref,
        fk,
        fv,
        bias_ref,
        spread_ref,
        pool_ref,
        same_ref,
        o_ref,
        lse_ref,
        g_ref,
        dq_ref,
        dk_ref,
        dv_ref,
        f4,
        f5a,
        f5b,
    ):
        pool_m = pool_ref[...]
        spread_m = spread_ref[...]
        lane, both, q2, ks, vs, qc2, kcs, vcs = head_tools(
            q_ref[...] * 0.125,
            k_ref[...],
            v_ref[...],
            fk[0, 0],
            fv[0, 0],
            pool_m,
            same_ref[...],
            local,
        )
        s0, st = pair_scores(q2, ks, qc2, kcs, spread_m, same_ref[...], bias_ref[0])
        logs = lse_ref[...]
        logs2 = jnp.concatenate([logs[:, 0:1], logs[:, 64:65]], axis=0)
        p0 = jnp.exp(s0 - logs2)
        pc = jnp.exp(st - logs2)
        g2f = both(g_ref[...])
        g2 = split(g2f)
        o_val = o_ref[...]
        delta = jnp.sum(g2f * jnp.concatenate([o_val, o_val], axis=0), axis=1, keepdims=True)
        dv = mm3(split(p0), g2, 0, 0)
        dvc = mm3(split(pc), g2, 0, 0)
        d0 = split(p0 * (mm3(g2, vs, 1, 1) - delta))
        dt = split(pc * (mm3(g2, vcs, 1, 1) - delta))
        dq2 = mm3(d0, ks, 1, 0)
        dk = mm3(d0, q2, 0, 0)
        dsc = jnp.concatenate(
            [
                mm2_left((dt[0][:length], dt[1][:length]), spread_m),
                mm2_left((dt[0][length:], dt[1][length:]), spread_m),
            ],
            axis=0,
        )
        dsc = split(dsc * jnp.concatenate([same_ref[...], same_ref[...]], axis=0))
        dqc2 = mm3(dsc, kcs, 1, 0)
        dkc = mm3(dsc, qc2, 0, 0)
        dqc = jnp.where(lane, dqc2[:length], dqc2[length:])
        near = lax.broadcasted_iota(jnp.int32, (length, 128), 0) < local
        zero = jnp.zeros((length, 128), F32)
        stacked = jnp.concatenate(
            [dqc, jnp.where(near, dkc, zero), jnp.where(near, dvc, zero)], axis=1
        )
        back = mm2(pool_m, split(stacked), 0, 0)
        dq_ref[...] = (jnp.where(lane, dq2[:length], dq2[length:]) + back[:, :128]) * 0.125
        dk_ref[...] = dk + back[:, 128:256]
        dv_ref[...] = dv + back[:, 256:]
        for j, value in ((0, dkc), (1, dvc)):
            f4[0, j] = value[local : local + n4]
            f5a[0, j] = value[local + n4 : local + n4 + n5]
            f5b[0, j] = value[local + n4 + n5 :]

    far_out = lambda n: pl.BlockSpec((1, 2, n, 128), lambda s, h: (s, 0, 0, h))
    return pl.pallas_call(
        body,
        grid=(seqs, width // 128),
        out_shape=[jax.ShapeDtypeStruct((rows_all, width), F32)] * 3
        + [jax.ShapeDtypeStruct((seqs, 2, n, width), F32) for n in (n4, n5, n5)],
        in_specs=[
            block(0),
            block(1),
            block(2),
            far_spec(0),
            far_spec(1),
            bias_spec,
            fixed,
            fixed,
            fixed,
            block(0),
            block(0),
            block(0),
        ],
        out_specs=[block(0)] * 3 + [far_out(n4), far_out(n5), far_out(n5)],
    )(packed, packed, packed, far, far, bias, spread, pool, same, attended, lse, grad)


def mm2_left(a, b):
    return mm(b, a[0], 0, 0) + mm(b, a[1], 0, 0)


def middle_stage(me, tokens, attended, slots, plan):
    rows_all, width = tokens.shape
    rows, lanes = width // plan.dp, width // plan.fsdp

    def body(me_ref, tok, att, *rest):
        refs = rest[: len(slots)]
        middle, xhat, inv, wh, wl, full = rest[len(slots) :]
        assemble(full, refs, plan, me_ref[0], me_ref[1], rows, lanes)
        w = split(full[...])
        wh[...] = w[0]
        wl[...] = w[1]
        x = tok[...] + mm3(split(att[...]), w, 1, 1)
        middle[...] = x
        centre = x - jnp.mean(x, axis=1, keepdims=True)
        scale = lax.rsqrt(jnp.mean(centre * centre, axis=1, keepdims=True) + EPSILON)
        xhat[...] = centre * scale
        inv[...] = jnp.broadcast_to(scale, inv.shape)

    return call(
        body,
        [
            ((rows_all, width), F32),
            ((rows_all, width), F32),
            ((rows_all, 128), F32),
            ((width, width), BF16),
            ((width, width), BF16),
        ],
        [pltpu.VMEM((width, width), F32)],
        in_specs=[SMEM, whole(), whole()] + [whole()] * len(slots),
        out_specs=[whole()] * 5,
    )(me, tokens, attended, *slots)


def grad_hidden_stage(me, cot, slots, plan, hidden_width):
    rows_all, width = cot.shape
    rows, lanes = width // plan.dp, hidden_width // plan.fsdp

    def body(me_ref, cot_ref, *rest):
        refs = rest[: len(slots)]
        gh, wh, wl, full = rest[len(slots) :]
        assemble(full, refs, plan, me_ref[0], me_ref[1], rows, lanes)
        w = split(full[...])
        wh[...] = w[0]
        wl[...] = w[1]
        gh[...] = mm3(split(cot_ref[...]), w, 1, 0)

    return call(
        body,
        [
            ((rows_all, hidden_width), F32),
            ((width, hidden_width), BF16),
            ((width, hidden_width), BF16),
        ],
        [pltpu.VMEM((width, hidden_width), F32)],
        in_specs=[SMEM, whole()] + [whole()] * len(slots),
        out_specs=[whole()] * 3,
    )(me, cot, *slots)


def hidden_stage(me, xhat, ln, gh, slots, plan):
    rows_all, width = xhat.shape
    hidden_width = gh.shape[1]
    rows, lanes = hidden_width // plan.dp, width // plan.fsdp
    chunk = 512
    steps = hidden_width // chunk
    root = float(np.sqrt(2.0 / np.pi))

    def body(me_ref, xhat_ref, ln_ref, gh_ref, *rest):
        refs = rest[: len(slots)]
        hh, hl, ph, plo, wh, wl, full, nh, nl = rest[len(slots) :]
        step = pl.program_id(0)

        @pl.when(step == 0)
        def _():
            assemble(full, refs, plan, me_ref[0], me_ref[1], rows, lanes)
            w = split(full[...])
            wh[...] = w[0]
            wl[...] = w[1]
            n = split(xhat_ref[...] * ln_ref[2:3, :] + ln_ref[3:4, :])
            nh[...] = n[0]
            nl[...] = n[1]

        part = pl.ds(pl.multiple_of(step * chunk, chunk), chunk)
        v = mm3((nh[...], nl[...]), (wh[part, :], wl[part, :]), 1, 1)
        square = v * v
        t = jnp.tanh(root * v * (1.0 + 0.044715 * square))
        half = 0.5 * (1.0 + t)
        h = split(v * half)
        hh[...] = h[0]
        hl[...] = h[1]
        slope = half + 0.5 * v * (1.0 - t * t) * root * (1.0 + 3 * 0.044715 * square)
        g = split(gh_ref[...] * slope)
        ph[...] = g[0]
        plo[...] = g[1]

    fixed = lambda shape: pl.BlockSpec(shape, lambda i: (0,) * len(shape))
    cols = pl.BlockSpec((rows_all, chunk), lambda i: (0, i))
    return pl.pallas_call(
        body,
        grid=(steps,),
        out_shape=[jax.ShapeDtypeStruct((rows_all, hidden_width), BF16)] * 4
        + [jax.ShapeDtypeStruct((hidden_width, width), BF16)] * 2,
        in_specs=[SMEM, fixed((rows_all, width)), fixed((8, width)), cols]
        + [fixed(s.shape) for s in slots],
        out_specs=[cols] * 4 + [fixed((hidden_width, width))] * 2,
        scratch_shapes=[
            pltpu.VMEM((hidden_width, width), F32),
            pltpu.VMEM((rows_all, width), BF16),
            pltpu.VMEM((rows_all, width), BF16),
        ],
    )(me, xhat, ln, gh, *slots)


def grad_down_stage(me, cot, hh, hl, plan):
    rows_all, width = cot.shape
    hidden_width = hh.shape[1]
    rows, lanes = width // plan.dp, hidden_width // plan.fsdp

    def body(me_ref, cot_ref, hh_ref, hl_ref, out):
        res = mm3(split(cot_ref[...]), (hh_ref[...], hl_ref[...]), 0, 0)
        for d in range(plan.dp):
            out[d ^ me_ref[0], 0] = res[d * rows : (d + 1) * rows, :]

    grid_spec = pltpu.PrefetchScalarGridSpec(
        num_scalar_prefetch=1,
        grid=(plan.fsdp,),
        in_specs=[
            pl.BlockSpec((rows_all, width), lambda i, m: (0, 0)),
            pl.BlockSpec((rows_all, lanes), lambda i, m: (0, m[1] ^ i)),
            pl.BlockSpec((rows_all, lanes), lambda i, m: (0, m[1] ^ i)),
        ],
        out_specs=pl.BlockSpec((plan.dp, 1, rows, lanes), lambda i, m: (0, i, 0, 0)),
    )
    return pl.pallas_call(
        body,
        grid_spec=grid_spec,
        out_shape=jax.ShapeDtypeStruct((plan.dp, plan.fsdp, rows, lanes), F32),
    )(me, cot, hh, hl)


def grad_up_stage(me, xhat, ln, ph, plo, plan):
    rows_all, width = xhat.shape
    hidden_width = ph.shape[1]
    rows, lanes = hidden_width // plan.dp, width // plan.fsdp
    chunk = 512
    steps = hidden_width // chunk
    per = chunk // rows

    def body(me_ref, xhat_ref, ln_ref, ph_ref, pl_ref, out, nh, nl):
        step = pl.program_id(0)

        @pl.when(step == 0)
        def _():
            n = split(xhat_ref[...] * ln_ref[2:3, :] + ln_ref[3:4, :])
            nh[...] = n[0]
            nl[...] = n[1]

        res = mm3((ph_ref[...], pl_ref[...]), (nh[...], nl[...]), 0, 0)
        for i in range(per):
            for f in range(plan.fsdp):
                d = step * per + i
                out[d ^ me_ref[0], f ^ me_ref[1]] = res[
                    i * rows : (i + 1) * rows, f * lanes : (f + 1) * lanes
                ]

    fixed = lambda shape: pl.BlockSpec(shape, lambda i: (0,) * len(shape))
    cols = pl.BlockSpec((rows_all, chunk), lambda i: (0, i))
    shape = (plan.dp, plan.fsdp, rows, lanes)
    return pl.pallas_call(
        body,
        grid=(steps,),
        out_shape=jax.ShapeDtypeStruct(shape, F32),
        in_specs=[SMEM, fixed((rows_all, width)), fixed((8, width)), cols, cols],
        out_specs=fixed(shape),
        scratch_shapes=[pltpu.VMEM((rows_all, width), BF16)] * 2,
    )(me, xhat, ln, ph, plo)


def norm_back(e, gain, xhat, inv):
    u = e * gain
    mean_u = jnp.mean(u, axis=1, keepdims=True)
    mean_ux = jnp.mean(u * xhat, axis=1, keepdims=True)
    return inv * (u - mean_u - xhat * mean_ux)


def output_stage(middle, cot, xhat, inv, ln, hh, hl, ph, plo, dh, dl, uh, ul):
    rows_all, width = middle.shape
    hidden_width = hh.shape[1]
    chunk = 512
    steps = hidden_width // chunk

    def body(mid, cot_ref, xhat_ref, inv_ref, ln_ref, h0, h1, p0, p1, d0, d1, u0, u1, out, gm, gln, acc):
        step = pl.program_id(0)

        @pl.when(step == 0)
        def _():
            out[...] = mid[...]
            acc[...] = jnp.zeros_like(acc)

        out[...] += mm3((h0[...], h1[...]), (d0[...], d1[...]), 1, 1)
        acc[...] += mm3((p0[...], p1[...]), (u0[...], u1[...]), 1, 0)

        @pl.when(step == steps - 1)
        def _():
            e = acc[...]
            xh = xhat_ref[...]
            gm[...] = cot_ref[...] + norm_back(e, ln_ref[2:3, :], xh, inv_ref[:, 0:1])
            gln[0:1, :] = jnp.sum(e * xh, axis=0, keepdims=True)
            gln[1:2, :] = jnp.sum(e, axis=0, keepdims=True)

    fixed = lambda shape: pl.BlockSpec(shape, lambda i: (0,) * len(shape))
    cols = pl.BlockSpec((rows_all, chunk), lambda i: (0, i))
    act = fixed((rows_all, width))
    return pl.pallas_call(
        body,
        grid=(steps,),
        out_shape=[
            jax.ShapeDtypeStruct((rows_all, width), F32),
            jax.ShapeDtypeStruct((rows_all, width), F32),
            jax.ShapeDtypeStruct((8, width), F32),
        ],
        in_specs=[act, act, act, fixed((rows_all, 128)), fixed((8, width))]
        + [cols] * 4
        + [pl.BlockSpec((width, chunk), lambda i: (0, i))] * 2
        + [pl.BlockSpec((chunk, width), lambda i: (i, 0))] * 2,
        out_specs=[act, act, fixed((8, width))],
        scratch_shapes=[pltpu.VMEM((rows_all, width), F32)],
    )(middle, cot, xhat, inv, ln, hh, hl, ph, plo, dh, dl, uh, ul)


def mixture_grad_stage(me, gm, attended, oh, ol, plan):
    rows_all, width = gm.shape
    rows, lanes = width // plan.dp, width // plan.fsdp

    def body(me_ref, gm_ref, att, oh_ref, ol_ref, gmix, out):
        g = split(gm_ref[...])
        gmix[...] = mm3(g, (oh_ref[...], ol_ref[...]), 1, 0)
        res = mm3(g, split(att[...]), 0, 0)
        for d in range(plan.dp):
            for f in range(plan.fsdp):
                out[d ^ me_ref[0], f ^ me_ref[1]] = res[
                    d * rows : (d + 1) * rows, f * lanes : (f + 1) * lanes
                ]

    return call(
        body,
        [((rows_all, width), F32), ((plan.dp, plan.fsdp, rows, lanes), F32)],
        in_specs=[SMEM] + [whole()] * 4,
        out_specs=[whole()] * 2,
    )(me, gm, attended, oh, ol)


def input_grad_stage(dq, dk, dv, g4, g5a, g5b, pool, wqh, wql, xhat, inv, ln, gm, gln, seqs):
    rows_all, width = dq.shape
    length = rows_all // seqs

    def body(dq_r, dk_r, dv_r, g4_r, g5a_r, g5b_r, pool_r, wh, wl, xhat_r, inv_r, ln_r, gm_r, gln_r, gph, gpl, gtok, lrow):
        for j, ref in ((0, None), (1, dk_r), (2, dv_r)):
            for s in range(seqs):
                rs = slice(s * length, (s + 1) * length)
                if j == 0:
                    value = dq_r[rs, :]
                else:
                    groups = jnp.concatenate(
                        [g4_r[s, j - 1], g5a_r[s, j - 1] + g5b_r[s, j - 1]], axis=0
                    )
                    value = ref[rs, :] + mm2(pool_r[...], split(groups), 0, 0)
                h = split(value)
                gph[rs, j * width : (j + 1) * width] = h[0]
                gpl[rs, j * width : (j + 1) * width] = h[1]
        e = mm3((gph[...], gpl[...]), (wh[...], wl[...]), 1, 0)
        xh = xhat_r[...]
        gtok[...] = gm_r[...] + norm_back(e, ln_r[0:1, :], xh, inv_r[:, 0:1])
        sums = [
            jnp.sum(e * xh, axis=0, keepdims=True),
            jnp.sum(e, axis=0, keepdims=True),
            gln_r[0:1, :],
            gln_r[1:2, :],
        ]
        for i in range(4):
            for p in range(4):
                lrow[4 * i + p : 4 * i + p + 1, :] = sums[p][:, 128 * i : 128 * (i + 1)]

    return call(
        body,
        [
            ((rows_all, 3 * width), BF16),
            ((rows_all, 3 * width), BF16),
            ((rows_all, width), F32),
            ((LN_ROWS, 128), F32),
        ],
        in_specs=[whole()] * 14,
        out_specs=[whole()] * 4,
    )(dq, dk, dv, g4, g5a, g5b, pool, wqh, wql, xhat, inv, ln, gm, gln)


def grad_qkv_stage(me, gph, gpl, xhat, ln, lrow, plan):
    rows_all, triple = gph.shape
    width = triple // 3
    rows, lanes = triple // plan.dp, width // plan.fsdp

    def body(me_ref, gph_r, gpl_r, xhat_r, ln_r, lrow_r, out):
        n = split(xhat_r[...] * ln_r[0:1, :] + ln_r[1:2, :])
        res = mm3((gph_r[...], gpl_r[...]), n, 0, 0)
        tail = lrow_r[...]
        for d in range(plan.dp):
            for f in range(plan.fsdp):
                out[d ^ me_ref[0], f ^ me_ref[1], :rows, :] = res[
                    d * rows : (d + 1) * rows, f * lanes : (f + 1) * lanes
                ]
                out[d, f, rows:, :] = tail

    return call(
        body,
        [((plan.dp, plan.fsdp, rows + LN_ROWS, lanes), F32)],
        in_specs=[SMEM] + [whole()] * 5,
        out_specs=[whole()],
    )(me, gph, gpl, xhat, ln, lrow)[0]


def swap(x, mask, axis="fsdp"):
    size = lax.axis_size(axis)
    return lax.ppermute(x, axis, [(i, i ^ mask) for i in range(size)])


def gather(piece, plan):
    out = lax.all_gather(piece, ("dp", "fsdp"), axis=0, tiled=False)
    return [out.reshape((plan.dp, plan.fsdp) + piece.shape)]


def reduce_pieces(pieces, plan):
    flat = pieces.reshape((plan.dp * plan.fsdp,) + pieces.shape[2:])
    return lax.psum_scatter(flat, ("dp", "fsdp"), scatter_dimension=0, tiled=False)


def local(
    tokens, segments, cotangent, ln1_gain, ln1_bias, w_qkv, w_out, ln2_gain, ln2_bias, w_up, w_down
):
    seqs, length, width = tokens.shape
    dp, fsdp = lax.axis_size("dp"), lax.axis_size("fsdp")
    plan = Plan(dp, fsdp)
    me_d = lax.axis_index("dp")
    me = jnp.zeros((2,), jnp.int32)
    rows_all = seqs * length
    hidden_width = w_down.shape[0] * fsdp

    spread, pool, same = pooling(length)
    layout, _ = level_layout(length)
    local_rows = [first for level, first, _ in layout if 2 * NR * (1 << level) > length][0]
    spread_c = jnp.asarray(spread, BF16)
    pool_c = jnp.asarray(pool, BF16)
    same_c = jnp.asarray(same, F32)
    far_pool = jnp.asarray(pool[local_rows : local_rows + (length >> 4) + (length >> 5)], BF16)

    share = width // dp
    norms = jnp.stack([ln1_gain, ln1_bias, ln2_gain, ln2_bias])
    placed = lax.dynamic_update_slice(jnp.zeros((4, width), F32), norms, (0, me_d * share))
    placed = placed.reshape(4, 4, 128).transpose(1, 0, 2).reshape(LN_ROWS, 128)
    qkv_slots = gather(jnp.concatenate([w_qkv.T, placed], axis=0), plan)
    near, far_a, far_b = (swap(segments, m) for m in (1, 2, 3))
    bias = score_bias(segments, near, far_a, far_b)
    down_slots = gather(w_down.T, plan)
    out_slots = gather(w_out.T, plan)
    up_slots = gather(w_up.T, plan)

    tok = tokens.reshape(rows_all, width)
    cot = cotangent.reshape(rows_all, width)
    packed, wqh, wql, xhat1, inv1, ln, s4, s5 = qkv_stage(
        me, tok, qkv_slots, plan, far_pool, seqs
    )
    far = jnp.concatenate([swap(s4, 1), swap(s5, 2), swap(s5, 3)], axis=2)
    attended, lse = attention_forward(
        packed, far, bias, spread_c, pool_c, same_c, seqs, local_rows
    )
    middle, xhat2, inv2, oh, ol = middle_stage(me, tok, attended, out_slots, plan)
    gh, dh, dl = grad_hidden_stage(me, cot, down_slots, plan, hidden_width)
    hh, hl, ph, plo, uh, ul = hidden_stage(me, xhat2, ln, gh, up_slots, plan)
    g_down = reduce_pieces(grad_down_stage(me, cot, hh, hl, plan), plan)
    g_up = reduce_pieces(grad_up_stage(me, xhat2, ln, ph, plo, plan), plan)
    output, gm, gln = output_stage(
        middle, cot, xhat2, inv2, ln, hh, hl, ph, plo, dh, dl, uh, ul
    )
    gmix, out_pieces = mixture_grad_stage(me, gm, attended, oh, ol, plan)
    g_out = reduce_pieces(out_pieces, plan)
    dq, dk, dv, f4, f5a, f5b = attention_backward(
        packed, far, bias, spread_c, pool_c, same_c, attended, lse, gmix, seqs, local_rows
    )
    g4, g5a, g5b = swap(f4, 1), swap(f5a, 2), swap(f5b, 3)
    gph, gpl, gtok, lrow = input_grad_stage(
        dq, dk, dv, g4, g5a, g5b, far_pool, wqh, wql, xhat1, inv1, ln, gm, gln, seqs
    )
    g_qkv = reduce_pieces(grad_qkv_stage(me, gph, gpl, xhat1, ln, lrow, plan), plan)
    rows = g_qkv.shape[0] - LN_ROWS
    sums = g_qkv[rows:].reshape(4, 4, 128).transpose(1, 0, 2).reshape(4, width)
    mine = lax.dynamic_slice(sums, (0, me_d * share), (4, share))
    shape = tokens.shape
    return (
        output.reshape(shape),
        gtok.reshape(shape),
        mine[0],
        mine[1],
        g_qkv[:rows].T,
        g_out.T,
        mine[2],
        mine[3],
        g_up.T,
        g_down.T,
    )


def solution(mesh):
    weight = P("fsdp", "dp")
    rows = P("dp", "fsdp", None)
    vector = P("dp")
    return jax.shard_map(
        local,
        mesh=mesh,
        in_specs=(rows, P("dp", "fsdp"), rows, vector, vector, weight, weight, vector, vector, weight, weight),
        out_specs=(rows, rows, vector, vector, weight, weight, vector, vector, weight, weight),
        check_vma=False,
    )
```

```python
import jax
import jax.numpy as jnp
import numpy as np
from jax import lax
from jax.experimental import pallas as pl
from jax.experimental.pallas import tpu as pltpu
from jax.sharding import PartitionSpec as P

HEADS = 8
NR = 16
LEVELS = 6
EPSILON = 1e-05
MASKED = -1e30
F32 = jnp.float32
BF16 = jnp.bfloat16
LN_ROWS = 16


def split(x):
    high = x.astype(BF16)
    return high, (x - high.astype(F32)).astype(BF16)


def mm(a, b, ca, cb):
    return lax.dot_general(a, b, (((ca,), (cb,)), ((), ())), preferred_element_type=F32)


def mm3(a, b, ca, cb):
    return mm(a[0], b[0], ca, cb) + mm(a[0], b[1], ca, cb) + mm(a[1], b[0], ca, cb)


def mm2(a, b, ca, cb):
    return mm(a, b[0], ca, cb) + mm(a, b[1], ca, cb)


def level_layout(length):
    rows, start = [], 0
    for level in range(1, LEVELS):
        count = length >> level
        rows.append((level, start, count))
        start += count
    return rows, start


def pooling(length):
    spread = np.zeros((length, length), np.float32)
    pool = np.zeros((length, length), np.float32)
    same = np.zeros((length, length), np.float32)
    layout, _ = level_layout(length)
    bounds = [first for _, first, _ in layout] + [length]
    for index, (level, first, count) in enumerate(layout):
        token = np.arange(length)
        spread[token, first + (token >> level)] = 1.0
        pool[first + (token >> level), token] = 0.5**level
        same[bounds[index] : bounds[index + 1], bounds[index] : bounds[index + 1]] = 1.0
    return spread, pool, same


def score_bias(seg, near, far_a, far_b):
    count, length = seg.shape
    token = np.arange(length)
    pair = (token[:, None] >> 5) == (token[None, :] >> 5)
    ok = pair[None] & (seg[:, :, None] == seg[:, None, :])
    parts = [jnp.where(ok, 0.0, MASKED)]
    for level in range(1, LEVELS):
        ratio = 1 << level

        def ends(values):
            grouped = values.reshape(count, length // ratio, ratio)
            return grouped[:, :, 0], grouped[:, :, -1]

        low_q, high_q = ends(seg)
        low_q = jnp.repeat(low_q, ratio, axis=1)
        high_q = jnp.repeat(high_q, ratio, axis=1)
        if 2 * NR * ratio <= length:
            low_k, high_k = ends(seg)
            block_q = (token >> level) >> 4
            block_k = np.arange(length >> level) >> 4
            where = (block_q[:, None] ^ 1) == block_k[None, :]
        else:
            if NR * ratio <= length:
                low_k, high_k = ends(near)
            else:
                pieces = [ends(far_a), ends(far_b)]
                low_k = jnp.concatenate([pieces[0][0], pieces[1][0]], axis=1)
                high_k = jnp.concatenate([pieces[0][1], pieces[1][1]], axis=1)
            where = np.ones((length, low_k.shape[1]), bool)
        ok = (
            where[None]
            & (low_q[:, :, None] <= high_k[:, None, :])
            & (low_k[:, None, :] <= high_q[:, :, None])
        )
        parts.append(jnp.where(ok, np.float32(level * np.log(2.0)), MASKED))
    return jnp.concatenate(parts, axis=2).astype(F32)


class Plan:
    def __init__(self, dp, fsdp):
        self.dp, self.fsdp = dp, fsdp
        self.dims = {}
        names = ["x", "z", "w"]
        bit = 1
        while bit < dp:
            name = names[len(self.dims)] if len(self.dims) < 3 else "d%d" % bit
            self.dims[name] = ("dp", bit)
            bit *= 2
        self.wide = tuple(reversed(list(self.dims)))
        self.dims["y"] = ("fsdp", 2)
        self.dims["c"] = ("fsdp", 1)
        self.tuned = (dp, fsdp) == (8, 4)

    def orders(self, text):
        if self.tuned:
            return [tuple(order) for order in text.split()]
        return [self.wide + ("y",)]

    def mask(self, names):
        d = f = 0
        for name in names:
            axis, bit = self.dims[name]
            if axis == "dp":
                d |= bit
            else:
                f |= bit
        return d, f

    def send(self, x, name):
        axis, bit = self.dims[name]
        size = self.dp if axis == "dp" else self.fsdp
        return lax.ppermute(x, axis, [(i, i ^ bit) for i in range(size)])

    def position(self, order, d, f):
        pos = 0
        for name in order:
            axis, bit = self.dims[name]
            value = d if axis == "dp" else f
            pos = pos * 2 + ((value // bit) & 1)
        return pos


def cut_rows(rows, parts, first):
    if parts == 1:
        return [(0, rows)]
    return [(0, first), (first, rows - first)]


class Gathered:
    def __init__(self):
        self.arrays, self.parts = [], []

    def add(self, array, names, base, spans):
        offset = 0
        for order, (start, count) in spans:
            self.parts.append((len(self.arrays), order[:names], base, start, count, offset))
            offset += count
        self.arrays.append(array)


def gather(plan, piece, orders, first):
    spans = list(zip(orders, cut_rows(piece.shape[0], len(orders), first)))
    held = [(piece[start : start + count][None], [(o, (start, count))]) for o, (start, count) in spans]
    if len(held) == 2 and orders[0][0] == orders[1][0]:
        held = [(piece[None], spans)]
    result = Gathered()
    stages = len(orders[0])
    for stage in range(stages):
        dims = {o[stage] for _, part in held for o, _ in part}
        if len(held) == 2 and len(dims) == 1:
            held = [(jnp.concatenate([held[0][0], held[1][0]], axis=1), held[0][1] + held[1][1])]
        elif len(held) == 1 and len(dims) == 2:
            array, part = held[0]
            cut = part[0][1][1]
            held = [(array[:, :cut], part[:1]), (array[:, cut:], part[1:])]
        got = [plan.send(array, part[0][0][stage]) for array, part in held]
        if stage < stages - 1:
            held = [
                (jnp.concatenate([array, new], axis=0), part) for (array, part), new in zip(held, got)
            ]
    for (array, part), new in zip(held, got):
        last = part[0][0][stages - 1]
        for core in ((), ("c",)):
            for value, base in ((array, ()), (new, (last,))):
                moved = plan.send(value, "c") if core else value
                result.add(moved, stages - 1, base + core, part)
    return result


def assemble(scratch, refs, gathered, plan, me_d, me_f, rows, lanes, segments):
    for index, names, base, start, count, offset in gathered.parts:
        base_d, base_f = plan.mask(base)
        for slot in range(1 << len(names)):
            d, f = plan.mask([n for i, n in enumerate(names) if (slot >> i) & 1])
            row0 = (me_d ^ (d | base_d)) * rows
            col0 = (me_f ^ (f | base_f)) * lanes
            for source, size, to_row, to_lane in segments:
                low, high = max(source, start), min(source + size, start + count)
                if low < high:
                    row = pl.multiple_of(row0 + (to_row + low - source), 8)
                    col = pl.multiple_of(col0 + to_lane, 128)
                    at = offset + low - start
                    scratch[pl.ds(row, high - low), pl.ds(col, 128)] = refs[index][
                        slot, at : at + high - low, :
                    ]


def norm_rows(refs, gathered, plan):
    total = None
    for index, names, base, start, count, offset in gathered.parts:
        if start or plan.mask(base)[1]:
            continue
        for slot in range(1 << len(names)):
            if plan.mask([n for i, n in enumerate(names) if (slot >> i) & 1])[1]:
                continue
            value = refs[index][slot, offset : offset + LN_ROWS, :]
            total = value if total is None else total + value
    return jnp.concatenate([total[4 * i : 4 * i + 4] for i in range(4)], axis=1)


class Stream:
    def __init__(self, plan, rows, orders, first=0):
        self.plan, self.rows, self.orders = plan, rows, orders
        self.spans = cut_rows(rows, len(orders), first)
        self.slots = plan.dp * plan.fsdp // 2

    def shapes(self):
        return [(self.slots, count, 128) for _, count in self.spans]

    def put(self, outs, d, f, row, value):
        size = value.shape[0]
        for ref, order, (start, count) in zip(outs, self.orders, self.spans):
            low, high = max(row, start), min(row + size, start + count)
            if low < high:
                ref[self.plan.position(order, d, f), low - start : high - start, :] = value[
                    low - row : high - row
                ]

    def reduce(self, away, keep):
        plan, parts = self.plan, range(len(self.orders))
        terms = [[keep[i], plan.send(away[i], "c")] for i in parts]
        half = self.slots // 2
        for stage in range(len(self.orders[0])):
            out = [sum(t[half : 2 * half] for t in terms[i]) for i in parts]
            names = [order[stage] for order in self.orders]
            if len(set(names)) == 1 and len(names) == 2:
                cut = self.spans[0][1]
                got = plan.send(jnp.concatenate(out, axis=1), names[0])
                got = [got[:, :cut], got[:, cut:]]
            else:
                got = [plan.send(o, n) for o, n in zip(out, names)]
            for i in parts:
                terms[i].append(got[i])
            half //= 2
        return jnp.concatenate([sum(t[0] for t in terms[i]) for i in parts], axis=0)


def whole(shape=None):
    return pl.BlockSpec(memory_space=pltpu.VMEM)


SMEM = pl.BlockSpec(memory_space=pltpu.SMEM)


def call(body, outs, scratch=(), **kw):
    return pl.pallas_call(
        body,
        out_shape=[jax.ShapeDtypeStruct(s, t) for s, t in outs],
        scratch_shapes=list(scratch),
        **kw,
    )


def qkv_stage(me, tokens, gathered, plan, pool, seqs):
    rows_all, width = tokens.shape
    length = rows_all // seqs
    triple = 3 * width
    rows = triple // plan.dp
    lanes = width // plan.fsdp
    n4, n5 = length >> 4, length >> 5
    slots = gathered.arrays

    def body(me_ref, tok, pool_ref, *rest):
        refs = rest[: len(slots)]
        packed, wh, wl, xhat, inv, ln, s4, s5, full = rest[len(slots) :]
        segments = [(LN_ROWS, rows, 0, 0)]
        assemble(full, refs, gathered, plan, me_ref[0], me_ref[1], rows, lanes, segments)
        params = norm_rows(refs, gathered, plan)
        ln[0:4, :] = params
        w = split(full[...])
        wh[...] = w[0]
        wl[...] = w[1]
        x = tok[...]
        centre = x - jnp.mean(x, axis=1, keepdims=True)
        scale = lax.rsqrt(jnp.mean(centre * centre, axis=1, keepdims=True) + EPSILON)
        xh = centre * scale
        xhat[...] = xh
        inv[...] = jnp.broadcast_to(scale, inv.shape)
        normed = xh * params[0:1, :] + params[1:2, :]
        packed[...] = mm3(split(normed), w, 1, 1)
        a24 = pool_ref[...]
        for s in range(seqs):
            for j in range(2):
                kv = packed[
                    s * length : (s + 1) * length, (j + 1) * width : (j + 2) * width
                ]
                means = mm2(a24, split(kv), 1, 0)
                s4[s, j] = means[:n4]
                s5[s, j] = means[n4 : n4 + n5]

    return call(
        body,
        [
            ((rows_all, triple), F32),
            ((triple, width), BF16),
            ((triple, width), BF16),
            ((rows_all, width), F32),
            ((rows_all, 128), F32),
            ((8, width), F32),
            ((seqs, 2, n4, width), F32),
            ((seqs, 2, n5, width), F32),
        ],
        [pltpu.VMEM((triple, width), F32)],
        in_specs=[SMEM, whole(), whole()] + [whole()] * len(slots),
        out_specs=[whole()] * 8,
    )(me, tokens, pool, *slots)


def head_tools(q, k, v, fk, fv, pool, same, local):
    length = q.shape[0]
    lane = lax.broadcasted_iota(jnp.int32, (length, 128), 1) < 64
    pooled = mm2(pool, split(jnp.concatenate([q, k, v], axis=1)), 1, 0)
    qc = pooled[:, :128]
    kc = jnp.concatenate([pooled[:local, 128:256], fk], axis=0)
    vc = jnp.concatenate([pooled[:local, 256:], fv], axis=0)

    def both(x):
        zero = jnp.zeros_like(x)
        return jnp.concatenate([jnp.where(lane, x, zero), jnp.where(lane, zero, x)], axis=0)

    return lane, both, split(both(q)), split(k), split(v), split(both(qc)), split(kc), split(vc)


def pair_scores(q2, ks, qc2, kcs, spread, same, bias):
    length = spread.shape[0]
    s0 = mm3(q2, ks, 1, 1)
    sc = mm3(qc2, kcs, 1, 1) * jnp.concatenate([same, same], axis=0)
    sch, scl = split(sc)
    st = jnp.concatenate(
        [
            mm2(spread, (sch[:length], scl[:length]), 1, 0),
            mm2(spread, (sch[length:], scl[length:]), 1, 0),
        ],
        axis=0,
    )
    b0 = bias[:, :length]
    bc = bias[:, length:]
    return s0 + jnp.concatenate([b0, b0], axis=0), st + jnp.concatenate([bc, bc], axis=0)


def attention_specs(length, width):
    pairs = width // 128
    block = lambda off: pl.BlockSpec((length, 128), lambda s, h: (s, off * pairs + h))
    far = lambda j: pl.BlockSpec((1, 1, 32, 128), lambda s, h: (s, j, 0, h))
    fixed = pl.BlockSpec((length, length), lambda s, h: (0, 0))
    bias = pl.BlockSpec((1, length, 2 * length), lambda s, h: (s, 0, 0))
    return block, far, fixed, bias


def attention_forward(packed, far, bias, spread, pool, same, seqs, local):
    rows_all, triple = packed.shape
    width = triple // 3
    length = rows_all // seqs
    block, far_spec, fixed, bias_spec = attention_specs(length, width)

    def body(q_ref, k_ref, v_ref, fk, fv, bias_ref, spread_ref, pool_ref, same_ref, out, lse):
        lane, both, q2, ks, vs, qc2, kcs, vcs = head_tools(
            q_ref[...] * 0.125,
            k_ref[...],
            v_ref[...],
            fk[0, 0],
            fv[0, 0],
            pool_ref[...],
            same_ref[...],
            local,
        )
        s0, st = pair_scores(q2, ks, qc2, kcs, spread_ref[...], same_ref[...], bias_ref[0])
        peak = jnp.maximum(
            jnp.max(s0, axis=1, keepdims=True), jnp.max(st, axis=1, keepdims=True)
        )
        p0 = jnp.exp(s0 - peak)
        pc = jnp.exp(st - peak)
        total = jnp.sum(p0, axis=1, keepdims=True) + jnp.sum(pc, axis=1, keepdims=True)
        mixed = (mm3(split(p0), vs, 1, 0) + mm3(split(pc), vcs, 1, 0)) / total
        out[...] = jnp.where(lane, mixed[:length], mixed[length:])
        logs = peak + jnp.log(total)
        lse[...] = jnp.where(lane, logs[:length], logs[length:])

    return pl.pallas_call(
        body,
        grid=(seqs, width // 128),
        out_shape=[jax.ShapeDtypeStruct((rows_all, width), F32)] * 2,
        in_specs=[
            block(0),
            block(1),
            block(2),
            far_spec(0),
            far_spec(1),
            bias_spec,
            fixed,
            fixed,
            fixed,
        ],
        out_specs=[block(0), block(0)],
    )(packed, packed, packed, far, far, bias, spread, pool, same)


def attention_backward(packed, far, bias, spread, pool, same, attended, lse, grad, seqs, local):
    rows_all, triple = packed.shape
    width = triple // 3
    length = rows_all // seqs
    block, far_spec, fixed, bias_spec = attention_specs(length, width)
    n4, n5 = length >> 4, length >> 5

    def body(
        q_ref,
        k_ref,
        v_ref,
        fk,
        fv,
        bias_ref,
        spread_ref,
        pool_ref,
        same_ref,
        o_ref,
        lse_ref,
        g_ref,
        dq_ref,
        dk_ref,
        dv_ref,
        f4,
        f5a,
        f5b,
    ):
        pool_m = pool_ref[...]
        spread_m = spread_ref[...]
        lane, both, q2, ks, vs, qc2, kcs, vcs = head_tools(
            q_ref[...] * 0.125,
            k_ref[...],
            v_ref[...],
            fk[0, 0],
            fv[0, 0],
            pool_m,
            same_ref[...],
            local,
        )
        s0, st = pair_scores(q2, ks, qc2, kcs, spread_m, same_ref[...], bias_ref[0])
        logs = lse_ref[...]
        logs2 = jnp.concatenate([logs[:, 0:1], logs[:, 64:65]], axis=0)
        p0 = jnp.exp(s0 - logs2)
        pc = jnp.exp(st - logs2)
        g2f = both(g_ref[...])
        g2 = split(g2f)
        o_val = o_ref[...]
        delta = jnp.sum(g2f * jnp.concatenate([o_val, o_val], axis=0), axis=1, keepdims=True)
        dv = mm3(split(p0), g2, 0, 0)
        dvc = mm3(split(pc), g2, 0, 0)
        d0 = split(p0 * (mm3(g2, vs, 1, 1) - delta))
        dt = split(pc * (mm3(g2, vcs, 1, 1) - delta))
        dq2 = mm3(d0, ks, 1, 0)
        dk = mm3(d0, q2, 0, 0)
        dsc = jnp.concatenate(
            [
                mm2_left((dt[0][:length], dt[1][:length]), spread_m),
                mm2_left((dt[0][length:], dt[1][length:]), spread_m),
            ],
            axis=0,
        )
        dsc = split(dsc * jnp.concatenate([same_ref[...], same_ref[...]], axis=0))
        dqc2 = mm3(dsc, kcs, 1, 0)
        dkc = mm3(dsc, qc2, 0, 0)
        dqc = jnp.where(lane, dqc2[:length], dqc2[length:])
        near = lax.broadcasted_iota(jnp.int32, (length, 128), 0) < local
        zero = jnp.zeros((length, 128), F32)
        stacked = jnp.concatenate(
            [dqc, jnp.where(near, dkc, zero), jnp.where(near, dvc, zero)], axis=1
        )
        back = mm2(pool_m, split(stacked), 0, 0)
        dq_ref[...] = (jnp.where(lane, dq2[:length], dq2[length:]) + back[:, :128]) * 0.125
        dk_ref[...] = dk + back[:, 128:256]
        dv_ref[...] = dv + back[:, 256:]
        for j, value in ((0, dkc), (1, dvc)):
            f4[0, j] = value[local : local + n4]
            f5a[0, j] = value[local + n4 : local + n4 + n5]
            f5b[0, j] = value[local + n4 + n5 :]

    far_out = lambda n: pl.BlockSpec((1, 2, n, 128), lambda s, h: (s, 0, 0, h))
    return pl.pallas_call(
        body,
        grid=(seqs, width // 128),
        out_shape=[jax.ShapeDtypeStruct((rows_all, width), F32)] * 3
        + [jax.ShapeDtypeStruct((seqs, 2, n, width), F32) for n in (n4, n5, n5)],
        in_specs=[
            block(0),
            block(1),
            block(2),
            far_spec(0),
            far_spec(1),
            bias_spec,
            fixed,
            fixed,
            fixed,
            block(0),
            block(0),
            block(0),
        ],
        out_specs=[block(0)] * 3 + [far_out(n4), far_out(n5), far_out(n5)],
    )(packed, packed, packed, far, far, bias, spread, pool, same, attended, lse, grad)


def mm2_left(a, b):
    return mm(b, a[0], 0, 0) + mm(b, a[1], 0, 0)


def middle_stage(tokens, attended, wh, wl):
    rows_all, width = tokens.shape

    def body(tok, att, wh_ref, wl_ref, middle, xhat, inv):
        x = tok[...] + mm3(split(att[...]), (wh_ref[...], wl_ref[...]), 1, 1)
        middle[...] = x
        centre = x - jnp.mean(x, axis=1, keepdims=True)
        scale = lax.rsqrt(jnp.mean(centre * centre, axis=1, keepdims=True) + EPSILON)
        xhat[...] = centre * scale
        inv[...] = jnp.broadcast_to(scale, inv.shape)

    return call(
        body,
        [((rows_all, width), F32), ((rows_all, width), F32), ((rows_all, 128), F32)],
        in_specs=[whole()] * 4,
        out_specs=[whole()] * 3,
    )(tokens, attended, wh, wl)


def grad_hidden_stage(me, cot, gathered, plan, hidden_width):
    rows_all, width = cot.shape
    rows, lanes = width // plan.dp, hidden_width // plan.fsdp
    out_lanes = width // plan.fsdp
    slots = gathered.arrays
    chunks = lanes // 128
    down_parts = [(k * rows, rows, 0, 128 * k) for k in range(chunks)]
    out_parts = [(chunks * rows, rows, 0, 0)]

    def body(me_ref, cot_ref, *rest):
        refs = rest[: len(slots)]
        gh, dh, dl, oh, ol, full, full_out = rest[len(slots) :]
        me_d, me_f = me_ref[0], me_ref[1]
        assemble(full_out, refs, gathered, plan, me_d, me_f, rows, out_lanes, out_parts)
        w = split(full_out[...])
        oh[...] = w[0]
        ol[...] = w[1]
        assemble(full, refs, gathered, plan, me_d, me_f, rows, lanes, down_parts)
        w = split(full[...])
        dh[...] = w[0]
        dl[...] = w[1]
        gh[...] = mm3(split(cot_ref[...]), w, 1, 0)

    return call(
        body,
        [
            ((rows_all, hidden_width), F32),
            ((width, hidden_width), BF16),
            ((width, hidden_width), BF16),
            ((width, width), BF16),
            ((width, width), BF16),
        ],
        [pltpu.VMEM((width, hidden_width), F32), pltpu.VMEM((width, width), F32)],
        in_specs=[SMEM, whole()] + [whole()] * len(slots),
        out_specs=[whole()] * 5,
    )(me, cot, *slots)


def hidden_stage(me, xhat, ln, gh, gathered, plan):
    rows_all, width = xhat.shape
    hidden_width = gh.shape[1]
    rows, lanes = hidden_width // plan.dp, width // plan.fsdp
    slots = gathered.arrays
    chunk = 512
    steps = hidden_width // chunk
    root = float(np.sqrt(2.0 / np.pi))

    def body(me_ref, xhat_ref, ln_ref, gh_ref, *rest):
        refs = rest[: len(slots)]
        hh, hl, ph, plo, wh, wl, full, nh, nl = rest[len(slots) :]
        step = pl.program_id(0)

        @pl.when(step == 0)
        def _():
            segments = [(0, rows, 0, 0)]
            assemble(full, refs, gathered, plan, me_ref[0], me_ref[1], rows, lanes, segments)
            w = split(full[...])
            wh[...] = w[0]
            wl[...] = w[1]
            n = split(xhat_ref[...] * ln_ref[2:3, :] + ln_ref[3:4, :])
            nh[...] = n[0]
            nl[...] = n[1]

        part = pl.ds(pl.multiple_of(step * chunk, chunk), chunk)
        v = mm3((nh[...], nl[...]), (wh[part, :], wl[part, :]), 1, 1)
        square = v * v
        t = jnp.tanh(root * v * (1.0 + 0.044715 * square))
        half = 0.5 * (1.0 + t)
        h = split(v * half)
        hh[...] = h[0]
        hl[...] = h[1]
        slope = half + 0.5 * v * (1.0 - t * t) * root * (1.0 + 3 * 0.044715 * square)
        g = split(gh_ref[...] * slope)
        ph[...] = g[0]
        plo[...] = g[1]

    fixed = lambda shape: pl.BlockSpec(shape, lambda i: (0,) * len(shape))
    cols = pl.BlockSpec((rows_all, chunk), lambda i: (0, i))
    return pl.pallas_call(
        body,
        grid=(steps,),
        out_shape=[jax.ShapeDtypeStruct((rows_all, hidden_width), BF16)] * 4
        + [jax.ShapeDtypeStruct((hidden_width, width), BF16)] * 2,
        in_specs=[SMEM, fixed((rows_all, width)), fixed((8, width)), cols]
        + [fixed(s.shape) for s in slots],
        out_specs=[cols] * 4 + [fixed((hidden_width, width))] * 2,
        scratch_shapes=[
            pltpu.VMEM((hidden_width, width), F32),
            pltpu.VMEM((rows_all, width), BF16),
            pltpu.VMEM((rows_all, width), BF16),
        ],
    )(me, xhat, ln, gh, *slots)


def grad_down_stage(me, cot, hh, hl, plan, stream, core):
    rows_all, width = cot.shape
    hidden_width = hh.shape[1]
    rows, lanes = width // plan.dp, hidden_width // plan.fsdp

    def body(me_ref, cot_ref, hh_ref, hl_ref, *outs):
        jf = core + 2 * pl.program_id(0)
        res = mm3(split(cot_ref[...]), (hh_ref[...], hl_ref[...]), 0, 0)
        for d in range(plan.dp):
            jd = me_ref[0] ^ d
            for k in range(lanes // 128):
                value = res[d * rows : (d + 1) * rows, 128 * k : 128 * (k + 1)]
                stream.put(outs, jd, jf, k * rows, value)

    cols = pl.BlockSpec((rows_all, lanes), lambda i, m: (0, m[1] ^ (core + 2 * i)))
    grid_spec = pltpu.PrefetchScalarGridSpec(
        num_scalar_prefetch=1,
        grid=(plan.fsdp // 2,),
        in_specs=[pl.BlockSpec((rows_all, width), lambda i, m: (0, 0)), cols, cols],
        out_specs=[pl.BlockSpec(shape, lambda i, m: (0, 0, 0)) for shape in stream.shapes()],
    )
    return pl.pallas_call(
        body,
        grid_spec=grid_spec,
        out_shape=[jax.ShapeDtypeStruct(shape, F32) for shape in stream.shapes()],
    )(me, cot, hh, hl)


def half_lanes(ref, me_f, core, lanes):
    parts = []
    for y in range(2):
        start = pl.multiple_of((me_f ^ (core + 2 * y)) * lanes, 128)
        parts.append(ref[:, pl.ds(start, lanes)])
    return jnp.concatenate(parts, axis=1)


def grad_up_stage(me, xhat, ln, ph, plo, plan, stream, core):
    rows_all, width = xhat.shape
    hidden_width = ph.shape[1]
    rows, lanes = hidden_width // plan.dp, width // plan.fsdp
    chunk = 512
    steps = hidden_width // chunk
    per = chunk // rows

    def body(me_ref, xhat_ref, ln_ref, ph_ref, pl_ref, *rest):
        outs = rest[: len(stream.spans)]
        full, nh, nl = rest[len(stream.spans) :]
        step = pl.program_id(0)

        @pl.when(step == 0)
        def _():
            full[...] = xhat_ref[...] * ln_ref[2:3, :] + ln_ref[3:4, :]
            n = split(half_lanes(full, me_ref[1], core, lanes))
            nh[...] = n[0]
            nl[...] = n[1]

        res = mm3((ph_ref[...], pl_ref[...]), (nh[...], nl[...]), 0, 0)
        for i in range(per):
            jd = (step * per + i) ^ me_ref[0]
            for y in range(2):
                value = res[i * rows : (i + 1) * rows, y * lanes : (y + 1) * lanes]
                stream.put(outs, jd, core + 2 * y, 0, value)

    fixed = lambda shape: pl.BlockSpec(shape, lambda i: (0,) * len(shape))
    cols = pl.BlockSpec((rows_all, chunk), lambda i: (0, i))
    return pl.pallas_call(
        body,
        grid=(steps,),
        out_shape=[jax.ShapeDtypeStruct(shape, F32) for shape in stream.shapes()],
        in_specs=[SMEM, fixed((rows_all, width)), fixed((8, width)), cols, cols],
        out_specs=[fixed(shape) for shape in stream.shapes()],
        scratch_shapes=[pltpu.VMEM((rows_all, width), F32)]
        + [pltpu.VMEM((rows_all, 2 * lanes), BF16)] * 2,
    )(me, xhat, ln, ph, plo)


def norm_back(e, gain, xhat, inv):
    u = e * gain
    mean_u = jnp.mean(u, axis=1, keepdims=True)
    mean_ux = jnp.mean(u * xhat, axis=1, keepdims=True)
    return inv * (u - mean_u - xhat * mean_ux)


def output_stage(middle, cot, xhat, inv, ln, hh, hl, ph, plo, dh, dl, uh, ul):
    rows_all, width = middle.shape
    hidden_width = hh.shape[1]
    chunk = 512
    steps = hidden_width // chunk

    def body(mid, cot_ref, xhat_ref, inv_ref, ln_ref, h0, h1, p0, p1, d0, d1, u0, u1, out, gm, gln, acc):
        step = pl.program_id(0)

        @pl.when(step == 0)
        def _():
            out[...] = mid[...]
            acc[...] = jnp.zeros_like(acc)

        out[...] += mm3((h0[...], h1[...]), (d0[...], d1[...]), 1, 1)
        acc[...] += mm3((p0[...], p1[...]), (u0[...], u1[...]), 1, 0)

        @pl.when(step == steps - 1)
        def _():
            e = acc[...]
            xh = xhat_ref[...]
            gm[...] = cot_ref[...] + norm_back(e, ln_ref[2:3, :], xh, inv_ref[:, 0:1])
            gln[0:1, :] = jnp.sum(e * xh, axis=0, keepdims=True)
            gln[1:2, :] = jnp.sum(e, axis=0, keepdims=True)

    fixed = lambda shape: pl.BlockSpec(shape, lambda i: (0,) * len(shape))
    cols = pl.BlockSpec((rows_all, chunk), lambda i: (0, i))
    act = fixed((rows_all, width))
    return pl.pallas_call(
        body,
        grid=(steps,),
        out_shape=[
            jax.ShapeDtypeStruct((rows_all, width), F32),
            jax.ShapeDtypeStruct((rows_all, width), F32),
            jax.ShapeDtypeStruct((8, width), F32),
        ],
        in_specs=[act, act, act, fixed((rows_all, 128)), fixed((8, width))]
        + [cols] * 4
        + [pl.BlockSpec((width, chunk), lambda i: (0, i))] * 2
        + [pl.BlockSpec((chunk, width), lambda i: (i, 0))] * 2,
        out_specs=[act, act, fixed((8, width))],
        scratch_shapes=[pltpu.VMEM((rows_all, width), F32)],
    )(middle, cot, xhat, inv, ln, hh, hl, ph, plo, dh, dl, uh, ul)


def mixture_grad_stage(me, gm, attended, oh, ol, plan, stream):
    rows_all, width = gm.shape
    rows, lanes = width // plan.dp, width // plan.fsdp
    count = len(stream.spans)

    def body(me_ref, gm_ref, att, oh_ref, ol_ref, gmix, *rest):
        outs = rest[: 2 * count]
        full = rest[2 * count]
        g = split(gm_ref[...])
        gmix[...] = mm3(g, (oh_ref[...], ol_ref[...]), 1, 0)
        full[...] = att[...]
        for core in range(2):
            res = mm3(g, split(half_lanes(full, me_ref[1], core, lanes)), 0, 0)
            mine = outs[count * (1 - core) : count * (2 - core)]
            for d in range(plan.dp):
                for y in range(2):
                    value = res[d * rows : (d + 1) * rows, y * lanes : (y + 1) * lanes]
                    stream.put(mine, d ^ me_ref[0], core + 2 * y, 0, value)

    got = call(
        body,
        [((rows_all, width), F32)] + [(shape, F32) for shape in stream.shapes() * 2],
        [pltpu.VMEM((rows_all, width), F32)],
        in_specs=[SMEM] + [whole()] * 4,
        out_specs=[whole()] * (1 + 2 * count),
    )(me, gm, attended, oh, ol)
    return got[0], got[1 : 1 + count], got[1 + count :]


def input_grad_stage(dq, dk, dv, g4, g5a, g5b, pool, wqh, wql, xhat, inv, ln, gm, gln, seqs):
    rows_all, width = dq.shape
    length = rows_all // seqs

    def body(dq_r, dk_r, dv_r, g4_r, g5a_r, g5b_r, pool_r, wh, wl, xhat_r, inv_r, ln_r, gm_r, gln_r, gph, gpl, gtok, lrow):
        for j, ref in ((0, None), (1, dk_r), (2, dv_r)):
            for s in range(seqs):
                rs = slice(s * length, (s + 1) * length)
                if j == 0:
                    value = dq_r[rs, :]
                else:
                    groups = jnp.concatenate(
                        [g4_r[s, j - 1], g5a_r[s, j - 1] + g5b_r[s, j - 1]], axis=0
                    )
                    value = ref[rs, :] + mm2(pool_r[...], split(groups), 0, 0)
                h = split(value)
                gph[rs, j * width : (j + 1) * width] = h[0]
                gpl[rs, j * width : (j + 1) * width] = h[1]
        e = mm3((gph[...], gpl[...]), (wh[...], wl[...]), 1, 0)
        xh = xhat_r[...]
        gtok[...] = gm_r[...] + norm_back(e, ln_r[0:1, :], xh, inv_r[:, 0:1])
        sums = [
            jnp.sum(e * xh, axis=0, keepdims=True),
            jnp.sum(e, axis=0, keepdims=True),
            gln_r[0:1, :],
            gln_r[1:2, :],
        ]
        for i in range(4):
            for p in range(4):
                lrow[4 * i + p : 4 * i + p + 1, :] = sums[p][:, 128 * i : 128 * (i + 1)]

    return call(
        body,
        [
            ((rows_all, 3 * width), BF16),
            ((rows_all, 3 * width), BF16),
            ((rows_all, width), F32),
            ((LN_ROWS, 128), F32),
        ],
        in_specs=[whole()] * 14,
        out_specs=[whole()] * 4,
    )(dq, dk, dv, g4, g5a, g5b, pool, wqh, wql, xhat, inv, ln, gm, gln)


def grad_qkv_stage(me, gph, gpl, xhat, ln, lrow, plan, stream, core):
    rows_all, triple = gph.shape
    width = triple // 3
    rows, lanes = triple // plan.dp, width // plan.fsdp

    def body(me_ref, gph_r, gpl_r, xhat_r, ln_r, lrow_r, *rest):
        outs, full = rest[:-1], rest[-1]
        full[...] = xhat_r[...] * ln_r[0:1, :] + ln_r[1:2, :]
        n = split(half_lanes(full, me_ref[1], core, lanes))
        res = mm3((gph_r[...], gpl_r[...]), n, 0, 0)
        tail = lrow_r[...]
        for d in range(plan.dp):
            jd = me_ref[0] ^ d
            for y in range(2):
                value = res[d * rows : (d + 1) * rows, y * lanes : (y + 1) * lanes]
                stream.put(outs, jd, core + 2 * y, LN_ROWS, value)
                stream.put(outs, jd, core + 2 * y, 0, tail)

    return call(
        body,
        [(shape, F32) for shape in stream.shapes()],
        [pltpu.VMEM((rows_all, width), F32)],
        in_specs=[SMEM] + [whole()] * 5,
        out_specs=[whole()] * len(stream.spans),
    )(me, gph, gpl, xhat, ln, lrow)


def swap(x, mask, axis="fsdp"):
    size = lax.axis_size(axis)
    return lax.ppermute(x, axis, [(i, i ^ mask) for i in range(size)])


def local(
    tokens, segments, cotangent, ln1_gain, ln1_bias, w_qkv, w_out, ln2_gain, ln2_bias, w_up, w_down
):
    seqs, length, width = tokens.shape
    dp, fsdp = lax.axis_size("dp"), lax.axis_size("fsdp")
    plan = Plan(dp, fsdp)
    me_d = lax.axis_index("dp")
    me = jnp.stack([me_d, lax.axis_index("fsdp")]).astype(jnp.int32)
    rows_all = seqs * length
    hidden_width = w_down.shape[0] * fsdp

    spread, pool, same = pooling(length)
    layout, _ = level_layout(length)
    local_rows = [first for level, first, _ in layout if 2 * NR * (1 << level) > length][0]
    spread_c = jnp.asarray(spread, BF16)
    pool_c = jnp.asarray(pool, BF16)
    same_c = jnp.asarray(same, F32)
    far_pool = jnp.asarray(pool[local_rows : local_rows + (length >> 4) + (length >> 5)], BF16)

    share = width // dp
    norms = jnp.stack([ln1_gain, ln1_bias, ln2_gain, ln2_bias])
    placed = lax.dynamic_update_slice(jnp.zeros((4, width), F32), norms, (0, me_d * share))
    placed = placed.reshape(4, 4, 128).transpose(1, 0, 2).reshape(LN_ROWS, 128)
    rows_qkv, rows_d, rows_up = 3 * share, share, hidden_width // dp
    chunks = hidden_width // fsdp // 128
    orders = plan.orders
    qkv_cut = LN_ROWS + rows_qkv // 2
    down_piece = w_down.T.reshape(rows_d, chunks, 128).transpose(1, 0, 2).reshape(-1, 128)
    down_piece = jnp.concatenate([down_piece, w_out.T], axis=0)
    qkv_slots = gather(
        plan, jnp.concatenate([placed, w_qkv.T], axis=0), orders("wzxy wzyx"), qkv_cut
    )
    near, far_a, far_b = (swap(segments, m) for m in (1, 2, 3))
    bias = score_bias(segments, near, far_a, far_b)
    down_slots = gather(plan, down_piece, orders("wzxy wzyx"), down_piece.shape[0] // 2)
    up_slots = gather(plan, w_up.T, orders("xywz yxwz"), rows_up // 2)

    tok = tokens.reshape(rows_all, width)
    cot = cotangent.reshape(rows_all, width)
    packed, wqh, wql, xhat1, inv1, ln, s4, s5 = qkv_stage(
        me, tok, qkv_slots, plan, far_pool, seqs
    )
    far = jnp.concatenate([swap(s4, 1), swap(s5, 2), swap(s5, 3)], axis=2)
    attended, lse = attention_forward(
        packed, far, bias, spread_c, pool_c, same_c, seqs, local_rows
    )
    gh, dh, dl, oh, ol = grad_hidden_stage(me, cot, down_slots, plan, hidden_width)
    middle, xhat2, inv2 = middle_stage(tok, attended, oh, ol)
    hh, hl, ph, plo, uh, ul = hidden_stage(me, xhat2, ln, gh, up_slots, plan)
    down = Stream(plan, chunks * rows_d, orders("yxzw xyzw"), chunks * rows_d // 2)
    up = Stream(plan, rows_up, orders("zwyx zwxy"), rows_up // 2)
    out = Stream(plan, rows_d, orders("xyzw"))
    qkv = Stream(plan, LN_ROWS + rows_qkv, orders("yxzw xyzw"), qkv_cut)
    g_down = down.reduce(
        *[grad_down_stage(me, cot, hh, hl, plan, down, core) for core in (1, 0)]
    )
    g_up = up.reduce(
        *[grad_up_stage(me, xhat2, ln, ph, plo, plan, up, core) for core in (1, 0)]
    )
    output, gm, gln = output_stage(
        middle, cot, xhat2, inv2, ln, hh, hl, ph, plo, dh, dl, uh, ul
    )
    gmix, away, keep = mixture_grad_stage(me, gm, attended, oh, ol, plan, out)
    g_out = out.reduce(away, keep)
    dq, dk, dv, f4, f5a, f5b = attention_backward(
        packed, far, bias, spread_c, pool_c, same_c, attended, lse, gmix, seqs, local_rows
    )
    g4, g5a, g5b = swap(f4, 1), swap(f5a, 2), swap(f5b, 3)
    gph, gpl, gtok, lrow = input_grad_stage(
        dq, dk, dv, g4, g5a, g5b, far_pool, wqh, wql, xhat1, inv1, ln, gm, gln, seqs
    )
    g_qkv = qkv.reduce(
        *[grad_qkv_stage(me, gph, gpl, xhat1, ln, lrow, plan, qkv, core) for core in (1, 0)]
    )
    sums = g_qkv[:LN_ROWS].reshape(4, 4, 128).transpose(1, 0, 2).reshape(4, width)
    mine = lax.dynamic_slice(sums, (0, me_d * share), (4, share))
    g_down = g_down.reshape(chunks, rows_d, 128).transpose(0, 2, 1).reshape(-1, rows_d)
    shape = tokens.shape
    return (
        output.reshape(shape),
        gtok.reshape(shape),
        mine[0],
        mine[1],
        g_qkv[LN_ROWS:].T,
        g_out.T,
        mine[2],
        mine[3],
        g_up.T,
        g_down,
    )


def solution(mesh):
    weight = P("fsdp", "dp")
    rows = P("dp", "fsdp", None)
    vector = P("dp")
    return jax.shard_map(
        local,
        mesh=mesh,
        in_specs=(rows, P("dp", "fsdp"), rows, vector, vector, weight, weight, vector, vector, weight, weight),
        out_specs=(rows, rows, vector, vector, weight, weight, vector, vector, weight, weight),
        check_vma=False,
    )
```

```python
import jax
import jax.numpy as jnp
import numpy as np
from jax import lax
from jax.experimental import pallas as pl
from jax.experimental.pallas import tpu as pltpu
from jax.sharding import PartitionSpec as P

HEADS = 8
NR = 16
LEVELS = 6
EPSILON = 1e-05
MASKED = -1e30
F32 = jnp.float32
BF16 = jnp.bfloat16
LN_ROWS = 16
SCALE = 0.05


def split(x):
    high = x.astype(BF16)
    return high, (x - high.astype(F32)).astype(BF16)


def mm(a, b, ca, cb):
    return lax.dot_general(a, b, (((ca,), (cb,)), ((), ())), preferred_element_type=F32)


def mm3(a, b, ca, cb):
    return mm(a[0], b[0], ca, cb) + mm(a[0], b[1], ca, cb) + mm(a[1], b[0], ca, cb)


def mm2(a, b, ca, cb):
    return mm(a, b[0], ca, cb) + mm(a, b[1], ca, cb)


def level_layout(length):
    rows, start = [], 0
    for level in range(1, LEVELS):
        count = length >> level
        rows.append((level, start, count))
        start += count
    return rows, start


def pooling(length):
    spread = np.zeros((length, length), np.float32)
    pool = np.zeros((length, length), np.float32)
    same = np.zeros((length, length), np.float32)
    layout, _ = level_layout(length)
    bounds = [first for _, first, _ in layout] + [length]
    for index, (level, first, count) in enumerate(layout):
        token = np.arange(length)
        spread[token, first + (token >> level)] = 1.0
        pool[first + (token >> level), token] = 0.5**level
        same[bounds[index] : bounds[index + 1], bounds[index] : bounds[index + 1]] = 1.0
    return spread, pool, same


def score_bias(seg, near, far_a, far_b):
    count, length = seg.shape
    token = np.arange(length)
    pair = (token[:, None] >> 5) == (token[None, :] >> 5)
    ok = pair[None] & (seg[:, :, None] == seg[:, None, :])
    parts = [jnp.where(ok, 0.0, MASKED)]
    for level in range(1, LEVELS):
        ratio = 1 << level

        def ends(values):
            grouped = values.reshape(count, length // ratio, ratio)
            return grouped[:, :, 0], grouped[:, :, -1]

        low_q, high_q = ends(seg)
        low_q = jnp.repeat(low_q, ratio, axis=1)
        high_q = jnp.repeat(high_q, ratio, axis=1)
        if 2 * NR * ratio <= length:
            low_k, high_k = ends(seg)
            block_q = (token >> level) >> 4
            block_k = np.arange(length >> level) >> 4
            where = (block_q[:, None] ^ 1) == block_k[None, :]
        else:
            if NR * ratio <= length:
                low_k, high_k = ends(near)
            else:
                pieces = [ends(far_a), ends(far_b)]
                low_k = jnp.concatenate([pieces[0][0], pieces[1][0]], axis=1)
                high_k = jnp.concatenate([pieces[0][1], pieces[1][1]], axis=1)
            where = np.ones((length, low_k.shape[1]), bool)
        ok = (
            where[None]
            & (low_q[:, :, None] <= high_k[:, None, :])
            & (low_k[:, None, :] <= high_q[:, :, None])
        )
        parts.append(jnp.where(ok, np.float32(level * np.log(2.0)), MASKED))
    return jnp.concatenate(parts, axis=2).astype(F32)


class Plan:
    def __init__(self, dp, fsdp):
        self.dp, self.fsdp = dp, fsdp
        self.dims = {}
        names = ["x", "z", "w"]
        bit = 1
        while bit < dp:
            name = names[len(self.dims)] if len(self.dims) < 3 else "d%d" % bit
            self.dims[name] = ("dp", bit)
            bit *= 2
        self.extra = list(self.dims)[3:]
        self.dims["y"] = ("fsdp", 2)
        self.dims["c"] = ("fsdp", 1)

    def corner(self, group, v):
        return tuple(name for i, name in enumerate(group) if (v >> i) & 1)

    def mask(self, names):
        d = f = 0
        for name in names:
            axis, bit = self.dims[name]
            if axis == "dp":
                d |= bit
            else:
                f |= bit
        return d, f

    def send(self, x, names):
        d, f = self.mask(names)
        if not f:
            return lax.ppermute(x, "dp", [(i, i ^ d) for i in range(self.dp)])
        if not d:
            return lax.ppermute(x, "fsdp", [(i, i ^ f) for i in range(self.fsdp)])
        n = self.fsdp
        pairs = [(i, ((i // n) ^ d) * n + ((i % n) ^ f)) for i in range(self.dp * n)]
        return lax.ppermute(x, ("dp", "fsdp"), pairs)

    def position(self, stages, d, f):
        pos = 0
        for group in stages:
            for name in reversed(group):
                axis, bit = self.dims[name]
                value = d if axis == "dp" else f
                pos = pos * 2 + ((value // bit) & 1)
        return pos


class Part:
    def __init__(self, start, held, names):
        self.start, self.held, self.names, self.got = start, held, names, []


class Gather:
    def __init__(self, plan, piece):
        self.plan, self.parts = plan, [Part(0, piece[None], [()])]
        self.arrays, self.slots = [], []

    def cut(self, row):
        (part,) = self.parts
        self.parts = [
            Part(0, part.held[:, :row], part.names),
            Part(row, part.held[:, row:], part.names),
        ]

    def send(self, groups, *earlier):
        for part, group in zip(self.parts, groups):
            if earlier:
                part.held = after(part.held, *earlier)
            for v in range(1, 1 << len(group)):
                names = self.plan.corner(group, v)
                part.got.append((self.plan.send(part.held, names), names))

    def came(self):
        return [value for part in self.parts for value, _ in part.got]

    def join(self):
        for part in self.parts:
            names = list(part.names)
            for _, corner in part.got:
                names += [n + corner for n in part.names]
            part.held = jnp.concatenate([part.held] + [v for v, _ in part.got], axis=0)
            part.names, part.got = names, []

    def stage(self, groups, *earlier):
        self.join()
        self.send(groups, *earlier)

    def share(self, held, *earlier):
        sent = []
        for part in self.parts:
            for value, corner in [(part.held, ())] if held else part.got:
                if earlier:
                    value = after(value, *earlier)
                other = self.plan.send(value, ("c",))
                sent.append(other)
                for array, core in ((value, ()), (other, ("c",))):
                    self.arrays.append(array)
                    slots = [self.plan.mask(n + corner + core) for n in part.names]
                    self.slots.append((slots, part.start))
        return sent


def assemble(scratch, refs, gathered, me_d, me_f, rows, lanes, segments):
    for ref, (slots, start) in zip(refs, gathered.slots):
        for slot, (d, f) in enumerate(slots):
            row0 = (me_d ^ d) * rows
            col0 = (me_f ^ f) * lanes
            for source, size, to_lane in segments:
                low, high = max(source, start), min(source + size, start + ref.shape[1])
                if low < high:
                    row = pl.multiple_of(row0 + (low - source), 8)
                    col = pl.multiple_of(col0 + to_lane, 128)
                    scratch[pl.ds(row, high - low), pl.ds(col, 128)] = ref[
                        slot, low - start : high - start, :
                    ]


def norm_rows(refs, gathered):
    total = None
    for ref, (slots, _) in zip(refs, gathered.slots):
        for slot, (d, f) in enumerate(slots):
            if f == 0:
                value = ref[slot, :LN_ROWS, :]
                total = value if total is None else total + value
    return jnp.concatenate([total[4 * i : 4 * i + 4] for i in range(4)], axis=1)


class Stream:
    def __init__(self, plan, rows, stages):
        self.plan, self.rows, self.stages = plan, rows, stages
        self.slots = plan.dp * plan.fsdp // 2

    def shape(self):
        return (self.slots, self.rows, 128)

    def put(self, out, d, f, row, value):
        size = value.shape[0]
        out[self.plan.position(self.stages, d, f), row : row + size, :] = value


class Reduce:
    def __init__(self, plan, stages):
        self.plan, self.stages = plan, list(stages)
        self.kept, self.came, self.last = [], [], []

    def begin(self, part, *earlier):
        part = after(part, *earlier) if earlier else part
        self.last = [self.plan.send(part, ("c",))]
        self.came.append(self.last[0])
        return self.last

    def keep(self, part):
        self.kept.append(part)

    def send(self, *earlier):
        if self.kept:
            self.terms = [self.kept, self.came]
            self.slots, self.kept = self.kept[0].shape[0], []
        group = self.stages.pop(0)
        self.slots >>= len(group)
        n = self.slots
        count = range(len(self.terms[0]))
        sizes = [part.shape[1] for part in self.terms[0]]
        cuts = np.cumsum([0] + sizes)
        out = []
        for v in range(1, 1 << len(group)):
            parts = [sum(term[i][v * n : (v + 1) * n] for term in self.terms) for i in count]
            out.append(parts[0] if len(parts) == 1 else jnp.concatenate(parts, axis=1))
        if earlier:
            out = after(out, *earlier)
        self.last = []
        for v, value in enumerate(out):
            got = self.plan.send(value, self.plan.corner(group, v + 1))
            self.last.append(got)
            self.terms.append([got[:, a:b] for a, b in zip(cuts[:-1], cuts[1:])])
        return out

    def total(self, *earlier):
        count = range(len(self.terms[0]))
        return [sum(term[i][0] for term in self.terms) for i in count]


def after(value, *earlier):
    return lax.optimization_barrier((value, earlier))[0]


def whole(shape=None):
    return pl.BlockSpec(memory_space=pltpu.VMEM)


SMEM = pl.BlockSpec(memory_space=pltpu.SMEM)


def cost(micros):
    return pl.CostEstimate(
        flops=int(micros * SCALE * 9e8), bytes_accessed=int(micros * SCALE * 2.5e6), transcendentals=0
    )


def call(body, outs, scratch=(), **kw):
    return pl.pallas_call(
        body,
        out_shape=[jax.ShapeDtypeStruct(s, t) for s, t in outs],
        scratch_shapes=list(scratch),
        **kw,
    )


def qkv_stage(me, tokens, gathered, plan, pool, seqs):
    rows_all, width = tokens.shape
    length = rows_all // seqs
    triple = 3 * width
    rows = triple // plan.dp
    lanes = width // plan.fsdp
    n4, n5 = length >> 4, length >> 5
    slots = gathered.arrays

    def body(me_ref, tok, pool_ref, *rest):
        refs = rest[: len(slots)]
        packed, wh, wl, xhat, inv, ln, s4, s5, full = rest[len(slots) :]
        segments = [(LN_ROWS, rows, 0)]
        assemble(full, refs, gathered, me_ref[0], me_ref[1], rows, lanes, segments)
        params = norm_rows(refs, gathered)
        ln[0:4, :] = params
        w = split(full[...])
        wh[...] = w[0]
        wl[...] = w[1]
        x = tok[...]
        centre = x - jnp.mean(x, axis=1, keepdims=True)
        scale = lax.rsqrt(jnp.mean(centre * centre, axis=1, keepdims=True) + EPSILON)
        xh = centre * scale
        xhat[...] = xh
        inv[...] = jnp.broadcast_to(scale, inv.shape)
        normed = xh * params[0:1, :] + params[1:2, :]
        packed[...] = mm3(split(normed), w, 1, 1)
        a24 = pool_ref[...]
        for s in range(seqs):
            for j in range(2):
                kv = packed[
                    s * length : (s + 1) * length, (j + 1) * width : (j + 2) * width
                ]
                means = mm2(a24, split(kv), 1, 0)
                s4[s, j] = means[:n4]
                s5[s, j] = means[n4 : n4 + n5]

    return call(
        body,
        [
            ((rows_all, triple), F32),
            ((triple, width), BF16),
            ((triple, width), BF16),
            ((rows_all, width), F32),
            ((rows_all, 128), F32),
            ((8, width), F32),
            ((seqs, 2, n4, width), F32),
            ((seqs, 2, n5, width), F32),
        ],
        [pltpu.VMEM((triple, width), F32)],
        cost_estimate=cost(7.4),
        in_specs=[SMEM, whole(), whole()] + [whole()] * len(slots),
        out_specs=[whole()] * 8,
    )(me, tokens, pool, *slots)


def head_tools(q, k, v, fk, fv, pool, same, local):
    length = q.shape[0]
    lane = lax.broadcasted_iota(jnp.int32, (length, 128), 1) < 64
    pooled = mm2(pool, split(jnp.concatenate([q, k, v], axis=1)), 1, 0)
    qc = pooled[:, :128]
    kc = jnp.concatenate([pooled[:local, 128:256], fk], axis=0)
    vc = jnp.concatenate([pooled[:local, 256:], fv], axis=0)

    def both(x):
        zero = jnp.zeros_like(x)
        return jnp.concatenate([jnp.where(lane, x, zero), jnp.where(lane, zero, x)], axis=0)

    return lane, both, split(both(q)), split(k), split(v), split(both(qc)), split(kc), split(vc)


def pair_scores(q2, ks, qc2, kcs, spread, same, bias):
    length = spread.shape[0]
    s0 = mm3(q2, ks, 1, 1)
    sc = mm3(qc2, kcs, 1, 1) * jnp.concatenate([same, same], axis=0)
    sch, scl = split(sc)
    st = jnp.concatenate(
        [
            mm2(spread, (sch[:length], scl[:length]), 1, 0),
            mm2(spread, (sch[length:], scl[length:]), 1, 0),
        ],
        axis=0,
    )
    b0 = bias[:, :length]
    bc = bias[:, length:]
    return s0 + jnp.concatenate([b0, b0], axis=0), st + jnp.concatenate([bc, bc], axis=0)


def attention_specs(length, width, first=0, pair=0):
    pairs = width // 128
    block = lambda off: pl.BlockSpec((length, 128), lambda s, h: (first + s, off * pairs + pair + h))
    far = lambda j: pl.BlockSpec((1, 1, 32, 128), lambda s, h: (first + s, j, 0, pair + h))
    fixed = pl.BlockSpec((length, length), lambda s, h: (0, 0))
    bias = pl.BlockSpec((1, length, 2 * length), lambda s, h: (first + s, 0, 0))
    return block, far, fixed, bias


def attention_forward(packed, far, bias, spread, pool, same, seqs, local, which, before):
    rows_all, triple = packed.shape
    width = triple // 3
    length = rows_all // seqs
    first, count, pair, pairs = which
    block, far_spec, fixed, bias_spec = attention_specs(length, width, first, pair)
    carried = len(before)

    def body(q_ref, k_ref, v_ref, fk, fv, bias_ref, spread_ref, pool_ref, same_ref, *rest):
        out, lse = rest[carried:]
        lane, both, q2, ks, vs, qc2, kcs, vcs = head_tools(
            q_ref[...] * 0.125,
            k_ref[...],
            v_ref[...],
            fk[0, 0],
            fv[0, 0],
            pool_ref[...],
            same_ref[...],
            local,
        )
        s0, st = pair_scores(q2, ks, qc2, kcs, spread_ref[...], same_ref[...], bias_ref[0])
        peak = jnp.maximum(
            jnp.max(s0, axis=1, keepdims=True), jnp.max(st, axis=1, keepdims=True)
        )
        p0 = jnp.exp(s0 - peak)
        pc = jnp.exp(st - peak)
        total = jnp.sum(p0, axis=1, keepdims=True) + jnp.sum(pc, axis=1, keepdims=True)
        mixed = (mm3(split(p0), vs, 1, 0) + mm3(split(pc), vcs, 1, 0)) / total
        out[...] = jnp.where(lane, mixed[:length], mixed[length:])
        logs = peak + jnp.log(total)
        lse[...] = jnp.where(lane, logs[:length], logs[length:])

    return pl.pallas_call(
        body,
        cost_estimate=cost(9.5),
        grid=(count, pairs),
        out_shape=[jax.ShapeDtypeStruct((rows_all, width), F32)] * 2,
        in_specs=[
            block(0),
            block(1),
            block(2),
            far_spec(0),
            far_spec(1),
            bias_spec,
            fixed,
            fixed,
            fixed,
        ]
        + [pl.BlockSpec(memory_space=pl.ANY)] * carried,
        out_specs=[block(0), block(0)],
        input_output_aliases={9 + i: i for i in range(carried)},
    )(packed, packed, packed, far, far, bias, spread, pool, same, *before)


def attention_backward(
    packed, far, bias, spread, pool, same, attended, lse, grad, seqs, local, which, before
):
    rows_all, triple = packed.shape
    width = triple // 3
    length = rows_all // seqs
    first, count, pair, pairs = which
    block, far_spec, fixed, bias_spec = attention_specs(length, width, first, pair)
    n4, n5 = length >> 4, length >> 5
    carried = len(before)

    def body(
        q_ref,
        k_ref,
        v_ref,
        fk,
        fv,
        bias_ref,
        spread_ref,
        pool_ref,
        same_ref,
        o_ref,
        lse_ref,
        g_ref,
        *rest,
    ):
        dq_ref, dk_ref, dv_ref, f4, f5a, f5b = rest[carried:]
        pool_m = pool_ref[...]
        spread_m = spread_ref[...]
        lane, both, q2, ks, vs, qc2, kcs, vcs = head_tools(
            q_ref[...] * 0.125,
            k_ref[...],
            v_ref[...],
            fk[0, 0],
            fv[0, 0],
            pool_m,
            same_ref[...],
            local,
        )
        s0, st = pair_scores(q2, ks, qc2, kcs, spread_m, same_ref[...], bias_ref[0])
        logs = lse_ref[...]
        logs2 = jnp.concatenate([logs[:, 0:1], logs[:, 64:65]], axis=0)
        p0 = jnp.exp(s0 - logs2)
        pc = jnp.exp(st - logs2)
        g2f = both(g_ref[...])
        g2 = split(g2f)
        o_val = o_ref[...]
        delta = jnp.sum(g2f * jnp.concatenate([o_val, o_val], axis=0), axis=1, keepdims=True)
        dv = mm3(split(p0), g2, 0, 0)
        dvc = mm3(split(pc), g2, 0, 0)
        d0 = split(p0 * (mm3(g2, vs, 1, 1) - delta))
        dt = split(pc * (mm3(g2, vcs, 1, 1) - delta))
        dq2 = mm3(d0, ks, 1, 0)
        dk = mm3(d0, q2, 0, 0)
        dsc = jnp.concatenate(
            [
                mm2_left((dt[0][:length], dt[1][:length]), spread_m),
                mm2_left((dt[0][length:], dt[1][length:]), spread_m),
            ],
            axis=0,
        )
        dsc = split(dsc * jnp.concatenate([same_ref[...], same_ref[...]], axis=0))
        dqc2 = mm3(dsc, kcs, 1, 0)
        dkc = mm3(dsc, qc2, 0, 0)
        dqc = jnp.where(lane, dqc2[:length], dqc2[length:])
        near = lax.broadcasted_iota(jnp.int32, (length, 128), 0) < local
        zero = jnp.zeros((length, 128), F32)
        stacked = jnp.concatenate(
            [dqc, jnp.where(near, dkc, zero), jnp.where(near, dvc, zero)], axis=1
        )
        back = mm2(pool_m, split(stacked), 0, 0)
        dq_ref[...] = (jnp.where(lane, dq2[:length], dq2[length:]) + back[:, :128]) * 0.125
        dk_ref[...] = dk + back[:, 128:256]
        dv_ref[...] = dv + back[:, 256:]
        for j, value in ((0, dkc), (1, dvc)):
            f4[0, j] = value[local : local + n4]
            f5a[0, j] = value[local + n4 : local + n4 + n5]
            f5b[0, j] = value[local + n4 + n5 :]

    far_out = lambda n: pl.BlockSpec((1, 2, n, 128), lambda s, h: (first + s, 0, 0, pair + h))
    return pl.pallas_call(
        body,
        cost_estimate=cost(8),
        grid=(count, pairs),
        out_shape=[jax.ShapeDtypeStruct((rows_all, width), F32)] * 3
        + [jax.ShapeDtypeStruct((seqs, 2, n, width), F32) for n in (n4, n5, n5)],
        in_specs=[
            block(0),
            block(1),
            block(2),
            far_spec(0),
            far_spec(1),
            bias_spec,
            fixed,
            fixed,
            fixed,
            block(0),
            block(0),
            block(0),
        ]
        + [pl.BlockSpec(memory_space=pl.ANY)] * carried,
        out_specs=[block(0)] * 3 + [far_out(n4), far_out(n5), far_out(n5)],
        input_output_aliases={12 + i: i for i in range(carried)},
    )(packed, packed, packed, far, far, bias, spread, pool, same, attended, lse, grad, *before)


def mm2_left(a, b):
    return mm(b, a[0], 0, 0) + mm(b, a[1], 0, 0)


def middle_stage(tokens, attended, wh, wl):
    rows_all, width = tokens.shape

    def body(tok, att, wh_ref, wl_ref, middle, xhat, inv):
        x = tok[...] + mm3(split(att[...]), (wh_ref[...], wl_ref[...]), 1, 1)
        middle[...] = x
        centre = x - jnp.mean(x, axis=1, keepdims=True)
        scale = lax.rsqrt(jnp.mean(centre * centre, axis=1, keepdims=True) + EPSILON)
        xhat[...] = centre * scale
        inv[...] = jnp.broadcast_to(scale, inv.shape)

    return call(
        body,
        [((rows_all, width), F32), ((rows_all, width), F32), ((rows_all, 128), F32)],
        cost_estimate=cost(4.3),
        in_specs=[whole()] * 4,
        out_specs=[whole()] * 3,
    )(tokens, attended, wh, wl)


def grad_hidden_stage(me, cot, gathered, plan, hidden_width):
    rows_all, width = cot.shape
    rows, lanes = width // plan.dp, hidden_width // plan.fsdp
    out_lanes = width // plan.fsdp
    slots = gathered.arrays
    chunks = lanes // 128
    down_parts = [(k * rows, rows, 128 * k) for k in range(chunks)]
    out_parts = [(chunks * rows, rows, 0)]

    def body(me_ref, cot_ref, *rest):
        refs = rest[: len(slots)]
        gh, dh, dl, oh, ol, full, full_out = rest[len(slots) :]
        me_d, me_f = me_ref[0], me_ref[1]
        assemble(full_out, refs, gathered, me_d, me_f, rows, out_lanes, out_parts)
        w = split(full_out[...])
        oh[...] = w[0]
        ol[...] = w[1]
        assemble(full, refs, gathered, me_d, me_f, rows, lanes, down_parts)
        w = split(full[...])
        dh[...] = w[0]
        dl[...] = w[1]
        gh[...] = mm3(split(cot_ref[...]), w, 1, 0)

    return call(
        body,
        [
            ((rows_all, hidden_width), F32),
            ((width, hidden_width), BF16),
            ((width, hidden_width), BF16),
            ((width, width), BF16),
            ((width, width), BF16),
        ],
        [pltpu.VMEM((width, hidden_width), F32), pltpu.VMEM((width, width), F32)],
        cost_estimate=cost(9.6),
        in_specs=[SMEM, whole()] + [whole()] * len(slots),
        out_specs=[whole()] * 5,
    )(me, cot, *slots)


def hidden_stage(me, xhat, ln, gh, gathered, plan):
    rows_all, width = xhat.shape
    hidden_width = gh.shape[1]
    rows, lanes = hidden_width // plan.dp, width // plan.fsdp
    slots = gathered.arrays
    chunk = 512
    steps = hidden_width // chunk
    root = float(np.sqrt(2.0 / np.pi))

    def body(me_ref, xhat_ref, ln_ref, gh_ref, *rest):
        refs = rest[: len(slots)]
        hh, hl, ph, plo, wh, wl, full, nh, nl = rest[len(slots) :]
        step = pl.program_id(0)

        @pl.when(step == 0)
        def _():
            segments = [(0, rows, 0)]
            assemble(full, refs, gathered, me_ref[0], me_ref[1], rows, lanes, segments)
            w = split(full[...])
            wh[...] = w[0]
            wl[...] = w[1]
            n = split(xhat_ref[...] * ln_ref[2:3, :] + ln_ref[3:4, :])
            nh[...] = n[0]
            nl[...] = n[1]

        part = pl.ds(pl.multiple_of(step * chunk, chunk), chunk)
        v = mm3((nh[...], nl[...]), (wh[part, :], wl[part, :]), 1, 1)
        square = v * v
        t = jnp.tanh(root * v * (1.0 + 0.044715 * square))
        half = 0.5 * (1.0 + t)
        h = split(v * half)
        hh[...] = h[0]
        hl[...] = h[1]
        slope = half + 0.5 * v * (1.0 - t * t) * root * (1.0 + 3 * 0.044715 * square)
        g = split(gh_ref[...] * slope)
        ph[...] = g[0]
        plo[...] = g[1]

    fixed = lambda shape: pl.BlockSpec(shape, lambda i: (0,) * len(shape))
    cols = pl.BlockSpec((rows_all, chunk), lambda i: (0, i))
    return pl.pallas_call(
        body,
        cost_estimate=cost(13.7),
        grid=(steps,),
        out_shape=[jax.ShapeDtypeStruct((rows_all, hidden_width), BF16)] * 4
        + [jax.ShapeDtypeStruct((hidden_width, width), BF16)] * 2,
        in_specs=[SMEM, fixed((rows_all, width)), fixed((8, width)), cols]
        + [fixed(s.shape) for s in slots],
        out_specs=[cols] * 4 + [fixed((hidden_width, width))] * 2,
        scratch_shapes=[
            pltpu.VMEM((hidden_width, width), F32),
            pltpu.VMEM((rows_all, width), BF16),
            pltpu.VMEM((rows_all, width), BF16),
        ],
    )(me, xhat, ln, gh, *slots)


def grad_down_stage(me, cot, hh, hl, plan, stream, core):
    rows_all, width = cot.shape
    hidden_width = hh.shape[1]
    rows, lanes = width // plan.dp, hidden_width // plan.fsdp

    def body(me_ref, cot_ref, hh_ref, hl_ref, out):
        jf = core + 2 * pl.program_id(0)
        res = mm3(split(cot_ref[...]), (hh_ref[...], hl_ref[...]), 0, 0)
        for d in range(plan.dp):
            jd = me_ref[0] ^ d
            for k in range(lanes // 128):
                value = res[d * rows : (d + 1) * rows, 128 * k : 128 * (k + 1)]
                stream.put(out, jd, jf, k * rows, value)

    cols = pl.BlockSpec((rows_all, lanes), lambda i, m: (0, m[1] ^ (core + 2 * i)))
    grid_spec = pltpu.PrefetchScalarGridSpec(
        num_scalar_prefetch=1,
        grid=(plan.fsdp // 2,),
        in_specs=[pl.BlockSpec((rows_all, width), lambda i, m: (0, 0)), cols, cols],
        out_specs=pl.BlockSpec(stream.shape(), lambda i, m: (0, 0, 0)),
    )
    return pl.pallas_call(
        body,
        cost_estimate=cost(5.5),
        grid_spec=grid_spec,
        out_shape=jax.ShapeDtypeStruct(stream.shape(), F32),
    )(me, cot, hh, hl)


def half_lanes(ref, me_f, core, lanes):
    parts = []
    for y in range(2):
        start = pl.multiple_of((me_f ^ (core + 2 * y)) * lanes, 128)
        parts.append(ref[:, pl.ds(start, lanes)])
    return jnp.concatenate(parts, axis=1)


def grad_up_stage(me, xhat, ln, ph, plo, plan, stream, core):
    rows_all, width = xhat.shape
    hidden_width = ph.shape[1]
    rows, lanes = hidden_width // plan.dp, width // plan.fsdp
    chunk = 512
    steps = hidden_width // chunk
    per = chunk // rows

    def body(me_ref, xhat_ref, ln_ref, ph_ref, pl_ref, out, full, nh, nl):
        step = pl.program_id(0)

        @pl.when(step == 0)
        def _():
            full[...] = xhat_ref[...] * ln_ref[2:3, :] + ln_ref[3:4, :]
            n = split(half_lanes(full, me_ref[1], core, lanes))
            nh[...] = n[0]
            nl[...] = n[1]

        res = mm3((ph_ref[...], pl_ref[...]), (nh[...], nl[...]), 0, 0)
        for i in range(per):
            jd = (step * per + i) ^ me_ref[0]
            for y in range(2):
                value = res[i * rows : (i + 1) * rows, y * lanes : (y + 1) * lanes]
                stream.put(out, jd, core + 2 * y, 0, value)

    fixed = lambda shape: pl.BlockSpec(shape, lambda i: (0,) * len(shape))
    cols = pl.BlockSpec((rows_all, chunk), lambda i: (0, i))
    return pl.pallas_call(
        body,
        cost_estimate=cost(6.4),
        grid=(steps,),
        out_shape=jax.ShapeDtypeStruct(stream.shape(), F32),
        in_specs=[SMEM, fixed((rows_all, width)), fixed((8, width)), cols, cols],
        out_specs=fixed(stream.shape()),
        scratch_shapes=[pltpu.VMEM((rows_all, width), F32)]
        + [pltpu.VMEM((rows_all, 2 * lanes), BF16)] * 2,
    )(me, xhat, ln, ph, plo)


def norm_back(e, gain, xhat, inv):
    u = e * gain
    mean_u = jnp.mean(u, axis=1, keepdims=True)
    mean_ux = jnp.mean(u * xhat, axis=1, keepdims=True)
    return inv * (u - mean_u - xhat * mean_ux)


def output_stage(middle, hh, hl, dh, dl):
    rows_all, width = middle.shape
    chunk = 512
    steps = hh.shape[1] // chunk

    def body(mid, h0, h1, d0, d1, out):
        @pl.when(pl.program_id(0) == 0)
        def _():
            out[...] = mid[...]

        out[...] += mm3((h0[...], h1[...]), (d0[...], d1[...]), 1, 1)

    cols = pl.BlockSpec((rows_all, chunk), lambda i: (0, i))
    act = pl.BlockSpec((rows_all, width), lambda i: (0, 0))
    return pl.pallas_call(
        body,
        cost_estimate=cost(8),
        grid=(steps,),
        out_shape=jax.ShapeDtypeStruct((rows_all, width), F32),
        in_specs=[act, cols, cols] + [pl.BlockSpec((width, chunk), lambda i: (0, i))] * 2,
        out_specs=act,
    )(middle, hh, hl, dh, dl)


def middle_grad_stage(cot, xhat, inv, ln, ph, plo, uh, ul):
    rows_all, width = cot.shape
    chunk = 512
    steps = ph.shape[1] // chunk

    def body(cot_ref, xhat_ref, inv_ref, ln_ref, p0, p1, u0, u1, gm, gln, acc):
        step = pl.program_id(0)

        @pl.when(step == 0)
        def _():
            acc[...] = jnp.zeros_like(acc)

        acc[...] += mm3((p0[...], p1[...]), (u0[...], u1[...]), 1, 0)

        @pl.when(step == steps - 1)
        def _():
            e = acc[...]
            xh = xhat_ref[...]
            gm[...] = cot_ref[...] + norm_back(e, ln_ref[2:3, :], xh, inv_ref[:, 0:1])
            gln[0:1, :] = jnp.sum(e * xh, axis=0, keepdims=True)
            gln[1:2, :] = jnp.sum(e, axis=0, keepdims=True)

    fixed = lambda shape: pl.BlockSpec(shape, lambda i: (0,) * len(shape))
    cols = pl.BlockSpec((rows_all, chunk), lambda i: (0, i))
    act = fixed((rows_all, width))
    return pl.pallas_call(
        body,
        cost_estimate=cost(8.5),
        grid=(steps,),
        out_shape=[
            jax.ShapeDtypeStruct((rows_all, width), F32),
            jax.ShapeDtypeStruct((8, width), F32),
        ],
        in_specs=[act, act, fixed((rows_all, 128)), fixed((8, width)), cols, cols]
        + [pl.BlockSpec((chunk, width), lambda i: (i, 0))] * 2,
        out_specs=[act, fixed((8, width))],
        scratch_shapes=[pltpu.VMEM((rows_all, width), F32)],
    )(cot, xhat, inv, ln, ph, plo, uh, ul)


def mixture_grad_stage(me, gm, attended, oh, ol, plan, stream):
    rows_all, width = gm.shape
    rows, lanes = width // plan.dp, width // plan.fsdp

    def body(me_ref, gm_ref, att, oh_ref, ol_ref, gmix, away, keep, full):
        g = split(gm_ref[...])
        gmix[...] = mm3(g, (oh_ref[...], ol_ref[...]), 1, 0)
        full[...] = att[...]
        for core in range(2):
            res = mm3(g, split(half_lanes(full, me_ref[1], core, lanes)), 0, 0)
            mine = away if core else keep
            for d in range(plan.dp):
                for y in range(2):
                    value = res[d * rows : (d + 1) * rows, y * lanes : (y + 1) * lanes]
                    stream.put(mine, d ^ me_ref[0], core + 2 * y, 0, value)

    return call(
        body,
        [((rows_all, width), F32), (stream.shape(), F32), (stream.shape(), F32)],
        [pltpu.VMEM((rows_all, width), F32)],
        cost_estimate=cost(5),
        in_specs=[SMEM] + [whole()] * 4,
        out_specs=[whole()] * 3,
    )(me, gm, attended, oh, ol)


def packed_grad_stage(dq, dk, dv, g4, g5a, g5b, pool, seqs):
    rows_all, width = dq.shape
    length = rows_all // seqs

    def body(dq_r, dk_r, dv_r, g4_r, g5a_r, g5b_r, pool_r, gph, gpl):
        for j, ref in enumerate((dq_r, dk_r, dv_r)):
            for s in range(seqs):
                rs = slice(s * length, (s + 1) * length)
                value = ref[rs, :]
                if j:
                    groups = jnp.concatenate(
                        [g4_r[s, j - 1], g5a_r[s, j - 1] + g5b_r[s, j - 1]], axis=0
                    )
                    value = value + mm2(pool_r[...], split(groups), 0, 0)
                h = split(value)
                gph[rs, j * width : (j + 1) * width] = h[0]
                gpl[rs, j * width : (j + 1) * width] = h[1]

    return call(
        body,
        [((rows_all, 3 * width), BF16)] * 2,
        cost_estimate=cost(4.5),
        in_specs=[whole()] * 7,
        out_specs=[whole()] * 2,
    )(dq, dk, dv, g4, g5a, g5b, pool)


def input_grad_stage(gph, gpl, wqh, wql, xhat, inv, ln, gm, gln):
    rows_all, width = gm.shape

    def body(gph_r, gpl_r, wh, wl, xhat_r, inv_r, ln_r, gm_r, gln_r, gtok, lrow):
        e = mm3((gph_r[...], gpl_r[...]), (wh[...], wl[...]), 1, 0)
        xh = xhat_r[...]
        gtok[...] = gm_r[...] + norm_back(e, ln_r[0:1, :], xh, inv_r[:, 0:1])
        sums = [
            jnp.sum(e * xh, axis=0, keepdims=True),
            jnp.sum(e, axis=0, keepdims=True),
            gln_r[0:1, :],
            gln_r[1:2, :],
        ]
        for p in range(4):
            lrow[p : p + 1, :] = sums[p]

    return call(
        body,
        [((rows_all, width), F32), ((4, width), F32)],
        cost_estimate=cost(7.4),
        in_specs=[whole()] * 9,
        out_specs=[whole()] * 2,
    )(gph, gpl, wqh, wql, xhat, inv, ln, gm, gln)


def grad_qkv_stage(me, gph, gpl, xhat, ln, plan, stream, core):
    rows_all, triple = gph.shape
    width = triple // 3
    rows, lanes = triple // plan.dp, width // plan.fsdp

    def body(me_ref, gph_r, gpl_r, xhat_r, ln_r, out, full):
        full[...] = xhat_r[...] * ln_r[0:1, :] + ln_r[1:2, :]
        n = split(half_lanes(full, me_ref[1], core, lanes))
        res = mm3((gph_r[...], gpl_r[...]), n, 0, 0)
        for d in range(plan.dp):
            jd = me_ref[0] ^ d
            for y in range(2):
                value = res[d * rows : (d + 1) * rows, y * lanes : (y + 1) * lanes]
                stream.put(out, jd, core + 2 * y, 0, value)

    return call(
        body,
        [(stream.shape(), F32)],
        [pltpu.VMEM((rows_all, width), F32)],
        cost_estimate=cost(4.9),
        in_specs=[SMEM] + [whole()] * 4,
        out_specs=[whole()],
    )(me, gph, gpl, xhat, ln)[0]


def swap(x, mask, axis="fsdp"):
    size = lax.axis_size(axis)
    return lax.ppermute(x, axis, [(i, i ^ mask) for i in range(size)])


def local(
    tokens, segments, cotangent, ln1_gain, ln1_bias, w_qkv, w_out, ln2_gain, ln2_bias, w_up, w_down
):
    seqs, length, width = tokens.shape
    dp, fsdp = lax.axis_size("dp"), lax.axis_size("fsdp")
    plan = Plan(dp, fsdp)
    me_d = lax.axis_index("dp")
    me = jnp.stack([me_d, lax.axis_index("fsdp")]).astype(jnp.int32)
    rows_all = seqs * length
    hidden_width = w_down.shape[0] * fsdp

    spread, pool, same = pooling(length)
    layout, _ = level_layout(length)
    local_rows = [first for level, first, _ in layout if 2 * NR * (1 << level) > length][0]
    spread_c = jnp.asarray(spread, BF16)
    pool_c = jnp.asarray(pool, BF16)
    same_c = jnp.asarray(same, F32)
    far_pool = jnp.asarray(pool[local_rows : local_rows + (length >> 4) + (length >> 5)], BF16)

    share = width // dp
    norms = jnp.stack([ln1_gain, ln1_bias, ln2_gain, ln2_bias])
    placed = lax.dynamic_update_slice(jnp.zeros((4, width), F32), norms, (0, me_d * share))
    placed = placed.reshape(4, 4, 128).transpose(1, 0, 2).reshape(LN_ROWS, 128)
    rows_qkv, rows_d, rows_up = 3 * share, share, hidden_width // dp
    chunks = hidden_width // fsdp // 128
    down_piece = w_down.T.reshape(rows_d, chunks, 128).transpose(1, 0, 2).reshape(-1, 128)
    down_piece = jnp.concatenate([down_piece, w_out.T], axis=0)
    extra = [(name,) for name in plan.extra]
    qkv_piece = jnp.concatenate([placed, w_qkv.T], axis=0)
    up_piece = w_up.T
    qkv_in, down_in, up_in = (Gather(plan, p) for p in (qkv_piece, down_piece, up_piece))
    tok = tokens.reshape(rows_all, width)
    cot = cotangent.reshape(rows_all, width)
    attend = (spread_c, pool_c, same_c)

    near = swap(segments, 1)
    far_segments = swap(jnp.stack([segments, near]), 2)
    bias = score_bias(segments, near, far_segments[0], far_segments[1])
    qkv_in.send([("z", "w")])
    for group in extra:
        qkv_in.stage([group])
    gate = qkv_in.came()
    qkv_in.stage([("x", "y")])
    down_in.send([("w",)], gate)
    for group in extra:
        down_in.stage([group])
    gate = down_in.came()
    down_in.stage([("z",)], gate)
    gate = (qkv_in.came(), down_in.came())
    cores = qkv_in.share(True, gate) + qkv_in.share(False, gate)
    up_in.send([("w",)], gate)
    for group in extra:
        up_in.stage([group])
    down_in.join()
    down_in.cut(down_piece.shape[0] // 16 * 8)
    down_in.send([("x",), ("y",)], cores)
    packed, wqh, wql, xhat1, inv1, ln, s4, s5 = qkv_stage(
        me, after(tok, cores, bias), qkv_in, plan, far_pool, seqs
    )
    gate = (packed, up_in.came())
    s4, s5 = after((s4, s5), gate)
    got = [swap(s4, 1), swap(s5, 2), swap(s5, 3)]
    far = jnp.concatenate(got, axis=2)
    gate = (far, down_in.came())
    down_in.stage([("y",), ("x",)], gate)
    down_in.share(True, gate)
    up_in.stage([("z",)], gate)
    calls = [(s, 1, 0, width // 128) for s in range(seqs)]
    before = ()
    for index, which in enumerate(calls):
        packed_in = after(packed, gate, before)
        before = attention_forward(packed_in, far, bias, *attend, seqs, local_rows, which, before)
        if index == 0:
            gate = (up_in.came(), before)
            up_in.join()
            up_in.cut(rows_up // 2 // 8 * 8)
            up_in.send([("x",), ("y",)], gate)
    attended, lse = before
    gate = (attended, down_in.came(), up_in.came())
    cores = down_in.share(False, gate)
    up_in.stage([("y",), ("x",)], gate)
    up_in.share(True, gate)
    gh, dh, dl, oh, ol = grad_hidden_stage(me, after(cot, cores), down_in, plan, hidden_width)
    gate = (gh, up_in.came())
    cores = up_in.share(False, gate)
    middle, xhat2, inv2 = middle_stage(tok, after(attended, gate), oh, ol)
    hh, hl, ph, plo, uh, ul = hidden_stage(me, after(xhat2, cores), ln, gh, up_in, plan)

    single = [("x", "y"), ("z",), ("w",)] + extra
    double = [("x", "y"), ("z", "w")] + extra
    down = Stream(plan, chunks * rows_d, single)
    up = Stream(plan, rows_up, single)
    out = Stream(plan, rows_d, single)
    qkv = Stream(plan, rows_qkv, double)
    down_sum, up_sum, qkv_sum = Reduce(plan, single), Reduce(plan, single), Reduce(plan, double)

    away = grad_down_stage(me, cot, hh, hl, plan, down, 1)
    got = down_sum.begin(away)
    keep = grad_down_stage(me, after(cot, away), hh, hl, plan, down, 0)
    down_sum.keep(keep)
    sent = down_sum.send(keep, got)
    away = grad_up_stage(me, after(xhat2, sent), ln, ph, plo, plan, up, 1)
    up_core = up_sum.begin(away)
    keep = grad_up_stage(me, after(xhat2, away), ln, ph, plo, plan, up, 0)
    up_sum.keep(keep)
    gm, gln = middle_grad_stage(after(cot, keep), xhat2, inv2, ln, ph, plo, uh, ul)
    gmix, away, keep = mixture_grad_stage(
        me, after(gm, up_core), attended, oh, ol, plan, out
    )
    got = up_sum.begin(away, down_sum.last)
    up_sum.keep(keep)
    down_sent = down_sum.send(gmix)
    sent = up_sum.send(got, down_sent)
    before = ()
    half = width // 256
    calls = [(s, 1, h, half) for s in range(seqs) for h in (0, half)]
    for index, which in enumerate(calls):
        grad = after(gmix, sent, before)
        before = attention_backward(
            packed, far, bias, *attend, attended, lse, grad, seqs, local_rows, which, before
        )
        if down_sum.stages:
            sent = down_sum.send(before, down_sum.last)
        else:
            sent = (sent, down_sum.last)
    gate = (before, up_sum.last)
    dq, dk, dv, f4, f5a, f5b = before
    sent = up_sum.send(gate)
    f4, f5a, f5b = after((f4, f5a, f5b), gate)
    g4, g5a, g5b = swap(f4, 1), swap(f5a, 2), swap(f5b, 3)
    gph, gpl = packed_grad_stage(dq, dk, dv, after(g4, sent), g5a, g5b, far_pool, seqs)
    while up_sum.stages:
        sent = up_sum.send(up_sum.last, gph)
    away = grad_qkv_stage(me, after(gph, sent), gpl, xhat1, ln, plan, qkv, 1)
    got = qkv_sum.begin(away)
    keep = grad_qkv_stage(me, gph, gpl, after(xhat1, away), ln, plan, qkv, 0)
    qkv_sum.keep(keep)
    sent = qkv_sum.send(got, up_sum.last)
    gtok, sums = input_grad_stage(gph, gpl, wqh, wql, after(xhat1, sent), inv1, ln, gm, gln)
    sums = sums + plan.send(sums, ("c",))
    output = output_stage(after(middle, sums), hh, hl, dh, dl)
    for name in ("x", "y"):
        sums = sums + plan.send(sums, (name,))
    (g_down,), (g_up, g_out) = down_sum.total(), up_sum.total()
    while qkv_sum.stages:
        sent = qkv_sum.send(qkv_sum.last, output)
    for name in ["z", "w"] + plan.extra:
        sums = sums + plan.send(after(sums, sent), (name,))
    (g_qkv,) = qkv_sum.total()
    mine = lax.dynamic_slice(sums, (0, me_d * share), (4, share))
    g_down = g_down.reshape(chunks, rows_d, 128).transpose(0, 2, 1).reshape(-1, rows_d)
    shape = tokens.shape
    return (
        output.reshape(shape),
        gtok.reshape(shape),
        mine[0],
        mine[1],
        g_qkv.T,
        g_out.T,
        mine[2],
        mine[3],
        g_up.T,
        g_down,
    )


def solution(mesh):
    weight = P("fsdp", "dp")
    rows = P("dp", "fsdp", None)
    vector = P("dp")
    return jax.shard_map(
        local,
        mesh=mesh,
        in_specs=(rows, P("dp", "fsdp"), rows, vector, vector, weight, weight, vector, vector, weight, weight),
        out_specs=(rows, rows, vector, vector, weight, weight, vector, vector, weight, weight),
        check_vma=False,
    )
```

```python
import jax
import jax.numpy as jnp
import numpy as np
from jax import lax
from jax.experimental import pallas as pl
from jax.experimental.pallas import tpu as pltpu
from jax.sharding import PartitionSpec as P

HEADS = 8
NR = 16
LEVELS = 6
EPSILON = 1e-05
MASKED = -1e30
F32 = jnp.float32
BF16 = jnp.bfloat16
LN_ROWS = 16
TILE = 128
SCALE = 0.05


def split(x):
    high = x.astype(BF16)
    return high, (x - high.astype(F32)).astype(BF16)


def mm(a, b, ca, cb):
    return lax.dot_general(a, b, (((ca,), (cb,)), ((), ())), preferred_element_type=F32)


def mm3(a, b, ca, cb):
    return mm(a[0], b[0], ca, cb) + mm(a[0], b[1], ca, cb) + mm(a[1], b[0], ca, cb)


def mm2(a, b, ca, cb):
    return mm(a, b[0], ca, cb) + mm(a, b[1], ca, cb)


def level_layout(length):
    rows, start = [], 0
    for level in range(1, LEVELS):
        count = length >> level
        rows.append((level, start, count))
        start += count
    return rows, start


def pooling(length):
    spread = np.zeros((length, length), np.float32)
    pool = np.zeros((length, length), np.float32)
    same = np.zeros((length, length), np.float32)
    layout, _ = level_layout(length)
    bounds = [first for _, first, _ in layout] + [length]
    for index, (level, first, count) in enumerate(layout):
        token = np.arange(length)
        spread[token, first + (token >> level)] = 1.0
        pool[first + (token >> level), token] = 0.5**level
        same[bounds[index] : bounds[index + 1], bounds[index] : bounds[index + 1]] = 1.0
    return spread, pool, same


def score_bias(seg, near, far_a, far_b):
    count, length = seg.shape
    token = np.arange(length)
    near_pair = (token[:TILE, None] >> 5) == (token[None, :TILE] >> 5)
    tiles = seg.reshape(count, length // TILE, TILE)
    ok = near_pair & (tiles[:, :, :, None] == tiles[:, :, None, :])
    inner = jnp.where(ok, 0.0, MASKED).astype(F32).reshape(count, length, TILE)
    parts = []
    for level in range(1, LEVELS):
        ratio = 1 << level

        def ends(values):
            grouped = values.reshape(count, length // ratio, ratio)
            return grouped[:, :, 0], grouped[:, :, -1]

        low_q, high_q = ends(seg)
        low_q = jnp.repeat(low_q, ratio, axis=1)
        high_q = jnp.repeat(high_q, ratio, axis=1)
        if 2 * NR * ratio <= length:
            low_k, high_k = ends(seg)
            block_q = (token >> level) >> 4
            block_k = np.arange(length >> level) >> 4
            where = (block_q[:, None] ^ 1) == block_k[None, :]
        else:
            if NR * ratio <= length:
                low_k, high_k = ends(near)
            else:
                pieces = [ends(far_a), ends(far_b)]
                low_k = jnp.concatenate([pieces[0][0], pieces[1][0]], axis=1)
                high_k = jnp.concatenate([pieces[0][1], pieces[1][1]], axis=1)
            where = np.ones((length, low_k.shape[1]), bool)
        ok = (
            where[None]
            & (low_q[:, :, None] <= high_k[:, None, :])
            & (low_k[:, None, :] <= high_q[:, :, None])
        )
        parts.append(jnp.where(ok, np.float32(level * np.log(2.0)), MASKED))
    return inner, jnp.concatenate(parts, axis=2).astype(F32)


class Plan:
    def __init__(self, dp, fsdp):
        self.dp, self.fsdp = dp, fsdp
        self.dims = {}
        names = ["x", "z", "w"]
        bit = 1
        while bit < dp:
            name = names[len(self.dims)] if len(self.dims) < 3 else "d%d" % bit
            self.dims[name] = ("dp", bit)
            bit *= 2
        self.extra = list(self.dims)[3:]
        self.dims["y"] = ("fsdp", 2)
        self.dims["c"] = ("fsdp", 1)

    def corner(self, group, v):
        return tuple(name for i, name in enumerate(group) if (v >> i) & 1)

    def mask(self, names):
        d = f = 0
        for name in names:
            axis, bit = self.dims[name]
            if axis == "dp":
                d |= bit
            else:
                f |= bit
        return d, f

    def send(self, x, names):
        d, f = self.mask(names)
        if not f:
            return lax.ppermute(x, "dp", [(i, i ^ d) for i in range(self.dp)])
        if not d:
            return lax.ppermute(x, "fsdp", [(i, i ^ f) for i in range(self.fsdp)])
        n = self.fsdp
        pairs = [(i, ((i // n) ^ d) * n + ((i % n) ^ f)) for i in range(self.dp * n)]
        return lax.ppermute(x, ("dp", "fsdp"), pairs)

    def position(self, stages, d, f):
        pos = 0
        for group in stages:
            for name in reversed(group):
                axis, bit = self.dims[name]
                value = d if axis == "dp" else f
                pos = pos * 2 + ((value // bit) & 1)
        return pos


class Part:
    def __init__(self, start, held, names):
        self.start, self.held, self.names, self.got = start, held, names, []


class Gather:
    def __init__(self, plan, piece):
        self.plan, self.parts = plan, [Part(0, piece[None], [()])]
        self.arrays, self.slots = [], []

    def cut(self, row):
        (part,) = self.parts
        self.parts = [
            Part(0, part.held[:, :row], part.names),
            Part(row, part.held[:, row:], part.names),
        ]

    def send(self, groups, *earlier):
        for part, group in zip(self.parts, groups):
            if earlier:
                part.held = after(part.held, *earlier)
            for v in range(1, 1 << len(group)):
                names = self.plan.corner(group, v)
                part.got.append((self.plan.send(part.held, names), names))

    def came(self):
        return [value for part in self.parts for value, _ in part.got]

    def join(self):
        for part in self.parts:
            names = list(part.names)
            for _, corner in part.got:
                names += [n + corner for n in part.names]
            part.held = jnp.concatenate([part.held] + [v for v, _ in part.got], axis=0)
            part.names, part.got = names, []

    def stage(self, groups, *earlier):
        self.join()
        self.send(groups, *earlier)

    def share(self, held, *earlier):
        sent = []
        for part in self.parts:
            for value, corner in [(part.held, ())] if held else part.got:
                if earlier:
                    value = after(value, *earlier)
                other = self.plan.send(value, ("c",))
                sent.append(other)
                for array, core in ((value, ()), (other, ("c",))):
                    self.arrays.append(array)
                    slots = [self.plan.mask(n + corner + core) for n in part.names]
                    self.slots.append((slots, part.start))
        return sent


def assemble(scratch, refs, gathered, me_d, me_f, rows, lanes, segments):
    for ref, (slots, start) in zip(refs, gathered.slots):
        for slot, (d, f) in enumerate(slots):
            row0 = (me_d ^ d) * rows
            col0 = (me_f ^ f) * lanes
            for source, size, to_lane in segments:
                low, high = max(source, start), min(source + size, start + ref.shape[1])
                if low < high:
                    row = pl.multiple_of(row0 + (low - source), 8)
                    col = pl.multiple_of(col0 + to_lane, 128)
                    scratch[pl.ds(row, high - low), pl.ds(col, 128)] = ref[
                        slot, low - start : high - start, :
                    ]


def norm_rows(refs, gathered):
    total = None
    for ref, (slots, start) in zip(refs, gathered.slots):
        for slot, (d, f) in enumerate(slots):
            if f == 0 and start == 0:
                value = ref[slot, :LN_ROWS, :]
                total = value if total is None else total + value
    return jnp.concatenate([total[4 * i : 4 * i + 4] for i in range(4)], axis=1)


class Stream:
    def __init__(self, plan, rows, stages):
        self.plan, self.rows, self.stages = plan, rows, stages
        self.slots = plan.dp * plan.fsdp // 2

    def shape(self):
        return (self.slots, self.rows, 128)

    def put(self, out, d, f, row, value):
        size = value.shape[0]
        out[self.plan.position(self.stages, d, f), row : row + size, :] = value


class Reduce:
    def __init__(self, plan, stages):
        self.plan, self.stages = plan, list(stages)
        self.kept, self.came, self.last = [], [], []

    def begin(self, part, *earlier):
        part = after(part, *earlier) if earlier else part
        self.last = [self.plan.send(part, ("c",))]
        self.came.append(self.last[0])
        return self.last

    def keep(self, part):
        self.kept.append(part)

    def send(self, *earlier, rider=None):
        if self.kept:
            self.terms = [self.kept, self.came]
            self.slots, self.kept = self.kept[0].shape[0], []
        if earlier:
            self.terms[-1] = after(self.terms[-1], *earlier)
        group = self.stages.pop(0)
        self.slots >>= len(group)
        n = self.slots
        count = range(len(self.terms[0]))
        sizes = [part.shape[1] for part in self.terms[0]]
        cuts = np.cumsum([0] + sizes)
        out = []
        for v in range(1, 1 << len(group)):
            parts = [sum(term[i][v * n : (v + 1) * n] for term in self.terms) for i in count]
            if rider is not None:
                parts.append(jnp.broadcast_to(rider[None], (n,) + rider.shape))
            out.append(parts[0] if len(parts) == 1 else jnp.concatenate(parts, axis=1))
        self.last, self.rode = [], rider
        for v, value in enumerate(out):
            got = self.plan.send(value, self.plan.corner(group, v + 1))
            self.last.append(got)
            self.terms.append([got[:, a:b] for a, b in zip(cuts[:-1], cuts[1:])])
            if rider is not None:
                self.rode = self.rode + got[0, cuts[-1] :]
        return out

    def total(self, *earlier):
        count = range(len(self.terms[0]))
        return [sum(term[i][0] for term in self.terms) for i in count]


def after(value, *earlier):
    return lax.optimization_barrier((value, earlier))[0]


def whole(shape=None):
    return pl.BlockSpec(memory_space=pltpu.VMEM)


SMEM = pl.BlockSpec(memory_space=pltpu.SMEM)


def cost(micros):
    return pl.CostEstimate(
        flops=int(micros * SCALE * 9e8), bytes_accessed=int(micros * SCALE * 2.5e6), transcendentals=0
    )


def call(body, outs, scratch=(), **kw):
    return pl.pallas_call(
        body,
        out_shape=[jax.ShapeDtypeStruct(s, t) for s, t in outs],
        scratch_shapes=list(scratch),
        **kw,
    )


def qkv_stage(me, tokens, gathered, plan, pool, seqs):
    rows_all, width = tokens.shape
    length = rows_all // seqs
    triple = 3 * width
    rows = triple // plan.dp
    lanes = width // plan.fsdp
    n4, n5 = length >> 4, length >> 5
    slots = gathered.arrays

    def body(me_ref, tok, pool_ref, *rest):
        refs = rest[: len(slots)]
        packed, wh, wl, xhat, inv, ln, s4, s5, full = rest[len(slots) :]
        segments = [(LN_ROWS, rows, 0)]
        assemble(full, refs, gathered, me_ref[0], me_ref[1], rows, lanes, segments)
        params = norm_rows(refs, gathered)
        ln[0:4, :] = params
        w = split(full[...])
        wh[...] = w[0]
        wl[...] = w[1]
        x = tok[...]
        centre = x - jnp.mean(x, axis=1, keepdims=True)
        scale = lax.rsqrt(jnp.mean(centre * centre, axis=1, keepdims=True) + EPSILON)
        xh = centre * scale
        xhat[...] = xh
        inv[...] = jnp.broadcast_to(scale, inv.shape)
        normed = xh * params[0:1, :] + params[1:2, :]
        packed[...] = mm3(split(normed), w, 1, 1)
        a24 = pool_ref[...]
        for s in range(seqs):
            for j in range(2):
                kv = packed[
                    s * length : (s + 1) * length, (j + 1) * width : (j + 2) * width
                ]
                means = mm2(a24, split(kv), 1, 0)
                s4[s, j] = means[:n4]
                s5[s, j] = means[n4 : n4 + n5]

    return call(
        body,
        [
            ((rows_all, triple), F32),
            ((triple, width), BF16),
            ((triple, width), BF16),
            ((rows_all, width), F32),
            ((rows_all, 128), F32),
            ((8, width), F32),
            ((seqs, 2, n4, width), F32),
            ((seqs, 2, n5, width), F32),
        ],
        [pltpu.VMEM((triple, width), F32)],
        cost_estimate=cost(7.4),
        in_specs=[SMEM, whole(), whole()] + [whole()] * len(slots),
        out_specs=[whole()] * 8,
    )(me, tokens, pool, *slots)


def lanes2(pair):
    return jnp.concatenate(pair, axis=1)


def fold(r):
    return r[:, :128] + r[:, 128:]


def wide_nt(a, b):
    first = mm(lanes2(a), lanes2((b[0], b[0])), 1, 1)
    return first + mm(a[0], b[1], 1, 1)


def wide_nn(a, b):
    return fold(mm(a[0], lanes2(b), 1, 0)) + mm(a[1], b[0], 1, 0)


def wide_tn(a, b):
    return fold(mm(a[0], lanes2(b), 0, 0)) + mm(a[1], b[0], 0, 0)


def tile_tn(a, b):
    left = jnp.concatenate(a, axis=0)
    right = jnp.concatenate([lanes2(b), lanes2((b[0], jnp.zeros_like(b[0])))], axis=0)
    return fold(mm(left, right, 0, 0))


def rows(pair, t):
    return tuple(x[t * TILE : (t + 1) * TILE] for x in pair)


class Heads:
    def __init__(self, q, k, v, fk, fv, pool, local):
        length = q.shape[0]
        self.tiles = range(length // TILE)
        self.lane = lax.broadcasted_iota(jnp.int32, (length, 128), 1) < 64
        qs, ks, vs = split(q), split(k), split(v)
        pooled = mm(pool, jnp.concatenate([qs[0], ks[0], vs[0], qs[1], ks[1], vs[1]], axis=1), 1, 0)
        pooled = pooled[:, :384] + pooled[:, 384:]
        kc = jnp.concatenate([pooled[:local, 128:256], fk], axis=0)
        vc = jnp.concatenate([pooled[:local, 256:], fv], axis=0)
        self.q, self.qc = qs, split(pooled[:, :128])
        self.k2 = [self.two(rows(ks, t)) for t in self.tiles]
        self.v2 = [self.two(rows(vs, t)) for t in self.tiles]
        self.kc2, self.vc2 = self.two(split(kc)), self.two(split(vc))

    def two(self, pair):
        out = []
        for x in pair:
            lane = self.lane[: x.shape[0]]
            zero = jnp.zeros_like(x)
            both = [jnp.where(lane, x, zero), jnp.where(lane, zero, x)]
            out.append(jnp.concatenate(both, axis=0))
        return tuple(out)

    def one(self, x):
        half = x.shape[0] // 2
        return jnp.where(self.lane[:half], x[:half], x[half:])

    def inner(self, left, right):
        return jnp.concatenate([wide_nt(rows(left, t), right[t]) for t in self.tiles], axis=0)

    def scores(self, spread, same, inner_bias, outer_bias):
        s0 = self.inner(self.q, self.k2) + lanes2((inner_bias, inner_bias))
        high, low = split(wide_nt(self.qc, self.kc2) * lanes2((same, same)))
        st = mm(spread, high, 1, 0) + mm(spread, low, 1, 0)
        return s0, st + lanes2((outer_bias, outer_bias))


def head_columns(x):
    half = x.shape[1] // 2
    return x[:, :half], x[:, half:]


def attention_specs(length, width, first=0, pair=0):
    pairs = width // 128
    block = lambda off: pl.BlockSpec((length, 128), lambda s, h: (first + s, off * pairs + pair + h))
    far = lambda j: pl.BlockSpec((1, 1, 32, 128), lambda s, h: (first + s, j, 0, pair + h))
    fixed = pl.BlockSpec((length, length), lambda s, h: (0, 0))
    bias = lambda n: pl.BlockSpec((1, length, n), lambda s, h: (first + s, 0, 0))
    return block, far, fixed, [bias(TILE), bias(length), fixed, fixed, fixed]


def attention_forward(packed, far, bias, spread, pool, same, seqs, local, which, before):
    rows_all, triple = packed.shape
    width = triple // 3
    length = rows_all // seqs
    first, count, pair, pairs = which
    block, far_spec, fixed, common = attention_specs(length, width, first, pair)
    carried = len(before)

    def body(q, k, v, fk, fv, inner_bias, outer_bias, spread_ref, pool_ref, same_ref, *rest):
        out, lse = rest[carried:]
        heads = Heads(q[...] * 0.125, k[...], v[...], fk[0, 0], fv[0, 0], pool_ref[...], local)
        s0, st = heads.scores(spread_ref[...], same_ref[...], inner_bias[0], outer_bias[0])
        p0, pc, peaks, sums = [], [], [], []
        for a, b in zip(head_columns(s0), head_columns(st)):
            peak = jnp.maximum(jnp.max(a, axis=1, keepdims=True), jnp.max(b, axis=1, keepdims=True))
            a, b = jnp.exp(a - peak), jnp.exp(b - peak)
            p0.append(a)
            pc.append(b)
            peaks.append(peak)
            sums.append(jnp.sum(a, axis=1, keepdims=True) + jnp.sum(b, axis=1, keepdims=True))
        p0, pc = split(lanes2(p0)), split(lanes2(pc))
        mixed = [wide_nn(rows(p0, t), heads.v2[t]) for t in heads.tiles]
        mixed = jnp.concatenate(mixed, axis=0) + wide_nn(pc, heads.vc2)
        total = jnp.where(heads.lane, sums[0], sums[1])
        out[...] = mixed / total
        lse[...] = jnp.where(heads.lane, peaks[0], peaks[1]) + jnp.log(total)

    return pl.pallas_call(
        body,
        cost_estimate=cost(9.5),
        grid=(count, pairs),
        out_shape=[jax.ShapeDtypeStruct((rows_all, width), F32)] * 2,
        in_specs=[block(0), block(1), block(2), far_spec(0), far_spec(1)]
        + common
        + [pl.BlockSpec(memory_space=pl.ANY)] * carried,
        out_specs=[block(0), block(0)],
        input_output_aliases={10 + i: i for i in range(carried)},
    )(packed, packed, packed, far, far, *bias, spread, pool, same, *before)


def attention_backward(
    packed, far, bias, spread, pool, same, attended, lse, grad, seqs, local, which, before
):
    rows_all, triple = packed.shape
    width = triple // 3
    length = rows_all // seqs
    first, count, pair, pairs = which
    block, far_spec, fixed, common = attention_specs(length, width, first, pair)
    n4, n5 = length >> 4, length >> 5
    carried = len(before)

    def body(q, k, v, fk, fv, inner_bias, outer_bias, spread_ref, pool_ref, same_ref, *rest):
        o_ref, lse_ref, g_ref = rest[:3]
        dq_ref, dk_ref, dv_ref, f4, f5a, f5b = rest[3 + carried :]
        spread_m, pool_m, same_m = spread_ref[...], pool_ref[...], same_ref[...]
        heads = Heads(q[...] * 0.125, k[...], v[...], fk[0, 0], fv[0, 0], pool_m, local)
        lane = heads.lane
        s0, st = heads.scores(spread_m, same_m, inner_bias[0], outer_bias[0])
        logs = lse_ref[...]
        logs = (logs[:, 0:1], logs[:, 64:65])
        p0 = lanes2([jnp.exp(a - x) for a, x in zip(head_columns(s0), logs)])
        pc = lanes2([jnp.exp(a - x) for a, x in zip(head_columns(st), logs)])
        grad_rows = g_ref[...]
        g = split(grad_rows)
        product = grad_rows * o_ref[...]
        zero = jnp.zeros_like(product)
        deltas = [
            jnp.sum(jnp.where(lane, product, zero), axis=1, keepdims=True),
            jnp.sum(jnp.where(lane, zero, product), axis=1, keepdims=True),
        ]
        d0 = heads.inner(g, heads.v2)
        d0 = split(p0 * lanes2([a - x for a, x in zip(head_columns(d0), deltas)]))
        dt = wide_nt(g, heads.vc2)
        dt = split(pc * lanes2([a - x for a, x in zip(head_columns(dt), deltas)]))
        p0, pc = split(p0), split(pc)
        dv = [heads.one(tile_tn(rows(p0, t), rows(g, t))) for t in heads.tiles]
        dk = [heads.one(tile_tn(rows(d0, t), rows(heads.q, t))) for t in heads.tiles]
        dq = [wide_nn(rows(d0, t), heads.k2[t]) for t in heads.tiles]
        dvc = heads.one(wide_tn(pc, g))
        dsc = mm(spread_m, dt[0], 0, 0) + mm(spread_m, dt[1], 0, 0)
        dsc = split(dsc * lanes2((same_m, same_m)))
        dqc = wide_nn(dsc, heads.kc2)
        dkc = heads.one(wide_tn(dsc, heads.qc))
        near = lax.broadcasted_iota(jnp.int32, (length, 128), 0) < local
        high, low = split(
            jnp.concatenate([dqc, jnp.where(near, dkc, zero), jnp.where(near, dvc, zero)], axis=1)
        )
        back = mm(pool_m, lanes2((high, low)), 0, 0)
        back = back[:, :384] + back[:, 384:]
        dq_ref[...] = (jnp.concatenate(dq, axis=0) + back[:, :128]) * 0.125
        dk_ref[...] = jnp.concatenate(dk, axis=0) + back[:, 128:256]
        dv_ref[...] = jnp.concatenate(dv, axis=0) + back[:, 256:]
        for j, value in ((0, dkc), (1, dvc)):
            f4[0, j] = value[local : local + n4]
            f5a[0, j] = value[local + n4 : local + n4 + n5]
            f5b[0, j] = value[local + n4 + n5 :]

    far_out = lambda n: pl.BlockSpec((1, 2, n, 128), lambda s, h: (first + s, 0, 0, pair + h))
    return pl.pallas_call(
        body,
        cost_estimate=cost(8),
        grid=(count, pairs),
        out_shape=[jax.ShapeDtypeStruct((rows_all, width), F32)] * 3
        + [jax.ShapeDtypeStruct((seqs, 2, n, width), F32) for n in (n4, n5, n5)],
        in_specs=[block(0), block(1), block(2), far_spec(0), far_spec(1)]
        + common
        + [block(0)] * 3
        + [pl.BlockSpec(memory_space=pl.ANY)] * carried,
        out_specs=[block(0)] * 3 + [far_out(n4), far_out(n5), far_out(n5)],
        input_output_aliases={13 + i: i for i in range(carried)},
    )(packed, packed, packed, far, far, *bias, spread, pool, same, attended, lse, grad, *before)


def middle_stage(tokens, attended, wh, wl):
    rows_all, width = tokens.shape

    def body(tok, att, wh_ref, wl_ref, middle, xhat, inv):
        x = tok[...] + mm3(split(att[...]), (wh_ref[...], wl_ref[...]), 1, 1)
        middle[...] = x
        centre = x - jnp.mean(x, axis=1, keepdims=True)
        scale = lax.rsqrt(jnp.mean(centre * centre, axis=1, keepdims=True) + EPSILON)
        xhat[...] = centre * scale
        inv[...] = jnp.broadcast_to(scale, inv.shape)

    return call(
        body,
        [((rows_all, width), F32), ((rows_all, width), F32), ((rows_all, 128), F32)],
        cost_estimate=cost(4.3),
        in_specs=[whole()] * 4,
        out_specs=[whole()] * 3,
    )(tokens, attended, wh, wl)


def grad_hidden_stage(me, cot, gathered, plan, hidden_width):
    rows_all, width = cot.shape
    rows, lanes = width // plan.dp, hidden_width // plan.fsdp
    out_lanes = width // plan.fsdp
    slots = gathered.arrays
    chunks = lanes // 128
    down_parts = [(k * rows, rows, 128 * k) for k in range(chunks)]
    out_parts = [(chunks * rows, rows, 0)]

    def body(me_ref, cot_ref, *rest):
        refs = rest[: len(slots)]
        gh, dh, dl, oh, ol, full, full_out = rest[len(slots) :]
        me_d, me_f = me_ref[0], me_ref[1]
        assemble(full_out, refs, gathered, me_d, me_f, rows, out_lanes, out_parts)
        w = split(full_out[...])
        oh[...] = w[0]
        ol[...] = w[1]
        assemble(full, refs, gathered, me_d, me_f, rows, lanes, down_parts)
        w = split(full[...])
        dh[...] = w[0]
        dl[...] = w[1]
        gh[...] = mm3(split(cot_ref[...]), w, 1, 0)

    return call(
        body,
        [
            ((rows_all, hidden_width), F32),
            ((width, hidden_width), BF16),
            ((width, hidden_width), BF16),
            ((width, width), BF16),
            ((width, width), BF16),
        ],
        [pltpu.VMEM((width, hidden_width), F32), pltpu.VMEM((width, width), F32)],
        cost_estimate=cost(9.6),
        in_specs=[SMEM, whole()] + [whole()] * len(slots),
        out_specs=[whole()] * 5,
    )(me, cot, *slots)


def hidden_stage(me, xhat, ln, gh, gathered, plan):
    rows_all, width = xhat.shape
    hidden_width = gh.shape[1]
    rows, lanes = hidden_width // plan.dp, width // plan.fsdp
    slots = gathered.arrays
    chunk = 512
    steps = hidden_width // chunk
    root = float(np.sqrt(2.0 / np.pi))

    def body(me_ref, xhat_ref, ln_ref, gh_ref, *rest):
        refs = rest[: len(slots)]
        hh, hl, ph, plo, wh, wl, full, nh, nl = rest[len(slots) :]
        step = pl.program_id(0)

        @pl.when(step == 0)
        def _():
            segments = [(0, rows, 0)]
            assemble(full, refs, gathered, me_ref[0], me_ref[1], rows, lanes, segments)
            w = split(full[...])
            wh[...] = w[0]
            wl[...] = w[1]
            n = split(xhat_ref[...] * ln_ref[2:3, :] + ln_ref[3:4, :])
            nh[...] = n[0]
            nl[...] = n[1]

        part = pl.ds(pl.multiple_of(step * chunk, chunk), chunk)
        v = mm3((nh[...], nl[...]), (wh[part, :], wl[part, :]), 1, 1)
        square = v * v
        t = jnp.tanh(root * v * (1.0 + 0.044715 * square))
        half = 0.5 * (1.0 + t)
        h = split(v * half)
        hh[...] = h[0]
        hl[...] = h[1]
        slope = half + 0.5 * v * (1.0 - t * t) * root * (1.0 + 3 * 0.044715 * square)
        g = split(gh_ref[...] * slope)
        ph[...] = g[0]
        plo[...] = g[1]

    fixed = lambda shape: pl.BlockSpec(shape, lambda i: (0,) * len(shape))
    cols = pl.BlockSpec((rows_all, chunk), lambda i: (0, i))
    return pl.pallas_call(
        body,
        cost_estimate=cost(13.7),
        grid=(steps,),
        out_shape=[jax.ShapeDtypeStruct((rows_all, hidden_width), BF16)] * 4
        + [jax.ShapeDtypeStruct((hidden_width, width), BF16)] * 2,
        in_specs=[SMEM, fixed((rows_all, width)), fixed((8, width)), cols]
        + [fixed(s.shape) for s in slots],
        out_specs=[cols] * 4 + [fixed((hidden_width, width))] * 2,
        scratch_shapes=[
            pltpu.VMEM((hidden_width, width), F32),
            pltpu.VMEM((rows_all, width), BF16),
            pltpu.VMEM((rows_all, width), BF16),
        ],
    )(me, xhat, ln, gh, *slots)


def grad_down_stage(me, cot, hh, hl, plan, stream, core):
    rows_all, width = cot.shape
    hidden_width = hh.shape[1]
    rows, lanes = width // plan.dp, hidden_width // plan.fsdp

    def body(me_ref, cot_ref, hh_ref, hl_ref, out):
        jf = core + 2 * pl.program_id(0)
        res = mm3(split(cot_ref[...]), (hh_ref[...], hl_ref[...]), 0, 0)
        for d in range(plan.dp):
            jd = me_ref[0] ^ d
            for k in range(lanes // 128):
                value = res[d * rows : (d + 1) * rows, 128 * k : 128 * (k + 1)]
                stream.put(out, jd, jf, k * rows, value)

    cols = pl.BlockSpec((rows_all, lanes), lambda i, m: (0, m[1] ^ (core + 2 * i)))
    grid_spec = pltpu.PrefetchScalarGridSpec(
        num_scalar_prefetch=1,
        grid=(plan.fsdp // 2,),
        in_specs=[pl.BlockSpec((rows_all, width), lambda i, m: (0, 0)), cols, cols],
        out_specs=pl.BlockSpec(stream.shape(), lambda i, m: (0, 0, 0)),
    )
    return pl.pallas_call(
        body,
        cost_estimate=cost(5.5),
        grid_spec=grid_spec,
        out_shape=jax.ShapeDtypeStruct(stream.shape(), F32),
    )(me, cot, hh, hl)


def half_lanes(ref, me_f, core, lanes):
    parts = []
    for y in range(2):
        start = pl.multiple_of((me_f ^ (core + 2 * y)) * lanes, 128)
        parts.append(ref[:, pl.ds(start, lanes)])
    return jnp.concatenate(parts, axis=1)


def grad_up_stage(me, xhat, ln, ph, plo, plan, stream, core):
    rows_all, width = xhat.shape
    hidden_width = ph.shape[1]
    rows, lanes = hidden_width // plan.dp, width // plan.fsdp
    chunk = 512
    steps = hidden_width // chunk
    per = chunk // rows

    def body(me_ref, xhat_ref, ln_ref, ph_ref, pl_ref, out, full, nh, nl):
        step = pl.program_id(0)

        @pl.when(step == 0)
        def _():
            full[...] = xhat_ref[...] * ln_ref[2:3, :] + ln_ref[3:4, :]
            n = split(half_lanes(full, me_ref[1], core, lanes))
            nh[...] = n[0]
            nl[...] = n[1]

        res = mm3((ph_ref[...], pl_ref[...]), (nh[...], nl[...]), 0, 0)
        for i in range(per):
            jd = (step * per + i) ^ me_ref[0]
            for y in range(2):
                value = res[i * rows : (i + 1) * rows, y * lanes : (y + 1) * lanes]
                stream.put(out, jd, core + 2 * y, 0, value)

    fixed = lambda shape: pl.BlockSpec(shape, lambda i: (0,) * len(shape))
    cols = pl.BlockSpec((rows_all, chunk), lambda i: (0, i))
    return pl.pallas_call(
        body,
        cost_estimate=cost(6.4),
        grid=(steps,),
        out_shape=jax.ShapeDtypeStruct(stream.shape(), F32),
        in_specs=[SMEM, fixed((rows_all, width)), fixed((8, width)), cols, cols],
        out_specs=fixed(stream.shape()),
        scratch_shapes=[pltpu.VMEM((rows_all, width), F32)]
        + [pltpu.VMEM((rows_all, 2 * lanes), BF16)] * 2,
    )(me, xhat, ln, ph, plo)


def norm_back(e, gain, xhat, inv):
    u = e * gain
    mean_u = jnp.mean(u, axis=1, keepdims=True)
    mean_ux = jnp.mean(u * xhat, axis=1, keepdims=True)
    return inv * (u - mean_u - xhat * mean_ux)


def output_stage(middle, hh, hl, dh, dl):
    rows_all, width = middle.shape
    chunk = 512
    steps = hh.shape[1] // chunk

    def body(mid, h0, h1, d0, d1, out):
        @pl.when(pl.program_id(0) == 0)
        def _():
            out[...] = mid[...]

        out[...] += mm3((h0[...], h1[...]), (d0[...], d1[...]), 1, 1)

    cols = pl.BlockSpec((rows_all, chunk), lambda i: (0, i))
    act = pl.BlockSpec((rows_all, width), lambda i: (0, 0))
    return pl.pallas_call(
        body,
        cost_estimate=cost(8),
        grid=(steps,),
        out_shape=jax.ShapeDtypeStruct((rows_all, width), F32),
        in_specs=[act, cols, cols] + [pl.BlockSpec((width, chunk), lambda i: (0, i))] * 2,
        out_specs=act,
    )(middle, hh, hl, dh, dl)


def middle_grad_stage(cot, xhat, inv, ln, ph, plo, uh, ul):
    rows_all, width = cot.shape
    chunk = 512
    steps = ph.shape[1] // chunk

    def body(cot_ref, xhat_ref, inv_ref, ln_ref, p0, p1, u0, u1, gm, gln, acc):
        step = pl.program_id(0)

        @pl.when(step == 0)
        def _():
            acc[...] = jnp.zeros_like(acc)

        acc[...] += mm3((p0[...], p1[...]), (u0[...], u1[...]), 1, 0)

        @pl.when(step == steps - 1)
        def _():
            e = acc[...]
            xh = xhat_ref[...]
            gm[...] = cot_ref[...] + norm_back(e, ln_ref[2:3, :], xh, inv_ref[:, 0:1])
            gln[0:1, :] = jnp.sum(e * xh, axis=0, keepdims=True)
            gln[1:2, :] = jnp.sum(e, axis=0, keepdims=True)

    fixed = lambda shape: pl.BlockSpec(shape, lambda i: (0,) * len(shape))
    cols = pl.BlockSpec((rows_all, chunk), lambda i: (0, i))
    act = fixed((rows_all, width))
    return pl.pallas_call(
        body,
        cost_estimate=cost(8.5),
        grid=(steps,),
        out_shape=[
            jax.ShapeDtypeStruct((rows_all, width), F32),
            jax.ShapeDtypeStruct((8, width), F32),
        ],
        in_specs=[act, act, fixed((rows_all, 128)), fixed((8, width)), cols, cols]
        + [pl.BlockSpec((chunk, width), lambda i: (i, 0))] * 2,
        out_specs=[act, fixed((8, width))],
        scratch_shapes=[pltpu.VMEM((rows_all, width), F32)],
    )(cot, xhat, inv, ln, ph, plo, uh, ul)


def mixture_grad_stage(me, gm, attended, oh, ol, plan, stream):
    rows_all, width = gm.shape
    rows, lanes = width // plan.dp, width // plan.fsdp

    def body(me_ref, gm_ref, att, oh_ref, ol_ref, gmix, away, keep, full):
        g = split(gm_ref[...])
        gmix[...] = mm3(g, (oh_ref[...], ol_ref[...]), 1, 0)
        full[...] = att[...]
        for core in range(2):
            res = mm3(g, split(half_lanes(full, me_ref[1], core, lanes)), 0, 0)
            mine = away if core else keep
            for d in range(plan.dp):
                for y in range(2):
                    value = res[d * rows : (d + 1) * rows, y * lanes : (y + 1) * lanes]
                    stream.put(mine, d ^ me_ref[0], core + 2 * y, 0, value)

    return call(
        body,
        [((rows_all, width), F32), (stream.shape(), F32), (stream.shape(), F32)],
        [pltpu.VMEM((rows_all, width), F32)],
        cost_estimate=cost(5),
        in_specs=[SMEM] + [whole()] * 4,
        out_specs=[whole()] * 3,
    )(me, gm, attended, oh, ol)


def packed_grad_stage(dq, dk, dv, g4, g5a, g5b, pool, seqs):
    rows_all, width = dq.shape
    length = rows_all // seqs

    def body(dq_r, dk_r, dv_r, g4_r, g5a_r, g5b_r, pool_r, gph, gpl):
        for j, ref in enumerate((dq_r, dk_r, dv_r)):
            for s in range(seqs):
                rs = slice(s * length, (s + 1) * length)
                value = ref[rs, :]
                if j:
                    groups = jnp.concatenate(
                        [g4_r[s, j - 1], g5a_r[s, j - 1] + g5b_r[s, j - 1]], axis=0
                    )
                    value = value + mm2(pool_r[...], split(groups), 0, 0)
                h = split(value)
                gph[rs, j * width : (j + 1) * width] = h[0]
                gpl[rs, j * width : (j + 1) * width] = h[1]

    return call(
        body,
        [((rows_all, 3 * width), BF16)] * 2,
        cost_estimate=cost(4.5),
        in_specs=[whole()] * 7,
        out_specs=[whole()] * 2,
    )(dq, dk, dv, g4, g5a, g5b, pool)


def input_grad_stage(gph, gpl, wqh, wql, xhat, inv, ln, gm):
    rows_all, width = gm.shape

    def body(gph_r, gpl_r, wh, wl, xhat_r, inv_r, ln_r, gm_r, gtok):
        e = mm3((gph_r[...], gpl_r[...]), (wh[...], wl[...]), 1, 0)
        gtok[...] = gm_r[...] + norm_back(e, ln_r[0:1, :], xhat_r[...], inv_r[:, 0:1])

    return call(
        body,
        [((rows_all, width), F32)],
        cost_estimate=cost(7.4),
        in_specs=[whole()] * 8,
        out_specs=[whole()],
    )(gph, gpl, wqh, wql, xhat, inv, ln, gm)[0]


def grad_qkv_stage(me, gph, gpl, xhat, ln, wh, wl, plan, stream, core):
    rows_all, triple = gph.shape
    width = triple // 3
    rows, lanes = triple // plan.dp, width // plan.fsdp

    def body(me_ref, gph_r, gpl_r, xhat_r, ln_r, wh_r, wl_r, out, sums):
        me_f = me_ref[1]
        pick = lambda ref: half_lanes(ref, me_f, core, lanes)
        params = pick(ln_r)
        gp = (gph_r[...], gpl_r[...])
        res = mm3(gp, split(pick(xhat_r)), 0, 0)
        w = (pick(wh_r), pick(wl_r))
        ones = jnp.ones((8, rows_all), BF16)
        total = mm(ones, gp[0], 1, 0) + mm(ones, gp[1], 1, 0)
        sums[0:1, :] = jnp.sum(res * (w[0].astype(F32) + w[1].astype(F32)), axis=0, keepdims=True)
        sums[1:2, :] = mm3(split(total), w, 1, 0)[0:1]
        column = mm(gp[0], ones[:, :], 0, 1) + mm(gp[1], ones[:, :], 0, 1)
        res = res * params[0:1, :] + column[:, 0:1] * params[1:2, :]
        for d in range(plan.dp):
            jd = me_ref[0] ^ d
            for y in range(2):
                value = res[d * rows : (d + 1) * rows, y * lanes : (y + 1) * lanes]
                stream.put(out, jd, core + 2 * y, 0, value)

    return call(
        body,
        [(stream.shape(), F32), ((2, 2 * lanes), F32)],
        cost_estimate=cost(4.9),
        in_specs=[SMEM] + [whole()] * 6,
        out_specs=[whole()] * 2,
    )(me, gph, gpl, xhat, ln, wh, wl)


def lane_order(me_f, away, keep, lanes):
    both = jnp.stack([keep, away], axis=1)
    parts = both.reshape(2, 2, 2, lanes)
    parts = parts.transpose(0, 2, 1, 3).reshape(2, 4, lanes)
    return parts[:, me_f ^ np.arange(4)].reshape(2, 4 * lanes)


def swap(x, mask, axis="fsdp"):
    size = lax.axis_size(axis)
    return lax.ppermute(x, axis, [(i, i ^ mask) for i in range(size)])


def local(
    tokens, segments, cotangent, ln1_gain, ln1_bias, w_qkv, w_out, ln2_gain, ln2_bias, w_up, w_down
):
    seqs, length, width = tokens.shape
    dp, fsdp = lax.axis_size("dp"), lax.axis_size("fsdp")
    plan = Plan(dp, fsdp)
    me_d = lax.axis_index("dp")
    me = jnp.stack([me_d, lax.axis_index("fsdp")]).astype(jnp.int32)
    rows_all = seqs * length
    hidden_width = w_down.shape[0] * fsdp

    spread, pool, same = pooling(length)
    layout, _ = level_layout(length)
    local_rows = [first for level, first, _ in layout if 2 * NR * (1 << level) > length][0]
    spread_c = jnp.asarray(spread, BF16)
    pool_c = jnp.asarray(pool, BF16)
    same_c = jnp.asarray(same, F32)
    far_pool = jnp.asarray(pool[local_rows : local_rows + (length >> 4) + (length >> 5)], BF16)

    share = width // dp
    norms = jnp.stack([ln1_gain, ln1_bias, ln2_gain, ln2_bias])
    placed = lax.dynamic_update_slice(jnp.zeros((4, width), F32), norms, (0, me_d * share))
    placed = placed.reshape(4, 4, 128).transpose(1, 0, 2).reshape(LN_ROWS, 128)
    rows_qkv, rows_d, rows_up = 3 * share, share, hidden_width // dp
    chunks = hidden_width // fsdp // 128
    down_piece = w_down.T.reshape(rows_d, chunks, 128).transpose(1, 0, 2).reshape(-1, 128)
    down_piece = jnp.concatenate([down_piece, w_out.T], axis=0)
    extra = [(name,) for name in plan.extra]
    qkv_piece = jnp.concatenate([placed, w_qkv.T], axis=0)
    up_piece = w_up.T
    qkv_in, down_in, up_in = (Gather(plan, p) for p in (qkv_piece, down_piece, up_piece))
    tok = tokens.reshape(rows_all, width)
    cot = cotangent.reshape(rows_all, width)
    attend = (spread_c, pool_c, same_c)

    near = swap(segments, 1)
    qkv_in.send([("z", "w")])
    for group in extra:
        qkv_in.stage([group])
    gate = qkv_in.came()
    qkv_in.join()
    qkv_in.cut(LN_ROWS + rows_qkv // 16 * 8)
    qkv_in.send([("x",), ("y",)], gate)
    down_in.send([("w",)], gate)
    for group in extra:
        down_in.stage([group])
    far_segments = swap(jnp.stack([segments, after(near, gate)]), 2)
    bias = score_bias(segments, near, far_segments[0], far_segments[1])
    gate = (qkv_in.came(), down_in.came(), far_segments)
    qkv_in.stage([("y",), ("x",)], gate)
    down_in.stage([("z",)], gate)
    up_in.send([("w",)], gate)
    for group in extra:
        up_in.stage([group])
    gate = (qkv_in.came(), down_in.came(), bias)
    cores = qkv_in.share(True, gate) + qkv_in.share(False, gate)
    down_in.join()
    down_in.cut(down_piece.shape[0] // 16 * 8)
    down_in.send([("x",), ("y",)], cores)
    packed, wqh, wql, xhat1, inv1, ln, s4, s5 = qkv_stage(
        me, after(tok, cores, bias), qkv_in, plan, far_pool, seqs
    )
    gate = (packed, down_in.came())
    s4, s5 = after((s4, s5), gate)
    got = [swap(s4, 1), swap(s5, 2), swap(s5, 3)]
    far = jnp.concatenate(got, axis=2)
    down_in.stage([("y",), ("x",)], gate)
    cores = down_in.share(True, gate)
    gate = (far, up_in.came())
    up_in.stage([("z",)], gate)
    calls = [(s, 1, 0, width // 128) for s in range(seqs)]
    before = ()
    for index, which in enumerate(calls):
        packed_in = after(packed, gate, before)
        before = attention_forward(packed_in, far, bias, *attend, seqs, local_rows, which, before)
        if index == 0:
            gate = (up_in.came(), before, cores)
            up_in.join()
            up_in.cut(rows_up // 2 // 8 * 8)
            up_in.send([("x",), ("y",)], gate)
    attended, lse = before
    gate = (attended, down_in.came(), up_in.came(), cores)
    cores = down_in.share(False, gate)
    up_in.stage([("y",), ("x",)], gate)
    gh, dh, dl, oh, ol = grad_hidden_stage(me, after(cot, cores), down_in, plan, hidden_width)
    up_in.share(True, gate)
    gate = (gh, up_in.came())
    cores = up_in.share(False, gate)
    middle, xhat2, inv2 = middle_stage(tok, after(attended, gate), oh, ol)
    hh, hl, ph, plo, uh, ul = hidden_stage(me, after(xhat2, cores), ln, gh, up_in, plan)

    single = [("x", "y"), ("z",), ("w",)] + extra
    double = [("x", "y"), ("z", "w")] + extra
    down = Stream(plan, chunks * rows_d, single)
    up = Stream(plan, rows_up, single)
    out = Stream(plan, rows_d, single)
    qkv = Stream(plan, rows_qkv, double)
    down_sum, up_sum, qkv_sum = Reduce(plan, single), Reduce(plan, single), Reduce(plan, double)

    away = grad_down_stage(me, cot, hh, hl, plan, down, 1)
    down_core = down_sum.begin(away)
    away = grad_up_stage(me, after(xhat2, away), ln, ph, plo, plan, up, 1)
    up_core = up_sum.begin(away)
    keep = grad_down_stage(me, after(cot, away), hh, hl, plan, down, 0)
    down_sum.keep(keep)
    sent = down_sum.send(keep, down_core)
    keep = grad_up_stage(me, after(xhat2, sent), ln, ph, plo, plan, up, 0)
    up_sum.keep(keep)
    gm, gln = middle_grad_stage(after(cot, keep, up_core), xhat2, inv2, ln, ph, plo, uh, ul)
    gmix, away, keep = mixture_grad_stage(me, gm, attended, oh, ol, plan, out)
    got = up_sum.begin(away, down_sum.last)
    up_sum.keep(keep)
    sent = (up_sum.send(got), down_sum.send(got))
    before = ()
    half = width // 256
    calls = [(s, 1, h, half) for s in range(seqs) for h in (0, half)]
    for index, which in enumerate(calls):
        grad = after(gmix, sent, before)
        before = attention_backward(
            packed, far, bias, *attend, attended, lse, grad, seqs, local_rows, which, before
        )
        if down_sum.stages:
            sent = down_sum.send(before, down_sum.last)
        else:
            sent = down_sum.last
    gate = (before, up_sum.last)
    dq, dk, dv, f4, f5a, f5b = before
    f4, f5a, f5b = after((f4, f5a, f5b), gate)
    g4, g5a, g5b = swap(f4, 1), swap(f5a, 2), swap(f5b, 3)
    gph, gpl = packed_grad_stage(dq, dk, dv, g4, g5a, g5b, far_pool, seqs)
    away, sums_away = grad_qkv_stage(me, gph, gpl, xhat1, ln, wqh, wql, plan, qkv, 1)
    got = qkv_sum.begin(away)
    keep, sums_keep = grad_qkv_stage(
        me, gph, gpl, after(xhat1, away), ln, wqh, wql, plan, qkv, 0
    )
    qkv_sum.keep(keep)
    sums = lane_order(me[1], sums_away, sums_keep, width // fsdp)
    sums = jnp.concatenate([sums, gln[0:2]], axis=0)
    sent = qkv_sum.send(got, rider=sums.reshape(-1, 128))
    up_sum.send(sent)
    gtok = input_grad_stage(gph, gpl, wqh, wql, after(xhat1, sent), inv1, ln, gm)
    output = output_stage(after(middle, gtok), hh, hl, dh, dl)
    rode = qkv_sum.rode
    sent = qkv_sum.send(qkv_sum.last, up_sum.last, output, rider=rode)
    while qkv_sum.stages:
        sent = qkv_sum.send(qkv_sum.last, rider=qkv_sum.rode)
    while up_sum.stages:
        up_sum.send(sent)
    for total in (down_sum, up_sum):
        total.terms[0] = after(total.terms[0], sent)
    sums = qkv_sum.rode
    sums = (sums + plan.send(sums, ("c",))).reshape(4, width)
    (g_down,), (g_up, g_out), (g_qkv,) = (t.total() for t in (down_sum, up_sum, qkv_sum))
    mine = lax.dynamic_slice(sums, (0, me_d * share), (4, share))
    g_down = g_down.reshape(chunks, rows_d, 128).transpose(0, 2, 1).reshape(-1, rows_d)
    shape = tokens.shape
    return (
        output.reshape(shape),
        gtok.reshape(shape),
        mine[0],
        mine[1],
        g_qkv.T,
        g_out.T,
        mine[2],
        mine[3],
        g_up.T,
        g_down,
    )


def solution(mesh):
    weight = P("fsdp", "dp")
    rows = P("dp", "fsdp", None)
    vector = P("dp")
    return jax.shard_map(
        local,
        mesh=mesh,
        in_specs=(rows, P("dp", "fsdp"), rows, vector, vector, weight, weight, vector, vector, weight, weight),
        out_specs=(rows, rows, vector, vector, weight, weight, vector, vector, weight, weight),
        check_vma=False,
    )
```

```python
import jax
import jax.numpy as jnp
import numpy as np
from jax import lax
from jax.experimental import pallas as pl
from jax.experimental.pallas import tpu as pltpu
from jax.sharding import PartitionSpec as P

HEADS = 8
NR = 16
LEVELS = 6
EPSILON = 1e-05
MASKED = -1e30
F32 = jnp.float32
BF16 = jnp.bfloat16
LN_ROWS = 16
TILE = 128
SCALE = 0.05


def split(x):
    high = x.astype(BF16)
    return high, (x - high.astype(F32)).astype(BF16)


def mm(a, b, ca, cb):
    return lax.dot_general(a, b, (((ca,), (cb,)), ((), ())), preferred_element_type=F32)


def mm3(a, b, ca, cb):
    return mm(a[0], b[0], ca, cb) + mm(a[0], b[1], ca, cb) + mm(a[1], b[0], ca, cb)


def mm2(a, b, ca, cb):
    return mm(a, b[0], ca, cb) + mm(a, b[1], ca, cb)


def level_layout(length):
    rows, start = [], 0
    for level in range(1, LEVELS):
        count = length >> level
        rows.append((level, start, count))
        start += count
    return rows, start


def pooling(length):
    spread = np.zeros((length, length), np.float32)
    pool = np.zeros((length, length), np.float32)
    same = np.zeros((length, length), np.float32)
    layout, _ = level_layout(length)
    bounds = [first for _, first, _ in layout] + [length]
    for index, (level, first, count) in enumerate(layout):
        token = np.arange(length)
        spread[token, first + (token >> level)] = 1.0
        pool[first + (token >> level), token] = 0.5**level
        same[bounds[index] : bounds[index + 1], bounds[index] : bounds[index + 1]] = 1.0
    return spread, pool, same


def score_bias(seg, near, far_a, far_b):
    count, length = seg.shape
    token = np.arange(length)
    near_pair = (token[:TILE, None] >> 5) == (token[None, :TILE] >> 5)
    tiles = seg.reshape(count, length // TILE, TILE)
    ok = near_pair & (tiles[:, :, :, None] == tiles[:, :, None, :])
    inner = jnp.where(ok, 0.0, MASKED).astype(F32).reshape(count, length, TILE)
    parts = []
    for level in range(1, LEVELS):
        ratio = 1 << level

        def ends(values):
            grouped = values.reshape(count, length // ratio, ratio)
            return grouped[:, :, 0], grouped[:, :, -1]

        low_q, high_q = ends(seg)
        low_q = jnp.repeat(low_q, ratio, axis=1)
        high_q = jnp.repeat(high_q, ratio, axis=1)
        if 2 * NR * ratio <= length:
            low_k, high_k = ends(seg)
            block_q = (token >> level) >> 4
            block_k = np.arange(length >> level) >> 4
            where = (block_q[:, None] ^ 1) == block_k[None, :]
        else:
            if NR * ratio <= length:
                low_k, high_k = ends(near)
            else:
                pieces = [ends(far_a), ends(far_b)]
                low_k = jnp.concatenate([pieces[0][0], pieces[1][0]], axis=1)
                high_k = jnp.concatenate([pieces[0][1], pieces[1][1]], axis=1)
            where = np.ones((length, low_k.shape[1]), bool)
        ok = (
            where[None]
            & (low_q[:, :, None] <= high_k[:, None, :])
            & (low_k[:, None, :] <= high_q[:, :, None])
        )
        parts.append(jnp.where(ok, np.float32(level * np.log(2.0)), MASKED))
    return inner, jnp.concatenate(parts, axis=2).astype(F32)


class Plan:
    def __init__(self, dp, fsdp):
        self.dp, self.fsdp = dp, fsdp
        self.dims = {}
        names = ["x", "z", "w"]
        bit = 1
        while bit < dp:
            name = names[len(self.dims)] if len(self.dims) < 3 else "d%d" % bit
            self.dims[name] = ("dp", bit)
            bit *= 2
        self.extra = list(self.dims)[3:]
        self.dims["y"] = ("fsdp", 2)
        self.dims["c"] = ("fsdp", 1)

    def corner(self, group, v):
        return tuple(name for i, name in enumerate(group) if (v >> i) & 1)

    def mask(self, names):
        d = f = 0
        for name in names:
            axis, bit = self.dims[name]
            if axis == "dp":
                d |= bit
            else:
                f |= bit
        return d, f

    def send(self, x, names):
        d, f = self.mask(names)
        if not f:
            return lax.ppermute(x, "dp", [(i, i ^ d) for i in range(self.dp)])
        if not d:
            return lax.ppermute(x, "fsdp", [(i, i ^ f) for i in range(self.fsdp)])
        n = self.fsdp
        pairs = [(i, ((i // n) ^ d) * n + ((i % n) ^ f)) for i in range(self.dp * n)]
        return lax.ppermute(x, ("dp", "fsdp"), pairs)

    def position(self, stages, d, f):
        pos = 0
        for group in stages:
            for name in reversed(group):
                axis, bit = self.dims[name]
                value = d if axis == "dp" else f
                pos = pos * 2 + ((value // bit) & 1)
        return pos


class Part:
    def __init__(self, start, held, names):
        self.start, self.held, self.names, self.got = start, held, names, []


class Gather:
    def __init__(self, plan, piece):
        self.plan, self.parts = plan, [Part(0, piece[None], [()])]
        self.arrays, self.slots = [], []

    def cut(self, row):
        (part,) = self.parts
        self.parts = [
            Part(0, part.held[:, :row], part.names),
            Part(row, part.held[:, row:], part.names),
        ]

    def send(self, groups, *earlier):
        for part, group in zip(self.parts, groups):
            if earlier:
                part.held = after(part.held, *earlier)
            for v in range(1, 1 << len(group)):
                names = self.plan.corner(group, v)
                part.got.append((self.plan.send(part.held, names), names))

    def came(self):
        return [value for part in self.parts for value, _ in part.got]

    def join(self):
        for part in self.parts:
            names = list(part.names)
            for _, corner in part.got:
                names += [n + corner for n in part.names]
            part.held = jnp.concatenate([part.held] + [v for v, _ in part.got], axis=0)
            part.names, part.got = names, []

    def stage(self, groups, *earlier):
        self.join()
        self.send(groups, *earlier)

    def share(self, held, *earlier):
        sent = []
        for part in self.parts:
            for value, corner in [(part.held, ())] if held else part.got:
                if earlier:
                    value = after(value, *earlier)
                other = self.plan.send(value, ("c",))
                sent.append(other)
                for array, core in ((value, ()), (other, ("c",))):
                    self.arrays.append(array)
                    slots = [self.plan.mask(n + corner + core) for n in part.names]
                    self.slots.append((slots, part.start))
        return sent


def assemble(scratch, refs, gathered, me_d, me_f, rows, lanes, segments):
    for ref, (slots, start) in zip(refs, gathered.slots):
        for slot, (d, f) in enumerate(slots):
            row0 = (me_d ^ d) * rows
            col0 = (me_f ^ f) * lanes
            for source, size, to_lane in segments:
                low, high = max(source, start), min(source + size, start + ref.shape[1])
                if low < high:
                    row = pl.multiple_of(row0 + (low - source), 8)
                    col = pl.multiple_of(col0 + to_lane, 128)
                    scratch[pl.ds(row, high - low), pl.ds(col, 128)] = ref[
                        slot, low - start : high - start, :
                    ]


def norm_rows(refs, gathered):
    total = None
    for ref, (slots, start) in zip(refs, gathered.slots):
        for slot, (d, f) in enumerate(slots):
            if f == 0 and start == 0:
                value = ref[slot, :LN_ROWS, :]
                total = value if total is None else total + value
    return jnp.concatenate([total[4 * i : 4 * i + 4] for i in range(4)], axis=1)


class Stream:
    def __init__(self, plan, rows, stages):
        self.plan, self.rows, self.stages = plan, rows, stages
        self.slots = plan.dp * plan.fsdp // 2

    def shape(self):
        return (self.slots, self.rows, 128)

    def put(self, out, d, f, row, value):
        size = value.shape[0]
        out[self.plan.position(self.stages, d, f), row : row + size, :] = value


class Reduce:
    def __init__(self, plan, stages):
        self.plan, self.stages = plan, list(stages)
        self.kept, self.came, self.last = [], [], []

    def begin(self, part, *earlier):
        part = after(part, *earlier) if earlier else part
        self.last = [self.plan.send(part, ("c",))]
        self.came.append(self.last[0])
        return self.last

    def keep(self, part):
        self.kept.append(part)

    def send(self, *earlier, rider=None):
        if self.kept:
            self.terms = [self.kept, self.came]
            self.slots, self.kept = self.kept[0].shape[0], []
        if earlier:
            self.terms[-1] = after(self.terms[-1], *earlier)
        group = self.stages.pop(0)
        self.slots >>= len(group)
        n = self.slots
        count = range(len(self.terms[0]))
        sizes = [part.shape[1] for part in self.terms[0]]
        cuts = np.cumsum([0] + sizes)
        out = []
        for v in range(1, 1 << len(group)):
            parts = [sum(term[i][v * n : (v + 1) * n] for term in self.terms) for i in count]
            if rider is not None:
                parts.append(jnp.broadcast_to(rider[None], (n,) + rider.shape))
            out.append(parts[0] if len(parts) == 1 else jnp.concatenate(parts, axis=1))
        self.last, self.rode = [], rider
        for v, value in enumerate(out):
            got = self.plan.send(value, self.plan.corner(group, v + 1))
            self.last.append(got)
            self.terms.append([got[:, a:b] for a, b in zip(cuts[:-1], cuts[1:])])
            if rider is not None:
                self.rode = self.rode + got[0, cuts[-1] :]
        return out

    def total(self, *earlier):
        count = range(len(self.terms[0]))
        return [sum(term[i][0] for term in self.terms) for i in count]


def after(value, *earlier):
    return lax.optimization_barrier((value, earlier))[0]


def whole(shape=None):
    return pl.BlockSpec(memory_space=pltpu.VMEM)


SMEM = pl.BlockSpec(memory_space=pltpu.SMEM)


def cost(micros):
    return pl.CostEstimate(
        flops=int(micros * SCALE * 9e8), bytes_accessed=int(micros * SCALE * 2.5e6), transcendentals=0
    )


def call(body, outs, scratch=(), **kw):
    return pl.pallas_call(
        body,
        out_shape=[jax.ShapeDtypeStruct(s, t) for s, t in outs],
        scratch_shapes=list(scratch),
        **kw,
    )


def qkv_stage(me, tokens, gathered, plan, pool, seqs):
    rows_all, width = tokens.shape
    length = rows_all // seqs
    n4, n5 = length >> 4, length >> 5
    slots = gathered.arrays
    triple = 3 * width
    rows = triple // plan.dp
    lanes = width // plan.fsdp

    def body(me_ref, tok, pool_ref, *rest):
        refs = rest[: len(slots)]
        packed, wh, wl, xhat, inv, ln, s4, s5, full, nh, nl = rest[len(slots) :]
        step = pl.program_id(0)

        @pl.when(step == 0)
        def _():
            assemble(full, refs, gathered, me_ref[0], me_ref[1], rows, lanes, [(LN_ROWS, rows, 0)])
            params = norm_rows(refs, gathered)
            ln[0:4, :] = params
            x = tok[...]
            centre = x - jnp.mean(x, axis=1, keepdims=True)
            scale = lax.rsqrt(jnp.mean(centre * centre, axis=1, keepdims=True) + EPSILON)
            xh = centre * scale
            xhat[...] = xh
            inv[...] = jnp.broadcast_to(scale, inv.shape)
            n = split(xh * params[0:1, :] + params[1:2, :])
            nh[...] = n[0]
            nl[...] = n[1]

        w = split(full[pl.ds(pl.multiple_of(step * width, width), width), :])
        wh[...] = w[0]
        wl[...] = w[1]
        packed[...] = mm3((nh[...], nl[...]), w, 1, 1)

        @pl.when(step > 0)
        def _():
            for s in range(seqs):
                means = mm2(pool_ref[...], split(packed[s * length : (s + 1) * length, :]), 1, 0)
                s4[s, 0] = means[:n4]
                s5[s, 0] = means[n4 : n4 + n5]

    fixed = lambda shape: pl.BlockSpec(shape, lambda i: (0,) * len(shape))
    later = lambda n: pl.BlockSpec((seqs, 1, n, width), lambda i: (0, jnp.maximum(i - 1, 0), 0, 0))
    outs = [
        ((rows_all, triple), F32, pl.BlockSpec((rows_all, width), lambda i: (0, i))),
        ((triple, width), BF16, pl.BlockSpec((width, width), lambda i: (i, 0))),
        ((triple, width), BF16, pl.BlockSpec((width, width), lambda i: (i, 0))),
        ((rows_all, width), F32, fixed((rows_all, width))),
        ((rows_all, 128), F32, fixed((rows_all, 128))),
        ((8, width), F32, fixed((8, width))),
        ((seqs, 2, n4, width), F32, later(n4)),
        ((seqs, 2, n5, width), F32, later(n5)),
    ]
    return pl.pallas_call(
        body,
        cost_estimate=cost(7.4),
        grid=(3,),
        out_shape=[jax.ShapeDtypeStruct(shape, kind) for shape, kind, _ in outs],
        in_specs=[SMEM, fixed((rows_all, width)), fixed(pool.shape)]
        + [fixed(x.shape) for x in slots],
        out_specs=[spec for _, _, spec in outs],
        scratch_shapes=[
            pltpu.VMEM((triple, width), F32),
            pltpu.VMEM((rows_all, width), BF16),
            pltpu.VMEM((rows_all, width), BF16),
        ],
    )(me, tokens, pool, *slots)


def lanes2(pair):
    return jnp.concatenate(pair, axis=1)


def fold(r):
    return r[:, :128] + r[:, 128:]


def wide_nt(a, b):
    first = mm(lanes2(a), lanes2((b[0], b[0])), 1, 1)
    return first + mm(a[0], b[1], 1, 1)


def wide_nn(a, b):
    return fold(mm(a[0], lanes2(b), 1, 0)) + mm(a[1], b[0], 1, 0)


def wide_tn(a, b):
    return fold(mm(a[0], lanes2(b), 0, 0)) + mm(a[1], b[0], 0, 0)


def tile_tn(a, b):
    left = jnp.concatenate(a, axis=0)
    right = jnp.concatenate([lanes2(b), lanes2((b[0], jnp.zeros_like(b[0])))], axis=0)
    return fold(mm(left, right, 0, 0))


def rows(pair, t):
    return tuple(x[t * TILE : (t + 1) * TILE] for x in pair)


class Heads:
    def __init__(self, q, k, v, fk, fv, pool, local):
        length = q.shape[0]
        self.tiles = range(length // TILE)
        self.lane = lax.broadcasted_iota(jnp.int32, (length, 128), 1) < 64
        qs, ks, vs = split(q), split(k), split(v)
        pooled = mm(pool, jnp.concatenate([qs[0], ks[0], vs[0], qs[1], ks[1], vs[1]], axis=1), 1, 0)
        pooled = pooled[:, :384] + pooled[:, 384:]
        kc = jnp.concatenate([pooled[:local, 128:256], fk], axis=0)
        vc = jnp.concatenate([pooled[:local, 256:], fv], axis=0)
        self.q, self.qc = qs, split(pooled[:, :128])
        self.k2 = [self.two(rows(ks, t)) for t in self.tiles]
        self.v2 = [self.two(rows(vs, t)) for t in self.tiles]
        self.kc2, self.vc2 = self.two(split(kc)), self.two(split(vc))

    def two(self, pair):
        out = []
        for x in pair:
            lane = self.lane[: x.shape[0]]
            zero = jnp.zeros_like(x)
            both = [jnp.where(lane, x, zero), jnp.where(lane, zero, x)]
            out.append(jnp.concatenate(both, axis=0))
        return tuple(out)

    def one(self, x):
        half = x.shape[0] // 2
        return jnp.where(self.lane[:half], x[:half], x[half:])

    def inner(self, left, right):
        return jnp.concatenate([wide_nt(rows(left, t), right[t]) for t in self.tiles], axis=0)

    def scores(self, spread, same, inner_bias, outer_bias):
        s0 = self.inner(self.q, self.k2) + lanes2((inner_bias, inner_bias))
        high, low = split(wide_nt(self.qc, self.kc2) * lanes2((same, same)))
        st = mm(spread, high, 1, 0) + mm(spread, low, 1, 0)
        return s0, st + lanes2((outer_bias, outer_bias))


def head_columns(x):
    half = x.shape[1] // 2
    return x[:, :half], x[:, half:]


def attention_specs(length, width, first=0, pair=0):
    pairs = width // 128
    block = lambda off: pl.BlockSpec((length, 128), lambda s, h: (first + s, off * pairs + pair + h))
    far = lambda j: pl.BlockSpec((1, 1, 32, 128), lambda s, h: (first + s, j, 0, pair + h))
    fixed = pl.BlockSpec((length, length), lambda s, h: (0, 0))
    bias = lambda n: pl.BlockSpec((1, length, n), lambda s, h: (first + s, 0, 0))
    return block, far, fixed, [bias(TILE), bias(length), fixed, fixed, fixed]


def attention_forward(packed, far, bias, spread, pool, same, seqs, local, which, before):
    rows_all, triple = packed.shape
    width = triple // 3
    length = rows_all // seqs
    first, count, pair, pairs = which
    block, far_spec, fixed, common = attention_specs(length, width, first, pair)
    carried = len(before)

    def body(q, k, v, fk, fv, inner_bias, outer_bias, spread_ref, pool_ref, same_ref, *rest):
        out, lse = rest[carried:]
        heads = Heads(q[...] * 0.125, k[...], v[...], fk[0, 0], fv[0, 0], pool_ref[...], local)
        s0, st = heads.scores(spread_ref[...], same_ref[...], inner_bias[0], outer_bias[0])
        p0, pc, peaks, sums = [], [], [], []
        for a, b in zip(head_columns(s0), head_columns(st)):
            peak = jnp.maximum(jnp.max(a, axis=1, keepdims=True), jnp.max(b, axis=1, keepdims=True))
            a, b = jnp.exp(a - peak), jnp.exp(b - peak)
            p0.append(a)
            pc.append(b)
            peaks.append(peak)
            sums.append(jnp.sum(a, axis=1, keepdims=True) + jnp.sum(b, axis=1, keepdims=True))
        p0, pc = split(lanes2(p0)), split(lanes2(pc))
        mixed = [wide_nn(rows(p0, t), heads.v2[t]) for t in heads.tiles]
        mixed = jnp.concatenate(mixed, axis=0) + wide_nn(pc, heads.vc2)
        total = jnp.where(heads.lane, sums[0], sums[1])
        out[...] = mixed / total
        lse[...] = jnp.where(heads.lane, peaks[0], peaks[1]) + jnp.log(total)

    return pl.pallas_call(
        body,
        cost_estimate=cost(9.5),
        grid=(count, pairs),
        out_shape=[jax.ShapeDtypeStruct((rows_all, width), F32)] * 2,
        in_specs=[block(0), block(1), block(2), far_spec(0), far_spec(1)]
        + common
        + [pl.BlockSpec(memory_space=pl.ANY)] * carried,
        out_specs=[block(0), block(0)],
        input_output_aliases={10 + i: i for i in range(carried)},
    )(packed, packed, packed, far, far, *bias, spread, pool, same, *before)


def attention_backward(
    packed, far, bias, spread, pool, same, attended, lse, grad, seqs, local, which, before
):
    rows_all, triple = packed.shape
    width = triple // 3
    length = rows_all // seqs
    first, count, pair, pairs = which
    block, far_spec, fixed, common = attention_specs(length, width, first, pair)
    n4, n5 = length >> 4, length >> 5
    carried = len(before)

    def body(q, k, v, fk, fv, inner_bias, outer_bias, spread_ref, pool_ref, same_ref, *rest):
        o_ref, lse_ref, g_ref = rest[:3]
        dq_ref, dk_ref, dv_ref, f4, f5a, f5b = rest[3 + carried :]
        spread_m, pool_m, same_m = spread_ref[...], pool_ref[...], same_ref[...]
        heads = Heads(q[...] * 0.125, k[...], v[...], fk[0, 0], fv[0, 0], pool_m, local)
        lane = heads.lane
        s0, st = heads.scores(spread_m, same_m, inner_bias[0], outer_bias[0])
        logs = lse_ref[...]
        logs = (logs[:, 0:1], logs[:, 64:65])
        p0 = lanes2([jnp.exp(a - x) for a, x in zip(head_columns(s0), logs)])
        pc = lanes2([jnp.exp(a - x) for a, x in zip(head_columns(st), logs)])
        grad_rows = g_ref[...]
        g = split(grad_rows)
        product = grad_rows * o_ref[...]
        zero = jnp.zeros_like(product)
        deltas = [
            jnp.sum(jnp.where(lane, product, zero), axis=1, keepdims=True),
            jnp.sum(jnp.where(lane, zero, product), axis=1, keepdims=True),
        ]
        d0 = heads.inner(g, heads.v2)
        d0 = split(p0 * lanes2([a - x for a, x in zip(head_columns(d0), deltas)]))
        dt = wide_nt(g, heads.vc2)
        dt = split(pc * lanes2([a - x for a, x in zip(head_columns(dt), deltas)]))
        p0, pc = split(p0), split(pc)
        dv = [heads.one(tile_tn(rows(p0, t), rows(g, t))) for t in heads.tiles]
        dk = [heads.one(tile_tn(rows(d0, t), rows(heads.q, t))) for t in heads.tiles]
        dq = [wide_nn(rows(d0, t), heads.k2[t]) for t in heads.tiles]
        dvc = heads.one(wide_tn(pc, g))
        dsc = mm(spread_m, dt[0], 0, 0) + mm(spread_m, dt[1], 0, 0)
        dsc = split(dsc * lanes2((same_m, same_m)))
        dqc = wide_nn(dsc, heads.kc2)
        dkc = heads.one(wide_tn(dsc, heads.qc))
        near = lax.broadcasted_iota(jnp.int32, (length, 128), 0) < local
        high, low = split(
            jnp.concatenate([dqc, jnp.where(near, dkc, zero), jnp.where(near, dvc, zero)], axis=1)
        )
        back = mm(pool_m, lanes2((high, low)), 0, 0)
        back = back[:, :384] + back[:, 384:]
        dq_ref[...] = (jnp.concatenate(dq, axis=0) + back[:, :128]) * 0.125
        dk_ref[...] = jnp.concatenate(dk, axis=0) + back[:, 128:256]
        dv_ref[...] = jnp.concatenate(dv, axis=0) + back[:, 256:]
        for j, value in ((0, dkc), (1, dvc)):
            f4[0, j] = value[local : local + n4]
            f5a[0, j] = value[local + n4 : local + n4 + n5]
            f5b[0, j] = value[local + n4 + n5 :]

    far_out = lambda n: pl.BlockSpec((1, 2, n, 128), lambda s, h: (first + s, 0, 0, pair + h))
    return pl.pallas_call(
        body,
        cost_estimate=cost(8),
        grid=(count, pairs),
        out_shape=[jax.ShapeDtypeStruct((rows_all, width), F32)] * 3
        + [jax.ShapeDtypeStruct((seqs, 2, n, width), F32) for n in (n4, n5, n5)],
        in_specs=[block(0), block(1), block(2), far_spec(0), far_spec(1)]
        + common
        + [block(0)] * 3
        + [pl.BlockSpec(memory_space=pl.ANY)] * carried,
        out_specs=[block(0)] * 3 + [far_out(n4), far_out(n5), far_out(n5)],
        input_output_aliases={13 + i: i for i in range(carried)},
    )(packed, packed, packed, far, far, *bias, spread, pool, same, attended, lse, grad, *before)


def middle_stage(tokens, attended, wh, wl):
    rows_all, width = tokens.shape

    def body(tok, att, wh_ref, wl_ref, middle, xhat, inv):
        x = tok[...] + mm3(split(att[...]), (wh_ref[...], wl_ref[...]), 1, 1)
        middle[...] = x
        centre = x - jnp.mean(x, axis=1, keepdims=True)
        scale = lax.rsqrt(jnp.mean(centre * centre, axis=1, keepdims=True) + EPSILON)
        xhat[...] = centre * scale
        inv[...] = jnp.broadcast_to(scale, inv.shape)

    return call(
        body,
        [((rows_all, width), F32), ((rows_all, width), F32), ((rows_all, 128), F32)],
        cost_estimate=cost(4.3),
        in_specs=[whole()] * 4,
        out_specs=[whole()] * 3,
    )(tokens, attended, wh, wl)


def projection_stage(me, gathered, plan, width, hidden_width):
    rows, lanes = width // plan.dp, hidden_width // plan.fsdp
    out_lanes = width // plan.fsdp
    slots = gathered.arrays
    chunks = lanes // 128
    down_parts = [(k * rows, rows, 128 * k) for k in range(chunks)]
    out_parts = [(chunks * rows, rows, 0)]
    chunk = 512

    def body(me_ref, *rest):
        refs = rest[: len(slots)]
        dh, dl, oh, ol, full, full_out = rest[len(slots) :]
        me_d, me_f = me_ref[0], me_ref[1]
        step = pl.program_id(0)

        @pl.when(step == 0)
        def _():
            assemble(full_out, refs, gathered, me_d, me_f, rows, out_lanes, out_parts)
            w = split(full_out[...])
            oh[...] = w[0]
            ol[...] = w[1]
            assemble(full, refs, gathered, me_d, me_f, rows, lanes, down_parts)

        w = split(full[:, pl.ds(pl.multiple_of(step * chunk, chunk), chunk)])
        dh[...] = w[0]
        dl[...] = w[1]

    fixed = lambda shape: pl.BlockSpec(shape, lambda i: (0,) * len(shape))
    cols = pl.BlockSpec((width, chunk), lambda i: (0, i))
    return pl.pallas_call(
        body,
        cost_estimate=cost(5),
        grid=(hidden_width // chunk,),
        out_shape=[jax.ShapeDtypeStruct((width, hidden_width), BF16)] * 2
        + [jax.ShapeDtypeStruct((width, width), BF16)] * 2,
        in_specs=[SMEM] + [fixed(x.shape) for x in slots],
        out_specs=[cols, cols, fixed((width, width)), fixed((width, width))],
        scratch_shapes=[pltpu.VMEM((width, hidden_width), F32), pltpu.VMEM((width, width), F32)],
    )(me, *slots)


def hidden_stage(me, xhat, ln, cot, dh, dl, gathered, plan):
    rows_all, width = xhat.shape
    hidden_width = dh.shape[1]
    rows, lanes = hidden_width // plan.dp, width // plan.fsdp
    slots = gathered.arrays
    chunk = 512
    steps = hidden_width // chunk
    root = float(np.sqrt(2.0 / np.pi))
    cubic = 0.044715 * root

    def body(me_ref, xhat_ref, ln_ref, cot_ref, d0, d1, *rest):
        refs = rest[: len(slots)]
        hh, hl, ph, plo, wh, wl, full, nh, nl, ch, cl = rest[len(slots) :]
        step = pl.program_id(0)

        @pl.when(step == 0)
        def _():
            assemble(full, refs, gathered, me_ref[0], me_ref[1], rows, lanes, [(0, rows, 0)])
            n = split(xhat_ref[...] * ln_ref[2:3, :] + ln_ref[3:4, :])
            nh[...] = n[0]
            nl[...] = n[1]
            c = split(cot_ref[...])
            ch[...] = c[0]
            cl[...] = c[1]

        w = split(full[pl.ds(pl.multiple_of(step * chunk, chunk), chunk), :])
        wh[...] = w[0]
        wl[...] = w[1]
        v = mm3((nh[...], nl[...]), w, 1, 1)
        square = v * v
        half = 0.5 + 0.5 * jnp.tanh(v * (root + cubic * square))
        h = split(v * half)
        hh[...] = h[0]
        hl[...] = h[1]
        slope = half + (half - half * half) * (v * (2.0 * root + 6.0 * cubic * square))
        g = split(mm3((ch[...], cl[...]), (d0[...], d1[...]), 1, 0) * slope)
        ph[...] = g[0]
        plo[...] = g[1]

    fixed = lambda shape: pl.BlockSpec(shape, lambda i: (0,) * len(shape))
    cols = pl.BlockSpec((rows_all, chunk), lambda i: (0, i))
    down = pl.BlockSpec((width, chunk), lambda i: (0, i))
    act = fixed((rows_all, width))
    return pl.pallas_call(
        body,
        cost_estimate=cost(15),
        grid=(steps,),
        out_shape=[jax.ShapeDtypeStruct((rows_all, hidden_width), BF16)] * 4
        + [jax.ShapeDtypeStruct((hidden_width, width), BF16)] * 2,
        in_specs=[SMEM, act, fixed((8, width)), act, down, down]
        + [fixed(x.shape) for x in slots],
        out_specs=[cols] * 4 + [pl.BlockSpec((chunk, width), lambda i: (i, 0))] * 2,
        scratch_shapes=[pltpu.VMEM((hidden_width, width), F32)]
        + [pltpu.VMEM((rows_all, width), BF16)] * 4,
    )(me, xhat, ln, cot, dh, dl, *slots)


def grad_down_stage(me, cot, hh, hl, plan, stream, core):
    rows_all, width = cot.shape
    hidden_width = hh.shape[1]
    rows, lanes = width // plan.dp, hidden_width // plan.fsdp

    def body(me_ref, cot_ref, hh_ref, hl_ref, out):
        jf = core + 2 * pl.program_id(0)
        res = mm3(split(cot_ref[...]), (hh_ref[...], hl_ref[...]), 0, 0)
        for d in range(plan.dp):
            jd = me_ref[0] ^ d
            for k in range(lanes // 128):
                value = res[d * rows : (d + 1) * rows, 128 * k : 128 * (k + 1)]
                stream.put(out, jd, jf, k * rows, value)

    cols = pl.BlockSpec((rows_all, lanes), lambda i, m: (0, m[1] ^ (core + 2 * i)))
    grid_spec = pltpu.PrefetchScalarGridSpec(
        num_scalar_prefetch=1,
        grid=(plan.fsdp // 2,),
        in_specs=[pl.BlockSpec((rows_all, width), lambda i, m: (0, 0)), cols, cols],
        out_specs=pl.BlockSpec(stream.shape(), lambda i, m: (0, 0, 0)),
    )
    return pl.pallas_call(
        body,
        cost_estimate=cost(5.5),
        grid_spec=grid_spec,
        out_shape=jax.ShapeDtypeStruct(stream.shape(), F32),
    )(me, cot, hh, hl)


def half_lanes(ref, me_f, core, lanes):
    parts = []
    for y in range(2):
        start = pl.multiple_of((me_f ^ (core + 2 * y)) * lanes, 128)
        parts.append(ref[:, pl.ds(start, lanes)])
    return jnp.concatenate(parts, axis=1)


def grad_up_stage(me, xhat, ln, ph, plo, plan, stream, core):
    rows_all, width = xhat.shape
    hidden_width = ph.shape[1]
    rows, lanes = hidden_width // plan.dp, width // plan.fsdp
    chunk = 512
    steps = hidden_width // chunk
    per = chunk // rows

    def body(me_ref, xhat_ref, ln_ref, ph_ref, pl_ref, out, full, nh, nl):
        step = pl.program_id(0)

        @pl.when(step == 0)
        def _():
            full[...] = xhat_ref[...] * ln_ref[2:3, :] + ln_ref[3:4, :]
            n = split(half_lanes(full, me_ref[1], core, lanes))
            nh[...] = n[0]
            nl[...] = n[1]

        res = mm3((ph_ref[...], pl_ref[...]), (nh[...], nl[...]), 0, 0)
        for i in range(per):
            jd = (step * per + i) ^ me_ref[0]
            for y in range(2):
                value = res[i * rows : (i + 1) * rows, y * lanes : (y + 1) * lanes]
                stream.put(out, jd, core + 2 * y, 0, value)

    fixed = lambda shape: pl.BlockSpec(shape, lambda i: (0,) * len(shape))
    cols = pl.BlockSpec((rows_all, chunk), lambda i: (0, i))
    return pl.pallas_call(
        body,
        cost_estimate=cost(6.4),
        grid=(steps,),
        out_shape=jax.ShapeDtypeStruct(stream.shape(), F32),
        in_specs=[SMEM, fixed((rows_all, width)), fixed((8, width)), cols, cols],
        out_specs=fixed(stream.shape()),
        scratch_shapes=[pltpu.VMEM((rows_all, width), F32)]
        + [pltpu.VMEM((rows_all, 2 * lanes), BF16)] * 2,
    )(me, xhat, ln, ph, plo)


def norm_back(e, gain, xhat, inv):
    u = e * gain
    mean_u = jnp.mean(u, axis=1, keepdims=True)
    mean_ux = jnp.mean(u * xhat, axis=1, keepdims=True)
    return inv * (u - mean_u - xhat * mean_ux)


def output_stage(middle, hh, hl, dh, dl):
    rows_all, width = middle.shape
    chunk = 512
    steps = hh.shape[1] // chunk

    def body(mid, h0, h1, d0, d1, out):
        @pl.when(pl.program_id(0) == 0)
        def _():
            out[...] = mid[...]

        out[...] += mm3((h0[...], h1[...]), (d0[...], d1[...]), 1, 1)

    cols = pl.BlockSpec((rows_all, chunk), lambda i: (0, i))
    act = pl.BlockSpec((rows_all, width), lambda i: (0, 0))
    return pl.pallas_call(
        body,
        cost_estimate=cost(8),
        grid=(steps,),
        out_shape=jax.ShapeDtypeStruct((rows_all, width), F32),
        in_specs=[act, cols, cols] + [pl.BlockSpec((width, chunk), lambda i: (0, i))] * 2,
        out_specs=act,
    )(middle, hh, hl, dh, dl)


def middle_grad_stage(cot, xhat, inv, ln, ph, plo, uh, ul):
    rows_all, width = cot.shape
    chunk = 512
    steps = ph.shape[1] // chunk

    def body(cot_ref, xhat_ref, inv_ref, ln_ref, p0, p1, u0, u1, gm, gln, acc):
        step = pl.program_id(0)

        @pl.when(step == 0)
        def _():
            acc[...] = jnp.zeros_like(acc)

        acc[...] += mm3((p0[...], p1[...]), (u0[...], u1[...]), 1, 0)

        @pl.when(step == steps - 1)
        def _():
            e = acc[...]
            xh = xhat_ref[...]
            gm[...] = cot_ref[...] + norm_back(e, ln_ref[2:3, :], xh, inv_ref[:, 0:1])
            gln[0:1, :] = jnp.sum(e * xh, axis=0, keepdims=True)
            gln[1:2, :] = jnp.sum(e, axis=0, keepdims=True)

    fixed = lambda shape: pl.BlockSpec(shape, lambda i: (0,) * len(shape))
    cols = pl.BlockSpec((rows_all, chunk), lambda i: (0, i))
    act = fixed((rows_all, width))
    return pl.pallas_call(
        body,
        cost_estimate=cost(8.5),
        grid=(steps,),
        out_shape=[
            jax.ShapeDtypeStruct((rows_all, width), F32),
            jax.ShapeDtypeStruct((8, width), F32),
        ],
        in_specs=[act, act, fixed((rows_all, 128)), fixed((8, width)), cols, cols]
        + [pl.BlockSpec((chunk, width), lambda i: (i, 0))] * 2,
        out_specs=[act, fixed((8, width))],
        scratch_shapes=[pltpu.VMEM((rows_all, width), F32)],
    )(cot, xhat, inv, ln, ph, plo, uh, ul)


def mixture_grad_stage(me, gm, attended, oh, ol, plan, stream):
    rows_all, width = gm.shape
    rows, lanes = width // plan.dp, width // plan.fsdp

    def body(me_ref, gm_ref, att, oh_ref, ol_ref, gmix, away, keep, full):
        g = split(gm_ref[...])
        gmix[...] = mm3(g, (oh_ref[...], ol_ref[...]), 1, 0)
        full[...] = att[...]
        for core in range(2):
            res = mm3(g, split(half_lanes(full, me_ref[1], core, lanes)), 0, 0)
            mine = away if core else keep
            for d in range(plan.dp):
                for y in range(2):
                    value = res[d * rows : (d + 1) * rows, y * lanes : (y + 1) * lanes]
                    stream.put(mine, d ^ me_ref[0], core + 2 * y, 0, value)

    return call(
        body,
        [((rows_all, width), F32), (stream.shape(), F32), (stream.shape(), F32)],
        [pltpu.VMEM((rows_all, width), F32)],
        cost_estimate=cost(5),
        in_specs=[SMEM] + [whole()] * 4,
        out_specs=[whole()] * 3,
    )(me, gm, attended, oh, ol)


def packed_grad_stage(dq, dk, dv, g4, g5a, g5b, pool, seqs):
    rows_all, width = dq.shape
    length = rows_all // seqs

    def body(dq_r, dk_r, dv_r, g4_r, g5a_r, g5b_r, pool_r, gph, gpl, column):
        for j, ref in enumerate((dq_r, dk_r, dv_r)):
            total = None
            for s in range(seqs):
                rs = slice(s * length, (s + 1) * length)
                value = ref[rs, :]
                if j:
                    groups = jnp.concatenate(
                        [g4_r[s, j - 1], g5a_r[s, j - 1] + g5b_r[s, j - 1]], axis=0
                    )
                    value = value + mm2(pool_r[...], split(groups), 0, 0)
                part = jnp.sum(value, axis=0, keepdims=True)
                total = part if total is None else total + part
                h = split(value)
                gph[rs, j * width : (j + 1) * width] = h[0]
                gpl[rs, j * width : (j + 1) * width] = h[1]
            column[j * width : (j + 1) * width, :] = jnp.transpose(
                jnp.broadcast_to(total, (128, width))
            )

    return call(
        body,
        [((rows_all, 3 * width), BF16)] * 2 + [((3 * width, 128), F32)],
        cost_estimate=cost(4.5),
        in_specs=[whole()] * 7,
        out_specs=[whole()] * 3,
    )(dq, dk, dv, g4, g5a, g5b, pool)


def input_grad_stage(gph, gpl, wqh, wql, xhat, inv, ln, gm):
    rows_all, width = gm.shape

    def body(gph_r, gpl_r, wh, wl, xhat_r, inv_r, ln_r, gm_r, gtok):
        e = mm3((gph_r[...], gpl_r[...]), (wh[...], wl[...]), 1, 0)
        gtok[...] = gm_r[...] + norm_back(e, ln_r[0:1, :], xhat_r[...], inv_r[:, 0:1])

    return call(
        body,
        [((rows_all, width), F32)],
        cost_estimate=cost(7.4),
        in_specs=[whole()] * 8,
        out_specs=[whole()],
    )(gph, gpl, wqh, wql, xhat, inv, ln, gm)[0]


def grad_qkv_stage(me, gph, gpl, column, xhat, ln, wh, wl, plan, stream, core):
    rows_all, triple = gph.shape
    width = triple // 3
    rows, lanes = triple // plan.dp, width // plan.fsdp
    steps = 2
    block = triple // steps

    def body(me_ref, gph_r, gpl_r, col_r, xhat_r, ln_r, wh_r, wl_r, out, sums, nh, nl):
        me_f = me_ref[1]
        step = pl.program_id(0)
        pick = lambda ref: half_lanes(ref, me_f, core, lanes)

        @pl.when(step == 0)
        def _():
            n = split(pick(xhat_r))
            nh[...] = n[0]
            nl[...] = n[1]
            sums[...] = jnp.zeros_like(sums)

        params = pick(ln_r)
        res = mm3((gph_r[...], gpl_r[...]), (nh[...], nl[...]), 0, 0)
        w = pick(wh_r).astype(F32) + pick(wl_r).astype(F32)
        col = col_r[:, 0:1]
        parts = [jnp.sum(res * w, axis=0, keepdims=True), jnp.sum(w * col, axis=0, keepdims=True)]
        for y in range(2):
            at = pl.ds(pl.multiple_of((me_f ^ (core + 2 * y)) * lanes, 128), lanes)
            for i in range(2):
                sums[i : i + 1, at] += parts[i][:, y * lanes : (y + 1) * lanes]
        res = res * params[0:1, :] + col * params[1:2, :]
        for i in range(block // rows):
            jd = me_ref[0] ^ (step * (block // rows) + i)
            for y in range(2):
                value = res[i * rows : (i + 1) * rows, y * lanes : (y + 1) * lanes]
                stream.put(out, jd, core + 2 * y, 0, value)

    fixed = lambda shape: pl.BlockSpec(shape, lambda i: (0,) * len(shape))
    cols = pl.BlockSpec((rows_all, block), lambda i: (0, i))
    down = lambda n: pl.BlockSpec((block, n), lambda i: (i, 0))
    return pl.pallas_call(
        body,
        cost_estimate=cost(0.25),
        grid=(steps,),
        out_shape=[
            jax.ShapeDtypeStruct(stream.shape(), F32),
            jax.ShapeDtypeStruct((8, width), F32),
        ],
        in_specs=[SMEM, cols, cols, down(128), fixed((rows_all, width)), fixed((8, width))]
        + [down(width)] * 2,
        out_specs=[fixed(stream.shape()), fixed((8, width))],
        scratch_shapes=[pltpu.VMEM((rows_all, 2 * lanes), BF16)] * 2,
    )(me, gph, gpl, column, xhat, ln, wh, wl)


def swap(x, mask, axis="fsdp"):
    size = lax.axis_size(axis)
    return lax.ppermute(x, axis, [(i, i ^ mask) for i in range(size)])


def local(
    tokens, segments, cotangent, ln1_gain, ln1_bias, w_qkv, w_out, ln2_gain, ln2_bias, w_up, w_down
):
    seqs, length, width = tokens.shape
    dp, fsdp = lax.axis_size("dp"), lax.axis_size("fsdp")
    plan = Plan(dp, fsdp)
    me_d = lax.axis_index("dp")
    me = jnp.stack([me_d, lax.axis_index("fsdp")]).astype(jnp.int32)
    rows_all = seqs * length
    hidden_width = w_down.shape[0] * fsdp

    spread, pool, same = pooling(length)
    layout, _ = level_layout(length)
    local_rows = [first for level, first, _ in layout if 2 * NR * (1 << level) > length][0]
    spread_c = jnp.asarray(spread, BF16)
    pool_c = jnp.asarray(pool, BF16)
    same_c = jnp.asarray(same, F32)
    far_pool = jnp.asarray(pool[local_rows : local_rows + (length >> 4) + (length >> 5)], BF16)

    share = width // dp
    norms = jnp.stack([ln1_gain, ln1_bias, ln2_gain, ln2_bias])
    placed = lax.dynamic_update_slice(jnp.zeros((4, width), F32), norms, (0, me_d * share))
    placed = placed.reshape(4, 4, 128).transpose(1, 0, 2).reshape(LN_ROWS, 128)
    rows_qkv, rows_d, rows_up = 3 * share, share, hidden_width // dp
    chunks = hidden_width // fsdp // 128
    down_piece = w_down.T.reshape(rows_d, chunks, 128).transpose(1, 0, 2).reshape(-1, 128)
    down_piece = jnp.concatenate([down_piece, w_out.T], axis=0)
    extra = [(name,) for name in plan.extra]
    qkv_piece = jnp.concatenate([placed, w_qkv.T], axis=0)
    up_piece = w_up.T
    qkv_in, down_in, up_in = (Gather(plan, p) for p in (qkv_piece, down_piece, up_piece))
    tok = tokens.reshape(rows_all, width)
    cot = cotangent.reshape(rows_all, width)
    attend = (spread_c, pool_c, same_c)

    near = swap(segments, 1)
    qkv_in.send([("z", "w")])
    for group in extra:
        qkv_in.stage([group])
    gate = qkv_in.came()
    qkv_in.join()
    qkv_in.cut(LN_ROWS + rows_qkv // 16 * 8)
    qkv_in.send([("x",), ("y",)], gate)
    down_in.send([("w",)], gate)
    for group in extra:
        down_in.stage([group])
    far_segments = swap(jnp.stack([segments, after(near, gate)]), 2)
    bias = score_bias(segments, near, far_segments[0], far_segments[1])
    gate = (qkv_in.came(), down_in.came(), far_segments)
    qkv_in.stage([("y",), ("x",)], gate)
    down_in.stage([("z",)], gate)
    up_in.send([("w",)], gate)
    for group in extra:
        up_in.stage([group])
    gate = (qkv_in.came(), down_in.came(), up_in.came(), bias)
    cores = qkv_in.share(True, gate) + qkv_in.share(False, gate)
    down_in.join()
    down_in.cut(down_piece.shape[0] // 16 * 8)
    down_in.send([("x",), ("y",)], cores)
    up_in.stage([("z",)], cores)
    packed, wqh, wql, xhat1, inv1, ln, s4, s5 = qkv_stage(
        me, after(tok, cores, bias), qkv_in, plan, far_pool, seqs
    )
    gate = (packed, down_in.came(), up_in.came())
    s4, s5 = after((s4, s5), gate)
    got = [swap(s4, 1), swap(s5, 2), swap(s5, 3)]
    far = jnp.concatenate(got, axis=2)
    down_in.stage([("y",), ("x",)], gate)
    cores = down_in.share(True, far)
    calls = [(s, 1, 0, width // 128) for s in range(seqs)]
    before = ()
    gate = far
    for index, which in enumerate(calls):
        packed_in = after(packed, gate, before)
        before = attention_forward(packed_in, far, bias, *attend, seqs, local_rows, which, before)
        if index == 0:
            gate = (before, down_in.came(), cores)
            cores = down_in.share(False, gate)
            up_in.join()
            up_in.cut(rows_up // 2 // 8 * 8)
            up_in.send([("x",), ("y",)], gate)
    attended, lse = before
    gate = (attended, up_in.came(), cores)
    up_in.stage([("y",), ("x",)], gate)
    dh, dl, oh, ol = projection_stage(after(me, gate), down_in, plan, width, hidden_width)
    cores = up_in.share(True, gate)
    middle, xhat2, inv2 = middle_stage(tok, attended, oh, ol)
    gate = (middle, up_in.came(), cores)
    cores = up_in.share(False, gate)
    hh, hl, ph, plo, uh, ul = hidden_stage(
        me, after(xhat2, cores), ln, cot, dh, dl, up_in, plan
    )

    single = [("x", "y"), ("z",), ("w",)] + extra
    double = [("x", "y"), ("z", "w")] + extra
    down = Stream(plan, chunks * rows_d, single)
    up = Stream(plan, rows_up, single)
    out = Stream(plan, rows_d, single)
    qkv = Stream(plan, rows_qkv, double)
    down_sum, up_sum, qkv_sum = Reduce(plan, single), Reduce(plan, single), Reduce(plan, double)

    away = grad_down_stage(me, cot, hh, hl, plan, down, 1)
    down_core = down_sum.begin(away)
    away = grad_up_stage(me, after(xhat2, away), ln, ph, plo, plan, up, 1)
    up_core = up_sum.begin(away)
    keep = grad_down_stage(me, after(cot, away), hh, hl, plan, down, 0)
    down_sum.keep(keep)
    sent = down_sum.send(keep, down_core)
    keep = grad_up_stage(me, after(xhat2, sent), ln, ph, plo, plan, up, 0)
    up_sum.keep(keep)
    gm, gln = middle_grad_stage(after(cot, keep, up_core), xhat2, inv2, ln, ph, plo, uh, ul)
    gmix, away, keep = mixture_grad_stage(me, gm, attended, oh, ol, plan, out)
    got = up_sum.begin(away, down_sum.last)
    up_sum.keep(keep)
    sent = (down_sum.send(), up_sum.send(got))
    before = ()
    calls = [(s, 1, 0, width // 128) for s in range(seqs)]
    for index, which in enumerate(calls):
        grad = after(gmix, sent, before)
        before = attention_backward(
            packed, far, bias, *attend, attended, lse, grad, seqs, local_rows, which, before
        )
        if down_sum.stages:
            sent = down_sum.send(before, down_sum.last)
        else:
            sent = down_sum.last
    gate = (before, up_sum.last)
    dq, dk, dv, f4, f5a, f5b = before
    f4, f5a, f5b = after((f4, f5a, f5b), gate)
    g4, g5a, g5b = swap(f4, 1), swap(f5a, 2), swap(f5b, 3)
    gph, gpl, column = packed_grad_stage(dq, dk, dv, g4, g5a, g5b, far_pool, seqs)
    away, sums_away = grad_qkv_stage(
        me, gph, gpl, column, xhat1, ln, wqh, wql, plan, qkv, 1
    )
    got = qkv_sum.begin(away)
    keep, sums_keep = grad_qkv_stage(
        me, gph, gpl, column, after(xhat1, away), ln, wqh, wql, plan, qkv, 0
    )
    qkv_sum.keep(keep)
    sums = jnp.concatenate([(sums_away + sums_keep)[0:2], gln[0:2]], axis=0)
    sent = qkv_sum.send(got, rider=sums.reshape(-1, 128))
    up_sum.send(sent)
    gtok = input_grad_stage(gph, gpl, wqh, wql, after(xhat1, sent), inv1, ln, gm)
    output = output_stage(after(middle, gtok), hh, hl, dh, dl)
    rode = qkv_sum.rode
    sent = qkv_sum.send(qkv_sum.last, up_sum.last, output, rider=rode)
    while qkv_sum.stages:
        sent = qkv_sum.send(qkv_sum.last, rider=qkv_sum.rode)
    while up_sum.stages:
        up_sum.send(sent)
    for total in (down_sum, up_sum):
        total.terms[0] = after(total.terms[0], sent)
    sums = qkv_sum.rode
    sums = (sums + plan.send(sums, ("c",))).reshape(4, width)
    (g_down,), (g_up, g_out), (g_qkv,) = (t.total() for t in (down_sum, up_sum, qkv_sum))
    mine = lax.dynamic_slice(sums, (0, me_d * share), (4, share))
    g_down = g_down.reshape(chunks, rows_d, 128).transpose(0, 2, 1).reshape(-1, rows_d)
    shape = tokens.shape
    return (
        output.reshape(shape),
        gtok.reshape(shape),
        mine[0],
        mine[1],
        g_qkv.T,
        g_out.T,
        mine[2],
        mine[3],
        g_up.T,
        g_down,
    )


def solution(mesh):
    weight = P("fsdp", "dp")
    rows = P("dp", "fsdp", None)
    vector = P("dp")
    return jax.shard_map(
        local,
        mesh=mesh,
        in_specs=(rows, P("dp", "fsdp"), rows, vector, vector, weight, weight, vector, vector, weight, weight),
        out_specs=(rows, rows, vector, vector, weight, weight, vector, vector, weight, weight),
        check_vma=False,
    )
```

```python
import jax
import jax.numpy as jnp
import numpy as np
from jax import lax
from jax.experimental import pallas as pl
from jax.experimental.pallas import tpu as pltpu
from jax.sharding import PartitionSpec as P

HEADS = 8
NR = 16
LEVELS = 6
EPSILON = 1e-05
MASKED = -1e30
F32 = jnp.float32
BF16 = jnp.bfloat16
LN_ROWS = 16
TILE = 128
ROOM = pltpu.CompilerParams(vmem_limit_bytes=23 << 20)
SCALE = 0.05


def split(x):
    high = x.astype(BF16)
    return high, (x - high.astype(F32)).astype(BF16)


def mm(a, b, ca, cb):
    return lax.dot_general(a, b, (((ca,), (cb,)), ((), ())), preferred_element_type=F32)


def mm3(a, b, ca, cb):
    return mm(a[0], b[0], ca, cb) + mm(a[0], b[1], ca, cb) + mm(a[1], b[0], ca, cb)


def mm2(a, b, ca, cb):
    return mm(a, b[0], ca, cb) + mm(a, b[1], ca, cb)


def level_layout(length):
    rows, start = [], 0
    for level in range(1, LEVELS):
        count = length >> level
        rows.append((level, start, count))
        start += count
    return rows, start


def pooling(length):
    spread = np.zeros((length, length), np.float32)
    pool = np.zeros((length, length), np.float32)
    same = np.zeros((length, length), np.float32)
    layout, _ = level_layout(length)
    bounds = [first for _, first, _ in layout] + [length]
    for index, (level, first, count) in enumerate(layout):
        token = np.arange(length)
        spread[token, first + (token >> level)] = 1.0
        pool[first + (token >> level), token] = 0.5**level
        same[bounds[index] : bounds[index + 1], bounds[index] : bounds[index + 1]] = 1.0
    return spread, pool, same


def score_bias(seg, near, far_a, far_b):
    count, length = seg.shape
    token = np.arange(length)
    near_pair = (token[:TILE, None] >> 5) == (token[None, :TILE] >> 5)
    tiles = seg.reshape(count, length // TILE, TILE)
    ok = near_pair & (tiles[:, :, :, None] == tiles[:, :, None, :])
    inner = jnp.where(ok, 0.0, MASKED).astype(F32).reshape(count, length, TILE)
    parts = []
    for level in range(1, LEVELS):
        ratio = 1 << level

        def ends(values):
            grouped = values.reshape(count, length // ratio, ratio)
            return grouped[:, :, 0], grouped[:, :, -1]

        low_q, high_q = ends(seg)
        low_q = jnp.repeat(low_q, ratio, axis=1)
        high_q = jnp.repeat(high_q, ratio, axis=1)
        if 2 * NR * ratio <= length:
            low_k, high_k = ends(seg)
            block_q = (token >> level) >> 4
            block_k = np.arange(length >> level) >> 4
            where = (block_q[:, None] ^ 1) == block_k[None, :]
        else:
            if NR * ratio <= length:
                low_k, high_k = ends(near)
            else:
                pieces = [ends(far_a), ends(far_b)]
                low_k = jnp.concatenate([pieces[0][0], pieces[1][0]], axis=1)
                high_k = jnp.concatenate([pieces[0][1], pieces[1][1]], axis=1)
            where = np.ones((length, low_k.shape[1]), bool)
        ok = (
            where[None]
            & (low_q[:, :, None] <= high_k[:, None, :])
            & (low_k[:, None, :] <= high_q[:, :, None])
        )
        parts.append(jnp.where(ok, np.float32(level * np.log(2.0)), MASKED))
    return inner, jnp.concatenate(parts, axis=2).astype(F32)


class Plan:
    def __init__(self, dp, fsdp):
        self.dp, self.fsdp = dp, fsdp
        self.dims = {}
        names = ["x", "z", "w"]
        bit = 1
        while bit < dp:
            name = names[len(self.dims)] if len(self.dims) < 3 else "d%d" % bit
            self.dims[name] = ("dp", bit)
            bit *= 2
        self.extra = list(self.dims)[3:]
        self.dims["y"] = ("fsdp", 2)
        self.dims["c"] = ("fsdp", 1)

    def corner(self, group, v):
        return tuple(name for i, name in enumerate(group) if (v >> i) & 1)

    def mask(self, names):
        d = f = 0
        for name in names:
            axis, bit = self.dims[name]
            if axis == "dp":
                d |= bit
            else:
                f |= bit
        return d, f

    def send(self, x, names):
        d, f = self.mask(names)
        if not f:
            return lax.ppermute(x, "dp", [(i, i ^ d) for i in range(self.dp)])
        if not d:
            return lax.ppermute(x, "fsdp", [(i, i ^ f) for i in range(self.fsdp)])
        n = self.fsdp
        pairs = [(i, ((i // n) ^ d) * n + ((i % n) ^ f)) for i in range(self.dp * n)]
        return lax.ppermute(x, ("dp", "fsdp"), pairs)

    def position(self, stages, d, f):
        pos = 0
        for group in stages:
            for name in reversed(group):
                axis, bit = self.dims[name]
                value = d if axis == "dp" else f
                pos = pos * 2 + ((value // bit) & 1)
        return pos


class Part:
    def __init__(self, start, held, names):
        self.start, self.held, self.names, self.got = start, held, names, []


class Gather:
    def __init__(self, plan, piece):
        self.plan, self.parts = plan, [Part(0, piece[None], [()])]
        self.arrays, self.slots = [], []

    def cut(self, row):
        (part,) = self.parts
        self.parts = [
            Part(0, part.held[:, :row], part.names),
            Part(row, part.held[:, row:], part.names),
        ]

    def send(self, groups, *earlier):
        for part, group in zip(self.parts, groups):
            if earlier:
                part.held = after(part.held, *earlier)
            for v in range(1, 1 << len(group)):
                names = self.plan.corner(group, v)
                part.got.append((self.plan.send(part.held, names), names))

    def came(self):
        return [value for part in self.parts for value, _ in part.got]

    def join(self):
        for part in self.parts:
            names = list(part.names)
            for _, corner in part.got:
                names += [n + corner for n in part.names]
            part.held = jnp.concatenate([part.held] + [v for v, _ in part.got], axis=0)
            part.names, part.got = names, []

    def stage(self, groups, *earlier):
        self.join()
        self.send(groups, *earlier)

    def share(self, held, *earlier):
        sent = []
        for part in self.parts:
            for value, corner in [(part.held, ())] if held else part.got:
                if earlier:
                    value = after(value, *earlier)
                other = self.plan.send(value, ("c",))
                sent.append(other)
                for array, core in ((value, ()), (other, ("c",))):
                    self.arrays.append(array)
                    slots = [self.plan.mask(n + corner + core) for n in part.names]
                    self.slots.append((slots, part.start))
        return sent


def assemble(scratch, refs, gathered, me_d, me_f, rows, lanes, segments):
    for ref, (slots, start) in zip(refs, gathered.slots):
        for slot, (d, f) in enumerate(slots):
            row0 = (me_d ^ d) * rows
            col0 = (me_f ^ f) * lanes
            for source, size, to_lane in segments:
                low, high = max(source, start), min(source + size, start + ref.shape[1])
                if low < high:
                    row = pl.multiple_of(row0 + (low - source), 8)
                    col = pl.multiple_of(col0 + to_lane, 128)
                    scratch[pl.ds(row, high - low), pl.ds(col, 128)] = ref[
                        slot, low - start : high - start, :
                    ]


def norm_rows(refs, gathered):
    total = None
    for ref, (slots, start) in zip(refs, gathered.slots):
        for slot, (d, f) in enumerate(slots):
            if f == 0 and start == 0:
                value = ref[slot, :LN_ROWS, :]
                total = value if total is None else total + value
    return jnp.concatenate([total[4 * i : 4 * i + 4] for i in range(4)], axis=1)


class Stream:
    def __init__(self, plan, rows, stages):
        self.plan, self.rows, self.stages = plan, rows, stages
        self.slots = plan.dp * plan.fsdp // 2

    def shape(self):
        return (self.slots, self.rows, 128)

    def put(self, out, d, f, row, value):
        size = value.shape[0]
        out[self.plan.position(self.stages, d, f), row : row + size, :] = value


class Reduce:
    def __init__(self, plan, stages):
        self.plan, self.stages = plan, list(stages)
        self.kept, self.came, self.last = [], [], []

    def begin(self, part, *earlier):
        part = after(part, *earlier) if earlier else part
        self.last = [self.plan.send(part, ("c",))]
        self.came.append(self.last[0])
        return self.last

    def keep(self, part):
        self.kept.append(part)

    def send(self, *earlier, rider=None):
        if self.kept:
            self.terms = [self.kept, self.came]
            self.slots, self.kept = self.kept[0].shape[0], []
        if earlier:
            self.terms[-1] = after(self.terms[-1], *earlier)
        group = self.stages.pop(0)
        self.slots >>= len(group)
        n = self.slots
        count = range(len(self.terms[0]))
        sizes = [part.shape[1] for part in self.terms[0]]
        cuts = np.cumsum([0] + sizes)
        out = []
        for v in range(1, 1 << len(group)):
            parts = [sum(term[i][v * n : (v + 1) * n] for term in self.terms) for i in count]
            if rider is not None:
                parts.append(jnp.broadcast_to(rider[None], (n,) + rider.shape))
            out.append(parts[0] if len(parts) == 1 else jnp.concatenate(parts, axis=1))
        self.last, self.rode = [], rider
        for v, value in enumerate(out):
            got = self.plan.send(value, self.plan.corner(group, v + 1))
            self.last.append(got)
            self.terms.append([got[:, a:b] for a, b in zip(cuts[:-1], cuts[1:])])
            if rider is not None:
                self.rode = self.rode + got[0, cuts[-1] :]
        return out

    def total(self, *earlier):
        count = range(len(self.terms[0]))
        return [sum(term[i][0] for term in self.terms) for i in count]


def after(value, *earlier):
    return lax.optimization_barrier((value, earlier))[0]


def whole(shape=None):
    return pl.BlockSpec(memory_space=pltpu.VMEM)


SMEM = pl.BlockSpec(memory_space=pltpu.SMEM)


def cost(micros):
    return pl.CostEstimate(
        flops=int(micros * SCALE * 9e8), bytes_accessed=int(micros * SCALE * 2.5e6), transcendentals=0
    )


def call(body, outs, scratch=(), **kw):
    return pl.pallas_call(
        body,
        out_shape=[jax.ShapeDtypeStruct(s, t) for s, t in outs],
        scratch_shapes=list(scratch),
        **kw,
    )


def qkv_stage(me, tokens, gathered, plan, pool, seqs):
    rows_all, width = tokens.shape
    length = rows_all // seqs
    n4, n5 = length >> 4, length >> 5
    slots = gathered.arrays
    triple = 3 * width
    rows = triple // plan.dp
    lanes = width // plan.fsdp

    def body(me_ref, tok, pool_ref, *rest):
        refs = rest[: len(slots)]
        packed, wh, wl, xhat, inv, ln, s4, s5, full, nh, nl = rest[len(slots) :]
        step = pl.program_id(0)

        @pl.when(step == 0)
        def _():
            assemble(full, refs, gathered, me_ref[0], me_ref[1], rows, lanes, [(LN_ROWS, rows, 0)])
            params = norm_rows(refs, gathered)
            ln[0:4, :] = params
            x = tok[...]
            centre = x - jnp.mean(x, axis=1, keepdims=True)
            scale = lax.rsqrt(jnp.mean(centre * centre, axis=1, keepdims=True) + EPSILON)
            xh = centre * scale
            xhat[...] = xh
            inv[...] = jnp.broadcast_to(scale, inv.shape)
            n = split(xh * params[0:1, :] + params[1:2, :])
            nh[...] = n[0]
            nl[...] = n[1]

        w = split(full[pl.ds(pl.multiple_of(step * width, width), width), :])
        wh[...] = w[0]
        wl[...] = w[1]
        packed[...] = mm3((nh[...], nl[...]), w, 1, 1)

        @pl.when(step > 0)
        def _():
            for s in range(seqs):
                means = mm2(pool_ref[...], split(packed[s * length : (s + 1) * length, :]), 1, 0)
                s4[s, 0] = means[:n4]
                s5[s, 0] = means[n4 : n4 + n5]

    fixed = lambda shape: pl.BlockSpec(shape, lambda i: (0,) * len(shape))
    later = lambda n: pl.BlockSpec((seqs, 1, n, width), lambda i: (0, jnp.maximum(i - 1, 0), 0, 0))
    outs = [
        ((rows_all, triple), F32, pl.BlockSpec((rows_all, width), lambda i: (0, i))),
        ((triple, width), BF16, pl.BlockSpec((width, width), lambda i: (i, 0))),
        ((triple, width), BF16, pl.BlockSpec((width, width), lambda i: (i, 0))),
        ((rows_all, width), F32, fixed((rows_all, width))),
        ((rows_all, 128), F32, fixed((rows_all, 128))),
        ((8, width), F32, fixed((8, width))),
        ((seqs, 2, n4, width), F32, later(n4)),
        ((seqs, 2, n5, width), F32, later(n5)),
    ]
    return pl.pallas_call(
        body,
        compiler_params=ROOM,
        cost_estimate=cost(7.4),
        grid=(3,),
        out_shape=[jax.ShapeDtypeStruct(shape, kind) for shape, kind, _ in outs],
        in_specs=[SMEM, fixed((rows_all, width)), fixed(pool.shape)]
        + [fixed(x.shape) for x in slots],
        out_specs=[spec for _, _, spec in outs],
        scratch_shapes=[
            pltpu.VMEM((triple, width), F32),
            pltpu.VMEM((rows_all, width), BF16),
            pltpu.VMEM((rows_all, width), BF16),
        ],
    )(me, tokens, pool, *slots)


def lanes2(pair):
    return jnp.concatenate(pair, axis=1)


def fold(r):
    return r[:, :128] + r[:, 128:]


def wide_nt(a, b):
    first = mm(lanes2(a), lanes2((b[0], b[0])), 1, 1)
    return first + mm(a[0], b[1], 1, 1)


def wide_nn(a, b):
    return fold(mm(a[0], lanes2(b), 1, 0)) + mm(a[1], b[0], 1, 0)


def wide_tn(a, b):
    return fold(mm(a[0], lanes2(b), 0, 0)) + mm(a[1], b[0], 0, 0)


def tile_tn(a, b):
    left = jnp.concatenate(a, axis=0)
    right = jnp.concatenate([lanes2(b), lanes2((b[0], jnp.zeros_like(b[0])))], axis=0)
    return fold(mm(left, right, 0, 0))


def rows(pair, t):
    return tuple(x[t * TILE : (t + 1) * TILE] for x in pair)


class Heads:
    def __init__(self, q, k, v, fk, fv, pool, local):
        length = q.shape[0]
        self.tiles = range(length // TILE)
        self.lane = lax.broadcasted_iota(jnp.int32, (length, 128), 1) < 64
        qs, ks, vs = split(q), split(k), split(v)
        pooled = mm(pool, jnp.concatenate([qs[0], ks[0], vs[0], qs[1], ks[1], vs[1]], axis=1), 1, 0)
        pooled = pooled[:, :384] + pooled[:, 384:]
        kc = jnp.concatenate([pooled[:local, 128:256], fk], axis=0)
        vc = jnp.concatenate([pooled[:local, 256:], fv], axis=0)
        self.q, self.qc = qs, split(pooled[:, :128])
        self.k2 = [self.two(rows(ks, t)) for t in self.tiles]
        self.v2 = [self.two(rows(vs, t)) for t in self.tiles]
        self.kc2, self.vc2 = self.two(split(kc)), self.two(split(vc))

    def two(self, pair):
        out = []
        for x in pair:
            lane = self.lane[: x.shape[0]]
            zero = jnp.zeros_like(x)
            both = [jnp.where(lane, x, zero), jnp.where(lane, zero, x)]
            out.append(jnp.concatenate(both, axis=0))
        return tuple(out)

    def one(self, x):
        half = x.shape[0] // 2
        return jnp.where(self.lane[:half], x[:half], x[half:])

    def inner(self, left, right):
        return jnp.concatenate([wide_nt(rows(left, t), right[t]) for t in self.tiles], axis=0)

    def scores(self, spread, same, inner_bias, outer_bias):
        s0 = self.inner(self.q, self.k2) + lanes2((inner_bias, inner_bias))
        high, low = split(wide_nt(self.qc, self.kc2) * lanes2((same, same)))
        st = mm(spread, high, 1, 0) + mm(spread, low, 1, 0)
        return s0, st + lanes2((outer_bias, outer_bias))


def head_columns(x):
    half = x.shape[1] // 2
    return x[:, :half], x[:, half:]


def attention_specs(length, width, first=0, pair=0):
    pairs = width // 128
    block = lambda off: pl.BlockSpec((length, 128), lambda s, h: (first + s, off * pairs + pair + h))
    far = lambda j: pl.BlockSpec((1, 1, 32, 128), lambda s, h: (first + s, j, 0, pair + h))
    fixed = pl.BlockSpec((length, length), lambda s, h: (0, 0))
    bias = lambda n: pl.BlockSpec((1, length, n), lambda s, h: (first + s, 0, 0))
    return block, far, fixed, [bias(TILE), bias(length), fixed, fixed, fixed]


def attention_forward(packed, far, bias, spread, pool, same, seqs, local, which, before):
    rows_all, triple = packed.shape
    width = triple // 3
    length = rows_all // seqs
    first, count, pair, pairs = which
    block, far_spec, fixed, common = attention_specs(length, width, first, pair)
    carried = len(before)

    def body(q, k, v, fk, fv, inner_bias, outer_bias, spread_ref, pool_ref, same_ref, *rest):
        out, lse = rest[carried:]
        heads = Heads(q[...] * 0.125, k[...], v[...], fk[0, 0], fv[0, 0], pool_ref[...], local)
        s0, st = heads.scores(spread_ref[...], same_ref[...], inner_bias[0], outer_bias[0])
        p0, pc, peaks, sums = [], [], [], []
        for a, b in zip(head_columns(s0), head_columns(st)):
            peak = jnp.maximum(jnp.max(a, axis=1, keepdims=True), jnp.max(b, axis=1, keepdims=True))
            a, b = jnp.exp(a - peak), jnp.exp(b - peak)
            p0.append(a)
            pc.append(b)
            peaks.append(peak)
            sums.append(jnp.sum(a, axis=1, keepdims=True) + jnp.sum(b, axis=1, keepdims=True))
        p0, pc = split(lanes2(p0)), split(lanes2(pc))
        mixed = [wide_nn(rows(p0, t), heads.v2[t]) for t in heads.tiles]
        mixed = jnp.concatenate(mixed, axis=0) + wide_nn(pc, heads.vc2)
        total = jnp.where(heads.lane, sums[0], sums[1])
        out[...] = mixed / total
        lse[...] = jnp.where(heads.lane, peaks[0], peaks[1]) + jnp.log(total)

    return pl.pallas_call(
        body,
        compiler_params=ROOM,
        cost_estimate=cost(9.5),
        grid=(count, pairs),
        out_shape=[jax.ShapeDtypeStruct((rows_all, width), F32)] * 2,
        in_specs=[block(0), block(1), block(2), far_spec(0), far_spec(1)]
        + common
        + [pl.BlockSpec(memory_space=pl.ANY)] * carried,
        out_specs=[block(0), block(0)],
        input_output_aliases={10 + i: i for i in range(carried)},
    )(packed, packed, packed, far, far, *bias, spread, pool, same, *before)


def attention_backward(
    packed, far, bias, spread, pool, same, attended, lse, grad, seqs, local, which, before
):
    rows_all, triple = packed.shape
    width = triple // 3
    length = rows_all // seqs
    first, count, pair, pairs = which
    block, far_spec, fixed, common = attention_specs(length, width, first, pair)
    n4, n5 = length >> 4, length >> 5
    carried = len(before)

    def body(q, k, v, fk, fv, inner_bias, outer_bias, spread_ref, pool_ref, same_ref, *rest):
        o_ref, lse_ref, g_ref = rest[:3]
        dq_ref, dk_ref, dv_ref, f4, f5a, f5b = rest[3 + carried :]
        spread_m, pool_m, same_m = spread_ref[...], pool_ref[...], same_ref[...]
        heads = Heads(q[...] * 0.125, k[...], v[...], fk[0, 0], fv[0, 0], pool_m, local)
        lane = heads.lane
        s0, st = heads.scores(spread_m, same_m, inner_bias[0], outer_bias[0])
        logs = lse_ref[...]
        logs = (logs[:, 0:1], logs[:, 64:65])
        p0 = lanes2([jnp.exp(a - x) for a, x in zip(head_columns(s0), logs)])
        pc = lanes2([jnp.exp(a - x) for a, x in zip(head_columns(st), logs)])
        grad_rows = g_ref[...]
        g = split(grad_rows)
        product = grad_rows * o_ref[...]
        zero = jnp.zeros_like(product)
        deltas = [
            jnp.sum(jnp.where(lane, product, zero), axis=1, keepdims=True),
            jnp.sum(jnp.where(lane, zero, product), axis=1, keepdims=True),
        ]
        d0 = heads.inner(g, heads.v2)
        d0 = split(p0 * lanes2([a - x for a, x in zip(head_columns(d0), deltas)]))
        dt = wide_nt(g, heads.vc2)
        dt = split(pc * lanes2([a - x for a, x in zip(head_columns(dt), deltas)]))
        p0, pc = split(p0), split(pc)
        dv = [heads.one(tile_tn(rows(p0, t), rows(g, t))) for t in heads.tiles]
        dk = [heads.one(tile_tn(rows(d0, t), rows(heads.q, t))) for t in heads.tiles]
        dq = [wide_nn(rows(d0, t), heads.k2[t]) for t in heads.tiles]
        dvc = heads.one(wide_tn(pc, g))
        dsc = mm(spread_m, dt[0], 0, 0) + mm(spread_m, dt[1], 0, 0)
        dsc = split(dsc * lanes2((same_m, same_m)))
        dqc = wide_nn(dsc, heads.kc2)
        dkc = heads.one(wide_tn(dsc, heads.qc))
        near = lax.broadcasted_iota(jnp.int32, (length, 128), 0) < local
        high, low = split(
            jnp.concatenate([dqc, jnp.where(near, dkc, zero), jnp.where(near, dvc, zero)], axis=1)
        )
        back = mm(pool_m, lanes2((high, low)), 0, 0)
        back = back[:, :384] + back[:, 384:]
        dq_ref[...] = (jnp.concatenate(dq, axis=0) + back[:, :128]) * 0.125
        dk_ref[...] = jnp.concatenate(dk, axis=0) + back[:, 128:256]
        dv_ref[...] = jnp.concatenate(dv, axis=0) + back[:, 256:]
        for j, value in ((0, dkc), (1, dvc)):
            f4[0, j] = value[local : local + n4]
            f5a[0, j] = value[local + n4 : local + n4 + n5]
            f5b[0, j] = value[local + n4 + n5 :]

    far_out = lambda n: pl.BlockSpec((1, 2, n, 128), lambda s, h: (first + s, 0, 0, pair + h))
    return pl.pallas_call(
        body,
        compiler_params=ROOM,
        cost_estimate=cost(8),
        grid=(count, pairs),
        out_shape=[jax.ShapeDtypeStruct((rows_all, width), F32)] * 3
        + [jax.ShapeDtypeStruct((seqs, 2, n, width), F32) for n in (n4, n5, n5)],
        in_specs=[block(0), block(1), block(2), far_spec(0), far_spec(1)]
        + common
        + [block(0)] * 3
        + [pl.BlockSpec(memory_space=pl.ANY)] * carried,
        out_specs=[block(0)] * 3 + [far_out(n4), far_out(n5), far_out(n5)],
        input_output_aliases={13 + i: i for i in range(carried)},
    )(packed, packed, packed, far, far, *bias, spread, pool, same, attended, lse, grad, *before)


def middle_stage(tokens, attended, wh, wl):
    rows_all, width = tokens.shape

    def body(tok, att, wh_ref, wl_ref, middle, xhat, inv):
        x = tok[...] + mm3(split(att[...]), (wh_ref[...], wl_ref[...]), 1, 1)
        middle[...] = x
        centre = x - jnp.mean(x, axis=1, keepdims=True)
        scale = lax.rsqrt(jnp.mean(centre * centre, axis=1, keepdims=True) + EPSILON)
        xhat[...] = centre * scale
        inv[...] = jnp.broadcast_to(scale, inv.shape)

    return call(
        body,
        [((rows_all, width), F32), ((rows_all, width), F32), ((rows_all, 128), F32)],
        compiler_params=ROOM,
        cost_estimate=cost(4.3),
        in_specs=[whole()] * 4,
        out_specs=[whole()] * 3,
    )(tokens, attended, wh, wl)


def projection_stage(me, gathered, plan, width, hidden_width):
    rows, lanes = width // plan.dp, hidden_width // plan.fsdp
    out_lanes = width // plan.fsdp
    slots = gathered.arrays
    chunks = lanes // 128
    down_parts = [(k * rows, rows, 128 * k) for k in range(chunks)]
    out_parts = [(chunks * rows, rows, 0)]
    chunk = 512

    def body(me_ref, *rest):
        refs = rest[: len(slots)]
        dh, dl, oh, ol, full, full_out = rest[len(slots) :]
        me_d, me_f = me_ref[0], me_ref[1]
        step = pl.program_id(0)

        @pl.when(step == 0)
        def _():
            assemble(full_out, refs, gathered, me_d, me_f, rows, out_lanes, out_parts)
            w = split(full_out[...])
            oh[...] = w[0]
            ol[...] = w[1]
            assemble(full, refs, gathered, me_d, me_f, rows, lanes, down_parts)

        w = split(full[:, pl.ds(pl.multiple_of(step * chunk, chunk), chunk)])
        dh[...] = w[0]
        dl[...] = w[1]

    fixed = lambda shape: pl.BlockSpec(shape, lambda i: (0,) * len(shape))
    cols = pl.BlockSpec((width, chunk), lambda i: (0, i))
    return pl.pallas_call(
        body,
        compiler_params=ROOM,
        cost_estimate=cost(5),
        grid=(hidden_width // chunk,),
        out_shape=[jax.ShapeDtypeStruct((width, hidden_width), BF16)] * 2
        + [jax.ShapeDtypeStruct((width, width), BF16)] * 2,
        in_specs=[SMEM] + [fixed(x.shape) for x in slots],
        out_specs=[cols, cols, fixed((width, width)), fixed((width, width))],
        scratch_shapes=[pltpu.VMEM((width, hidden_width), F32), pltpu.VMEM((width, width), F32)],
    )(me, *slots)


def hidden_stage(me, xhat, ln, cot, dh, dl, gathered, plan):
    rows_all, width = xhat.shape
    hidden_width = dh.shape[1]
    rows, lanes = hidden_width // plan.dp, width // plan.fsdp
    slots = gathered.arrays
    chunk = 512
    steps = hidden_width // chunk
    root = float(np.sqrt(2.0 / np.pi))
    cubic = 0.044715 * root

    def body(me_ref, xhat_ref, ln_ref, cot_ref, d0, d1, *rest):
        refs = rest[: len(slots)]
        hh, hl, ph, plo, wh, wl, nth, ntl, cth, ctl, full, nh, nl, ch, cl = rest[len(slots) :]
        step = pl.program_id(0)

        @pl.when(step == 0)
        def _():
            assemble(full, refs, gathered, me_ref[0], me_ref[1], rows, lanes, [(0, rows, 0)])
            n = xhat_ref[...] * ln_ref[2:3, :] + ln_ref[3:4, :]
            c = cot_ref[...]
            for value, high, low in (
                (n, nh, nl),
                (c, ch, cl),
                (jnp.transpose(n), nth, ntl),
                (jnp.transpose(c), cth, ctl),
            ):
                halves = split(value)
                high[...] = halves[0]
                low[...] = halves[1]

        w = split(full[pl.ds(pl.multiple_of(step * chunk, chunk), chunk), :])
        wh[...] = w[0]
        wl[...] = w[1]
        v = mm3((nh[...], nl[...]), w, 1, 1)
        square = v * v
        half = 0.5 + 0.5 * jnp.tanh(v * (root + cubic * square))
        h = split(v * half)
        hh[...] = h[0]
        hl[...] = h[1]
        slope = half + (half - half * half) * (v * (2.0 * root + 6.0 * cubic * square))
        g = split(mm3((ch[...], cl[...]), (d0[...], d1[...]), 1, 0) * slope)
        ph[...] = g[0]
        plo[...] = g[1]

    fixed = lambda shape: pl.BlockSpec(shape, lambda i: (0,) * len(shape))
    cols = pl.BlockSpec((rows_all, chunk), lambda i: (0, i))
    down = pl.BlockSpec((width, chunk), lambda i: (0, i))
    act = fixed((rows_all, width))
    return pl.pallas_call(
        body,
        compiler_params=ROOM,
        cost_estimate=cost(15),
        grid=(steps,),
        out_shape=[jax.ShapeDtypeStruct((rows_all, hidden_width), BF16)] * 4
        + [jax.ShapeDtypeStruct((hidden_width, width), BF16)] * 2
        + [jax.ShapeDtypeStruct((width, rows_all), BF16)] * 4,
        in_specs=[SMEM, act, fixed((8, width)), act, down, down]
        + [fixed(x.shape) for x in slots],
        out_specs=[cols] * 4
        + [pl.BlockSpec((chunk, width), lambda i: (i, 0))] * 2
        + [fixed((width, rows_all))] * 4,
        scratch_shapes=[pltpu.VMEM((hidden_width, width), F32)]
        + [pltpu.VMEM((rows_all, width), BF16)] * 4,
    )(me, xhat, ln, cot, dh, dl, *slots)


def grad_down_stage(me, cth, ctl, hh, hl, plan, stream, core):
    width, rows_all = cth.shape
    hidden_width = hh.shape[1]
    rows, lanes = width // plan.dp, hidden_width // plan.fsdp

    def body(me_ref, c0, c1, h0, h1, out):
        jf = core + 2 * pl.program_id(0)
        res = mm3((c0[...], c1[...]), (h0[...], h1[...]), 1, 0)
        for d in range(plan.dp):
            jd = me_ref[0] ^ d
            for k in range(lanes // 128):
                value = res[d * rows : (d + 1) * rows, 128 * k : 128 * (k + 1)]
                stream.put(out, jd, jf, k * rows, value)

    cols = pl.BlockSpec((rows_all, lanes), lambda i, m: (0, m[1] ^ (core + 2 * i)))
    grid_spec = pltpu.PrefetchScalarGridSpec(
        num_scalar_prefetch=1,
        grid=(plan.fsdp // 2,),
        in_specs=[pl.BlockSpec((width, rows_all), lambda i, m: (0, 0))] * 2 + [cols, cols],
        out_specs=pl.BlockSpec(stream.shape(), lambda i, m: (0, 0, 0)),
    )
    return pl.pallas_call(
        body,
        compiler_params=ROOM,
        cost_estimate=cost(0.27),
        grid_spec=grid_spec,
        out_shape=jax.ShapeDtypeStruct(stream.shape(), F32),
    )(me, cth, ctl, hh, hl)


def half_lanes(ref, me_f, core, lanes):
    parts = []
    for y in range(2):
        start = pl.multiple_of((me_f ^ (core + 2 * y)) * lanes, 128)
        parts.append(ref[:, pl.ds(start, lanes)])
    return jnp.concatenate(parts, axis=1)


def half_rows(ref, me_f, core, count):
    parts = []
    for y in range(2):
        start = pl.multiple_of((me_f ^ (core + 2 * y)) * count, 128)
        parts.append(ref[pl.ds(start, count), :])
    return jnp.concatenate(parts, axis=0)


def grad_up_stage(me, nth, ntl, ph, plo, plan, stream, core):
    width, rows_all = nth.shape
    hidden_width = ph.shape[1]
    rows, lanes = hidden_width // plan.dp, width // plan.fsdp
    chunk = 512
    steps = hidden_width // chunk
    per = chunk // rows
    natural = rows % 128 == 0

    def body(me_ref, n0, n1, p0, p1, out):
        step = pl.program_id(0)
        n = (half_rows(n0, me_ref[1], core, lanes), half_rows(n1, me_ref[1], core, lanes))
        p = (p0[...], p1[...])
        res = mm3(n, p, 1, 0) if natural else mm3(p, n, 0, 1)
        for i in range(per):
            jd = (step * per + i) ^ me_ref[0]
            for y in range(2):
                if natural:
                    for k in range(rows // 128):
                        at = i * rows + 128 * k
                        value = res[y * lanes : (y + 1) * lanes, at : at + 128]
                        stream.put(out, jd, core + 2 * y, k * lanes, value)
                else:
                    value = res[i * rows : (i + 1) * rows, y * lanes : (y + 1) * lanes]
                    stream.put(out, jd, core + 2 * y, 0, value)

    fixed = lambda shape: pl.BlockSpec(shape, lambda i: (0,) * len(shape))
    cols = pl.BlockSpec((rows_all, chunk), lambda i: (0, i))
    return pl.pallas_call(
        body,
        compiler_params=ROOM,
        cost_estimate=cost(0.32),
        grid=(steps,),
        out_shape=jax.ShapeDtypeStruct(stream.shape(), F32),
        in_specs=[SMEM] + [fixed((width, rows_all))] * 2 + [cols, cols],
        out_specs=fixed(stream.shape()),
    )(me, nth, ntl, ph, plo)


def norm_back(e, gain, xhat, inv):
    u = e * gain
    mean_u = jnp.mean(u, axis=1, keepdims=True)
    mean_ux = jnp.mean(u * xhat, axis=1, keepdims=True)
    return inv * (u - mean_u - xhat * mean_ux)


def output_stage(middle, hh, hl, dh, dl):
    rows_all, width = middle.shape
    chunk = 512
    steps = hh.shape[1] // chunk

    def body(mid, h0, h1, d0, d1, out):
        @pl.when(pl.program_id(0) == 0)
        def _():
            out[...] = mid[...]

        out[...] += mm3((h0[...], h1[...]), (d0[...], d1[...]), 1, 1)

    cols = pl.BlockSpec((rows_all, chunk), lambda i: (0, i))
    act = pl.BlockSpec((rows_all, width), lambda i: (0, 0))
    return pl.pallas_call(
        body,
        compiler_params=ROOM,
        cost_estimate=cost(8),
        grid=(steps,),
        out_shape=jax.ShapeDtypeStruct((rows_all, width), F32),
        in_specs=[act, cols, cols] + [pl.BlockSpec((width, chunk), lambda i: (0, i))] * 2,
        out_specs=act,
    )(middle, hh, hl, dh, dl)


def middle_grad_stage(cot, xhat, inv, ln, ph, plo, uh, ul):
    rows_all, width = cot.shape
    chunk = 512
    steps = ph.shape[1] // chunk

    def body(cot_ref, xhat_ref, inv_ref, ln_ref, p0, p1, u0, u1, gm, gln, acc):
        step = pl.program_id(0)

        @pl.when(step == 0)
        def _():
            acc[...] = jnp.zeros_like(acc)

        acc[...] += mm3((p0[...], p1[...]), (u0[...], u1[...]), 1, 0)

        @pl.when(step == steps - 1)
        def _():
            e = acc[...]
            xh = xhat_ref[...]
            gm[...] = cot_ref[...] + norm_back(e, ln_ref[2:3, :], xh, inv_ref[:, 0:1])
            gln[0:1, :] = jnp.sum(e * xh, axis=0, keepdims=True)
            gln[1:2, :] = jnp.sum(e, axis=0, keepdims=True)

    fixed = lambda shape: pl.BlockSpec(shape, lambda i: (0,) * len(shape))
    cols = pl.BlockSpec((rows_all, chunk), lambda i: (0, i))
    act = fixed((rows_all, width))
    return pl.pallas_call(
        body,
        compiler_params=ROOM,
        cost_estimate=cost(8.5),
        grid=(steps,),
        out_shape=[
            jax.ShapeDtypeStruct((rows_all, width), F32),
            jax.ShapeDtypeStruct((8, width), F32),
        ],
        in_specs=[act, act, fixed((rows_all, 128)), fixed((8, width)), cols, cols]
        + [pl.BlockSpec((chunk, width), lambda i: (i, 0))] * 2,
        out_specs=[act, fixed((8, width))],
        scratch_shapes=[pltpu.VMEM((rows_all, width), F32)],
    )(cot, xhat, inv, ln, ph, plo, uh, ul)


def mixture_grad_stage(me, gm, attended, oh, ol, plan, stream):
    rows_all, width = gm.shape
    rows, lanes = width // plan.dp, width // plan.fsdp

    def body(me_ref, gm_ref, att, oh_ref, ol_ref, gmix, away, keep, full):
        g = split(gm_ref[...])
        gmix[...] = mm3(g, (oh_ref[...], ol_ref[...]), 1, 0)
        full[...] = att[...]
        for core in range(2):
            res = mm3(g, split(half_lanes(full, me_ref[1], core, lanes)), 0, 0)
            mine = away if core else keep
            for d in range(plan.dp):
                for y in range(2):
                    value = res[d * rows : (d + 1) * rows, y * lanes : (y + 1) * lanes]
                    stream.put(mine, d ^ me_ref[0], core + 2 * y, 0, value)

    return call(
        body,
        [((rows_all, width), F32), (stream.shape(), F32), (stream.shape(), F32)],
        [pltpu.VMEM((rows_all, width), F32)],
        compiler_params=ROOM,
        cost_estimate=cost(5),
        in_specs=[SMEM] + [whole()] * 4,
        out_specs=[whole()] * 3,
    )(me, gm, attended, oh, ol)


def packed_grad_stage(dq, dk, dv, g4, g5a, g5b, pool, seqs):
    rows_all, width = dq.shape
    length = rows_all // seqs

    def body(dq_r, dk_r, dv_r, g4_r, g5a_r, g5b_r, pool_r, gph, gpl, column):
        for j, ref in enumerate((dq_r, dk_r, dv_r)):
            total = None
            for s in range(seqs):
                rs = slice(s * length, (s + 1) * length)
                value = ref[rs, :]
                if j:
                    groups = jnp.concatenate(
                        [g4_r[s, j - 1], g5a_r[s, j - 1] + g5b_r[s, j - 1]], axis=0
                    )
                    value = value + mm2(pool_r[...], split(groups), 0, 0)
                part = jnp.sum(value, axis=0, keepdims=True)
                total = part if total is None else total + part
                h = split(value)
                gph[rs, j * width : (j + 1) * width] = h[0]
                gpl[rs, j * width : (j + 1) * width] = h[1]
            column[j * width : (j + 1) * width, :] = jnp.transpose(
                jnp.broadcast_to(total, (128, width))
            )

    return call(
        body,
        [((rows_all, 3 * width), BF16)] * 2 + [((3 * width, 128), F32)],
        compiler_params=ROOM,
        cost_estimate=cost(4.5),
        in_specs=[whole()] * 7,
        out_specs=[whole()] * 3,
    )(dq, dk, dv, g4, g5a, g5b, pool)


def input_grad_stage(gph, gpl, wqh, wql, xhat, inv, ln, gm):
    rows_all, width = gm.shape

    def body(gph_r, gpl_r, wh, wl, xhat_r, inv_r, ln_r, gm_r, gtok):
        e = mm3((gph_r[...], gpl_r[...]), (wh[...], wl[...]), 1, 0)
        gtok[...] = gm_r[...] + norm_back(e, ln_r[0:1, :], xhat_r[...], inv_r[:, 0:1])

    return call(
        body,
        [((rows_all, width), F32)],
        compiler_params=ROOM,
        cost_estimate=cost(7.4),
        in_specs=[whole()] * 8,
        out_specs=[whole()],
    )(gph, gpl, wqh, wql, xhat, inv, ln, gm)[0]


def grad_qkv_stage(me, gph, gpl, column, xhat, ln, wh, wl, plan, stream, core):
    rows_all, triple = gph.shape
    width = triple // 3
    rows, lanes = triple // plan.dp, width // plan.fsdp
    steps = 2
    block = triple // steps

    def body(me_ref, gph_r, gpl_r, col_r, xhat_r, ln_r, wh_r, wl_r, out, sums, nh, nl):
        me_f = me_ref[1]
        step = pl.program_id(0)
        pick = lambda ref: half_lanes(ref, me_f, core, lanes)

        @pl.when(step == 0)
        def _():
            n = split(pick(xhat_r))
            nh[...] = n[0]
            nl[...] = n[1]
            sums[...] = jnp.zeros_like(sums)

        params = pick(ln_r)
        res = mm3((gph_r[...], gpl_r[...]), (nh[...], nl[...]), 0, 0)
        w = pick(wh_r).astype(F32) + pick(wl_r).astype(F32)
        col = col_r[:, 0:1]
        parts = [jnp.sum(res * w, axis=0, keepdims=True), jnp.sum(w * col, axis=0, keepdims=True)]
        for y in range(2):
            at = pl.ds(pl.multiple_of((me_f ^ (core + 2 * y)) * lanes, 128), lanes)
            for i in range(2):
                sums[i : i + 1, at] += parts[i][:, y * lanes : (y + 1) * lanes]
        res = res * params[0:1, :] + col * params[1:2, :]
        for i in range(block // rows):
            jd = me_ref[0] ^ (step * (block // rows) + i)
            for y in range(2):
                value = res[i * rows : (i + 1) * rows, y * lanes : (y + 1) * lanes]
                stream.put(out, jd, core + 2 * y, 0, value)

    fixed = lambda shape: pl.BlockSpec(shape, lambda i: (0,) * len(shape))
    cols = pl.BlockSpec((rows_all, block), lambda i: (0, i))
    down = lambda n: pl.BlockSpec((block, n), lambda i: (i, 0))
    return pl.pallas_call(
        body,
        compiler_params=ROOM,
        cost_estimate=cost(0.25),
        grid=(steps,),
        out_shape=[
            jax.ShapeDtypeStruct(stream.shape(), F32),
            jax.ShapeDtypeStruct((8, width), F32),
        ],
        in_specs=[SMEM, cols, cols, down(128), fixed((rows_all, width)), fixed((8, width))]
        + [down(width)] * 2,
        out_specs=[fixed(stream.shape()), fixed((8, width))],
        scratch_shapes=[pltpu.VMEM((rows_all, 2 * lanes), BF16)] * 2,
    )(me, gph, gpl, column, xhat, ln, wh, wl)


def swap(x, mask, axis="fsdp"):
    size = lax.axis_size(axis)
    return lax.ppermute(x, axis, [(i, i ^ mask) for i in range(size)])


def local(
    tokens, segments, cotangent, ln1_gain, ln1_bias, w_qkv, w_out, ln2_gain, ln2_bias, w_up, w_down
):
    seqs, length, width = tokens.shape
    dp, fsdp = lax.axis_size("dp"), lax.axis_size("fsdp")
    plan = Plan(dp, fsdp)
    me_d = lax.axis_index("dp")
    me = jnp.stack([me_d, lax.axis_index("fsdp")]).astype(jnp.int32)
    rows_all = seqs * length
    hidden_width = w_down.shape[0] * fsdp

    spread, pool, same = pooling(length)
    layout, _ = level_layout(length)
    local_rows = [first for level, first, _ in layout if 2 * NR * (1 << level) > length][0]
    spread_c = jnp.asarray(spread, BF16)
    pool_c = jnp.asarray(pool, BF16)
    same_c = jnp.asarray(same, F32)
    far_pool = jnp.asarray(pool[local_rows : local_rows + (length >> 4) + (length >> 5)], BF16)

    share = width // dp
    norms = jnp.stack([ln1_gain, ln1_bias, ln2_gain, ln2_bias])
    placed = lax.dynamic_update_slice(jnp.zeros((4, width), F32), norms, (0, me_d * share))
    placed = placed.reshape(4, 4, 128).transpose(1, 0, 2).reshape(LN_ROWS, 128)
    rows_qkv, rows_d, rows_up = 3 * share, share, hidden_width // dp
    chunks = hidden_width // fsdp // 128
    down_piece = w_down.T.reshape(rows_d, chunks, 128).transpose(1, 0, 2).reshape(-1, 128)
    down_piece = jnp.concatenate([down_piece, w_out.T], axis=0)
    extra = [(name,) for name in plan.extra]
    qkv_piece = jnp.concatenate([placed, w_qkv.T], axis=0)
    up_piece = w_up.T
    qkv_piece = after(qkv_piece, me)
    qkv_in, down_in, up_in = (Gather(plan, p) for p in (qkv_piece, down_piece, up_piece))
    tok = tokens.reshape(rows_all, width)
    cot = cotangent.reshape(rows_all, width)
    attend = (spread_c, pool_c, same_c)

    near = swap(segments, 1)
    qkv_in.send([("z", "w")])
    for group in extra:
        qkv_in.stage([group])
    gate = qkv_in.came()
    qkv_in.join()
    qkv_in.cut(LN_ROWS + rows_qkv // 16 * 8)
    qkv_in.send([("x",), ("y",)], gate)
    down_in.send([("w",)], gate)
    for group in extra:
        down_in.stage([group])
    far_segments = swap(jnp.stack([segments, after(near, gate)]), 2)
    bias = score_bias(segments, near, far_segments[0], far_segments[1])
    qkv_in.stage([("y",), ("x",)], qkv_in.came())
    gate = (down_in.came(), far_segments)
    down_in.stage([("z",)], gate)
    up_in.send([("w",)], gate)
    for group in extra:
        up_in.stage([group])
    gate = (qkv_in.came(), down_in.came(), up_in.came(), bias)
    cores = qkv_in.share(True, gate) + qkv_in.share(False, gate)
    down_in.join()
    down_in.cut(down_piece.shape[0] // 16 * 8)
    down_in.send([("x",), ("y",)], cores)
    up_in.stage([("z",)], cores)
    packed, wqh, wql, xhat1, inv1, ln, s4, s5 = qkv_stage(
        me, after(tok, cores, bias), qkv_in, plan, far_pool, seqs
    )
    gate = (packed, down_in.came(), up_in.came())
    s4, s5 = after((s4, s5), gate)
    got = [swap(s4, 1), swap(s5, 2), swap(s5, 3)]
    far = jnp.concatenate(got, axis=2)
    down_in.stage([("y",), ("x",)], gate)
    cores = down_in.share(True, far)
    calls = [(s, 1, 0, width // 128) for s in range(seqs)]
    before = ()
    gate = far
    for index, which in enumerate(calls):
        packed_in = after(packed, gate, before)
        before = attention_forward(packed_in, far, bias, *attend, seqs, local_rows, which, before)
        if index == 0:
            gate = (before, down_in.came(), cores)
            cores = down_in.share(False, gate)
            up_in.join()
            up_in.cut(rows_up // 2 // 8 * 8)
            up_in.send([("x",), ("y",)], gate)
    attended, lse = before
    gate = (attended, up_in.came(), cores)
    up_in.stage([("y",), ("x",)], gate)
    dh, dl, oh, ol = projection_stage(after(me, gate), down_in, plan, width, hidden_width)
    cores = up_in.share(True, gate)
    middle, xhat2, inv2 = middle_stage(tok, attended, oh, ol)
    gate = (middle, up_in.came(), cores)
    cores = up_in.share(False, gate)
    hh, hl, ph, plo, uh, ul, nth, ntl, cth, ctl = hidden_stage(
        me, after(xhat2, cores), ln, cot, dh, dl, up_in, plan
    )

    single = [("x", "y"), ("z",), ("w",)] + extra
    double = [("x", "y"), ("z", "w")] + extra
    down = Stream(plan, chunks * rows_d, single)
    up = Stream(plan, rows_up, single)
    out = Stream(plan, rows_d, single)
    qkv = Stream(plan, rows_qkv, double)
    down_sum, up_sum, qkv_sum = Reduce(plan, single), Reduce(plan, single), Reduce(plan, double)

    away = grad_down_stage(me, cth, ctl, hh, hl, plan, down, 1)
    down_core = down_sum.begin(away)
    away = grad_up_stage(me, after(nth, away), ntl, ph, plo, plan, up, 1)
    up_core = up_sum.begin(away)
    keep = grad_down_stage(me, after(cth, away), ctl, hh, hl, plan, down, 0)
    down_sum.keep(keep)
    sent = down_sum.send(keep, down_core)
    keep = grad_up_stage(me, after(nth, sent), ntl, ph, plo, plan, up, 0)
    up_sum.keep(keep)
    gm, gln = middle_grad_stage(after(cot, keep, up_core), xhat2, inv2, ln, ph, plo, uh, ul)
    gmix, away, keep = mixture_grad_stage(me, gm, attended, oh, ol, plan, out)
    got = up_sum.begin(away, down_sum.last)
    up_sum.keep(keep)
    sent = (down_sum.send(), up_sum.send(got))
    before = ()
    calls = [(s, 1, 0, width // 128) for s in range(seqs)]
    for index, which in enumerate(calls):
        grad = after(gmix, sent, before)
        before = attention_backward(
            packed, far, bias, *attend, attended, lse, grad, seqs, local_rows, which, before
        )
        if down_sum.stages:
            sent = down_sum.send(before, down_sum.last)
        else:
            sent = down_sum.last
    gate = (before, up_sum.last)
    dq, dk, dv, f4, f5a, f5b = before
    f4, f5a, f5b = after((f4, f5a, f5b), gate)
    g4, g5a, g5b = swap(f4, 1), swap(f5a, 2), swap(f5b, 3)
    gph, gpl, column = packed_grad_stage(dq, dk, dv, g4, g5a, g5b, far_pool, seqs)
    away, sums_away = grad_qkv_stage(
        me, gph, gpl, column, xhat1, ln, wqh, wql, plan, qkv, 1
    )
    got = qkv_sum.begin(away)
    keep, sums_keep = grad_qkv_stage(
        me, gph, gpl, column, after(xhat1, away), ln, wqh, wql, plan, qkv, 0
    )
    qkv_sum.keep(keep)
    sums = jnp.concatenate([(sums_away + sums_keep)[0:2], gln[0:2]], axis=0)
    sent = qkv_sum.send(got, rider=sums.reshape(-1, 128))
    up_sum.send(sent)
    gtok = input_grad_stage(gph, gpl, wqh, wql, after(xhat1, sent), inv1, ln, gm)
    output = output_stage(after(middle, gtok), hh, hl, dh, dl)
    rode = qkv_sum.rode
    sent = qkv_sum.send(qkv_sum.last, up_sum.last, output, rider=rode)
    while qkv_sum.stages:
        sent = qkv_sum.send(qkv_sum.last, rider=qkv_sum.rode)
    while up_sum.stages:
        up_sum.send(sent)
    for total in (down_sum, up_sum):
        total.terms[0] = after(total.terms[0], sent)
    sums = qkv_sum.rode
    sums = (sums + plan.send(sums, ("c",))).reshape(4, width)
    (g_down,), (g_up, g_out), (g_qkv,) = (t.total() for t in (down_sum, up_sum, qkv_sum))
    mine = lax.dynamic_slice(sums, (0, me_d * share), (4, share))
    if rows_up % 128 == 0:
        g_up = g_up.reshape(-1, width // fsdp, 128).transpose(1, 0, 2).reshape(-1, rows_up)
    else:
        g_up = g_up.T
    g_down = g_down.reshape(chunks, rows_d, 128).transpose(0, 2, 1).reshape(-1, rows_d)
    shape = tokens.shape
    return (
        output.reshape(shape),
        gtok.reshape(shape),
        mine[0],
        mine[1],
        g_qkv.T,
        g_out.T,
        mine[2],
        mine[3],
        g_up,
        g_down,
    )


def solution(mesh):
    weight = P("fsdp", "dp")
    rows = P("dp", "fsdp", None)
    vector = P("dp")
    return jax.shard_map(
        local,
        mesh=mesh,
        in_specs=(rows, P("dp", "fsdp"), rows, vector, vector, weight, weight, vector, vector, weight, weight),
        out_specs=(rows, rows, vector, vector, weight, weight, vector, vector, weight, weight),
        check_vma=False,
    )
```

```python
import jax
import jax.numpy as jnp
import numpy as np
from jax import lax
from jax.experimental import pallas as pl
from jax.experimental.pallas import tpu as pltpu
from jax.sharding import PartitionSpec as P

HEADS = 8
NR = 16
LEVELS = 6
EPSILON = 1e-05
MASKED = -1e30
F32 = jnp.float32
BF16 = jnp.bfloat16
LN_ROWS = 16
TILE = 128
ROOM = pltpu.CompilerParams(vmem_limit_bytes=23 << 20)
SCALE = 0.05


def split(x):
    high = x.astype(BF16)
    return high, (x - high.astype(F32)).astype(BF16)


def mm(a, b, ca, cb):
    return lax.dot_general(a, b, (((ca,), (cb,)), ((), ())), preferred_element_type=F32)


def mm3(a, b, ca, cb):
    return mm(a[0], b[0], ca, cb) + mm(a[0], b[1], ca, cb) + mm(a[1], b[0], ca, cb)


def mm2(a, b, ca, cb):
    return mm(a, b[0], ca, cb) + mm(a, b[1], ca, cb)


def level_layout(length):
    rows, start = [], 0
    for level in range(1, LEVELS):
        count = length >> level
        rows.append((level, start, count))
        start += count
    return rows, start


def pooling(length):
    spread = np.zeros((length, length), np.float32)
    pool = np.zeros((length, length), np.float32)
    same = np.zeros((length, length), np.float32)
    layout, _ = level_layout(length)
    bounds = [first for _, first, _ in layout] + [length]
    for index, (level, first, count) in enumerate(layout):
        token = np.arange(length)
        spread[token, first + (token >> level)] = 1.0
        pool[first + (token >> level), token] = 0.5**level
        same[bounds[index] : bounds[index + 1], bounds[index] : bounds[index + 1]] = 1.0
    return spread, pool, same


def score_bias(seg, near, far_a, far_b):
    count, length = seg.shape
    token = np.arange(length)
    near_pair = (token[:TILE, None] >> 5) == (token[None, :TILE] >> 5)
    tiles = seg.reshape(count, length // TILE, TILE)
    ok = near_pair & (tiles[:, :, :, None] == tiles[:, :, None, :])
    inner = jnp.where(ok, 0.0, MASKED).astype(F32).reshape(count, length, TILE)
    parts = []
    for level in range(1, LEVELS):
        ratio = 1 << level

        def ends(values):
            grouped = values.reshape(count, length // ratio, ratio)
            return grouped[:, :, 0], grouped[:, :, -1]

        low_q, high_q = ends(seg)
        low_q = jnp.repeat(low_q, ratio, axis=1)
        high_q = jnp.repeat(high_q, ratio, axis=1)
        if 2 * NR * ratio <= length:
            low_k, high_k = ends(seg)
            block_q = (token >> level) >> 4
            block_k = np.arange(length >> level) >> 4
            where = (block_q[:, None] ^ 1) == block_k[None, :]
        else:
            if NR * ratio <= length:
                low_k, high_k = ends(near)
            else:
                pieces = [ends(far_a), ends(far_b)]
                low_k = jnp.concatenate([pieces[0][0], pieces[1][0]], axis=1)
                high_k = jnp.concatenate([pieces[0][1], pieces[1][1]], axis=1)
            where = np.ones((length, low_k.shape[1]), bool)
        ok = (
            where[None]
            & (low_q[:, :, None] <= high_k[:, None, :])
            & (low_k[:, None, :] <= high_q[:, :, None])
        )
        parts.append(jnp.where(ok, np.float32(level * np.log(2.0)), MASKED))
    return inner, jnp.concatenate(parts, axis=2).astype(F32)


class Plan:
    def __init__(self, dp, fsdp):
        self.dp, self.fsdp = dp, fsdp
        self.dims = {}
        names = ["x", "z", "w"]
        bit = 1
        while bit < dp:
            name = names[len(self.dims)] if len(self.dims) < 3 else "d%d" % bit
            self.dims[name] = ("dp", bit)
            bit *= 2
        self.extra = list(self.dims)[3:]
        self.dims["y"] = ("fsdp", 2)
        self.dims["c"] = ("fsdp", 1)

    def corner(self, group, v):
        return tuple(name for i, name in enumerate(group) if (v >> i) & 1)

    def mask(self, names):
        d = f = 0
        for name in names:
            axis, bit = self.dims[name]
            if axis == "dp":
                d |= bit
            else:
                f |= bit
        return d, f

    def send(self, x, names):
        d, f = self.mask(names)
        if not f:
            return lax.ppermute(x, "dp", [(i, i ^ d) for i in range(self.dp)])
        if not d:
            return lax.ppermute(x, "fsdp", [(i, i ^ f) for i in range(self.fsdp)])
        n = self.fsdp
        pairs = [(i, ((i // n) ^ d) * n + ((i % n) ^ f)) for i in range(self.dp * n)]
        return lax.ppermute(x, ("dp", "fsdp"), pairs)

    def position(self, stages, d, f):
        pos = 0
        for group in stages:
            for name in reversed(group):
                axis, bit = self.dims[name]
                value = d if axis == "dp" else f
                pos = pos * 2 + ((value // bit) & 1)
        return pos


class Part:
    def __init__(self, start, held, names):
        self.start, self.held, self.names, self.got = start, held, names, []


class Gather:
    def __init__(self, plan, piece):
        self.plan, self.parts = plan, [Part(0, piece[None], [()])]
        self.arrays, self.slots = [], []

    def cut(self, row):
        (part,) = self.parts
        self.parts = [
            Part(0, part.held[:, :row], part.names),
            Part(row, part.held[:, row:], part.names),
        ]

    def send(self, groups, *earlier):
        for part, group in zip(self.parts, groups):
            if earlier:
                part.held = after(part.held, *earlier)
            for v in range(1, 1 << len(group)):
                names = self.plan.corner(group, v)
                part.got.append((self.plan.send(part.held, names), names))

    def came(self):
        return [value for part in self.parts for value, _ in part.got]

    def join(self):
        for part in self.parts:
            names = list(part.names)
            for _, corner in part.got:
                names += [n + corner for n in part.names]
            part.held = jnp.concatenate([part.held] + [v for v, _ in part.got], axis=0)
            part.names, part.got = names, []

    def stage(self, groups, *earlier):
        self.join()
        self.send(groups, *earlier)

    def share(self, held, *earlier):
        sent = []
        for part in self.parts:
            for value, corner in [(part.held, ())] if held else part.got:
                if earlier:
                    value = after(value, *earlier)
                other = self.plan.send(value, ("c",))
                sent.append(other)
                for array, core in ((value, ()), (other, ("c",))):
                    self.arrays.append(array)
                    slots = [self.plan.mask(n + corner + core) for n in part.names]
                    self.slots.append((slots, part.start))
        return sent


def assemble(scratch, refs, gathered, me_d, me_f, rows, lanes, segments):
    for ref, (slots, start) in zip(refs, gathered.slots):
        for slot, (d, f) in enumerate(slots):
            row0 = (me_d ^ d) * rows
            col0 = (me_f ^ f) * lanes
            for source, size, to_lane in segments:
                low, high = max(source, start), min(source + size, start + ref.shape[1])
                if low < high:
                    row = pl.multiple_of(row0 + (low - source), 8)
                    col = pl.multiple_of(col0 + to_lane, 128)
                    scratch[pl.ds(row, high - low), pl.ds(col, 128)] = ref[
                        slot, low - start : high - start, :
                    ]


def norm_rows(refs, gathered):
    total = None
    for ref, (slots, start) in zip(refs, gathered.slots):
        for slot, (d, f) in enumerate(slots):
            if f == 0 and start == 0:
                value = ref[slot, :LN_ROWS, :]
                total = value if total is None else total + value
    return jnp.concatenate([total[4 * i : 4 * i + 4] for i in range(4)], axis=1)


class Stream:
    def __init__(self, plan, rows, stages):
        self.plan, self.rows, self.stages = plan, rows, stages
        self.slots = plan.dp * plan.fsdp // 2

    def shape(self):
        return (self.slots, self.rows, 128)

    def put(self, out, d, f, row, value):
        size = value.shape[0]
        out[self.plan.position(self.stages, d, f), row : row + size, :] = value


class Reduce:
    def __init__(self, plan, stages):
        self.plan, self.stages = plan, list(stages)
        self.kept, self.came, self.last = [], [], []

    def begin(self, part, *earlier):
        part = after(part, *earlier) if earlier else part
        self.last = [self.plan.send(part, ("c",))]
        self.came.append(self.last[0])
        return self.last

    def keep(self, part):
        self.kept.append(part)

    def send(self, *earlier, rider=None):
        if self.kept:
            self.terms = [self.kept, self.came]
            self.slots, self.kept = self.kept[0].shape[0], []
        if earlier:
            self.terms[-1] = after(self.terms[-1], *earlier)
        group = self.stages.pop(0)
        self.slots >>= len(group)
        n = self.slots
        count = range(len(self.terms[0]))
        sizes = [part.shape[1] for part in self.terms[0]]
        cuts = np.cumsum([0] + sizes)
        out = []
        for v in range(1, 1 << len(group)):
            parts = [sum(term[i][v * n : (v + 1) * n] for term in self.terms) for i in count]
            if rider is not None:
                parts.append(jnp.broadcast_to(rider[None], (n,) + rider.shape))
            out.append(parts[0] if len(parts) == 1 else jnp.concatenate(parts, axis=1))
        self.last, self.rode = [], rider
        for v, value in enumerate(out):
            got = self.plan.send(value, self.plan.corner(group, v + 1))
            self.last.append(got)
            self.terms.append([got[:, a:b] for a, b in zip(cuts[:-1], cuts[1:])])
            if rider is not None:
                self.rode = self.rode + got[0, cuts[-1] :]
        return out

    def total(self, *earlier):
        count = range(len(self.terms[0]))
        return [sum(term[i][0] for term in self.terms) for i in count]


def after(value, *earlier):
    return lax.optimization_barrier((value, earlier))[0]


def whole(shape=None):
    return pl.BlockSpec(memory_space=pltpu.VMEM)


SMEM = pl.BlockSpec(memory_space=pltpu.SMEM)


def cost(micros):
    return pl.CostEstimate(
        flops=int(micros * SCALE * 9e8), bytes_accessed=int(micros * SCALE * 2.5e6), transcendentals=0
    )


def call(body, outs, scratch=(), **kw):
    return pl.pallas_call(
        body,
        out_shape=[jax.ShapeDtypeStruct(s, t) for s, t in outs],
        scratch_shapes=list(scratch),
        **kw,
    )


def qkv_stage(me, tokens, gathered, plan, pool, seqs):
    rows_all, width = tokens.shape
    length = rows_all // seqs
    n4, n5 = length >> 4, length >> 5
    slots = gathered.arrays
    triple = 3 * width
    rows = triple // plan.dp
    lanes = width // plan.fsdp

    def body(me_ref, tok, pool_ref, *rest):
        refs = rest[: len(slots)]
        packed, wh, wl, xhat, inv, ln, s4, s5, full, nh, nl = rest[len(slots) :]
        step = pl.program_id(0)

        @pl.when(step == 0)
        def _():
            assemble(full, refs, gathered, me_ref[0], me_ref[1], rows, lanes, [(LN_ROWS, rows, 0)])
            params = norm_rows(refs, gathered)
            ln[0:4, :] = params
            x = tok[...]
            centre = x - jnp.mean(x, axis=1, keepdims=True)
            scale = lax.rsqrt(jnp.mean(centre * centre, axis=1, keepdims=True) + EPSILON)
            xh = centre * scale
            xhat[...] = xh
            inv[...] = jnp.broadcast_to(scale, inv.shape)
            n = split(xh * params[0:1, :] + params[1:2, :])
            nh[...] = n[0]
            nl[...] = n[1]

        w = split(full[pl.ds(pl.multiple_of(step * width, width), width), :])
        wh[...] = w[0]
        wl[...] = w[1]
        packed[...] = mm3((nh[...], nl[...]), w, 1, 1)

        @pl.when(step > 0)
        def _():
            for s in range(seqs):
                means = mm2(pool_ref[...], split(packed[s * length : (s + 1) * length, :]), 1, 0)
                s4[s, 0] = means[:n4]
                s5[s, 0] = means[n4 : n4 + n5]

    fixed = lambda shape: pl.BlockSpec(shape, lambda i: (0,) * len(shape))
    later = lambda n: pl.BlockSpec((seqs, 1, n, width), lambda i: (0, jnp.maximum(i - 1, 0), 0, 0))
    outs = [
        ((rows_all, triple), F32, pl.BlockSpec((rows_all, width), lambda i: (0, i))),
        ((triple, width), BF16, pl.BlockSpec((width, width), lambda i: (i, 0))),
        ((triple, width), BF16, pl.BlockSpec((width, width), lambda i: (i, 0))),
        ((rows_all, width), F32, fixed((rows_all, width))),
        ((rows_all, 128), F32, fixed((rows_all, 128))),
        ((8, width), F32, fixed((8, width))),
        ((seqs, 2, n4, width), F32, later(n4)),
        ((seqs, 2, n5, width), F32, later(n5)),
    ]
    return pl.pallas_call(
        body,
        compiler_params=ROOM,
        cost_estimate=cost(7.4),
        grid=(3,),
        out_shape=[jax.ShapeDtypeStruct(shape, kind) for shape, kind, _ in outs],
        in_specs=[SMEM, fixed((rows_all, width)), fixed(pool.shape)]
        + [fixed(x.shape) for x in slots],
        out_specs=[spec for _, _, spec in outs],
        scratch_shapes=[
            pltpu.VMEM((triple, width), F32),
            pltpu.VMEM((rows_all, width), BF16),
            pltpu.VMEM((rows_all, width), BF16),
        ],
    )(me, tokens, pool, *slots)


def lanes2(pair):
    return jnp.concatenate(pair, axis=1)


def fold(r):
    return r[:, :128] + r[:, 128:]


def wide_nt(a, b):
    first = mm(lanes2(a), lanes2((b[0], b[0])), 1, 1)
    return first + mm(a[0], b[1], 1, 1)


def wide_nn(a, b):
    return fold(mm(a[0], lanes2(b), 1, 0)) + mm(a[1], b[0], 1, 0)


def wide_tn(a, b):
    return fold(mm(a[0], lanes2(b), 0, 0)) + mm(a[1], b[0], 0, 0)


def tile_tn(a, b):
    left = jnp.concatenate(a, axis=0)
    right = jnp.concatenate([lanes2(b), lanes2((b[0], jnp.zeros_like(b[0])))], axis=0)
    return fold(mm(left, right, 0, 0))


def rows(pair, t):
    return tuple(x[t * TILE : (t + 1) * TILE] for x in pair)


class Heads:
    def __init__(self, q, k, v, fk, fv, pool, local):
        length = q.shape[0]
        self.tiles = range(length // TILE)
        self.lane = lax.broadcasted_iota(jnp.int32, (length, 128), 1) < 64
        qs, ks, vs = split(q), split(k), split(v)
        pooled = mm(pool, jnp.concatenate([qs[0], ks[0], vs[0], qs[1], ks[1], vs[1]], axis=1), 1, 0)
        pooled = pooled[:, :384] + pooled[:, 384:]
        kc = jnp.concatenate([pooled[:local, 128:256], fk], axis=0)
        vc = jnp.concatenate([pooled[:local, 256:], fv], axis=0)
        self.q, self.qc = qs, split(pooled[:, :128])
        self.k2 = [self.two(rows(ks, t)) for t in self.tiles]
        self.v2 = [self.two(rows(vs, t)) for t in self.tiles]
        self.kc2, self.vc2 = self.two(split(kc)), self.two(split(vc))

    def two(self, pair):
        out = []
        for x in pair:
            lane = self.lane[: x.shape[0]]
            zero = jnp.zeros_like(x)
            both = [jnp.where(lane, x, zero), jnp.where(lane, zero, x)]
            out.append(jnp.concatenate(both, axis=0))
        return tuple(out)

    def one(self, x):
        half = x.shape[0] // 2
        return jnp.where(self.lane[:half], x[:half], x[half:])

    def inner(self, left, right):
        return jnp.concatenate([wide_nt(rows(left, t), right[t]) for t in self.tiles], axis=0)

    def scores(self, spread, same, inner_bias, outer_bias):
        s0 = self.inner(self.q, self.k2) + lanes2((inner_bias, inner_bias))
        high, low = split(wide_nt(self.qc, self.kc2) * lanes2((same, same)))
        st = mm(spread, high, 1, 0) + mm(spread, low, 1, 0)
        return s0, st + lanes2((outer_bias, outer_bias))


def head_columns(x):
    half = x.shape[1] // 2
    return x[:, :half], x[:, half:]


def attention_specs(length, width, first=0, pair=0):
    pairs = width // 128
    block = lambda off: pl.BlockSpec((length, 128), lambda s, h: (first + s, off * pairs + pair + h))
    far = lambda j: pl.BlockSpec((1, 1, 32, 128), lambda s, h: (first + s, j, 0, pair + h))
    fixed = pl.BlockSpec((length, length), lambda s, h: (0, 0))
    bias = lambda n: pl.BlockSpec((1, length, n), lambda s, h: (first + s, 0, 0))
    return block, far, fixed, [bias(TILE), bias(length), fixed, fixed, fixed]


def attention_forward(packed, far, bias, spread, pool, same, seqs, local, which, before):
    rows_all, triple = packed.shape
    width = triple // 3
    length = rows_all // seqs
    first, count, pair, pairs = which
    block, far_spec, fixed, common = attention_specs(length, width, first, pair)
    carried = len(before)

    def body(q, k, v, fk, fv, inner_bias, outer_bias, spread_ref, pool_ref, same_ref, *rest):
        out, lse = rest[carried:]
        heads = Heads(q[...] * 0.125, k[...], v[...], fk[0, 0], fv[0, 0], pool_ref[...], local)
        s0, st = heads.scores(spread_ref[...], same_ref[...], inner_bias[0], outer_bias[0])
        p0, pc, peaks, sums = [], [], [], []
        for a, b in zip(head_columns(s0), head_columns(st)):
            peak = jnp.maximum(jnp.max(a, axis=1, keepdims=True), jnp.max(b, axis=1, keepdims=True))
            a, b = jnp.exp(a - peak), jnp.exp(b - peak)
            p0.append(a)
            pc.append(b)
            peaks.append(peak)
            sums.append(jnp.sum(a, axis=1, keepdims=True) + jnp.sum(b, axis=1, keepdims=True))
        p0, pc = split(lanes2(p0)), split(lanes2(pc))
        mixed = [wide_nn(rows(p0, t), heads.v2[t]) for t in heads.tiles]
        mixed = jnp.concatenate(mixed, axis=0) + wide_nn(pc, heads.vc2)
        total = jnp.where(heads.lane, sums[0], sums[1])
        out[...] = mixed / total
        lse[...] = jnp.where(heads.lane, peaks[0], peaks[1]) + jnp.log(total)

    return pl.pallas_call(
        body,
        compiler_params=ROOM,
        cost_estimate=cost(9.5),
        grid=(count, pairs),
        out_shape=[jax.ShapeDtypeStruct((rows_all, width), F32)] * 2,
        in_specs=[block(0), block(1), block(2), far_spec(0), far_spec(1)]
        + common
        + [pl.BlockSpec(memory_space=pl.ANY)] * carried,
        out_specs=[block(0), block(0)],
        input_output_aliases={10 + i: i for i in range(carried)},
    )(packed, packed, packed, far, far, *bias, spread, pool, same, *before)


def attention_backward(
    packed, far, bias, spread, pool, same, attended, lse, grad, seqs, local, which, before
):
    rows_all, triple = packed.shape
    width = triple // 3
    length = rows_all // seqs
    first, count, pair, pairs = which
    block, far_spec, fixed, common = attention_specs(length, width, first, pair)
    n4, n5 = length >> 4, length >> 5
    carried = len(before)

    def body(q, k, v, fk, fv, inner_bias, outer_bias, spread_ref, pool_ref, same_ref, *rest):
        o_ref, lse_ref, g_ref = rest[:3]
        dq_ref, dk_ref, dv_ref, f4, f5a, f5b = rest[3 + carried :]
        spread_m, pool_m, same_m = spread_ref[...], pool_ref[...], same_ref[...]
        heads = Heads(q[...] * 0.125, k[...], v[...], fk[0, 0], fv[0, 0], pool_m, local)
        lane = heads.lane
        s0, st = heads.scores(spread_m, same_m, inner_bias[0], outer_bias[0])
        logs = lse_ref[...]
        logs = (logs[:, 0:1], logs[:, 64:65])
        p0 = lanes2([jnp.exp(a - x) for a, x in zip(head_columns(s0), logs)])
        pc = lanes2([jnp.exp(a - x) for a, x in zip(head_columns(st), logs)])
        grad_rows = g_ref[...]
        g = split(grad_rows)
        product = grad_rows * o_ref[...]
        zero = jnp.zeros_like(product)
        deltas = [
            jnp.sum(jnp.where(lane, product, zero), axis=1, keepdims=True),
            jnp.sum(jnp.where(lane, zero, product), axis=1, keepdims=True),
        ]
        d0 = heads.inner(g, heads.v2)
        d0 = split(p0 * lanes2([a - x for a, x in zip(head_columns(d0), deltas)]))
        dt = wide_nt(g, heads.vc2)
        dt = split(pc * lanes2([a - x for a, x in zip(head_columns(dt), deltas)]))
        p0, pc = split(p0), split(pc)
        dv = [heads.one(tile_tn(rows(p0, t), rows(g, t))) for t in heads.tiles]
        dk = [heads.one(tile_tn(rows(d0, t), rows(heads.q, t))) for t in heads.tiles]
        dq = [wide_nn(rows(d0, t), heads.k2[t]) for t in heads.tiles]
        dvc = heads.one(wide_tn(pc, g))
        dsc = mm(spread_m, dt[0], 0, 0) + mm(spread_m, dt[1], 0, 0)
        dsc = split(dsc * lanes2((same_m, same_m)))
        dqc = wide_nn(dsc, heads.kc2)
        dkc = heads.one(wide_tn(dsc, heads.qc))
        near = lax.broadcasted_iota(jnp.int32, (length, 128), 0) < local
        high, low = split(
            jnp.concatenate([dqc, jnp.where(near, dkc, zero), jnp.where(near, dvc, zero)], axis=1)
        )
        back = mm(pool_m, lanes2((high, low)), 0, 0)
        back = back[:, :384] + back[:, 384:]
        dq_ref[...] = (jnp.concatenate(dq, axis=0) + back[:, :128]) * 0.125
        dk_ref[...] = jnp.concatenate(dk, axis=0) + back[:, 128:256]
        dv_ref[...] = jnp.concatenate(dv, axis=0) + back[:, 256:]
        for j, value in ((0, dkc), (1, dvc)):
            f4[0, j] = value[local : local + n4]
            f5a[0, j] = value[local + n4 : local + n4 + n5]
            f5b[0, j] = value[local + n4 + n5 :]

    far_out = lambda n: pl.BlockSpec((1, 2, n, 128), lambda s, h: (first + s, 0, 0, pair + h))
    return pl.pallas_call(
        body,
        compiler_params=ROOM,
        cost_estimate=cost(8),
        grid=(count, pairs),
        out_shape=[jax.ShapeDtypeStruct((rows_all, width), F32)] * 3
        + [jax.ShapeDtypeStruct((seqs, 2, n, width), F32) for n in (n4, n5, n5)],
        in_specs=[block(0), block(1), block(2), far_spec(0), far_spec(1)]
        + common
        + [block(0)] * 3
        + [pl.BlockSpec(memory_space=pl.ANY)] * carried,
        out_specs=[block(0)] * 3 + [far_out(n4), far_out(n5), far_out(n5)],
        input_output_aliases={13 + i: i for i in range(carried)},
    )(packed, packed, packed, far, far, *bias, spread, pool, same, attended, lse, grad, *before)


def middle_stage(tokens, attended, wh, wl):
    rows_all, width = tokens.shape

    def body(tok, att, wh_ref, wl_ref, middle, xhat, inv):
        x = tok[...] + mm3(split(att[...]), (wh_ref[...], wl_ref[...]), 1, 1)
        middle[...] = x
        centre = x - jnp.mean(x, axis=1, keepdims=True)
        scale = lax.rsqrt(jnp.mean(centre * centre, axis=1, keepdims=True) + EPSILON)
        xhat[...] = centre * scale
        inv[...] = jnp.broadcast_to(scale, inv.shape)

    return call(
        body,
        [((rows_all, width), F32), ((rows_all, width), F32), ((rows_all, 128), F32)],
        compiler_params=ROOM,
        cost_estimate=cost(4.3),
        in_specs=[whole()] * 4,
        out_specs=[whole()] * 3,
    )(tokens, attended, wh, wl)


def projection_stage(me, gathered, plan, width, hidden_width):
    rows, lanes = width // plan.dp, hidden_width // plan.fsdp
    out_lanes = width // plan.fsdp
    slots = gathered.arrays
    chunks = lanes // 128
    down_parts = [(k * rows, rows, 128 * k) for k in range(chunks)]
    out_parts = [(chunks * rows, rows, 0)]
    chunk = 512

    def body(me_ref, *rest):
        refs = rest[: len(slots)]
        dh, dl, oh, ol, full, full_out = rest[len(slots) :]
        me_d, me_f = me_ref[0], me_ref[1]
        step = pl.program_id(0)

        @pl.when(step == 0)
        def _():
            assemble(full_out, refs, gathered, me_d, me_f, rows, out_lanes, out_parts)
            w = split(full_out[...])
            oh[...] = w[0]
            ol[...] = w[1]
            assemble(full, refs, gathered, me_d, me_f, rows, lanes, down_parts)

        w = split(full[:, pl.ds(pl.multiple_of(step * chunk, chunk), chunk)])
        dh[...] = w[0]
        dl[...] = w[1]

    fixed = lambda shape: pl.BlockSpec(shape, lambda i: (0,) * len(shape))
    cols = pl.BlockSpec((width, chunk), lambda i: (0, i))
    return pl.pallas_call(
        body,
        compiler_params=ROOM,
        cost_estimate=cost(5),
        grid=(hidden_width // chunk,),
        out_shape=[jax.ShapeDtypeStruct((width, hidden_width), BF16)] * 2
        + [jax.ShapeDtypeStruct((width, width), BF16)] * 2,
        in_specs=[SMEM] + [fixed(x.shape) for x in slots],
        out_specs=[cols, cols, fixed((width, width)), fixed((width, width))],
        scratch_shapes=[pltpu.VMEM((width, hidden_width), F32), pltpu.VMEM((width, width), F32)],
    )(me, *slots)


def hidden_stage(me, xhat, ln, cot, dh, dl, gathered, plan):
    rows_all, width = xhat.shape
    hidden_width = dh.shape[1]
    rows, lanes = hidden_width // plan.dp, width // plan.fsdp
    slots = gathered.arrays
    chunk = 512
    steps = hidden_width // chunk
    root = float(np.sqrt(2.0 / np.pi))
    cubic = 0.044715 * root

    def body(me_ref, xhat_ref, ln_ref, cot_ref, d0, d1, *rest):
        refs = rest[: len(slots)]
        hh, hl, ph, plo, wh, wl, nth, ntl, cth, ctl, full, nh, nl, ch, cl = rest[len(slots) :]
        step = pl.program_id(0)

        @pl.when(step == 0)
        def _():
            assemble(full, refs, gathered, me_ref[0], me_ref[1], rows, lanes, [(0, rows, 0)])
            n = xhat_ref[...] * ln_ref[2:3, :] + ln_ref[3:4, :]
            c = cot_ref[...]
            for value, high, low in (
                (n, nh, nl),
                (c, ch, cl),
                (jnp.transpose(n), nth, ntl),
                (jnp.transpose(c), cth, ctl),
            ):
                halves = split(value)
                high[...] = halves[0]
                low[...] = halves[1]

        w = split(full[pl.ds(pl.multiple_of(step * chunk, chunk), chunk), :])
        wh[...] = w[0]
        wl[...] = w[1]
        v = mm3((nh[...], nl[...]), w, 1, 1)
        square = v * v
        half = 0.5 + 0.5 * jnp.tanh(v * (root + cubic * square))
        h = split(v * half)
        hh[...] = h[0]
        hl[...] = h[1]
        slope = half + (half - half * half) * (v * (2.0 * root + 6.0 * cubic * square))
        g = split(mm3((ch[...], cl[...]), (d0[...], d1[...]), 1, 0) * slope)
        ph[...] = g[0]
        plo[...] = g[1]

    fixed = lambda shape: pl.BlockSpec(shape, lambda i: (0,) * len(shape))
    cols = pl.BlockSpec((rows_all, chunk), lambda i: (0, i))
    down = pl.BlockSpec((width, chunk), lambda i: (0, i))
    act = fixed((rows_all, width))
    return pl.pallas_call(
        body,
        compiler_params=ROOM,
        cost_estimate=cost(15),
        grid=(steps,),
        out_shape=[jax.ShapeDtypeStruct((rows_all, hidden_width), BF16)] * 4
        + [jax.ShapeDtypeStruct((hidden_width, width), BF16)] * 2
        + [jax.ShapeDtypeStruct((width, rows_all), BF16)] * 4,
        in_specs=[SMEM, act, fixed((8, width)), act, down, down]
        + [fixed(x.shape) for x in slots],
        out_specs=[cols] * 4
        + [pl.BlockSpec((chunk, width), lambda i: (i, 0))] * 2
        + [fixed((width, rows_all))] * 4,
        scratch_shapes=[pltpu.VMEM((hidden_width, width), F32)]
        + [pltpu.VMEM((rows_all, width), BF16)] * 4,
    )(me, xhat, ln, cot, dh, dl, *slots)


def grad_down_stage(me, cth, ctl, hh, hl, plan, stream, core):
    width, rows_all = cth.shape
    hidden_width = hh.shape[1]
    rows, lanes = width // plan.dp, hidden_width // plan.fsdp

    def body(me_ref, c0, c1, h0, h1, out):
        jf = core + 2 * pl.program_id(0)
        res = mm3((c0[...], c1[...]), (h0[...], h1[...]), 1, 0)
        for d in range(plan.dp):
            jd = me_ref[0] ^ d
            for k in range(lanes // 128):
                value = res[d * rows : (d + 1) * rows, 128 * k : 128 * (k + 1)]
                stream.put(out, jd, jf, k * rows, value)

    cols = pl.BlockSpec((rows_all, lanes), lambda i, m: (0, m[1] ^ (core + 2 * i)))
    grid_spec = pltpu.PrefetchScalarGridSpec(
        num_scalar_prefetch=1,
        grid=(plan.fsdp // 2,),
        in_specs=[pl.BlockSpec((width, rows_all), lambda i, m: (0, 0))] * 2 + [cols, cols],
        out_specs=pl.BlockSpec(stream.shape(), lambda i, m: (0, 0, 0)),
    )
    return pl.pallas_call(
        body,
        compiler_params=ROOM,
        cost_estimate=cost(0.27),
        grid_spec=grid_spec,
        out_shape=jax.ShapeDtypeStruct(stream.shape(), F32),
    )(me, cth, ctl, hh, hl)


def half_lanes(ref, me_f, core, lanes):
    parts = []
    for y in range(2):
        start = pl.multiple_of((me_f ^ (core + 2 * y)) * lanes, 128)
        parts.append(ref[:, pl.ds(start, lanes)])
    return jnp.concatenate(parts, axis=1)


def half_rows(ref, me_f, core, count):
    parts = []
    for y in range(2):
        start = pl.multiple_of((me_f ^ (core + 2 * y)) * count, 128)
        parts.append(ref[pl.ds(start, count), :])
    return jnp.concatenate(parts, axis=0)


def grad_up_stage(me, nth, ntl, ph, plo, plan, stream, core):
    width, rows_all = nth.shape
    hidden_width = ph.shape[1]
    rows, lanes = hidden_width // plan.dp, width // plan.fsdp
    chunk = 512
    steps = hidden_width // chunk
    per = chunk // rows
    natural = rows % 128 == 0

    def body(me_ref, n0, n1, p0, p1, out):
        step = pl.program_id(0)
        n = (half_rows(n0, me_ref[1], core, lanes), half_rows(n1, me_ref[1], core, lanes))
        p = (p0[...], p1[...])
        res = mm3(n, p, 1, 0) if natural else mm3(p, n, 0, 1)
        for i in range(per):
            jd = (step * per + i) ^ me_ref[0]
            for y in range(2):
                if natural:
                    for k in range(rows // 128):
                        at = i * rows + 128 * k
                        value = res[y * lanes : (y + 1) * lanes, at : at + 128]
                        stream.put(out, jd, core + 2 * y, k * lanes, value)
                else:
                    value = res[i * rows : (i + 1) * rows, y * lanes : (y + 1) * lanes]
                    stream.put(out, jd, core + 2 * y, 0, value)

    fixed = lambda shape: pl.BlockSpec(shape, lambda i: (0,) * len(shape))
    cols = pl.BlockSpec((rows_all, chunk), lambda i: (0, i))
    return pl.pallas_call(
        body,
        compiler_params=ROOM,
        cost_estimate=cost(0.32),
        grid=(steps,),
        out_shape=jax.ShapeDtypeStruct(stream.shape(), F32),
        in_specs=[SMEM] + [fixed((width, rows_all))] * 2 + [cols, cols],
        out_specs=fixed(stream.shape()),
    )(me, nth, ntl, ph, plo)


def norm_back(e, gain, xhat, inv):
    u = e * gain
    mean_u = jnp.mean(u, axis=1, keepdims=True)
    mean_ux = jnp.mean(u * xhat, axis=1, keepdims=True)
    return inv * (u - mean_u - xhat * mean_ux)


def output_stage(middle, hh, hl, dh, dl):
    rows_all, width = middle.shape
    chunk = 512
    steps = hh.shape[1] // chunk

    def body(mid, h0, h1, d0, d1, out):
        @pl.when(pl.program_id(0) == 0)
        def _():
            out[...] = mid[...]

        out[...] += mm3((h0[...], h1[...]), (d0[...], d1[...]), 1, 1)

    cols = pl.BlockSpec((rows_all, chunk), lambda i: (0, i))
    act = pl.BlockSpec((rows_all, width), lambda i: (0, 0))
    return pl.pallas_call(
        body,
        compiler_params=ROOM,
        cost_estimate=cost(8),
        grid=(steps,),
        out_shape=jax.ShapeDtypeStruct((rows_all, width), F32),
        in_specs=[act, cols, cols] + [pl.BlockSpec((width, chunk), lambda i: (0, i))] * 2,
        out_specs=act,
    )(middle, hh, hl, dh, dl)


def middle_grad_stage(cot, xhat, inv, ln, ph, plo, uh, ul):
    rows_all, width = cot.shape
    chunk = 512
    steps = ph.shape[1] // chunk

    def body(cot_ref, xhat_ref, inv_ref, ln_ref, p0, p1, u0, u1, gm, gln, acc):
        step = pl.program_id(0)

        @pl.when(step == 0)
        def _():
            acc[...] = jnp.zeros_like(acc)

        acc[...] += mm3((p0[...], p1[...]), (u0[...], u1[...]), 1, 0)

        @pl.when(step == steps - 1)
        def _():
            e = acc[...]
            xh = xhat_ref[...]
            gm[...] = cot_ref[...] + norm_back(e, ln_ref[2:3, :], xh, inv_ref[:, 0:1])
            gln[0:1, :] = jnp.sum(e * xh, axis=0, keepdims=True)
            gln[1:2, :] = jnp.sum(e, axis=0, keepdims=True)

    fixed = lambda shape: pl.BlockSpec(shape, lambda i: (0,) * len(shape))
    cols = pl.BlockSpec((rows_all, chunk), lambda i: (0, i))
    act = fixed((rows_all, width))
    return pl.pallas_call(
        body,
        compiler_params=ROOM,
        cost_estimate=cost(8.5),
        grid=(steps,),
        out_shape=[
            jax.ShapeDtypeStruct((rows_all, width), F32),
            jax.ShapeDtypeStruct((8, width), F32),
        ],
        in_specs=[act, act, fixed((rows_all, 128)), fixed((8, width)), cols, cols]
        + [pl.BlockSpec((chunk, width), lambda i: (i, 0))] * 2,
        out_specs=[act, fixed((8, width))],
        scratch_shapes=[pltpu.VMEM((rows_all, width), F32)],
    )(cot, xhat, inv, ln, ph, plo, uh, ul)


def mixture_grad_stage(me, gm, attended, oh, ol, plan, stream):
    rows_all, width = gm.shape
    rows, lanes = width // plan.dp, width // plan.fsdp

    def body(me_ref, gm_ref, att, oh_ref, ol_ref, gmix, away, keep, full):
        g = split(gm_ref[...])
        gmix[...] = mm3(g, (oh_ref[...], ol_ref[...]), 1, 0)
        full[...] = att[...]
        for core in range(2):
            res = mm3(g, split(half_lanes(full, me_ref[1], core, lanes)), 0, 0)
            mine = away if core else keep
            for d in range(plan.dp):
                for y in range(2):
                    value = res[d * rows : (d + 1) * rows, y * lanes : (y + 1) * lanes]
                    stream.put(mine, d ^ me_ref[0], core + 2 * y, 0, value)

    return call(
        body,
        [((rows_all, width), F32), (stream.shape(), F32), (stream.shape(), F32)],
        [pltpu.VMEM((rows_all, width), F32)],
        compiler_params=ROOM,
        cost_estimate=cost(5),
        in_specs=[SMEM] + [whole()] * 4,
        out_specs=[whole()] * 3,
    )(me, gm, attended, oh, ol)


def packed_grad_stage(dq, dk, dv, g4, g5a, g5b, pool, seqs):
    rows_all, width = dq.shape
    length = rows_all // seqs

    def body(dq_r, dk_r, dv_r, g4_r, g5a_r, g5b_r, pool_r, gph, gpl, column):
        for j, ref in enumerate((dq_r, dk_r, dv_r)):
            total = None
            for s in range(seqs):
                rs = slice(s * length, (s + 1) * length)
                value = ref[rs, :]
                if j:
                    groups = jnp.concatenate(
                        [g4_r[s, j - 1], g5a_r[s, j - 1] + g5b_r[s, j - 1]], axis=0
                    )
                    value = value + mm2(pool_r[...], split(groups), 0, 0)
                part = jnp.sum(value, axis=0, keepdims=True)
                total = part if total is None else total + part
                h = split(value)
                gph[rs, j * width : (j + 1) * width] = h[0]
                gpl[rs, j * width : (j + 1) * width] = h[1]
            column[j * width : (j + 1) * width, :] = jnp.transpose(
                jnp.broadcast_to(total, (128, width))
            )

    return call(
        body,
        [((rows_all, 3 * width), BF16)] * 2 + [((3 * width, 128), F32)],
        compiler_params=ROOM,
        cost_estimate=cost(4.5),
        in_specs=[whole()] * 7,
        out_specs=[whole()] * 3,
    )(dq, dk, dv, g4, g5a, g5b, pool)


def input_grad_stage(gph, gpl, wqh, wql, xhat, inv, ln, gm):
    rows_all, width = gm.shape

    def body(gph_r, gpl_r, wh, wl, xhat_r, inv_r, ln_r, gm_r, gtok):
        e = mm3((gph_r[...], gpl_r[...]), (wh[...], wl[...]), 1, 0)
        gtok[...] = gm_r[...] + norm_back(e, ln_r[0:1, :], xhat_r[...], inv_r[:, 0:1])

    return call(
        body,
        [((rows_all, width), F32)],
        compiler_params=ROOM,
        cost_estimate=cost(7.4),
        in_specs=[whole()] * 8,
        out_specs=[whole()],
    )(gph, gpl, wqh, wql, xhat, inv, ln, gm)[0]


def grad_qkv_stage(me, gph, gpl, column, xhat, ln, wh, wl, plan, stream, core):
    rows_all, triple = gph.shape
    width = triple // 3
    rows, lanes = triple // plan.dp, width // plan.fsdp
    steps = 2
    block = triple // steps

    def body(me_ref, gph_r, gpl_r, col_r, xhat_r, ln_r, wh_r, wl_r, out, sums, nh, nl):
        me_f = me_ref[1]
        step = pl.program_id(0)
        pick = lambda ref: half_lanes(ref, me_f, core, lanes)

        @pl.when(step == 0)
        def _():
            n = split(pick(xhat_r))
            nh[...] = n[0]
            nl[...] = n[1]
            sums[...] = jnp.zeros_like(sums)

        params = pick(ln_r)
        res = mm3((gph_r[...], gpl_r[...]), (nh[...], nl[...]), 0, 0)
        w = pick(wh_r).astype(F32) + pick(wl_r).astype(F32)
        col = col_r[:, 0:1]
        parts = [jnp.sum(res * w, axis=0, keepdims=True), jnp.sum(w * col, axis=0, keepdims=True)]
        for y in range(2):
            at = pl.ds(pl.multiple_of((me_f ^ (core + 2 * y)) * lanes, 128), lanes)
            for i in range(2):
                sums[i : i + 1, at] += parts[i][:, y * lanes : (y + 1) * lanes]
        res = res * params[0:1, :] + col * params[1:2, :]
        for i in range(block // rows):
            jd = me_ref[0] ^ (step * (block // rows) + i)
            for y in range(2):
                value = res[i * rows : (i + 1) * rows, y * lanes : (y + 1) * lanes]
                stream.put(out, jd, core + 2 * y, 0, value)

    fixed = lambda shape: pl.BlockSpec(shape, lambda i: (0,) * len(shape))
    cols = pl.BlockSpec((rows_all, block), lambda i: (0, i))
    down = lambda n: pl.BlockSpec((block, n), lambda i: (i, 0))
    return pl.pallas_call(
        body,
        compiler_params=ROOM,
        cost_estimate=cost(0.25),
        grid=(steps,),
        out_shape=[
            jax.ShapeDtypeStruct(stream.shape(), F32),
            jax.ShapeDtypeStruct((8, width), F32),
        ],
        in_specs=[SMEM, cols, cols, down(128), fixed((rows_all, width)), fixed((8, width))]
        + [down(width)] * 2,
        out_specs=[fixed(stream.shape()), fixed((8, width))],
        scratch_shapes=[pltpu.VMEM((rows_all, 2 * lanes), BF16)] * 2,
    )(me, gph, gpl, column, xhat, ln, wh, wl)


def swap(x, mask, axis="fsdp"):
    size = lax.axis_size(axis)
    return lax.ppermute(x, axis, [(i, i ^ mask) for i in range(size)])


def local(
    tokens, segments, cotangent, ln1_gain, ln1_bias, w_qkv, w_out, ln2_gain, ln2_bias, w_up, w_down
):
    seqs, length, width = tokens.shape
    dp, fsdp = lax.axis_size("dp"), lax.axis_size("fsdp")
    plan = Plan(dp, fsdp)
    me_d = lax.axis_index("dp")
    me = jnp.stack([me_d, lax.axis_index("fsdp")]).astype(jnp.int32)
    rows_all = seqs * length
    hidden_width = w_down.shape[0] * fsdp

    spread, pool, same = pooling(length)
    layout, _ = level_layout(length)
    local_rows = [first for level, first, _ in layout if 2 * NR * (1 << level) > length][0]
    spread_c = jnp.asarray(spread, BF16)
    pool_c = jnp.asarray(pool, BF16)
    same_c = jnp.asarray(same, F32)
    far_pool = jnp.asarray(pool[local_rows : local_rows + (length >> 4) + (length >> 5)], BF16)

    share = width // dp
    norms = jnp.stack([ln1_gain, ln1_bias, ln2_gain, ln2_bias])
    placed = lax.dynamic_update_slice(jnp.zeros((4, width), F32), norms, (0, me_d * share))
    placed = placed.reshape(4, 4, 128).transpose(1, 0, 2).reshape(LN_ROWS, 128)
    rows_qkv, rows_d, rows_up = 3 * share, share, hidden_width // dp
    chunks = hidden_width // fsdp // 128
    down_piece = w_down.T.reshape(rows_d, chunks, 128).transpose(1, 0, 2).reshape(-1, 128)
    down_piece = jnp.concatenate([down_piece, w_out.T], axis=0)
    extra = [(name,) for name in plan.extra]
    qkv_piece = jnp.concatenate([placed, w_qkv.T], axis=0)
    up_piece = w_up.T
    qkv_piece = after(qkv_piece, me)
    qkv_in, down_in, up_in = (Gather(plan, p) for p in (qkv_piece, down_piece, up_piece))
    tok = tokens.reshape(rows_all, width)
    cot = cotangent.reshape(rows_all, width)
    attend = (spread_c, pool_c, same_c)

    near = swap(segments, 1)
    qkv_in.send([("z", "w")])
    for group in extra:
        qkv_in.stage([group])
    gate = qkv_in.came()
    qkv_in.join()
    qkv_in.cut(LN_ROWS + rows_qkv // 16 * 8)
    qkv_in.send([("x",), ("y",)], gate)
    down_in.send([("w",)], gate)
    for group in extra:
        down_in.stage([group])
    far_segments = swap(jnp.stack([segments, after(near, gate)]), 2)
    bias = score_bias(segments, near, far_segments[0], far_segments[1])
    qkv_in.stage([("y",), ("x",)], qkv_in.came())
    gate = (down_in.came(), far_segments)
    down_in.stage([("z",)], gate)
    up_in.send([("w",)], gate)
    for group in extra:
        up_in.stage([group])
    gate = (qkv_in.came(), down_in.came(), up_in.came(), bias)
    cores = qkv_in.share(True, gate) + qkv_in.share(False, gate)
    down_in.join()
    down_in.cut(down_piece.shape[0] // 16 * 8)
    down_in.send([("x",), ("y",)], cores)
    up_in.stage([("z",)], cores)
    packed, wqh, wql, xhat1, inv1, ln, s4, s5 = qkv_stage(
        me, after(tok, cores, bias), qkv_in, plan, far_pool, seqs
    )
    gate = (packed, down_in.came(), up_in.came())
    s4, s5 = after((s4, s5), gate)
    got = [swap(s4, 1), swap(s5, 2), swap(s5, 3)]
    far = jnp.concatenate(got, axis=2)
    down_in.stage([("y",), ("x",)], gate)
    cores = down_in.share(True, far)
    calls = [(s, 1, 0, width // 128) for s in range(seqs)]
    before = ()
    gate = far
    for index, which in enumerate(calls):
        packed_in = after(packed, gate, before)
        before = attention_forward(packed_in, far, bias, *attend, seqs, local_rows, which, before)
        if index == 0:
            gate = (before, down_in.came(), cores)
            cores = down_in.share(False, gate)
            up_in.join()
            up_in.cut(rows_up // 2 // 8 * 8)
            up_in.send([("x",), ("y",)], gate)
    attended, lse = before
    gate = (attended, up_in.came(), cores)
    up_in.stage([("y",), ("x",)], gate)
    dh, dl, oh, ol = projection_stage(after(me, gate), down_in, plan, width, hidden_width)
    cores = up_in.share(True, gate)
    middle, xhat2, inv2 = middle_stage(tok, attended, oh, ol)
    gate = (middle, up_in.came(), cores)
    cores = up_in.share(False, gate)
    hh, hl, ph, plo, uh, ul, nth, ntl, cth, ctl = hidden_stage(
        me, after(xhat2, cores), ln, cot, dh, dl, up_in, plan
    )

    single = [("x", "y"), ("z",), ("w",)] + extra
    double = [("x", "y"), ("z", "w")] + extra
    outer = [("z",), ("x",), ("w",)] + extra + [("y",)]
    down = Stream(plan, chunks * rows_d, outer)
    up = Stream(plan, rows_up, single)
    out = Stream(plan, rows_d, single)
    qkv = Stream(plan, rows_qkv, double)
    down_sum, up_sum, qkv_sum = Reduce(plan, outer), Reduce(plan, single), Reduce(plan, double)

    gm, gln = middle_grad_stage(cot, xhat2, inv2, ln, ph, plo, uh, ul)
    gmix, away_out, keep_out = mixture_grad_stage(me, gm, attended, oh, ol, plan, out)
    away = grad_down_stage(me, after(cth, away_out), ctl, hh, hl, plan, down, 1)
    cores = down_sum.begin(away)
    away = grad_up_stage(me, after(nth, away), ntl, ph, plo, plan, up, 1)
    cores += up_sum.begin(away)
    cores += up_sum.begin(away_out)
    keep = grad_down_stage(me, after(cth, away), ctl, hh, hl, plan, down, 0)
    down_sum.keep(keep)
    keep = grad_up_stage(me, after(nth, keep), ntl, ph, plo, plan, up, 0)
    up_sum.keep(keep)
    up_sum.keep(keep_out)
    sent = (down_sum.send(keep, cores), up_sum.send(keep, cores))
    before = ()
    calls = [(s, 1, 0, width // 128) for s in range(seqs)]
    for which in calls:
        grad = after(gmix, sent, before)
        before = attention_backward(
            packed, far, bias, *attend, attended, lse, grad, seqs, local_rows, which, before
        )
    output = output_stage(after(middle, before), hh, hl, dh, dl)
    gate = (output, down_sum.last, up_sum.last)
    dq, dk, dv, f4, f5a, f5b = before
    f4, f5a, f5b = after((f4, f5a, f5b), gate)
    g4, g5a, g5b = swap(f4, 1), swap(f5a, 2), swap(f5b, 3)
    down_sum.send(gate)
    gph, gpl, column = packed_grad_stage(dq, dk, dv, g4, g5a, g5b, far_pool, seqs)
    away, sums_away = grad_qkv_stage(
        me, gph, gpl, column, xhat1, ln, wqh, wql, plan, qkv, 1
    )
    got = qkv_sum.begin(away)
    keep, sums_keep = grad_qkv_stage(
        me, gph, gpl, column, after(xhat1, away), ln, wqh, wql, plan, qkv, 0
    )
    qkv_sum.keep(keep)
    sums = jnp.concatenate([(sums_away + sums_keep)[0:2], gln[0:2]], axis=0)
    sent = qkv_sum.send(got, rider=sums.reshape(-1, 128))
    down_sum.send(sent)
    up_sum.send(sent)
    gtok = input_grad_stage(gph, gpl, wqh, wql, after(xhat1, sent), inv1, ln, gm)
    rode = qkv_sum.rode
    gate = (up_sum.last, down_sum.last, gtok)
    sent = qkv_sum.send(qkv_sum.last, gate, rider=rode)
    while qkv_sum.stages:
        sent = qkv_sum.send(qkv_sum.last, rider=qkv_sum.rode)
    for total in (down_sum, up_sum):
        while total.stages:
            total.send(gate, sent)
    sums = qkv_sum.rode
    sums = (sums + plan.send(sums, ("c",))).reshape(4, width)
    (g_down,), (g_up, g_out), (g_qkv,) = (t.total() for t in (down_sum, up_sum, qkv_sum))
    mine = lax.dynamic_slice(sums, (0, me_d * share), (4, share))
    if rows_up % 128 == 0:
        g_up = g_up.reshape(-1, width // fsdp, 128).transpose(1, 0, 2).reshape(-1, rows_up)
    else:
        g_up = g_up.T
    g_down = g_down.reshape(chunks, rows_d, 128).transpose(0, 2, 1).reshape(-1, rows_d)
    shape = tokens.shape
    return (
        output.reshape(shape),
        gtok.reshape(shape),
        mine[0],
        mine[1],
        g_qkv.T,
        g_out.T,
        mine[2],
        mine[3],
        g_up,
        g_down,
    )


def solution(mesh):
    weight = P("fsdp", "dp")
    rows = P("dp", "fsdp", None)
    vector = P("dp")
    return jax.shard_map(
        local,
        mesh=mesh,
        in_specs=(rows, P("dp", "fsdp"), rows, vector, vector, weight, weight, vector, vector, weight, weight),
        out_specs=(rows, rows, vector, vector, weight, weight, vector, vector, weight, weight),
        check_vma=False,
    )
```

```python
import jax
import jax.numpy as jnp
import numpy as np
from jax import lax
from jax.experimental import pallas as pl
from jax.experimental.pallas import tpu as pltpu
from jax.sharding import PartitionSpec as P

HEADS = 8
NR = 16
LEVELS = 6
EPSILON = 1e-05
MASKED = -1e30
F32 = jnp.float32
BF16 = jnp.bfloat16
LN_ROWS = 16
TILE = 128
ROOM = pltpu.CompilerParams(vmem_limit_bytes=23 << 20)
SCALE = 0.05


def split(x):
    high = x.astype(BF16)
    return high, (x - high.astype(F32)).astype(BF16)


def mm(a, b, ca, cb):
    return lax.dot_general(a, b, (((ca,), (cb,)), ((), ())), preferred_element_type=F32)


def mm3(a, b, ca, cb):
    return mm(a[0], b[0], ca, cb) + mm(a[0], b[1], ca, cb) + mm(a[1], b[0], ca, cb)


def mm2(a, b, ca, cb):
    return mm(a, b[0], ca, cb) + mm(a, b[1], ca, cb)


def level_layout(length):
    rows, start = [], 0
    for level in range(1, LEVELS):
        count = length >> level
        rows.append((level, start, count))
        start += count
    return rows, start


def pooling(length):
    spread = np.zeros((length, length), np.float32)
    pool = np.zeros((length, length), np.float32)
    same = np.zeros((length, length), np.float32)
    layout, _ = level_layout(length)
    bounds = [first for _, first, _ in layout] + [length]
    for index, (level, first, count) in enumerate(layout):
        token = np.arange(length)
        spread[token, first + (token >> level)] = 1.0
        pool[first + (token >> level), token] = 0.5**level
        same[bounds[index] : bounds[index + 1], bounds[index] : bounds[index + 1]] = 1.0
    return spread, pool, same


def score_bias(seg, near, far_a, far_b):
    count, length = seg.shape
    token = np.arange(length)
    near_pair = (token[:TILE, None] >> 5) == (token[None, :TILE] >> 5)
    tiles = seg.reshape(count, length // TILE, TILE)
    ok = near_pair & (tiles[:, :, :, None] == tiles[:, :, None, :])
    inner = jnp.where(ok, 0.0, MASKED).astype(F32).reshape(count, length, TILE)
    parts = []
    for level in range(1, LEVELS):
        ratio = 1 << level

        def ends(values):
            grouped = values.reshape(count, length // ratio, ratio)
            return grouped[:, :, 0], grouped[:, :, -1]

        low_q, high_q = ends(seg)
        low_q = jnp.repeat(low_q, ratio, axis=1)
        high_q = jnp.repeat(high_q, ratio, axis=1)
        if 2 * NR * ratio <= length:
            low_k, high_k = ends(seg)
            block_q = (token >> level) >> 4
            block_k = np.arange(length >> level) >> 4
            where = (block_q[:, None] ^ 1) == block_k[None, :]
        else:
            if NR * ratio <= length:
                low_k, high_k = ends(near)
            else:
                pieces = [ends(far_a), ends(far_b)]
                low_k = jnp.concatenate([pieces[0][0], pieces[1][0]], axis=1)
                high_k = jnp.concatenate([pieces[0][1], pieces[1][1]], axis=1)
            where = np.ones((length, low_k.shape[1]), bool)
        ok = (
            where[None]
            & (low_q[:, :, None] <= high_k[:, None, :])
            & (low_k[:, None, :] <= high_q[:, :, None])
        )
        parts.append(jnp.where(ok, np.float32(level * np.log(2.0)), MASKED))
    return inner, jnp.concatenate(parts, axis=2).astype(F32)


class Plan:
    def __init__(self, dp, fsdp):
        self.dp, self.fsdp = dp, fsdp
        self.dims = {}
        names = ["x", "z", "w"]
        bit = 1
        while bit < dp:
            name = names[len(self.dims)] if len(self.dims) < 3 else "d%d" % bit
            self.dims[name] = ("dp", bit)
            bit *= 2
        self.extra = list(self.dims)[3:]
        self.dims["y"] = ("fsdp", 2)
        self.dims["c"] = ("fsdp", 1)

    def corner(self, group, v):
        return tuple(name for i, name in enumerate(group) if (v >> i) & 1)

    def mask(self, names):
        d = f = 0
        for name in names:
            axis, bit = self.dims[name]
            if axis == "dp":
                d |= bit
            else:
                f |= bit
        return d, f

    def send(self, x, names):
        d, f = self.mask(names)
        if not f:
            return lax.ppermute(x, "dp", [(i, i ^ d) for i in range(self.dp)])
        if not d:
            return lax.ppermute(x, "fsdp", [(i, i ^ f) for i in range(self.fsdp)])
        n = self.fsdp
        pairs = [(i, ((i // n) ^ d) * n + ((i % n) ^ f)) for i in range(self.dp * n)]
        return lax.ppermute(x, ("dp", "fsdp"), pairs)

    def position(self, stages, d, f):
        pos = 0
        for group in stages:
            for name in reversed(group):
                axis, bit = self.dims[name]
                value = d if axis == "dp" else f
                pos = pos * 2 + ((value // bit) & 1)
        return pos


class Part:
    def __init__(self, start, held, names):
        self.start, self.held, self.names, self.got = start, held, names, []


class Gather:
    def __init__(self, plan, piece):
        self.plan, self.parts = plan, [Part(0, piece[None], [()])]
        self.arrays, self.slots = [], []

    def cut(self, row):
        (part,) = self.parts
        self.parts = [
            Part(0, part.held[:, :row], part.names),
            Part(row, part.held[:, row:], part.names),
        ]

    def send(self, groups, *earlier):
        for part, group in zip(self.parts, groups):
            if earlier:
                part.held = after(part.held, *earlier)
            for v in range(1, 1 << len(group)):
                names = self.plan.corner(group, v)
                part.got.append((self.plan.send(part.held, names), names))

    def came(self):
        return [value for part in self.parts for value, _ in part.got]

    def join(self):
        for part in self.parts:
            names = list(part.names)
            for _, corner in part.got:
                names += [n + corner for n in part.names]
            part.held = jnp.concatenate([part.held] + [v for v, _ in part.got], axis=0)
            part.names, part.got = names, []

    def stage(self, groups, *earlier):
        self.join()
        self.send(groups, *earlier)

    def share(self, held, *earlier):
        sent = []
        for part in self.parts:
            for value, corner in [(part.held, ())] if held else part.got:
                if earlier:
                    value = after(value, *earlier)
                other = self.plan.send(value, ("c",))
                sent.append(other)
                for array, core in ((value, ()), (other, ("c",))):
                    self.arrays.append(array)
                    slots = [self.plan.mask(n + corner + core) for n in part.names]
                    self.slots.append((slots, part.start))
        return sent


def assemble(scratch, refs, gathered, me_d, me_f, rows, lanes, segments):
    for ref, (slots, start) in zip(refs, gathered.slots):
        for slot, (d, f) in enumerate(slots):
            row0 = (me_d ^ d) * rows
            col0 = (me_f ^ f) * lanes
            for source, size, to_lane in segments:
                low, high = max(source, start), min(source + size, start + ref.shape[1])
                if low < high:
                    row = pl.multiple_of(row0 + (low - source), 8)
                    col = pl.multiple_of(col0 + to_lane, 128)
                    scratch[pl.ds(row, high - low), pl.ds(col, 128)] = ref[
                        slot, low - start : high - start, :
                    ]


def norm_rows(refs, gathered):
    total = None
    for ref, (slots, start) in zip(refs, gathered.slots):
        for slot, (d, f) in enumerate(slots):
            if f == 0 and start == 0:
                value = ref[slot, :LN_ROWS, :]
                total = value if total is None else total + value
    return jnp.concatenate([total[4 * i : 4 * i + 4] for i in range(4)], axis=1)


class Stream:
    def __init__(self, plan, rows, stages):
        self.plan, self.rows, self.stages = plan, rows, stages
        self.slots = plan.dp * plan.fsdp // 2

    def shape(self):
        return (self.slots, self.rows, 128)

    def put(self, out, d, f, row, value):
        size = value.shape[0]
        out[self.plan.position(self.stages, d, f), row : row + size, :] = value


class Reduce:
    def __init__(self, plan, stages):
        self.plan, self.stages = plan, list(stages)
        self.kept, self.came, self.last = [], [], []

    def begin(self, part, *earlier):
        part = after(part, *earlier) if earlier else part
        self.last = [self.plan.send(part, ("c",))]
        self.came.append(self.last[0])
        return self.last

    def keep(self, part):
        self.kept.append(part)

    def send(self, *earlier, rider=None):
        if self.kept:
            self.terms = [self.kept, self.came]
            self.slots, self.kept = self.kept[0].shape[0], []
        if earlier:
            self.terms[-1] = after(self.terms[-1], *earlier)
        group = self.stages.pop(0)
        self.slots >>= len(group)
        n = self.slots
        count = range(len(self.terms[0]))
        join = len(count) > 1 or rider is not None
        out = []
        for v in range(0 if join else 1, 1 << len(group)):
            parts = [sum(term[i][v * n : (v + 1) * n] for term in self.terms) for i in count]
            if rider is not None:
                parts.append(jnp.broadcast_to(rider[None], (n,) + rider.shape))
            out.append(parts[0] if len(parts) == 1 else jnp.concatenate(parts, axis=1))
        if join:
            self.terms = [[out.pop(0)]]
        self.last = []
        for v, value in enumerate(out):
            got = self.plan.send(value, self.plan.corner(group, v + 1))
            self.last.append(got)
            self.terms.append([got])
        return out

    def total(self):
        return sum(term[0][0] for term in self.terms)


def after(value, *earlier):
    return lax.optimization_barrier((value, earlier))[0]


def whole(shape=None):
    return pl.BlockSpec(memory_space=pltpu.VMEM)


SMEM = pl.BlockSpec(memory_space=pltpu.SMEM)


def cost(micros):
    return pl.CostEstimate(
        flops=int(micros * SCALE * 9e8), bytes_accessed=int(micros * SCALE * 2.5e6), transcendentals=0
    )


def call(body, outs, scratch=(), **kw):
    return pl.pallas_call(
        body,
        out_shape=[jax.ShapeDtypeStruct(s, t) for s, t in outs],
        scratch_shapes=list(scratch),
        **kw,
    )


def qkv_stage(me, tokens, gathered, plan, pool, seqs):
    rows_all, width = tokens.shape
    length = rows_all // seqs
    n4, n5 = length >> 4, length >> 5
    slots = gathered.arrays
    triple = 3 * width
    rows = triple // plan.dp
    lanes = width // plan.fsdp

    def body(me_ref, tok, pool_ref, *rest):
        refs = rest[: len(slots)]
        packed, wh, wl, xhat, inv, ln, s4, s5, full, nh, nl = rest[len(slots) :]
        step = pl.program_id(0)

        @pl.when(step == 0)
        def _():
            assemble(full, refs, gathered, me_ref[0], me_ref[1], rows, lanes, [(LN_ROWS, rows, 0)])
            params = norm_rows(refs, gathered)
            ln[0:4, :] = params
            x = tok[...]
            centre = x - jnp.mean(x, axis=1, keepdims=True)
            scale = lax.rsqrt(jnp.mean(centre * centre, axis=1, keepdims=True) + EPSILON)
            xh = centre * scale
            xhat[...] = xh
            inv[...] = jnp.broadcast_to(scale, inv.shape)
            n = split(xh * params[0:1, :] + params[1:2, :])
            nh[...] = n[0]
            nl[...] = n[1]

        w = split(full[pl.ds(pl.multiple_of(step * width, width), width), :])
        wh[...] = w[0]
        wl[...] = w[1]
        packed[...] = mm3((nh[...], nl[...]), w, 1, 1)

        @pl.when(step > 0)
        def _():
            for s in range(seqs):
                means = mm2(pool_ref[...], split(packed[s * length : (s + 1) * length, :]), 1, 0)
                s4[s, 0] = means[:n4]
                s5[s, 0] = means[n4 : n4 + n5]

    fixed = lambda shape: pl.BlockSpec(shape, lambda i: (0,) * len(shape))
    later = lambda n: pl.BlockSpec((seqs, 1, n, width), lambda i: (0, jnp.maximum(i - 1, 0), 0, 0))
    outs = [
        ((rows_all, triple), F32, pl.BlockSpec((rows_all, width), lambda i: (0, i))),
        ((triple, width), BF16, pl.BlockSpec((width, width), lambda i: (i, 0))),
        ((triple, width), BF16, pl.BlockSpec((width, width), lambda i: (i, 0))),
        ((rows_all, width), F32, fixed((rows_all, width))),
        ((rows_all, 128), F32, fixed((rows_all, 128))),
        ((8, width), F32, fixed((8, width))),
        ((seqs, 2, n4, width), F32, later(n4)),
        ((seqs, 2, n5, width), F32, later(n5)),
    ]
    return pl.pallas_call(
        body,
        compiler_params=ROOM,
        cost_estimate=cost(7.4),
        grid=(3,),
        out_shape=[jax.ShapeDtypeStruct(shape, kind) for shape, kind, _ in outs],
        in_specs=[SMEM, fixed((rows_all, width)), fixed(pool.shape)]
        + [fixed(x.shape) for x in slots],
        out_specs=[spec for _, _, spec in outs],
        scratch_shapes=[
            pltpu.VMEM((triple, width), F32),
            pltpu.VMEM((rows_all, width), BF16),
            pltpu.VMEM((rows_all, width), BF16),
        ],
    )(me, tokens, pool, *slots)


def lanes2(pair):
    return jnp.concatenate(pair, axis=1)


def fold(r):
    return r[:, :128] + r[:, 128:]


def wide_nt(a, b):
    first = mm(lanes2(a), lanes2((b[0], b[0])), 1, 1)
    return first + mm(a[0], b[1], 1, 1)


def wide_nn(a, b):
    return fold(mm(a[0], lanes2(b), 1, 0)) + mm(a[1], b[0], 1, 0)


def wide_tn(a, b):
    return fold(mm(a[0], lanes2(b), 0, 0)) + mm(a[1], b[0], 0, 0)


def tile_tn(a, b):
    left = jnp.concatenate(a, axis=0)
    right = jnp.concatenate([lanes2(b), lanes2((b[0], jnp.zeros_like(b[0])))], axis=0)
    return fold(mm(left, right, 0, 0))


def rows(pair, t):
    return tuple(x[t * TILE : (t + 1) * TILE] for x in pair)


class Heads:
    def __init__(self, q, k, v, fk, fv, pool, local):
        length = q.shape[0]
        self.tiles = range(length // TILE)
        self.lane = lax.broadcasted_iota(jnp.int32, (length, 128), 1) < 64
        qs, ks, vs = split(q), split(k), split(v)
        pooled = mm(pool, jnp.concatenate([qs[0], ks[0], vs[0], qs[1], ks[1], vs[1]], axis=1), 1, 0)
        pooled = pooled[:, :384] + pooled[:, 384:]
        kc = jnp.concatenate([pooled[:local, 128:256], fk], axis=0)
        vc = jnp.concatenate([pooled[:local, 256:], fv], axis=0)
        self.q, self.qc = qs, split(pooled[:, :128])
        self.k2 = [self.two(rows(ks, t)) for t in self.tiles]
        self.v2 = [self.two(rows(vs, t)) for t in self.tiles]
        self.kc2, self.vc2 = self.two(split(kc)), self.two(split(vc))

    def two(self, pair):
        out = []
        for x in pair:
            lane = self.lane[: x.shape[0]]
            zero = jnp.zeros_like(x)
            both = [jnp.where(lane, x, zero), jnp.where(lane, zero, x)]
            out.append(jnp.concatenate(both, axis=0))
        return tuple(out)

    def one(self, x):
        half = x.shape[0] // 2
        return jnp.where(self.lane[:half], x[:half], x[half:])

    def inner(self, left, right):
        return jnp.concatenate([wide_nt(rows(left, t), right[t]) for t in self.tiles], axis=0)

    def scores(self, spread, same, inner_bias, outer_bias):
        s0 = self.inner(self.q, self.k2) + lanes2((inner_bias, inner_bias))
        high, low = split(wide_nt(self.qc, self.kc2) * lanes2((same, same)))
        st = mm(spread, high, 1, 0) + mm(spread, low, 1, 0)
        return s0, st + lanes2((outer_bias, outer_bias))


def head_columns(x):
    half = x.shape[1] // 2
    return x[:, :half], x[:, half:]


def attention_specs(length, width, first=0, pair=0):
    pairs = width // 128
    block = lambda off: pl.BlockSpec((length, 128), lambda s, h: (first + s, off * pairs + pair + h))
    far = lambda j: pl.BlockSpec((1, 1, 32, 128), lambda s, h: (first + s, j, 0, pair + h))
    fixed = pl.BlockSpec((length, length), lambda s, h: (0, 0))
    bias = lambda n: pl.BlockSpec((1, length, n), lambda s, h: (first + s, 0, 0))
    return block, far, fixed, [bias(TILE), bias(length), fixed, fixed, fixed]


def attention_forward(packed, far, bias, spread, pool, same, seqs, local, which, before):
    rows_all, triple = packed.shape
    width = triple // 3
    length = rows_all // seqs
    first, count, pair, pairs = which
    block, far_spec, fixed, common = attention_specs(length, width, first, pair)
    carried = len(before)

    def body(q, k, v, fk, fv, inner_bias, outer_bias, spread_ref, pool_ref, same_ref, *rest):
        out, lse = rest[carried:]
        heads = Heads(q[...] * 0.125, k[...], v[...], fk[0, 0], fv[0, 0], pool_ref[...], local)
        s0, st = heads.scores(spread_ref[...], same_ref[...], inner_bias[0], outer_bias[0])
        p0, pc, peaks, sums = [], [], [], []
        for a, b in zip(head_columns(s0), head_columns(st)):
            peak = jnp.maximum(jnp.max(a, axis=1, keepdims=True), jnp.max(b, axis=1, keepdims=True))
            a, b = jnp.exp(a - peak), jnp.exp(b - peak)
            p0.append(a)
            pc.append(b)
            peaks.append(peak)
            sums.append(jnp.sum(a, axis=1, keepdims=True) + jnp.sum(b, axis=1, keepdims=True))
        p0, pc = split(lanes2(p0)), split(lanes2(pc))
        mixed = [wide_nn(rows(p0, t), heads.v2[t]) for t in heads.tiles]
        mixed = jnp.concatenate(mixed, axis=0) + wide_nn(pc, heads.vc2)
        total = jnp.where(heads.lane, sums[0], sums[1])
        out[...] = mixed / total
        lse[...] = jnp.where(heads.lane, peaks[0], peaks[1]) + jnp.log(total)

    return pl.pallas_call(
        body,
        compiler_params=ROOM,
        cost_estimate=cost(9.5),
        grid=(count, pairs),
        out_shape=[jax.ShapeDtypeStruct((rows_all, width), F32)] * 2,
        in_specs=[block(0), block(1), block(2), far_spec(0), far_spec(1)]
        + common
        + [pl.BlockSpec(memory_space=pl.ANY)] * carried,
        out_specs=[block(0), block(0)],
        input_output_aliases={10 + i: i for i in range(carried)},
    )(packed, packed, packed, far, far, *bias, spread, pool, same, *before)


def attention_backward(
    packed, far, bias, spread, pool, same, attended, lse, grad, seqs, local, which, before
):
    rows_all, triple = packed.shape
    width = triple // 3
    length = rows_all // seqs
    first, count, pair, pairs = which
    block, far_spec, fixed, common = attention_specs(length, width, first, pair)
    n4, n5 = length >> 4, length >> 5
    carried = len(before)

    def body(q, k, v, fk, fv, inner_bias, outer_bias, spread_ref, pool_ref, same_ref, *rest):
        o_ref, lse_ref, g_ref = rest[:3]
        dq_ref, dk_ref, dv_ref, f4, f5a, f5b = rest[3 + carried :]
        spread_m, pool_m, same_m = spread_ref[...], pool_ref[...], same_ref[...]
        heads = Heads(q[...] * 0.125, k[...], v[...], fk[0, 0], fv[0, 0], pool_m, local)
        lane = heads.lane
        s0, st = heads.scores(spread_m, same_m, inner_bias[0], outer_bias[0])
        logs = lse_ref[...]
        logs = (logs[:, 0:1], logs[:, 64:65])
        p0 = lanes2([jnp.exp(a - x) for a, x in zip(head_columns(s0), logs)])
        pc = lanes2([jnp.exp(a - x) for a, x in zip(head_columns(st), logs)])
        grad_rows = g_ref[...]
        g = split(grad_rows)
        product = grad_rows * o_ref[...]
        zero = jnp.zeros_like(product)
        deltas = [
            jnp.sum(jnp.where(lane, product, zero), axis=1, keepdims=True),
            jnp.sum(jnp.where(lane, zero, product), axis=1, keepdims=True),
        ]
        d0 = heads.inner(g, heads.v2)
        d0 = split(p0 * lanes2([a - x for a, x in zip(head_columns(d0), deltas)]))
        dt = wide_nt(g, heads.vc2)
        dt = split(pc * lanes2([a - x for a, x in zip(head_columns(dt), deltas)]))
        p0, pc = split(p0), split(pc)
        dv = [heads.one(tile_tn(rows(p0, t), rows(g, t))) for t in heads.tiles]
        dk = [heads.one(tile_tn(rows(d0, t), rows(heads.q, t))) for t in heads.tiles]
        dq = [wide_nn(rows(d0, t), heads.k2[t]) for t in heads.tiles]
        dvc = heads.one(wide_tn(pc, g))
        dsc = mm(spread_m, dt[0], 0, 0) + mm(spread_m, dt[1], 0, 0)
        dsc = split(dsc * lanes2((same_m, same_m)))
        dqc = wide_nn(dsc, heads.kc2)
        dkc = heads.one(wide_tn(dsc, heads.qc))
        near = lax.broadcasted_iota(jnp.int32, (length, 128), 0) < local
        high, low = split(
            jnp.concatenate([dqc, jnp.where(near, dkc, zero), jnp.where(near, dvc, zero)], axis=1)
        )
        back = mm(pool_m, lanes2((high, low)), 0, 0)
        back = back[:, :384] + back[:, 384:]
        dq_ref[...] = (jnp.concatenate(dq, axis=0) + back[:, :128]) * 0.125
        dk_ref[...] = jnp.concatenate(dk, axis=0) + back[:, 128:256]
        dv_ref[...] = jnp.concatenate(dv, axis=0) + back[:, 256:]
        for j, value in ((0, dkc), (1, dvc)):
            f4[0, j] = value[local : local + n4]
            f5a[0, j] = value[local + n4 : local + n4 + n5]
            f5b[0, j] = value[local + n4 + n5 :]

    far_out = lambda n: pl.BlockSpec((1, 2, n, 128), lambda s, h: (first + s, 0, 0, pair + h))
    return pl.pallas_call(
        body,
        compiler_params=ROOM,
        cost_estimate=cost(8),
        grid=(count, pairs),
        out_shape=[jax.ShapeDtypeStruct((rows_all, width), F32)] * 3
        + [jax.ShapeDtypeStruct((seqs, 2, n, width), F32) for n in (n4, n5, n5)],
        in_specs=[block(0), block(1), block(2), far_spec(0), far_spec(1)]
        + common
        + [block(0)] * 3
        + [pl.BlockSpec(memory_space=pl.ANY)] * carried,
        out_specs=[block(0)] * 3 + [far_out(n4), far_out(n5), far_out(n5)],
        input_output_aliases={13 + i: i for i in range(carried)},
    )(packed, packed, packed, far, far, *bias, spread, pool, same, attended, lse, grad, *before)


def middle_stage(tokens, attended, wh, wl):
    rows_all, width = tokens.shape

    def body(tok, att, wh_ref, wl_ref, middle, xhat, inv):
        x = tok[...] + mm3(split(att[...]), (wh_ref[...], wl_ref[...]), 1, 1)
        middle[...] = x
        centre = x - jnp.mean(x, axis=1, keepdims=True)
        scale = lax.rsqrt(jnp.mean(centre * centre, axis=1, keepdims=True) + EPSILON)
        xhat[...] = centre * scale
        inv[...] = jnp.broadcast_to(scale, inv.shape)

    return call(
        body,
        [((rows_all, width), F32), ((rows_all, width), F32), ((rows_all, 128), F32)],
        compiler_params=ROOM,
        cost_estimate=cost(4.3),
        in_specs=[whole()] * 4,
        out_specs=[whole()] * 3,
    )(tokens, attended, wh, wl)


def projection_stage(me, gathered, plan, width, hidden_width):
    rows, lanes = width // plan.dp, hidden_width // plan.fsdp
    out_lanes = width // plan.fsdp
    slots = gathered.arrays
    chunks = lanes // 128
    down_parts = [(k * rows, rows, 128 * k) for k in range(chunks)]
    out_parts = [(chunks * rows, rows, 0)]
    chunk = 512

    def body(me_ref, *rest):
        refs = rest[: len(slots)]
        dh, dl, oh, ol, full, full_out = rest[len(slots) :]
        me_d, me_f = me_ref[0], me_ref[1]
        step = pl.program_id(0)

        @pl.when(step == 0)
        def _():
            assemble(full_out, refs, gathered, me_d, me_f, rows, out_lanes, out_parts)
            w = split(full_out[...])
            oh[...] = w[0]
            ol[...] = w[1]
            assemble(full, refs, gathered, me_d, me_f, rows, lanes, down_parts)

        w = split(full[:, pl.ds(pl.multiple_of(step * chunk, chunk), chunk)])
        dh[...] = w[0]
        dl[...] = w[1]

    fixed = lambda shape: pl.BlockSpec(shape, lambda i: (0,) * len(shape))
    cols = pl.BlockSpec((width, chunk), lambda i: (0, i))
    return pl.pallas_call(
        body,
        compiler_params=ROOM,
        cost_estimate=cost(5),
        grid=(hidden_width // chunk,),
        out_shape=[jax.ShapeDtypeStruct((width, hidden_width), BF16)] * 2
        + [jax.ShapeDtypeStruct((width, width), BF16)] * 2,
        in_specs=[SMEM] + [fixed(x.shape) for x in slots],
        out_specs=[cols, cols, fixed((width, width)), fixed((width, width))],
        scratch_shapes=[pltpu.VMEM((width, hidden_width), F32), pltpu.VMEM((width, width), F32)],
    )(me, *slots)


def hidden_stage(me, xhat, ln, cot, dh, dl, gathered, plan):
    rows_all, width = xhat.shape
    hidden_width = dh.shape[1]
    rows, lanes = hidden_width // plan.dp, width // plan.fsdp
    slots = gathered.arrays
    chunk = 512
    steps = hidden_width // chunk
    root = float(np.sqrt(2.0 / np.pi))
    cubic = 0.044715 * root

    def body(me_ref, xhat_ref, ln_ref, cot_ref, d0, d1, *rest):
        refs = rest[: len(slots)]
        hh, hl, ph, plo, wh, wl, nth, ntl, cth, ctl, full, nh, nl, ch, cl = rest[len(slots) :]
        step = pl.program_id(0)

        @pl.when(step == 0)
        def _():
            assemble(full, refs, gathered, me_ref[0], me_ref[1], rows, lanes, [(0, rows, 0)])
            n = xhat_ref[...] * ln_ref[2:3, :] + ln_ref[3:4, :]
            c = cot_ref[...]
            for value, high, low in (
                (n, nh, nl),
                (c, ch, cl),
                (jnp.transpose(n), nth, ntl),
                (jnp.transpose(c), cth, ctl),
            ):
                halves = split(value)
                high[...] = halves[0]
                low[...] = halves[1]

        w = split(full[pl.ds(pl.multiple_of(step * chunk, chunk), chunk), :])
        wh[...] = w[0]
        wl[...] = w[1]
        v = mm3((nh[...], nl[...]), w, 1, 1)
        square = v * v
        half = 0.5 + 0.5 * jnp.tanh(v * (root + cubic * square))
        h = split(v * half)
        hh[...] = h[0]
        hl[...] = h[1]
        slope = half + (half - half * half) * (v * (2.0 * root + 6.0 * cubic * square))
        g = split(mm3((ch[...], cl[...]), (d0[...], d1[...]), 1, 0) * slope)
        ph[...] = g[0]
        plo[...] = g[1]

    fixed = lambda shape: pl.BlockSpec(shape, lambda i: (0,) * len(shape))
    cols = pl.BlockSpec((rows_all, chunk), lambda i: (0, i))
    down = pl.BlockSpec((width, chunk), lambda i: (0, i))
    act = fixed((rows_all, width))
    return pl.pallas_call(
        body,
        compiler_params=ROOM,
        cost_estimate=cost(15),
        grid=(steps,),
        out_shape=[jax.ShapeDtypeStruct((rows_all, hidden_width), BF16)] * 4
        + [jax.ShapeDtypeStruct((hidden_width, width), BF16)] * 2
        + [jax.ShapeDtypeStruct((width, rows_all), BF16)] * 4,
        in_specs=[SMEM, act, fixed((8, width)), act, down, down]
        + [fixed(x.shape) for x in slots],
        out_specs=[cols] * 4
        + [pl.BlockSpec((chunk, width), lambda i: (i, 0))] * 2
        + [fixed((width, rows_all))] * 4,
        scratch_shapes=[pltpu.VMEM((hidden_width, width), F32)]
        + [pltpu.VMEM((rows_all, width), BF16)] * 4,
    )(me, xhat, ln, cot, dh, dl, *slots)


def grad_down_stage(me, cth, ctl, hh, hl, plan, stream, core):
    width, rows_all = cth.shape
    hidden_width = hh.shape[1]
    rows, lanes = width // plan.dp, hidden_width // plan.fsdp

    def body(me_ref, c0, c1, h0, h1, out):
        jf = core + 2 * pl.program_id(0)
        res = mm3((c0[...], c1[...]), (h0[...], h1[...]), 1, 0)
        for d in range(plan.dp):
            jd = me_ref[0] ^ d
            for k in range(lanes // 128):
                value = res[d * rows : (d + 1) * rows, 128 * k : 128 * (k + 1)]
                stream.put(out, jd, jf, k * rows, value)

    cols = pl.BlockSpec((rows_all, lanes), lambda i, m: (0, m[1] ^ (core + 2 * i)))
    grid_spec = pltpu.PrefetchScalarGridSpec(
        num_scalar_prefetch=1,
        grid=(plan.fsdp // 2,),
        in_specs=[pl.BlockSpec((width, rows_all), lambda i, m: (0, 0))] * 2 + [cols, cols],
        out_specs=pl.BlockSpec(stream.shape(), lambda i, m: (0, 0, 0)),
    )
    return pl.pallas_call(
        body,
        compiler_params=ROOM,
        cost_estimate=cost(0.27),
        grid_spec=grid_spec,
        out_shape=jax.ShapeDtypeStruct(stream.shape(), F32),
    )(me, cth, ctl, hh, hl)


def half_lanes(ref, me_f, core, lanes):
    parts = []
    for y in range(2):
        start = pl.multiple_of((me_f ^ (core + 2 * y)) * lanes, 128)
        parts.append(ref[:, pl.ds(start, lanes)])
    return jnp.concatenate(parts, axis=1)


def half_rows(ref, me_f, core, count):
    parts = []
    for y in range(2):
        start = pl.multiple_of((me_f ^ (core + 2 * y)) * count, 128)
        parts.append(ref[pl.ds(start, count), :])
    return jnp.concatenate(parts, axis=0)


def grad_up_stage(me, nth, ntl, ph, plo, plan, stream, core):
    width, rows_all = nth.shape
    hidden_width = ph.shape[1]
    rows, lanes = hidden_width // plan.dp, width // plan.fsdp
    chunk = 512
    steps = hidden_width // chunk
    per = chunk // rows
    natural = rows % 128 == 0

    def body(me_ref, n0, n1, p0, p1, out):
        step = pl.program_id(0)
        n = (half_rows(n0, me_ref[1], core, lanes), half_rows(n1, me_ref[1], core, lanes))
        p = (p0[...], p1[...])
        res = mm3(n, p, 1, 0) if natural else mm3(p, n, 0, 1)
        for i in range(per):
            jd = (step * per + i) ^ me_ref[0]
            for y in range(2):
                if natural:
                    for k in range(rows // 128):
                        at = i * rows + 128 * k
                        value = res[y * lanes : (y + 1) * lanes, at : at + 128]
                        stream.put(out, jd, core + 2 * y, k * lanes, value)
                else:
                    value = res[i * rows : (i + 1) * rows, y * lanes : (y + 1) * lanes]
                    stream.put(out, jd, core + 2 * y, 0, value)

    fixed = lambda shape: pl.BlockSpec(shape, lambda i: (0,) * len(shape))
    cols = pl.BlockSpec((rows_all, chunk), lambda i: (0, i))
    return pl.pallas_call(
        body,
        compiler_params=ROOM,
        cost_estimate=cost(0.32),
        grid=(steps,),
        out_shape=jax.ShapeDtypeStruct(stream.shape(), F32),
        in_specs=[SMEM] + [fixed((width, rows_all))] * 2 + [cols, cols],
        out_specs=fixed(stream.shape()),
    )(me, nth, ntl, ph, plo)


def norm_back(e, gain, xhat, inv):
    u = e * gain
    mean_u = jnp.mean(u, axis=1, keepdims=True)
    mean_ux = jnp.mean(u * xhat, axis=1, keepdims=True)
    return inv * (u - mean_u - xhat * mean_ux)


def output_stage(middle, hh, hl, dh, dl):
    rows_all, width = middle.shape
    chunk = 512
    steps = hh.shape[1] // chunk

    def body(mid, h0, h1, d0, d1, out):
        @pl.when(pl.program_id(0) == 0)
        def _():
            out[...] = mid[...]

        out[...] += mm3((h0[...], h1[...]), (d0[...], d1[...]), 1, 1)

    cols = pl.BlockSpec((rows_all, chunk), lambda i: (0, i))
    act = pl.BlockSpec((rows_all, width), lambda i: (0, 0))
    return pl.pallas_call(
        body,
        compiler_params=ROOM,
        cost_estimate=cost(8),
        grid=(steps,),
        out_shape=jax.ShapeDtypeStruct((rows_all, width), F32),
        in_specs=[act, cols, cols] + [pl.BlockSpec((width, chunk), lambda i: (0, i))] * 2,
        out_specs=act,
    )(middle, hh, hl, dh, dl)


def middle_grad_stage(cot, xhat, inv, ln, ph, plo, uh, ul):
    rows_all, width = cot.shape
    chunk = 512
    steps = ph.shape[1] // chunk

    def body(cot_ref, xhat_ref, inv_ref, ln_ref, p0, p1, u0, u1, gm, gln, acc):
        step = pl.program_id(0)

        @pl.when(step == 0)
        def _():
            acc[...] = jnp.zeros_like(acc)

        acc[...] += mm3((p0[...], p1[...]), (u0[...], u1[...]), 1, 0)

        @pl.when(step == steps - 1)
        def _():
            e = acc[...]
            xh = xhat_ref[...]
            gm[...] = cot_ref[...] + norm_back(e, ln_ref[2:3, :], xh, inv_ref[:, 0:1])
            gln[0:1, :] = jnp.sum(e * xh, axis=0, keepdims=True)
            gln[1:2, :] = jnp.sum(e, axis=0, keepdims=True)

    fixed = lambda shape: pl.BlockSpec(shape, lambda i: (0,) * len(shape))
    cols = pl.BlockSpec((rows_all, chunk), lambda i: (0, i))
    act = fixed((rows_all, width))
    return pl.pallas_call(
        body,
        compiler_params=ROOM,
        cost_estimate=cost(8.5),
        grid=(steps,),
        out_shape=[
            jax.ShapeDtypeStruct((rows_all, width), F32),
            jax.ShapeDtypeStruct((8, width), F32),
        ],
        in_specs=[act, act, fixed((rows_all, 128)), fixed((8, width)), cols, cols]
        + [pl.BlockSpec((chunk, width), lambda i: (i, 0))] * 2,
        out_specs=[act, fixed((8, width))],
        scratch_shapes=[pltpu.VMEM((rows_all, width), F32)],
    )(cot, xhat, inv, ln, ph, plo, uh, ul)


def mixture_grad_stage(me, gm, attended, oh, ol, plan, stream):
    rows_all, width = gm.shape
    rows, lanes = width // plan.dp, width // plan.fsdp

    def body(me_ref, gm_ref, att, oh_ref, ol_ref, gmix, away, keep, full):
        g = split(gm_ref[...])
        gmix[...] = mm3(g, (oh_ref[...], ol_ref[...]), 1, 0)
        full[...] = att[...]
        for core in range(2):
            res = mm3(g, split(half_lanes(full, me_ref[1], core, lanes)), 0, 0)
            mine = away if core else keep
            for d in range(plan.dp):
                for y in range(2):
                    value = res[d * rows : (d + 1) * rows, y * lanes : (y + 1) * lanes]
                    stream.put(mine, d ^ me_ref[0], core + 2 * y, 0, value)

    return call(
        body,
        [((rows_all, width), F32), (stream.shape(), F32), (stream.shape(), F32)],
        [pltpu.VMEM((rows_all, width), F32)],
        compiler_params=ROOM,
        cost_estimate=cost(5),
        in_specs=[SMEM] + [whole()] * 4,
        out_specs=[whole()] * 3,
    )(me, gm, attended, oh, ol)


def packed_grad_stage(dq, dk, dv, g4, g5a, g5b, pool, seqs):
    rows_all, width = dq.shape
    length = rows_all // seqs

    def body(dq_r, dk_r, dv_r, g4_r, g5a_r, g5b_r, pool_r, gph, gpl, column):
        for j, ref in enumerate((dq_r, dk_r, dv_r)):
            total = None
            for s in range(seqs):
                rs = slice(s * length, (s + 1) * length)
                value = ref[rs, :]
                if j:
                    groups = jnp.concatenate(
                        [g4_r[s, j - 1], g5a_r[s, j - 1] + g5b_r[s, j - 1]], axis=0
                    )
                    value = value + mm2(pool_r[...], split(groups), 0, 0)
                part = jnp.sum(value, axis=0, keepdims=True)
                total = part if total is None else total + part
                h = split(value)
                gph[rs, j * width : (j + 1) * width] = h[0]
                gpl[rs, j * width : (j + 1) * width] = h[1]
            column[j * width : (j + 1) * width, :] = jnp.transpose(
                jnp.broadcast_to(total, (128, width))
            )

    return call(
        body,
        [((rows_all, 3 * width), BF16)] * 2 + [((3 * width, 128), F32)],
        compiler_params=ROOM,
        cost_estimate=cost(4.5),
        in_specs=[whole()] * 7,
        out_specs=[whole()] * 3,
    )(dq, dk, dv, g4, g5a, g5b, pool)


def input_grad_stage(gph, gpl, wqh, wql, xhat, inv, ln, gm):
    rows_all, width = gm.shape

    def body(gph_r, gpl_r, wh, wl, xhat_r, inv_r, ln_r, gm_r, gtok):
        e = mm3((gph_r[...], gpl_r[...]), (wh[...], wl[...]), 1, 0)
        gtok[...] = gm_r[...] + norm_back(e, ln_r[0:1, :], xhat_r[...], inv_r[:, 0:1])

    return call(
        body,
        [((rows_all, width), F32)],
        compiler_params=ROOM,
        cost_estimate=cost(7.4),
        in_specs=[whole()] * 8,
        out_specs=[whole()],
    )(gph, gpl, wqh, wql, xhat, inv, ln, gm)[0]


def grad_qkv_stage(me, gph, gpl, column, xhat, ln, wh, wl, plan, stream, core):
    rows_all, triple = gph.shape
    width = triple // 3
    rows, lanes = triple // plan.dp, width // plan.fsdp
    steps = 2
    block = triple // steps

    def body(me_ref, gph_r, gpl_r, col_r, xhat_r, ln_r, wh_r, wl_r, out, sums, nh, nl):
        me_f = me_ref[1]
        step = pl.program_id(0)
        pick = lambda ref: half_lanes(ref, me_f, core, lanes)

        @pl.when(step == 0)
        def _():
            n = split(pick(xhat_r))
            nh[...] = n[0]
            nl[...] = n[1]
            sums[...] = jnp.zeros_like(sums)

        params = pick(ln_r)
        res = mm3((gph_r[...], gpl_r[...]), (nh[...], nl[...]), 0, 0)
        w = pick(wh_r).astype(F32) + pick(wl_r).astype(F32)
        col = col_r[:, 0:1]
        parts = [jnp.sum(res * w, axis=0, keepdims=True), jnp.sum(w * col, axis=0, keepdims=True)]
        for y in range(2):
            at = pl.ds(pl.multiple_of((me_f ^ (core + 2 * y)) * lanes, 128), lanes)
            for i in range(2):
                sums[i : i + 1, at] += parts[i][:, y * lanes : (y + 1) * lanes]
        res = res * params[0:1, :] + col * params[1:2, :]
        for i in range(block // rows):
            jd = me_ref[0] ^ (step * (block // rows) + i)
            for y in range(2):
                value = res[i * rows : (i + 1) * rows, y * lanes : (y + 1) * lanes]
                stream.put(out, jd, core + 2 * y, 0, value)

    fixed = lambda shape: pl.BlockSpec(shape, lambda i: (0,) * len(shape))
    cols = pl.BlockSpec((rows_all, block), lambda i: (0, i))
    down = lambda n: pl.BlockSpec((block, n), lambda i: (i, 0))
    return pl.pallas_call(
        body,
        compiler_params=ROOM,
        cost_estimate=cost(0.25),
        grid=(steps,),
        out_shape=[
            jax.ShapeDtypeStruct(stream.shape(), F32),
            jax.ShapeDtypeStruct((8, width), F32),
        ],
        in_specs=[SMEM, cols, cols, down(128), fixed((rows_all, width)), fixed((8, width))]
        + [down(width)] * 2,
        out_specs=[fixed(stream.shape()), fixed((8, width))],
        scratch_shapes=[pltpu.VMEM((rows_all, 2 * lanes), BF16)] * 2,
    )(me, gph, gpl, column, xhat, ln, wh, wl)


def swap(x, mask, axis="fsdp"):
    size = lax.axis_size(axis)
    return lax.ppermute(x, axis, [(i, i ^ mask) for i in range(size)])


def local(
    tokens, segments, cotangent, ln1_gain, ln1_bias, w_qkv, w_out, ln2_gain, ln2_bias, w_up, w_down
):
    seqs, length, width = tokens.shape
    dp, fsdp = lax.axis_size("dp"), lax.axis_size("fsdp")
    plan = Plan(dp, fsdp)
    me_d = lax.axis_index("dp")
    me = jnp.stack([me_d, lax.axis_index("fsdp")]).astype(jnp.int32)
    rows_all = seqs * length
    hidden_width = w_down.shape[0] * fsdp

    spread, pool, same = pooling(length)
    layout, _ = level_layout(length)
    local_rows = [first for level, first, _ in layout if 2 * NR * (1 << level) > length][0]
    spread_c = jnp.asarray(spread, BF16)
    pool_c = jnp.asarray(pool, BF16)
    same_c = jnp.asarray(same, F32)
    far_pool = jnp.asarray(pool[local_rows : local_rows + (length >> 4) + (length >> 5)], BF16)

    share = width // dp
    norms = jnp.stack([ln1_gain, ln1_bias, ln2_gain, ln2_bias])
    placed = lax.dynamic_update_slice(jnp.zeros((4, width), F32), norms, (0, me_d * share))
    placed = placed.reshape(4, 4, 128).transpose(1, 0, 2).reshape(LN_ROWS, 128)
    rows_qkv, rows_d, rows_up = 3 * share, share, hidden_width // dp
    chunks = hidden_width // fsdp // 128
    down_piece = w_down.T.reshape(rows_d, chunks, 128).transpose(1, 0, 2).reshape(-1, 128)
    down_piece = jnp.concatenate([down_piece, w_out.T], axis=0)
    extra = [(name,) for name in plan.extra]
    qkv_piece = jnp.concatenate([placed, w_qkv.T], axis=0)
    up_piece = w_up.T
    qkv_piece = after(qkv_piece, me)
    qkv_in, down_in, up_in = (Gather(plan, p) for p in (qkv_piece, down_piece, up_piece))
    tok = tokens.reshape(rows_all, width)
    cot = cotangent.reshape(rows_all, width)
    attend = (spread_c, pool_c, same_c)

    near = swap(segments, 1)
    qkv_in.send([("z", "w")])
    for group in extra:
        qkv_in.stage([group])
    gate = qkv_in.came()
    qkv_in.join()
    qkv_in.cut(LN_ROWS + rows_qkv // 16 * 8)
    qkv_in.send([("x",), ("y",)], gate)
    down_in.send([("w",)], gate)
    for group in extra:
        down_in.stage([group])
    far_segments = swap(jnp.stack([segments, after(near, gate)]), 2)
    bias = score_bias(segments, near, far_segments[0], far_segments[1])
    qkv_in.stage([("y",), ("x",)], qkv_in.came())
    gate = (down_in.came(), far_segments)
    down_in.stage([("z",)], gate)
    up_in.send([("w",)], gate)
    for group in extra:
        up_in.stage([group])
    gate = (qkv_in.came(), down_in.came(), up_in.came(), bias)
    cores = qkv_in.share(True, gate) + qkv_in.share(False, gate)
    down_in.join()
    down_in.cut(down_piece.shape[0] // 16 * 8)
    down_in.send([("x",), ("y",)], cores)
    up_in.stage([("z",)], cores)
    packed, wqh, wql, xhat1, inv1, ln, s4, s5 = qkv_stage(
        me, after(tok, cores, bias), qkv_in, plan, far_pool, seqs
    )
    gate = (packed, down_in.came(), up_in.came())
    s4, s5 = after((s4, s5), gate)
    got = [swap(s4, 1), swap(s5, 2), swap(s5, 3)]
    far = jnp.concatenate(got, axis=2)
    down_in.stage([("y",), ("x",)], gate)
    cores = down_in.share(True, far)
    calls = [(s, 1, 0, width // 128) for s in range(seqs)]
    before = ()
    gate = far
    for index, which in enumerate(calls):
        packed_in = after(packed, gate, before)
        before = attention_forward(packed_in, far, bias, *attend, seqs, local_rows, which, before)
        if index == 0:
            gate = (before, down_in.came(), cores)
            cores = down_in.share(False, gate)
            up_in.join()
            up_in.cut(rows_up // 2 // 8 * 8)
            up_in.send([("x",), ("y",)], gate)
    attended, lse = before
    gate = (attended, up_in.came(), cores)
    up_in.stage([("y",), ("x",)], gate)
    dh, dl, oh, ol = projection_stage(after(me, gate), down_in, plan, width, hidden_width)
    cores = up_in.share(True, gate)
    middle, xhat2, inv2 = middle_stage(tok, attended, oh, ol)
    gate = (middle, up_in.came(), cores)
    cores = up_in.share(False, gate)
    hh, hl, ph, plo, uh, ul, nth, ntl, cth, ctl = hidden_stage(
        me, after(xhat2, cores), ln, cot, dh, dl, up_in, plan
    )

    single = [("x", "y"), ("z",), ("w",)] + extra
    double = [("x", "y"), ("z", "w")] + extra
    outer = [("z",), ("x",), ("w",)] + extra + [("y",)]
    down = Stream(plan, chunks * rows_d, outer)
    up = Stream(plan, rows_up, single)
    out = Stream(plan, rows_d, single)
    qkv = Stream(plan, rows_qkv, double)
    down_sum, up_sum, qkv_sum = Reduce(plan, outer), Reduce(plan, single), Reduce(plan, double)

    gm, gln = middle_grad_stage(cot, xhat2, inv2, ln, ph, plo, uh, ul)
    gmix, away_out, keep_out = mixture_grad_stage(me, gm, attended, oh, ol, plan, out)
    away = grad_down_stage(me, after(cth, away_out), ctl, hh, hl, plan, down, 1)
    cores = down_sum.begin(away)
    away = grad_up_stage(me, after(nth, away), ntl, ph, plo, plan, up, 1)
    cores += up_sum.begin(away)
    cores += up_sum.begin(away_out)
    keep = grad_down_stage(me, after(cth, away), ctl, hh, hl, plan, down, 0)
    down_sum.keep(keep)
    keep = grad_up_stage(me, after(nth, keep), ntl, ph, plo, plan, up, 0)
    up_sum.keep(keep)
    up_sum.keep(keep_out)
    sent = (down_sum.send(keep, cores), up_sum.send(keep, cores))
    before = ()
    calls = [(s, 1, 0, width // 128) for s in range(seqs)]
    for which in calls:
        grad = after(gmix, sent, before)
        before = attention_backward(
            packed, far, bias, *attend, attended, lse, grad, seqs, local_rows, which, before
        )
    output = output_stage(after(middle, before), hh, hl, dh, dl)
    gate = (output, down_sum.last, up_sum.last)
    dq, dk, dv, f4, f5a, f5b = before
    f4, f5a, f5b = after((f4, f5a, f5b), gate)
    g4, g5a, g5b = swap(f4, 1), swap(f5a, 2), swap(f5b, 3)
    down_sum.send(gate)
    gph, gpl, column = packed_grad_stage(dq, dk, dv, g4, g5a, g5b, far_pool, seqs)
    away, sums_away = grad_qkv_stage(
        me, gph, gpl, column, xhat1, ln, wqh, wql, plan, qkv, 1
    )
    got = qkv_sum.begin(away)
    keep, sums_keep = grad_qkv_stage(
        me, gph, gpl, column, after(xhat1, away), ln, wqh, wql, plan, qkv, 0
    )
    qkv_sum.keep(keep)
    sums = jnp.concatenate([(sums_away + sums_keep)[0:2], gln[0:2]], axis=0)
    sent = qkv_sum.send(got, rider=sums.reshape(-1, 128))
    down_sum.send(sent)
    up_sum.send(sent)
    gtok = input_grad_stage(gph, gpl, wqh, wql, after(xhat1, sent), inv1, ln, gm)
    gate = (up_sum.last, down_sum.last, gtok)
    sent = qkv_sum.send(qkv_sum.last, gate)
    while qkv_sum.stages:
        sent = qkv_sum.send(qkv_sum.last)
    for total in (down_sum, up_sum):
        while total.stages:
            total.send(gate, sent)
    g_down, g_up = down_sum.total(), up_sum.total()
    g_up, g_out = g_up[:rows_up], g_up[rows_up:]
    if rows_up % 128 == 0:
        g_up = g_up.reshape(-1, width // fsdp, 128).transpose(1, 0, 2).reshape(-1, rows_up)
    else:
        g_up = g_up.T
    g_down = g_down.reshape(chunks, rows_d, 128).transpose(0, 2, 1).reshape(-1, rows_d)
    g_out = g_out.T
    qkv_sum.terms[-1] = after(qkv_sum.terms[-1], g_down, g_up, g_out)
    g_qkv = qkv_sum.total()
    g_qkv, sums = g_qkv[:rows_qkv], g_qkv[rows_qkv:]
    sums = (sums + plan.send(sums, ("c",))).reshape(4, width)
    mine = lax.dynamic_slice(sums, (0, me_d * share), (4, share))
    shape = tokens.shape
    return (
        output.reshape(shape),
        gtok.reshape(shape),
        mine[0],
        mine[1],
        g_qkv.T,
        g_out,
        mine[2],
        mine[3],
        g_up,
        g_down,
    )


def solution(mesh):
    weight = P("fsdp", "dp")
    rows = P("dp", "fsdp", None)
    vector = P("dp")
    return jax.shard_map(
        local,
        mesh=mesh,
        in_specs=(rows, P("dp", "fsdp"), rows, vector, vector, weight, weight, vector, vector, weight, weight),
        out_specs=(rows, rows, vector, vector, weight, weight, vector, vector, weight, weight),
        check_vma=False,
    )
```

```python
import jax
import jax.numpy as jnp
import numpy as np
from jax import lax
from jax.experimental import pallas as pl
from jax.experimental.pallas import tpu as pltpu
from jax.sharding import PartitionSpec as P

HEADS = 8
NR = 16
LEVELS = 6
EPSILON = 1e-05
MASKED = -1e30
F32 = jnp.float32
BF16 = jnp.bfloat16
LN_ROWS = 16
TILE = 128
ROOM = pltpu.CompilerParams(vmem_limit_bytes=23 << 20)
SCALE = 0.05


def split(x):
    high = x.astype(BF16)
    return high, (x - high.astype(F32)).astype(BF16)


def mm(a, b, ca, cb):
    return lax.dot_general(a, b, (((ca,), (cb,)), ((), ())), preferred_element_type=F32)


def mm3(a, b, ca, cb):
    return mm(a[0], b[0], ca, cb) + mm(a[0], b[1], ca, cb) + mm(a[1], b[0], ca, cb)


def mm2(a, b, ca, cb):
    return mm(a, b[0], ca, cb) + mm(a, b[1], ca, cb)


def level_layout(length):
    rows, start = [], 0
    for level in range(1, LEVELS):
        count = length >> level
        rows.append((level, start, count))
        start += count
    return rows, start


def pooling(length):
    spread = np.zeros((length, length), np.float32)
    pool = np.zeros((length, length), np.float32)
    same = np.zeros((length, length), np.float32)
    layout, _ = level_layout(length)
    bounds = [first for _, first, _ in layout] + [length]
    for index, (level, first, count) in enumerate(layout):
        token = np.arange(length)
        spread[token, first + (token >> level)] = 1.0
        pool[first + (token >> level), token] = 0.5**level
        same[bounds[index] : bounds[index + 1], bounds[index] : bounds[index + 1]] = 1.0
    return spread, pool, same


def score_bias(seg, near, far_a, far_b):
    count, length = seg.shape
    token = np.arange(length)
    near_pair = (token[:TILE, None] >> 5) == (token[None, :TILE] >> 5)
    tiles = seg.reshape(count, length // TILE, TILE)
    ok = near_pair & (tiles[:, :, :, None] == tiles[:, :, None, :])
    inner = jnp.where(ok, 0.0, MASKED).astype(F32).reshape(count, length, TILE)
    parts = []
    for level in range(1, LEVELS):
        ratio = 1 << level

        def ends(values):
            grouped = values.reshape(count, length // ratio, ratio)
            return grouped[:, :, 0], grouped[:, :, -1]

        low_q, high_q = ends(seg)
        low_q = jnp.repeat(low_q, ratio, axis=1)
        high_q = jnp.repeat(high_q, ratio, axis=1)
        if 2 * NR * ratio <= length:
            low_k, high_k = ends(seg)
            block_q = (token >> level) >> 4
            block_k = np.arange(length >> level) >> 4
            where = (block_q[:, None] ^ 1) == block_k[None, :]
        else:
            if NR * ratio <= length:
                low_k, high_k = ends(near)
            else:
                pieces = [ends(far_a), ends(far_b)]
                low_k = jnp.concatenate([pieces[0][0], pieces[1][0]], axis=1)
                high_k = jnp.concatenate([pieces[0][1], pieces[1][1]], axis=1)
            where = np.ones((length, low_k.shape[1]), bool)
        ok = (
            where[None]
            & (low_q[:, :, None] <= high_k[:, None, :])
            & (low_k[:, None, :] <= high_q[:, :, None])
        )
        parts.append(jnp.where(ok, np.float32(level * np.log(2.0)), MASKED))
    return inner, jnp.concatenate(parts, axis=2).astype(F32)


class Plan:
    def __init__(self, dp, fsdp):
        self.dp, self.fsdp = dp, fsdp
        self.dims = {}
        names = ["x", "z", "w"]
        bit = 1
        while bit < dp:
            name = names[len(self.dims)] if len(self.dims) < 3 else "d%d" % bit
            self.dims[name] = ("dp", bit)
            bit *= 2
        self.extra = list(self.dims)[3:]
        self.dims["y"] = ("fsdp", 2)
        self.dims["c"] = ("fsdp", 1)

    def corner(self, group, v):
        return tuple(name for i, name in enumerate(group) if (v >> i) & 1)

    def mask(self, names):
        d = f = 0
        for name in names:
            axis, bit = self.dims[name]
            if axis == "dp":
                d |= bit
            else:
                f |= bit
        return d, f

    def send(self, x, names):
        d, f = self.mask(names)
        if not f:
            return lax.ppermute(x, "dp", [(i, i ^ d) for i in range(self.dp)])
        if not d:
            return lax.ppermute(x, "fsdp", [(i, i ^ f) for i in range(self.fsdp)])
        n = self.fsdp
        pairs = [(i, ((i // n) ^ d) * n + ((i % n) ^ f)) for i in range(self.dp * n)]
        return lax.ppermute(x, ("dp", "fsdp"), pairs)

    def position(self, stages, d, f):
        pos = 0
        for group in stages:
            for name in reversed(group):
                axis, bit = self.dims[name]
                value = d if axis == "dp" else f
                pos = pos * 2 + ((value // bit) & 1)
        return pos


class Part:
    def __init__(self, start, held, names):
        self.start, self.held, self.names, self.got = start, held, names, []


class Gather:
    def __init__(self, plan, piece):
        self.plan, self.parts = plan, [Part(0, piece[None], [()])]
        self.arrays, self.slots = [], []

    def cut(self, row):
        (part,) = self.parts
        self.parts = [
            Part(0, part.held[:, :row], part.names),
            Part(row, part.held[:, row:], part.names),
        ]

    def send(self, groups, *earlier):
        for part, group in zip(self.parts, groups):
            if earlier:
                part.held = after(part.held, *earlier)
            for v in range(1, 1 << len(group)):
                names = self.plan.corner(group, v)
                part.got.append((self.plan.send(part.held, names), names))

    def came(self):
        return [value for part in self.parts for value, _ in part.got]

    def join(self):
        for part in self.parts:
            names = list(part.names)
            for _, corner in part.got:
                names += [n + corner for n in part.names]
            part.held = jnp.concatenate([part.held] + [v for v, _ in part.got], axis=0)
            part.names, part.got = names, []

    def stage(self, groups, *earlier):
        self.join()
        self.send(groups, *earlier)

    def share(self, held, *earlier):
        sent = []
        for part in self.parts:
            for value, corner in [(part.held, ())] if held else part.got:
                if earlier:
                    value = after(value, *earlier)
                other = self.plan.send(value, ("c",))
                sent.append(other)
                for array, core in ((value, ()), (other, ("c",))):
                    self.arrays.append(array)
                    slots = [self.plan.mask(n + corner + core) for n in part.names]
                    self.slots.append((slots, part.start))
        return sent


def assemble(scratch, refs, gathered, me_d, me_f, rows, lanes, segments):
    for ref, (slots, start) in zip(refs, gathered.slots):
        for slot, (d, f) in enumerate(slots):
            row0 = (me_d ^ d) * rows
            col0 = (me_f ^ f) * lanes
            for source, size, to_lane in segments:
                low, high = max(source, start), min(source + size, start + ref.shape[1])
                if low < high:
                    row = pl.multiple_of(row0 + (low - source), 8)
                    col = pl.multiple_of(col0 + to_lane, 128)
                    scratch[pl.ds(row, high - low), pl.ds(col, 128)] = ref[
                        slot, low - start : high - start, :
                    ]


def norm_rows(refs, gathered):
    total = None
    for ref, (slots, start) in zip(refs, gathered.slots):
        for slot, (d, f) in enumerate(slots):
            if f == 0 and start == 0:
                value = ref[slot, :LN_ROWS, :]
                total = value if total is None else total + value
    return jnp.concatenate([total[4 * i : 4 * i + 4] for i in range(4)], axis=1)


class Stream:
    def __init__(self, plan, rows, stages):
        self.plan, self.rows, self.stages = plan, rows, stages
        self.slots = plan.dp * plan.fsdp // 2

    def shape(self):
        return (self.slots, self.rows, 128)

    def put(self, out, d, f, row, value):
        size = value.shape[0]
        out[self.plan.position(self.stages, d, f), row : row + size, :] = value


class Reduce:
    def __init__(self, plan, stages):
        self.plan, self.stages = plan, list(stages)
        self.kept, self.came, self.last = [], [], []

    def begin(self, part, *earlier):
        part = after(part, *earlier) if earlier else part
        self.last = [self.plan.send(part, ("c",))]
        self.came.append(self.last[0])
        return self.last

    def keep(self, part):
        self.kept.append(part)

    def send(self, *earlier, rider=None):
        if self.kept:
            self.terms = [self.kept, self.came]
            self.slots, self.kept = self.kept[0].shape[0], []
        if earlier:
            self.terms[-1] = after(self.terms[-1], *earlier)
        group = self.stages.pop(0)
        self.slots >>= len(group)
        n = self.slots
        count = range(len(self.terms[0]))
        join = len(count) > 1 or rider is not None
        out = []
        for v in range(0 if join else 1, 1 << len(group)):
            parts = [sum(term[i][v * n : (v + 1) * n] for term in self.terms) for i in count]
            if rider is not None:
                parts.append(jnp.broadcast_to(rider[None], (n,) + rider.shape))
            out.append(parts[0] if len(parts) == 1 else jnp.concatenate(parts, axis=1))
        if join:
            self.terms = [[out.pop(0)]]
        self.last = []
        for v, value in enumerate(out):
            got = self.plan.send(value, self.plan.corner(group, v + 1))
            self.last.append(got)
            self.terms.append([got])
        return out

    def absorb(self, other, *earlier):
        n = self.slots
        other.terms[-1] = after(other.terms[-1], *earlier)
        parts = [sum(term[0][0:n] for term in x.terms) for x in (self, other)]
        self.terms = [[jnp.concatenate(parts, axis=1)]]

    def total(self):
        return sum(term[0][0] for term in self.terms)


def after(value, *earlier):
    return lax.optimization_barrier((value, earlier))[0]


def whole(shape=None):
    return pl.BlockSpec(memory_space=pltpu.VMEM)


SMEM = pl.BlockSpec(memory_space=pltpu.SMEM)


def cost(micros):
    return pl.CostEstimate(
        flops=int(micros * SCALE * 9e8), bytes_accessed=int(micros * SCALE * 2.5e6), transcendentals=0
    )


def call(body, outs, scratch=(), **kw):
    return pl.pallas_call(
        body,
        out_shape=[jax.ShapeDtypeStruct(s, t) for s, t in outs],
        scratch_shapes=list(scratch),
        **kw,
    )


def qkv_stage(me, tokens, gathered, plan, pool, seqs):
    rows_all, width = tokens.shape
    length = rows_all // seqs
    n4, n5 = length >> 4, length >> 5
    slots = gathered.arrays
    triple = 3 * width
    rows = triple // plan.dp
    lanes = width // plan.fsdp

    def body(me_ref, tok, pool_ref, *rest):
        refs = rest[: len(slots)]
        packed, wh, wl, xhat, inv, ln, s4, s5, full, nh, nl = rest[len(slots) :]
        step = pl.program_id(0)

        @pl.when(step == 0)
        def _():
            assemble(full, refs, gathered, me_ref[0], me_ref[1], rows, lanes, [(LN_ROWS, rows, 0)])
            params = norm_rows(refs, gathered)
            ln[0:4, :] = params
            x = tok[...]
            centre = x - jnp.mean(x, axis=1, keepdims=True)
            scale = lax.rsqrt(jnp.mean(centre * centre, axis=1, keepdims=True) + EPSILON)
            xh = centre * scale
            xhat[...] = xh
            inv[...] = jnp.broadcast_to(scale, inv.shape)
            n = split(xh * params[0:1, :] + params[1:2, :])
            nh[...] = n[0]
            nl[...] = n[1]

        w = split(full[pl.ds(pl.multiple_of(step * width, width), width), :])
        wh[...] = w[0]
        wl[...] = w[1]
        packed[...] = mm3((nh[...], nl[...]), w, 1, 1)

        @pl.when(step > 0)
        def _():
            for s in range(seqs):
                means = mm2(pool_ref[...], split(packed[s * length : (s + 1) * length, :]), 1, 0)
                s4[s, 0] = means[:n4]
                s5[s, 0] = means[n4 : n4 + n5]

    fixed = lambda shape: pl.BlockSpec(shape, lambda i: (0,) * len(shape))
    later = lambda n: pl.BlockSpec((seqs, 1, n, width), lambda i: (0, jnp.maximum(i - 1, 0), 0, 0))
    outs = [
        ((rows_all, triple), F32, pl.BlockSpec((rows_all, width), lambda i: (0, i))),
        ((triple, width), BF16, pl.BlockSpec((width, width), lambda i: (i, 0))),
        ((triple, width), BF16, pl.BlockSpec((width, width), lambda i: (i, 0))),
        ((rows_all, width), F32, fixed((rows_all, width))),
        ((rows_all, 128), F32, fixed((rows_all, 128))),
        ((8, width), F32, fixed((8, width))),
        ((seqs, 2, n4, width), F32, later(n4)),
        ((seqs, 2, n5, width), F32, later(n5)),
    ]
    return pl.pallas_call(
        body,
        compiler_params=ROOM,
        cost_estimate=cost(7.4),
        grid=(3,),
        out_shape=[jax.ShapeDtypeStruct(shape, kind) for shape, kind, _ in outs],
        in_specs=[SMEM, fixed((rows_all, width)), fixed(pool.shape)]
        + [fixed(x.shape) for x in slots],
        out_specs=[spec for _, _, spec in outs],
        scratch_shapes=[
            pltpu.VMEM((triple, width), F32),
            pltpu.VMEM((rows_all, width), BF16),
            pltpu.VMEM((rows_all, width), BF16),
        ],
    )(me, tokens, pool, *slots)


def lanes2(pair):
    return jnp.concatenate(pair, axis=1)


def fold(r):
    return r[:, :128] + r[:, 128:]


def wide_nt(a, b):
    first = mm(lanes2(a), lanes2((b[0], b[0])), 1, 1)
    return first + mm(a[0], b[1], 1, 1)


def wide_nn(a, b):
    return fold(mm(a[0], lanes2(b), 1, 0)) + mm(a[1], b[0], 1, 0)


def wide_tn(a, b):
    return fold(mm(a[0], lanes2(b), 0, 0)) + mm(a[1], b[0], 0, 0)


def tile_tn(a, b):
    left = jnp.concatenate(a, axis=0)
    right = jnp.concatenate([lanes2(b), lanes2((b[0], jnp.zeros_like(b[0])))], axis=0)
    return fold(mm(left, right, 0, 0))


def rows(pair, t):
    return tuple(x[t * TILE : (t + 1) * TILE] for x in pair)


class Heads:
    def __init__(self, q, k, v, fk, fv, pool, local):
        length = q.shape[0]
        self.tiles = range(length // TILE)
        self.lane = lax.broadcasted_iota(jnp.int32, (length, 128), 1) < 64
        qs, ks, vs = split(q), split(k), split(v)
        pooled = mm(pool, jnp.concatenate([qs[0], ks[0], vs[0], qs[1], ks[1], vs[1]], axis=1), 1, 0)
        pooled = pooled[:, :384] + pooled[:, 384:]
        kc = jnp.concatenate([pooled[:local, 128:256], fk], axis=0)
        vc = jnp.concatenate([pooled[:local, 256:], fv], axis=0)
        self.q, self.qc = qs, split(pooled[:, :128])
        self.k2 = [self.two(rows(ks, t)) for t in self.tiles]
        self.v2 = [self.two(rows(vs, t)) for t in self.tiles]
        self.kc2, self.vc2 = self.two(split(kc)), self.two(split(vc))

    def two(self, pair):
        out = []
        for x in pair:
            lane = self.lane[: x.shape[0]]
            zero = jnp.zeros_like(x)
            both = [jnp.where(lane, x, zero), jnp.where(lane, zero, x)]
            out.append(jnp.concatenate(both, axis=0))
        return tuple(out)

    def one(self, x):
        half = x.shape[0] // 2
        return jnp.where(self.lane[:half], x[:half], x[half:])

    def inner(self, left, right):
        return jnp.concatenate([wide_nt(rows(left, t), right[t]) for t in self.tiles], axis=0)

    def scores(self, spread, same, inner_bias, outer_bias):
        s0 = self.inner(self.q, self.k2) + lanes2((inner_bias, inner_bias))
        high, low = split(wide_nt(self.qc, self.kc2) * lanes2((same, same)))
        st = mm(spread, high, 1, 0) + mm(spread, low, 1, 0)
        return s0, st + lanes2((outer_bias, outer_bias))


def head_columns(x):
    half = x.shape[1] // 2
    return x[:, :half], x[:, half:]


def attention_specs(length, width, first=0, pair=0):
    pairs = width // 128
    block = lambda off: pl.BlockSpec((length, 128), lambda s, h: (first + s, off * pairs + pair + h))
    far = lambda j: pl.BlockSpec((1, 1, 32, 128), lambda s, h: (first + s, j, 0, pair + h))
    fixed = pl.BlockSpec((length, length), lambda s, h: (0, 0))
    bias = lambda n: pl.BlockSpec((1, length, n), lambda s, h: (first + s, 0, 0))
    return block, far, fixed, [bias(TILE), bias(length), fixed, fixed, fixed]


def attention_forward(packed, far, bias, spread, pool, same, seqs, local, which, before):
    rows_all, triple = packed.shape
    width = triple // 3
    length = rows_all // seqs
    first, count, pair, pairs = which
    block, far_spec, fixed, common = attention_specs(length, width, first, pair)
    carried = len(before)

    def body(q, k, v, fk, fv, inner_bias, outer_bias, spread_ref, pool_ref, same_ref, *rest):
        out, lse = rest[carried:]
        heads = Heads(q[...] * 0.125, k[...], v[...], fk[0, 0], fv[0, 0], pool_ref[...], local)
        s0, st = heads.scores(spread_ref[...], same_ref[...], inner_bias[0], outer_bias[0])
        p0, pc, peaks, sums = [], [], [], []
        for a, b in zip(head_columns(s0), head_columns(st)):
            peak = jnp.maximum(jnp.max(a, axis=1, keepdims=True), jnp.max(b, axis=1, keepdims=True))
            a, b = jnp.exp(a - peak), jnp.exp(b - peak)
            p0.append(a)
            pc.append(b)
            peaks.append(peak)
            sums.append(jnp.sum(a, axis=1, keepdims=True) + jnp.sum(b, axis=1, keepdims=True))
        p0, pc = split(lanes2(p0)), split(lanes2(pc))
        mixed = [wide_nn(rows(p0, t), heads.v2[t]) for t in heads.tiles]
        mixed = jnp.concatenate(mixed, axis=0) + wide_nn(pc, heads.vc2)
        total = jnp.where(heads.lane, sums[0], sums[1])
        out[...] = mixed / total
        lse[...] = jnp.where(heads.lane, peaks[0], peaks[1]) + jnp.log(total)

    return pl.pallas_call(
        body,
        compiler_params=ROOM,
        cost_estimate=cost(9.5),
        grid=(count, pairs),
        out_shape=[jax.ShapeDtypeStruct((rows_all, width), F32)] * 2,
        in_specs=[block(0), block(1), block(2), far_spec(0), far_spec(1)]
        + common
        + [pl.BlockSpec(memory_space=pl.ANY)] * carried,
        out_specs=[block(0), block(0)],
        input_output_aliases={10 + i: i for i in range(carried)},
    )(packed, packed, packed, far, far, *bias, spread, pool, same, *before)


def attention_backward(
    packed, far, bias, spread, pool, same, attended, lse, grad, seqs, local, which, before
):
    rows_all, triple = packed.shape
    width = triple // 3
    length = rows_all // seqs
    first, count, pair, pairs = which
    block, far_spec, fixed, common = attention_specs(length, width, first, pair)
    n4, n5 = length >> 4, length >> 5
    carried = len(before)

    def body(q, k, v, fk, fv, inner_bias, outer_bias, spread_ref, pool_ref, same_ref, *rest):
        o_ref, lse_ref, g_ref = rest[:3]
        dq_ref, dk_ref, dv_ref, f4, f5a, f5b = rest[3 + carried :]
        spread_m, pool_m, same_m = spread_ref[...], pool_ref[...], same_ref[...]
        heads = Heads(q[...] * 0.125, k[...], v[...], fk[0, 0], fv[0, 0], pool_m, local)
        lane = heads.lane
        s0, st = heads.scores(spread_m, same_m, inner_bias[0], outer_bias[0])
        logs = lse_ref[...]
        logs = (logs[:, 0:1], logs[:, 64:65])
        p0 = lanes2([jnp.exp(a - x) for a, x in zip(head_columns(s0), logs)])
        pc = lanes2([jnp.exp(a - x) for a, x in zip(head_columns(st), logs)])
        grad_rows = g_ref[...]
        g = split(grad_rows)
        product = grad_rows * o_ref[...]
        zero = jnp.zeros_like(product)
        deltas = [
            jnp.sum(jnp.where(lane, product, zero), axis=1, keepdims=True),
            jnp.sum(jnp.where(lane, zero, product), axis=1, keepdims=True),
        ]
        d0 = heads.inner(g, heads.v2)
        d0 = split(p0 * lanes2([a - x for a, x in zip(head_columns(d0), deltas)]))
        dt = wide_nt(g, heads.vc2)
        dt = split(pc * lanes2([a - x for a, x in zip(head_columns(dt), deltas)]))
        p0, pc = split(p0), split(pc)
        dv = [heads.one(tile_tn(rows(p0, t), rows(g, t))) for t in heads.tiles]
        dk = [heads.one(tile_tn(rows(d0, t), rows(heads.q, t))) for t in heads.tiles]
        dq = [wide_nn(rows(d0, t), heads.k2[t]) for t in heads.tiles]
        dvc = heads.one(wide_tn(pc, g))
        dsc = mm(spread_m, dt[0], 0, 0) + mm(spread_m, dt[1], 0, 0)
        dsc = split(dsc * lanes2((same_m, same_m)))
        dqc = wide_nn(dsc, heads.kc2)
        dkc = heads.one(wide_tn(dsc, heads.qc))
        near = lax.broadcasted_iota(jnp.int32, (length, 128), 0) < local
        high, low = split(
            jnp.concatenate([dqc, jnp.where(near, dkc, zero), jnp.where(near, dvc, zero)], axis=1)
        )
        back = mm(pool_m, lanes2((high, low)), 0, 0)
        back = back[:, :384] + back[:, 384:]
        dq_ref[...] = (jnp.concatenate(dq, axis=0) + back[:, :128]) * 0.125
        dk_ref[...] = jnp.concatenate(dk, axis=0) + back[:, 128:256]
        dv_ref[...] = jnp.concatenate(dv, axis=0) + back[:, 256:]
        for j, value in ((0, dkc), (1, dvc)):
            f4[0, j] = value[local : local + n4]
            f5a[0, j] = value[local + n4 : local + n4 + n5]
            f5b[0, j] = value[local + n4 + n5 :]

    far_out = lambda n: pl.BlockSpec((1, 2, n, 128), lambda s, h: (first + s, 0, 0, pair + h))
    return pl.pallas_call(
        body,
        compiler_params=ROOM,
        cost_estimate=cost(8),
        grid=(count, pairs),
        out_shape=[jax.ShapeDtypeStruct((rows_all, width), F32)] * 3
        + [jax.ShapeDtypeStruct((seqs, 2, n, width), F32) for n in (n4, n5, n5)],
        in_specs=[block(0), block(1), block(2), far_spec(0), far_spec(1)]
        + common
        + [block(0)] * 3
        + [pl.BlockSpec(memory_space=pl.ANY)] * carried,
        out_specs=[block(0)] * 3 + [far_out(n4), far_out(n5), far_out(n5)],
        input_output_aliases={13 + i: i for i in range(carried)},
    )(packed, packed, packed, far, far, *bias, spread, pool, same, attended, lse, grad, *before)


def middle_stage(tokens, attended, wh, wl):
    rows_all, width = tokens.shape

    def body(tok, att, wh_ref, wl_ref, middle, xhat, inv):
        x = tok[...] + mm3(split(att[...]), (wh_ref[...], wl_ref[...]), 1, 1)
        middle[...] = x
        centre = x - jnp.mean(x, axis=1, keepdims=True)
        scale = lax.rsqrt(jnp.mean(centre * centre, axis=1, keepdims=True) + EPSILON)
        xhat[...] = centre * scale
        inv[...] = jnp.broadcast_to(scale, inv.shape)

    return call(
        body,
        [((rows_all, width), F32), ((rows_all, width), F32), ((rows_all, 128), F32)],
        compiler_params=ROOM,
        cost_estimate=cost(4.3),
        in_specs=[whole()] * 4,
        out_specs=[whole()] * 3,
    )(tokens, attended, wh, wl)


def projection_stage(me, gathered, plan, width, hidden_width):
    rows, lanes = width // plan.dp, hidden_width // plan.fsdp
    out_lanes = width // plan.fsdp
    slots = gathered.arrays
    chunks = lanes // 128
    down_parts = [(k * rows, rows, 128 * k) for k in range(chunks)]
    out_parts = [(chunks * rows, rows, 0)]
    chunk = 512

    def body(me_ref, *rest):
        refs = rest[: len(slots)]
        dh, dl, oh, ol, full, full_out = rest[len(slots) :]
        me_d, me_f = me_ref[0], me_ref[1]
        step = pl.program_id(0)

        @pl.when(step == 0)
        def _():
            assemble(full_out, refs, gathered, me_d, me_f, rows, out_lanes, out_parts)
            w = split(full_out[...])
            oh[...] = w[0]
            ol[...] = w[1]
            assemble(full, refs, gathered, me_d, me_f, rows, lanes, down_parts)

        w = split(full[:, pl.ds(pl.multiple_of(step * chunk, chunk), chunk)])
        dh[...] = w[0]
        dl[...] = w[1]

    fixed = lambda shape: pl.BlockSpec(shape, lambda i: (0,) * len(shape))
    cols = pl.BlockSpec((width, chunk), lambda i: (0, i))
    return pl.pallas_call(
        body,
        compiler_params=ROOM,
        cost_estimate=cost(5),
        grid=(hidden_width // chunk,),
        out_shape=[jax.ShapeDtypeStruct((width, hidden_width), BF16)] * 2
        + [jax.ShapeDtypeStruct((width, width), BF16)] * 2,
        in_specs=[SMEM] + [fixed(x.shape) for x in slots],
        out_specs=[cols, cols, fixed((width, width)), fixed((width, width))],
        scratch_shapes=[pltpu.VMEM((width, hidden_width), F32), pltpu.VMEM((width, width), F32)],
    )(me, *slots)


def hidden_stage(me, xhat, ln, cot, dh, dl, gathered, plan):
    rows_all, width = xhat.shape
    hidden_width = dh.shape[1]
    rows, lanes = hidden_width // plan.dp, width // plan.fsdp
    slots = gathered.arrays
    chunk = 512
    steps = hidden_width // chunk
    root = float(np.sqrt(2.0 / np.pi))
    cubic = 0.044715 * root

    def body(me_ref, xhat_ref, ln_ref, cot_ref, d0, d1, *rest):
        refs = rest[: len(slots)]
        hh, hl, ph, plo, wh, wl, nth, ntl, cth, ctl, full, nh, nl, ch, cl = rest[len(slots) :]
        step = pl.program_id(0)

        @pl.when(step == 0)
        def _():
            assemble(full, refs, gathered, me_ref[0], me_ref[1], rows, lanes, [(0, rows, 0)])
            n = xhat_ref[...] * ln_ref[2:3, :] + ln_ref[3:4, :]
            c = cot_ref[...]
            for value, high, low in (
                (n, nh, nl),
                (c, ch, cl),
                (jnp.transpose(n), nth, ntl),
                (jnp.transpose(c), cth, ctl),
            ):
                halves = split(value)
                high[...] = halves[0]
                low[...] = halves[1]

        w = split(full[pl.ds(pl.multiple_of(step * chunk, chunk), chunk), :])
        wh[...] = w[0]
        wl[...] = w[1]
        v = mm3((nh[...], nl[...]), w, 1, 1)
        square = v * v
        half = 0.5 + 0.5 * jnp.tanh(v * (root + cubic * square))
        h = split(v * half)
        hh[...] = h[0]
        hl[...] = h[1]
        slope = half + (half - half * half) * (v * (2.0 * root + 6.0 * cubic * square))
        g = split(mm3((ch[...], cl[...]), (d0[...], d1[...]), 1, 0) * slope)
        ph[...] = g[0]
        plo[...] = g[1]

    fixed = lambda shape: pl.BlockSpec(shape, lambda i: (0,) * len(shape))
    cols = pl.BlockSpec((rows_all, chunk), lambda i: (0, i))
    down = pl.BlockSpec((width, chunk), lambda i: (0, i))
    act = fixed((rows_all, width))
    return pl.pallas_call(
        body,
        compiler_params=ROOM,
        cost_estimate=cost(15),
        grid=(steps,),
        out_shape=[jax.ShapeDtypeStruct((rows_all, hidden_width), BF16)] * 4
        + [jax.ShapeDtypeStruct((hidden_width, width), BF16)] * 2
        + [jax.ShapeDtypeStruct((width, rows_all), BF16)] * 4,
        in_specs=[SMEM, act, fixed((8, width)), act, down, down]
        + [fixed(x.shape) for x in slots],
        out_specs=[cols] * 4
        + [pl.BlockSpec((chunk, width), lambda i: (i, 0))] * 2
        + [fixed((width, rows_all))] * 4,
        scratch_shapes=[pltpu.VMEM((hidden_width, width), F32)]
        + [pltpu.VMEM((rows_all, width), BF16)] * 4,
    )(me, xhat, ln, cot, dh, dl, *slots)


def grad_down_stage(me, cth, ctl, hh, hl, plan, stream, core):
    width, rows_all = cth.shape
    hidden_width = hh.shape[1]
    rows, lanes = width // plan.dp, hidden_width // plan.fsdp

    def body(me_ref, c0, c1, h0, h1, out):
        jf = core + 2 * pl.program_id(0)
        res = mm3((c0[...], c1[...]), (h0[...], h1[...]), 1, 0)
        for d in range(plan.dp):
            jd = me_ref[0] ^ d
            for k in range(lanes // 128):
                value = res[d * rows : (d + 1) * rows, 128 * k : 128 * (k + 1)]
                stream.put(out, jd, jf, k * rows, value)

    cols = pl.BlockSpec((rows_all, lanes), lambda i, m: (0, m[1] ^ (core + 2 * i)))
    grid_spec = pltpu.PrefetchScalarGridSpec(
        num_scalar_prefetch=1,
        grid=(plan.fsdp // 2,),
        in_specs=[pl.BlockSpec((width, rows_all), lambda i, m: (0, 0))] * 2 + [cols, cols],
        out_specs=pl.BlockSpec(stream.shape(), lambda i, m: (0, 0, 0)),
    )
    return pl.pallas_call(
        body,
        compiler_params=ROOM,
        cost_estimate=cost(0.27),
        grid_spec=grid_spec,
        out_shape=jax.ShapeDtypeStruct(stream.shape(), F32),
    )(me, cth, ctl, hh, hl)


def half_lanes(ref, me_f, core, lanes):
    parts = []
    for y in range(2):
        start = pl.multiple_of((me_f ^ (core + 2 * y)) * lanes, 128)
        parts.append(ref[:, pl.ds(start, lanes)])
    return jnp.concatenate(parts, axis=1)


def half_rows(ref, me_f, core, count):
    parts = []
    for y in range(2):
        start = pl.multiple_of((me_f ^ (core + 2 * y)) * count, 128)
        parts.append(ref[pl.ds(start, count), :])
    return jnp.concatenate(parts, axis=0)


def grad_up_stage(me, nth, ntl, ph, plo, plan, stream, core):
    width, rows_all = nth.shape
    hidden_width = ph.shape[1]
    rows, lanes = hidden_width // plan.dp, width // plan.fsdp
    chunk = 512
    steps = hidden_width // chunk
    per = chunk // rows
    natural = rows % 128 == 0

    def body(me_ref, n0, n1, p0, p1, out):
        step = pl.program_id(0)
        n = (half_rows(n0, me_ref[1], core, lanes), half_rows(n1, me_ref[1], core, lanes))
        p = (p0[...], p1[...])
        res = mm3(n, p, 1, 0) if natural else mm3(p, n, 0, 1)
        for i in range(per):
            jd = (step * per + i) ^ me_ref[0]
            for y in range(2):
                if natural:
                    for k in range(rows // 128):
                        at = i * rows + 128 * k
                        value = res[y * lanes : (y + 1) * lanes, at : at + 128]
                        stream.put(out, jd, core + 2 * y, k * lanes, value)
                else:
                    value = res[i * rows : (i + 1) * rows, y * lanes : (y + 1) * lanes]
                    stream.put(out, jd, core + 2 * y, 0, value)

    fixed = lambda shape: pl.BlockSpec(shape, lambda i: (0,) * len(shape))
    cols = pl.BlockSpec((rows_all, chunk), lambda i: (0, i))
    return pl.pallas_call(
        body,
        compiler_params=ROOM,
        cost_estimate=cost(0.32),
        grid=(steps,),
        out_shape=jax.ShapeDtypeStruct(stream.shape(), F32),
        in_specs=[SMEM] + [fixed((width, rows_all))] * 2 + [cols, cols],
        out_specs=fixed(stream.shape()),
    )(me, nth, ntl, ph, plo)


def norm_back(e, gain, xhat, inv):
    u = e * gain
    mean_u = jnp.mean(u, axis=1, keepdims=True)
    mean_ux = jnp.mean(u * xhat, axis=1, keepdims=True)
    return inv * (u - mean_u - xhat * mean_ux)


def output_stage(middle, hh, hl, dh, dl):
    rows_all, width = middle.shape
    chunk = 512
    steps = hh.shape[1] // chunk

    def body(mid, h0, h1, d0, d1, out):
        @pl.when(pl.program_id(0) == 0)
        def _():
            out[...] = mid[...]

        out[...] += mm3((h0[...], h1[...]), (d0[...], d1[...]), 1, 1)

    cols = pl.BlockSpec((rows_all, chunk), lambda i: (0, i))
    act = pl.BlockSpec((rows_all, width), lambda i: (0, 0))
    return pl.pallas_call(
        body,
        compiler_params=ROOM,
        cost_estimate=cost(8),
        grid=(steps,),
        out_shape=jax.ShapeDtypeStruct((rows_all, width), F32),
        in_specs=[act, cols, cols] + [pl.BlockSpec((width, chunk), lambda i: (0, i))] * 2,
        out_specs=act,
    )(middle, hh, hl, dh, dl)


def middle_grad_stage(cot, xhat, inv, ln, ph, plo, uh, ul):
    rows_all, width = cot.shape
    chunk = 512
    steps = ph.shape[1] // chunk

    def body(cot_ref, xhat_ref, inv_ref, ln_ref, p0, p1, u0, u1, gm, gln, acc):
        step = pl.program_id(0)

        @pl.when(step == 0)
        def _():
            acc[...] = jnp.zeros_like(acc)

        acc[...] += mm3((p0[...], p1[...]), (u0[...], u1[...]), 1, 0)

        @pl.when(step == steps - 1)
        def _():
            e = acc[...]
            xh = xhat_ref[...]
            gm[...] = cot_ref[...] + norm_back(e, ln_ref[2:3, :], xh, inv_ref[:, 0:1])
            gln[0:1, :] = jnp.sum(e * xh, axis=0, keepdims=True)
            gln[1:2, :] = jnp.sum(e, axis=0, keepdims=True)

    fixed = lambda shape: pl.BlockSpec(shape, lambda i: (0,) * len(shape))
    cols = pl.BlockSpec((rows_all, chunk), lambda i: (0, i))
    act = fixed((rows_all, width))
    return pl.pallas_call(
        body,
        compiler_params=ROOM,
        cost_estimate=cost(8.5),
        grid=(steps,),
        out_shape=[
            jax.ShapeDtypeStruct((rows_all, width), F32),
            jax.ShapeDtypeStruct((8, width), F32),
        ],
        in_specs=[act, act, fixed((rows_all, 128)), fixed((8, width)), cols, cols]
        + [pl.BlockSpec((chunk, width), lambda i: (i, 0))] * 2,
        out_specs=[act, fixed((8, width))],
        scratch_shapes=[pltpu.VMEM((rows_all, width), F32)],
    )(cot, xhat, inv, ln, ph, plo, uh, ul)


def mixture_grad_stage(me, gm, attended, oh, ol, plan, stream):
    rows_all, width = gm.shape
    rows, lanes = width // plan.dp, width // plan.fsdp

    def body(me_ref, gm_ref, att, oh_ref, ol_ref, gmix, away, keep, full):
        g = split(gm_ref[...])
        gmix[...] = mm3(g, (oh_ref[...], ol_ref[...]), 1, 0)
        full[...] = att[...]
        for core in range(2):
            res = mm3(g, split(half_lanes(full, me_ref[1], core, lanes)), 0, 0)
            mine = away if core else keep
            for d in range(plan.dp):
                for y in range(2):
                    value = res[d * rows : (d + 1) * rows, y * lanes : (y + 1) * lanes]
                    stream.put(mine, d ^ me_ref[0], core + 2 * y, 0, value)

    return call(
        body,
        [((rows_all, width), F32), (stream.shape(), F32), (stream.shape(), F32)],
        [pltpu.VMEM((rows_all, width), F32)],
        compiler_params=ROOM,
        cost_estimate=cost(5),
        in_specs=[SMEM] + [whole()] * 4,
        out_specs=[whole()] * 3,
    )(me, gm, attended, oh, ol)


def packed_grad_stage(dq, dk, dv, g4, g5a, g5b, pool, seqs):
    rows_all, width = dq.shape
    length = rows_all // seqs

    def body(dq_r, dk_r, dv_r, g4_r, g5a_r, g5b_r, pool_r, gph, gpl, column):
        for j, ref in enumerate((dq_r, dk_r, dv_r)):
            total = None
            for s in range(seqs):
                rs = slice(s * length, (s + 1) * length)
                value = ref[rs, :]
                if j:
                    groups = jnp.concatenate(
                        [g4_r[s, j - 1], g5a_r[s, j - 1] + g5b_r[s, j - 1]], axis=0
                    )
                    value = value + mm2(pool_r[...], split(groups), 0, 0)
                part = jnp.sum(value, axis=0, keepdims=True)
                total = part if total is None else total + part
                h = split(value)
                gph[rs, j * width : (j + 1) * width] = h[0]
                gpl[rs, j * width : (j + 1) * width] = h[1]
            column[j * width : (j + 1) * width, :] = jnp.transpose(
                jnp.broadcast_to(total, (128, width))
            )

    return call(
        body,
        [((rows_all, 3 * width), BF16)] * 2 + [((3 * width, 128), F32)],
        compiler_params=ROOM,
        cost_estimate=cost(4.5),
        in_specs=[whole()] * 7,
        out_specs=[whole()] * 3,
    )(dq, dk, dv, g4, g5a, g5b, pool)


def input_grad_stage(gph, gpl, wqh, wql, xhat, inv, ln, gm):
    rows_all, width = gm.shape

    def body(gph_r, gpl_r, wh, wl, xhat_r, inv_r, ln_r, gm_r, gtok):
        e = mm3((gph_r[...], gpl_r[...]), (wh[...], wl[...]), 1, 0)
        gtok[...] = gm_r[...] + norm_back(e, ln_r[0:1, :], xhat_r[...], inv_r[:, 0:1])

    return call(
        body,
        [((rows_all, width), F32)],
        compiler_params=ROOM,
        cost_estimate=cost(7.4),
        in_specs=[whole()] * 8,
        out_specs=[whole()],
    )(gph, gpl, wqh, wql, xhat, inv, ln, gm)[0]


def grad_qkv_stage(me, gph, gpl, column, xhat, ln, wh, wl, plan, stream, core):
    rows_all, triple = gph.shape
    width = triple // 3
    rows, lanes = triple // plan.dp, width // plan.fsdp
    steps = 2
    block = triple // steps

    def body(me_ref, gph_r, gpl_r, col_r, xhat_r, ln_r, wh_r, wl_r, out, sums, nh, nl):
        me_f = me_ref[1]
        step = pl.program_id(0)
        pick = lambda ref: half_lanes(ref, me_f, core, lanes)

        @pl.when(step == 0)
        def _():
            n = split(pick(xhat_r))
            nh[...] = n[0]
            nl[...] = n[1]
            sums[...] = jnp.zeros_like(sums)

        params = pick(ln_r)
        res = mm3((gph_r[...], gpl_r[...]), (nh[...], nl[...]), 0, 0)
        w = pick(wh_r).astype(F32) + pick(wl_r).astype(F32)
        col = col_r[:, 0:1]
        parts = [jnp.sum(res * w, axis=0, keepdims=True), jnp.sum(w * col, axis=0, keepdims=True)]
        for y in range(2):
            at = pl.ds(pl.multiple_of((me_f ^ (core + 2 * y)) * lanes, 128), lanes)
            for i in range(2):
                sums[i : i + 1, at] += parts[i][:, y * lanes : (y + 1) * lanes]
        res = res * params[0:1, :] + col * params[1:2, :]
        for i in range(block // rows):
            jd = me_ref[0] ^ (step * (block // rows) + i)
            for y in range(2):
                value = res[i * rows : (i + 1) * rows, y * lanes : (y + 1) * lanes]
                stream.put(out, jd, core + 2 * y, 0, value)

    fixed = lambda shape: pl.BlockSpec(shape, lambda i: (0,) * len(shape))
    cols = pl.BlockSpec((rows_all, block), lambda i: (0, i))
    down = lambda n: pl.BlockSpec((block, n), lambda i: (i, 0))
    return pl.pallas_call(
        body,
        compiler_params=ROOM,
        cost_estimate=cost(0.25),
        grid=(steps,),
        out_shape=[
            jax.ShapeDtypeStruct(stream.shape(), F32),
            jax.ShapeDtypeStruct((8, width), F32),
        ],
        in_specs=[SMEM, cols, cols, down(128), fixed((rows_all, width)), fixed((8, width))]
        + [down(width)] * 2,
        out_specs=[fixed(stream.shape()), fixed((8, width))],
        scratch_shapes=[pltpu.VMEM((rows_all, 2 * lanes), BF16)] * 2,
    )(me, gph, gpl, column, xhat, ln, wh, wl)


def swap(x, mask, axis="fsdp"):
    size = lax.axis_size(axis)
    return lax.ppermute(x, axis, [(i, i ^ mask) for i in range(size)])


def local(
    tokens, segments, cotangent, ln1_gain, ln1_bias, w_qkv, w_out, ln2_gain, ln2_bias, w_up, w_down
):
    seqs, length, width = tokens.shape
    dp, fsdp = lax.axis_size("dp"), lax.axis_size("fsdp")
    plan = Plan(dp, fsdp)
    me_d = lax.axis_index("dp")
    me = jnp.stack([me_d, lax.axis_index("fsdp")]).astype(jnp.int32)
    rows_all = seqs * length
    hidden_width = w_down.shape[0] * fsdp

    spread, pool, same = pooling(length)
    layout, _ = level_layout(length)
    local_rows = [first for level, first, _ in layout if 2 * NR * (1 << level) > length][0]
    spread_c = jnp.asarray(spread, BF16)
    pool_c = jnp.asarray(pool, BF16)
    same_c = jnp.asarray(same, F32)
    far_pool = jnp.asarray(pool[local_rows : local_rows + (length >> 4) + (length >> 5)], BF16)

    share = width // dp
    norms = jnp.stack([ln1_gain, ln1_bias, ln2_gain, ln2_bias])
    placed = lax.dynamic_update_slice(jnp.zeros((4, width), F32), norms, (0, me_d * share))
    placed = placed.reshape(4, 4, 128).transpose(1, 0, 2).reshape(LN_ROWS, 128)
    rows_qkv, rows_d, rows_up = 3 * share, share, hidden_width // dp
    chunks = hidden_width // fsdp // 128
    down_piece = w_down.T.reshape(rows_d, chunks, 128).transpose(1, 0, 2).reshape(-1, 128)
    down_piece = jnp.concatenate([down_piece, w_out.T], axis=0)
    extra = [(name,) for name in plan.extra]
    qkv_piece = jnp.concatenate([placed, w_qkv.T], axis=0)
    up_piece = w_up.T
    qkv_piece = after(qkv_piece, me)
    qkv_in, down_in, up_in = (Gather(plan, p) for p in (qkv_piece, down_piece, up_piece))
    tok = tokens.reshape(rows_all, width)
    cot = cotangent.reshape(rows_all, width)
    attend = (spread_c, pool_c, same_c)

    near = swap(segments, 1)
    qkv_in.send([("z", "w")])
    for group in extra:
        qkv_in.stage([group])
    gate = qkv_in.came()
    qkv_in.join()
    qkv_in.cut(LN_ROWS + rows_qkv // 16 * 8)
    qkv_in.send([("x",), ("y",)], gate)
    down_in.send([("w",)], gate)
    for group in extra:
        down_in.stage([group])
    far_segments = swap(jnp.stack([segments, after(near, gate)]), 2)
    bias = score_bias(segments, near, far_segments[0], far_segments[1])
    qkv_in.stage([("y",), ("x",)], qkv_in.came())
    gate = (down_in.came(), far_segments)
    down_in.stage([("z",)], gate)
    up_in.send([("w",)], gate)
    for group in extra:
        up_in.stage([group])
    gate = (qkv_in.came(), down_in.came(), up_in.came(), bias)
    cores = qkv_in.share(True, gate) + qkv_in.share(False, gate)
    down_in.join()
    down_in.cut(down_piece.shape[0] // 16 * 8)
    down_in.send([("x",), ("y",)], cores)
    up_in.stage([("z",)], cores)
    packed, wqh, wql, xhat1, inv1, ln, s4, s5 = qkv_stage(
        me, after(tok, cores, bias), qkv_in, plan, far_pool, seqs
    )
    gate = (packed, down_in.came(), up_in.came())
    s4, s5 = after((s4, s5), gate)
    got = [swap(s4, 1), swap(s5, 2), swap(s5, 3)]
    far = jnp.concatenate(got, axis=2)
    down_in.stage([("y",), ("x",)], gate)
    cores = down_in.share(True, far)
    calls = [(s, 1, 0, width // 128) for s in range(seqs)]
    before = ()
    gate = far
    for index, which in enumerate(calls):
        packed_in = after(packed, gate, before)
        before = attention_forward(packed_in, far, bias, *attend, seqs, local_rows, which, before)
        if index == 0:
            gate = (before, down_in.came(), cores)
            cores = down_in.share(False, gate)
            up_in.join()
            up_in.cut(rows_up // 2 // 8 * 8)
            up_in.send([("x",), ("y",)], gate)
    attended, lse = before
    gate = (attended, up_in.came(), cores)
    up_in.stage([("y",), ("x",)], gate)
    dh, dl, oh, ol = projection_stage(after(me, gate), down_in, plan, width, hidden_width)
    cores = up_in.share(True, gate)
    middle, xhat2, inv2 = middle_stage(tok, attended, oh, ol)
    gate = (middle, up_in.came(), cores)
    cores = up_in.share(False, gate)
    hh, hl, ph, plo, uh, ul, nth, ntl, cth, ctl = hidden_stage(
        me, after(xhat2, cores), ln, cot, dh, dl, up_in, plan
    )

    single = [("x", "y"), ("z",), ("w",)] + extra
    double = [("x", "y"), ("z", "w")] + extra
    outer = [("z",), ("x",), ("w",)] + extra + [("y",)]
    down = Stream(plan, chunks * rows_d, outer)
    up = Stream(plan, rows_up, single)
    out = Stream(plan, rows_d, single)
    qkv = Stream(plan, rows_qkv, double)
    down_sum, up_sum, qkv_sum = Reduce(plan, outer), Reduce(plan, single), Reduce(plan, double)

    away = grad_down_stage(me, cth, ctl, hh, hl, plan, down, 1)
    cores = down_sum.begin(away)
    away = grad_up_stage(me, after(nth, away), ntl, ph, plo, plan, up, 1)
    cores += up_sum.begin(away)
    keep = grad_down_stage(me, after(cth, away), ctl, hh, hl, plan, down, 0)
    down_sum.keep(keep)
    keep = grad_up_stage(me, after(nth, keep), ntl, ph, plo, plan, up, 0)
    up_sum.keep(keep)
    sent = (down_sum.send(keep, cores), up_sum.send(keep, cores))
    gm, gln = middle_grad_stage(after(cot, sent), xhat2, inv2, ln, ph, plo, uh, ul)
    gmix, away_out, keep_out = mixture_grad_stage(me, gm, attended, oh, ol, plan, out)
    before = ()
    calls = [(s, 1, 0, width // 128) for s in range(seqs)]
    for which in calls:
        grad = after(gmix, sent, before)
        before = attention_backward(
            packed, far, bias, *attend, attended, lse, grad, seqs, local_rows, which, before
        )
    gate = (before, down_sum.last, up_sum.last)
    dq, dk, dv, f4, f5a, f5b = before
    f4, f5a, f5b = after((f4, f5a, f5b), gate)
    g4, g5a, g5b = swap(f4, 1), swap(f5a, 2), swap(f5b, 3)
    down_sum.send(gate)
    out_sum = Reduce(plan, single)
    out_cores = out_sum.begin(away_out, gate)
    out_sum.keep(keep_out)
    gph, gpl, column = packed_grad_stage(dq, dk, dv, g4, g5a, g5b, far_pool, seqs)
    away, sums_away = grad_qkv_stage(
        me, gph, gpl, column, xhat1, ln, wqh, wql, plan, qkv, 1
    )
    out_sum.send(gph, out_cores)
    got = qkv_sum.begin(away)
    keep, sums_keep = grad_qkv_stage(
        me, gph, gpl, column, after(xhat1, away), ln, wqh, wql, plan, qkv, 0
    )
    qkv_sum.keep(keep)
    sums = jnp.concatenate([(sums_away + sums_keep)[0:2], gln[0:2]], axis=0)
    sent = qkv_sum.send(got, rider=sums.reshape(-1, 128))
    down_sum.send(sent)
    up_sum.absorb(out_sum, sent)
    up_sum.send()
    gtok = input_grad_stage(gph, gpl, wqh, wql, after(xhat1, sent), inv1, ln, gm)
    output = output_stage(after(middle, gtok), hh, hl, dh, dl)
    gate = (up_sum.last, down_sum.last, output)
    sent = qkv_sum.send(qkv_sum.last, gate)
    while qkv_sum.stages:
        sent = qkv_sum.send(qkv_sum.last)
    for total in (down_sum, up_sum):
        while total.stages:
            total.send(gate, sent)
    g_down, g_up = down_sum.total(), up_sum.total()
    g_up, g_out = g_up[:rows_up], g_up[rows_up:]
    if rows_up % 128 == 0:
        g_up = g_up.reshape(-1, width // fsdp, 128).transpose(1, 0, 2).reshape(-1, rows_up)
    else:
        g_up = g_up.T
    g_down = g_down.reshape(chunks, rows_d, 128).transpose(0, 2, 1).reshape(-1, rows_d)
    g_out = g_out.T
    qkv_sum.terms[-1] = after(qkv_sum.terms[-1], g_down, g_up, g_out)
    g_qkv = qkv_sum.total()
    g_qkv, sums = g_qkv[:rows_qkv], g_qkv[rows_qkv:]
    sums = (sums + plan.send(sums, ("c",))).reshape(4, width)
    mine = lax.dynamic_slice(sums, (0, me_d * share), (4, share))
    shape = tokens.shape
    return (
        output.reshape(shape),
        gtok.reshape(shape),
        mine[0],
        mine[1],
        g_qkv.T,
        g_out,
        mine[2],
        mine[3],
        g_up,
        g_down,
    )


def solution(mesh):
    weight = P("fsdp", "dp")
    rows = P("dp", "fsdp", None)
    vector = P("dp")
    return jax.shard_map(
        local,
        mesh=mesh,
        in_specs=(rows, P("dp", "fsdp"), rows, vector, vector, weight, weight, vector, vector, weight, weight),
        out_specs=(rows, rows, vector, vector, weight, weight, vector, vector, weight, weight),
        check_vma=False,
    )
```

```python
import jax
import jax.numpy as jnp
import numpy as np
from jax import lax
from jax.experimental import pallas as pl
from jax.experimental.pallas import tpu as pltpu
from jax.sharding import PartitionSpec as P

HEADS = 8
NR = 16
LEVELS = 6
EPSILON = 1e-05
MASKED = -1e30
F32 = jnp.float32
BF16 = jnp.bfloat16
LN_ROWS = 16
TILE = 128
ROOM = pltpu.CompilerParams(vmem_limit_bytes=23 << 20)
SCALE = 0.05


def split(x):
    high = x.astype(BF16)
    return high, (x - high.astype(F32)).astype(BF16)


def mm(a, b, ca, cb):
    return lax.dot_general(a, b, (((ca,), (cb,)), ((), ())), preferred_element_type=F32)


def mm3(a, b, ca, cb):
    return mm(a[0], b[0], ca, cb) + mm(a[0], b[1], ca, cb) + mm(a[1], b[0], ca, cb)


def mm2(a, b, ca, cb):
    return mm(a, b[0], ca, cb) + mm(a, b[1], ca, cb)


def level_layout(length):
    rows, start = [], 0
    for level in range(1, LEVELS):
        count = length >> level
        rows.append((level, start, count))
        start += count
    return rows, start


def pooling(length):
    spread = np.zeros((length, length), np.float32)
    pool = np.zeros((length, length), np.float32)
    same = np.zeros((length, length), np.float32)
    layout, _ = level_layout(length)
    bounds = [first for _, first, _ in layout] + [length]
    for index, (level, first, count) in enumerate(layout):
        token = np.arange(length)
        spread[token, first + (token >> level)] = 1.0
        pool[first + (token >> level), token] = 0.5**level
        same[bounds[index] : bounds[index + 1], bounds[index] : bounds[index + 1]] = 1.0
    return spread, pool, same


def score_bias(seg, near, far_a, far_b):
    count, length = seg.shape
    token = np.arange(length)
    near_pair = (token[:TILE, None] >> 5) == (token[None, :TILE] >> 5)
    tiles = seg.reshape(count, length // TILE, TILE)
    ok = near_pair & (tiles[:, :, :, None] == tiles[:, :, None, :])
    inner = jnp.where(ok, 0.0, MASKED).astype(F32).reshape(count, length, TILE)
    parts = []
    for level in range(1, LEVELS):
        ratio = 1 << level

        def ends(values):
            grouped = values.reshape(count, length // ratio, ratio)
            return grouped[:, :, 0], grouped[:, :, -1]

        low_q, high_q = ends(seg)
        low_q = jnp.repeat(low_q, ratio, axis=1)
        high_q = jnp.repeat(high_q, ratio, axis=1)
        if 2 * NR * ratio <= length:
            low_k, high_k = ends(seg)
            block_q = (token >> level) >> 4
            block_k = np.arange(length >> level) >> 4
            where = (block_q[:, None] ^ 1) == block_k[None, :]
        else:
            if NR * ratio <= length:
                low_k, high_k = ends(near)
            else:
                pieces = [ends(far_a), ends(far_b)]
                low_k = jnp.concatenate([pieces[0][0], pieces[1][0]], axis=1)
                high_k = jnp.concatenate([pieces[0][1], pieces[1][1]], axis=1)
            where = np.ones((length, low_k.shape[1]), bool)
        ok = (
            where[None]
            & (low_q[:, :, None] <= high_k[:, None, :])
            & (low_k[:, None, :] <= high_q[:, :, None])
        )
        parts.append(jnp.where(ok, np.float32(level * np.log(2.0)), MASKED))
    return inner, jnp.concatenate(parts, axis=2).astype(F32)


class Plan:
    def __init__(self, dp, fsdp):
        self.dp, self.fsdp = dp, fsdp
        self.dims = {}
        names = ["x", "z", "w"]
        bit = 1
        while bit < dp:
            name = names[len(self.dims)] if len(self.dims) < 3 else "d%d" % bit
            self.dims[name] = ("dp", bit)
            bit *= 2
        self.extra = list(self.dims)[3:]
        self.dims["y"] = ("fsdp", 2)
        self.dims["c"] = ("fsdp", 1)

    def corner(self, group, v):
        return tuple(name for i, name in enumerate(group) if (v >> i) & 1)

    def mask(self, names):
        d = f = 0
        for name in names:
            axis, bit = self.dims[name]
            if axis == "dp":
                d |= bit
            else:
                f |= bit
        return d, f

    def send(self, x, names):
        d, f = self.mask(names)
        if not f:
            return lax.ppermute(x, "dp", [(i, i ^ d) for i in range(self.dp)])
        if not d:
            return lax.ppermute(x, "fsdp", [(i, i ^ f) for i in range(self.fsdp)])
        n = self.fsdp
        pairs = [(i, ((i // n) ^ d) * n + ((i % n) ^ f)) for i in range(self.dp * n)]
        return lax.ppermute(x, ("dp", "fsdp"), pairs)

    def position(self, stages, d, f):
        pos = 0
        for group in stages:
            for name in reversed(group):
                axis, bit = self.dims[name]
                value = d if axis == "dp" else f
                pos = pos * 2 + ((value // bit) & 1)
        return pos


class Part:
    def __init__(self, start, held, names):
        self.start, self.held, self.names, self.got = start, held, names, []


class Gather:
    def __init__(self, plan, piece):
        self.plan, self.parts = plan, [Part(0, piece[None], [()])]
        self.arrays, self.slots = [], []

    def cut(self, row):
        (part,) = self.parts
        self.parts = [
            Part(0, part.held[:, :row], part.names),
            Part(row, part.held[:, row:], part.names),
        ]

    def send(self, groups, *earlier):
        for part, group in zip(self.parts, groups):
            if earlier:
                part.held = after(part.held, *earlier)
            for v in range(1, 1 << len(group)):
                names = self.plan.corner(group, v)
                part.got.append((self.plan.send(part.held, names), names))

    def came(self):
        return [value for part in self.parts for value, _ in part.got]

    def join(self):
        for part in self.parts:
            names = list(part.names)
            for _, corner in part.got:
                names += [n + corner for n in part.names]
            part.held = jnp.concatenate([part.held] + [v for v, _ in part.got], axis=0)
            part.names, part.got = names, []

    def stage(self, groups, *earlier):
        self.join()
        self.send(groups, *earlier)

    def share(self, held, *earlier):
        sent = []
        for part in self.parts:
            for value, corner in [(part.held, ())] if held else part.got:
                if earlier:
                    value = after(value, *earlier)
                other = self.plan.send(value, ("c",))
                sent.append(other)
                for array, core in ((value, ()), (other, ("c",))):
                    self.arrays.append(array)
                    slots = [self.plan.mask(n + corner + core) for n in part.names]
                    self.slots.append((slots, part.start))
        return sent


def assemble(scratch, refs, gathered, me_d, me_f, rows, lanes, segments):
    for ref, (slots, start) in zip(refs, gathered.slots):
        for slot, (d, f) in enumerate(slots):
            row0 = (me_d ^ d) * rows
            col0 = (me_f ^ f) * lanes
            for source, size, to_lane in segments:
                low, high = max(source, start), min(source + size, start + ref.shape[1])
                if low < high:
                    row = pl.multiple_of(row0 + (low - source), 8)
                    col = pl.multiple_of(col0 + to_lane, 128)
                    scratch[pl.ds(row, high - low), pl.ds(col, 128)] = ref[
                        slot, low - start : high - start, :
                    ]


def norm_rows(refs, gathered):
    total = None
    for ref, (slots, start) in zip(refs, gathered.slots):
        for slot, (d, f) in enumerate(slots):
            if f == 0 and start == 0:
                value = ref[slot, :LN_ROWS, :]
                total = value if total is None else total + value
    return jnp.concatenate([total[4 * i : 4 * i + 4] for i in range(4)], axis=1)


class Stream:
    def __init__(self, plan, rows, stages):
        self.plan, self.rows, self.stages = plan, rows, stages
        self.slots = plan.dp * plan.fsdp // 2

    def shape(self):
        return (self.slots, self.rows, 128)

    def put(self, out, d, f, row, value):
        size = value.shape[0]
        out[self.plan.position(self.stages, d, f), row : row + size, :] = value


class Reduce:
    def __init__(self, plan, stages):
        self.plan, self.stages = plan, list(stages)
        self.kept, self.came, self.last = [], [], []

    def begin(self, part, *earlier):
        part = after(part, *earlier) if earlier else part
        self.last = [self.plan.send(part, ("c",))]
        self.came.append(self.last[0])
        return self.last

    def keep(self, part):
        self.kept.append(part)

    def send(self, *earlier, rider=None):
        if self.kept:
            self.terms = [self.kept, self.came]
            self.slots, self.kept = self.kept[0].shape[0], []
        if earlier:
            self.terms[-1] = after(self.terms[-1], *earlier)
        group = self.stages.pop(0)
        self.slots >>= len(group)
        n = self.slots
        count = range(len(self.terms[0]))
        join = len(count) > 1 or rider is not None
        out = []
        for v in range(0 if join else 1, 1 << len(group)):
            parts = [sum(term[i][v * n : (v + 1) * n] for term in self.terms) for i in count]
            if rider is not None:
                parts.append(jnp.broadcast_to(rider[None], (n,) + rider.shape))
            out.append(parts[0] if len(parts) == 1 else jnp.concatenate(parts, axis=1))
        if join:
            self.terms = [[out.pop(0)]]
        self.last = []
        for v, value in enumerate(out):
            got = self.plan.send(value, self.plan.corner(group, v + 1))
            self.last.append(got)
            self.terms.append([got])
        return out

    def absorb(self, other, *earlier):
        n = self.slots
        other.terms[-1] = after(other.terms[-1], *earlier)
        parts = [sum(term[0][0:n] for term in x.terms) for x in (self, other)]
        self.terms = [[jnp.concatenate(parts, axis=1)]]

    def total(self):
        return sum(term[0][0] for term in self.terms)


def after(value, *earlier):
    return lax.optimization_barrier((value, earlier))[0]


def whole(shape=None):
    return pl.BlockSpec(memory_space=pltpu.VMEM)


SMEM = pl.BlockSpec(memory_space=pltpu.SMEM)


def cost(micros):
    return pl.CostEstimate(
        flops=int(micros * SCALE * 9e8), bytes_accessed=int(micros * SCALE * 2.5e6), transcendentals=0
    )


def call(body, outs, scratch=(), **kw):
    return pl.pallas_call(
        body,
        out_shape=[jax.ShapeDtypeStruct(s, t) for s, t in outs],
        scratch_shapes=list(scratch),
        **kw,
    )


def qkv_stage(me, tokens, gathered, plan, pool, seqs):
    rows_all, width = tokens.shape
    length = rows_all // seqs
    n4, n5 = length >> 4, length >> 5
    slots = gathered.arrays
    triple = 3 * width
    rows = triple // plan.dp
    lanes = width // plan.fsdp

    def body(me_ref, tok, pool_ref, *rest):
        refs = rest[: len(slots)]
        packed, wh, wl, xhat, inv, ln, s4, s5, full, nh, nl = rest[len(slots) :]
        step = pl.program_id(0)

        @pl.when(step == 0)
        def _():
            assemble(full, refs, gathered, me_ref[0], me_ref[1], rows, lanes, [(LN_ROWS, rows, 0)])
            params = norm_rows(refs, gathered)
            ln[0:4, :] = params
            x = tok[...]
            centre = x - jnp.mean(x, axis=1, keepdims=True)
            scale = lax.rsqrt(jnp.mean(centre * centre, axis=1, keepdims=True) + EPSILON)
            xh = centre * scale
            xhat[...] = xh
            inv[...] = jnp.broadcast_to(scale, inv.shape)
            n = split(xh * params[0:1, :] + params[1:2, :])
            nh[...] = n[0]
            nl[...] = n[1]

        w = split(full[pl.ds(pl.multiple_of(step * width, width), width), :])
        wh[...] = w[0]
        wl[...] = w[1]
        packed[...] = mm3((nh[...], nl[...]), w, 1, 1)

        @pl.when(step > 0)
        def _():
            for s in range(seqs):
                means = mm2(pool_ref[...], split(packed[s * length : (s + 1) * length, :]), 1, 0)
                s4[s, 0] = means[:n4]
                s5[s, 0] = means[n4 : n4 + n5]

    fixed = lambda shape: pl.BlockSpec(shape, lambda i: (0,) * len(shape))
    later = lambda n: pl.BlockSpec((seqs, 1, n, width), lambda i: (0, jnp.maximum(i - 1, 0), 0, 0))
    outs = [
        ((rows_all, triple), F32, pl.BlockSpec((rows_all, width), lambda i: (0, i))),
        ((triple, width), BF16, pl.BlockSpec((width, width), lambda i: (i, 0))),
        ((triple, width), BF16, pl.BlockSpec((width, width), lambda i: (i, 0))),
        ((rows_all, width), F32, fixed((rows_all, width))),
        ((rows_all, 128), F32, fixed((rows_all, 128))),
        ((8, width), F32, fixed((8, width))),
        ((seqs, 2, n4, width), F32, later(n4)),
        ((seqs, 2, n5, width), F32, later(n5)),
    ]
    return pl.pallas_call(
        body,
        compiler_params=ROOM,
        cost_estimate=cost(7.4),
        grid=(3,),
        out_shape=[jax.ShapeDtypeStruct(shape, kind) for shape, kind, _ in outs],
        in_specs=[SMEM, fixed((rows_all, width)), fixed(pool.shape)]
        + [fixed(x.shape) for x in slots],
        out_specs=[spec for _, _, spec in outs],
        scratch_shapes=[
            pltpu.VMEM((triple, width), F32),
            pltpu.VMEM((rows_all, width), BF16),
            pltpu.VMEM((rows_all, width), BF16),
        ],
    )(me, tokens, pool, *slots)


def lanes2(pair):
    return jnp.concatenate(pair, axis=1)


def fold(r):
    return r[:, :128] + r[:, 128:]


def wide_nt(a, b):
    first = mm(lanes2(a), lanes2((b[0], b[0])), 1, 1)
    return first + mm(a[0], b[1], 1, 1)


def wide_nn(a, b):
    return fold(mm(a[0], lanes2(b), 1, 0)) + mm(a[1], b[0], 1, 0)


def wide_tn(a, b):
    return fold(mm(a[0], lanes2(b), 0, 0)) + mm(a[1], b[0], 0, 0)


def tile_tn(a, b):
    left = jnp.concatenate(a, axis=0)
    right = jnp.concatenate([lanes2(b), lanes2((b[0], jnp.zeros_like(b[0])))], axis=0)
    return fold(mm(left, right, 0, 0))


def rows(pair, t):
    return tuple(x[t * TILE : (t + 1) * TILE] for x in pair)


class Heads:
    def __init__(self, q, k, v, fk, fv, pool, local):
        length = q.shape[0]
        self.tiles = range(length // TILE)
        self.lane = lax.broadcasted_iota(jnp.int32, (length, 128), 1) < 64
        qs, ks, vs = split(q), split(k), split(v)
        pooled = mm(pool, jnp.concatenate([qs[0], ks[0], vs[0], qs[1], ks[1], vs[1]], axis=1), 1, 0)
        pooled = pooled[:, :384] + pooled[:, 384:]
        kc = jnp.concatenate([pooled[:local, 128:256], fk], axis=0)
        vc = jnp.concatenate([pooled[:local, 256:], fv], axis=0)
        self.q, self.qc = qs, split(pooled[:, :128])
        self.k2 = [self.two(rows(ks, t)) for t in self.tiles]
        self.v2 = [self.two(rows(vs, t)) for t in self.tiles]
        self.kc2, self.vc2 = self.two(split(kc)), self.two(split(vc))

    def two(self, pair):
        out = []
        for x in pair:
            lane = self.lane[: x.shape[0]]
            zero = jnp.zeros_like(x)
            both = [jnp.where(lane, x, zero), jnp.where(lane, zero, x)]
            out.append(jnp.concatenate(both, axis=0))
        return tuple(out)

    def one(self, x):
        half = x.shape[0] // 2
        return jnp.where(self.lane[:half], x[:half], x[half:])

    def inner(self, left, right):
        return jnp.concatenate([wide_nt(rows(left, t), right[t]) for t in self.tiles], axis=0)

    def scores(self, spread, same, inner_bias, outer_bias):
        s0 = self.inner(self.q, self.k2) + lanes2((inner_bias, inner_bias))
        high, low = split(wide_nt(self.qc, self.kc2) * lanes2((same, same)))
        st = mm(spread, high, 1, 0) + mm(spread, low, 1, 0)
        return s0, st + lanes2((outer_bias, outer_bias))


def head_columns(x):
    half = x.shape[1] // 2
    return x[:, :half], x[:, half:]


def attention_specs(length, width, first=0, pair=0):
    pairs = width // 128
    block = lambda off: pl.BlockSpec((length, 128), lambda s, h: (first + s, off * pairs + pair + h))
    far = lambda j: pl.BlockSpec((1, 1, 32, 128), lambda s, h: (first + s, j, 0, pair + h))
    fixed = pl.BlockSpec((length, length), lambda s, h: (0, 0))
    bias = lambda n: pl.BlockSpec((1, length, n), lambda s, h: (first + s, 0, 0))
    return block, far, fixed, [bias(TILE), bias(length), fixed, fixed, fixed]


def attention_forward(packed, far, bias, spread, pool, same, seqs, local, which, before):
    rows_all, triple = packed.shape
    width = triple // 3
    length = rows_all // seqs
    first, count, pair, pairs = which
    block, far_spec, fixed, common = attention_specs(length, width, first, pair)
    carried = len(before)

    def body(q, k, v, fk, fv, inner_bias, outer_bias, spread_ref, pool_ref, same_ref, *rest):
        out, lse = rest[carried:]
        heads = Heads(q[...] * 0.125, k[...], v[...], fk[0, 0], fv[0, 0], pool_ref[...], local)
        s0, st = heads.scores(spread_ref[...], same_ref[...], inner_bias[0], outer_bias[0])
        p0, pc, peaks, sums = [], [], [], []
        for a, b in zip(head_columns(s0), head_columns(st)):
            peak = jnp.maximum(jnp.max(a, axis=1, keepdims=True), jnp.max(b, axis=1, keepdims=True))
            a, b = jnp.exp(a - peak), jnp.exp(b - peak)
            p0.append(a)
            pc.append(b)
            peaks.append(peak)
            sums.append(jnp.sum(a, axis=1, keepdims=True) + jnp.sum(b, axis=1, keepdims=True))
        p0, pc = split(lanes2(p0)), split(lanes2(pc))
        mixed = [wide_nn(rows(p0, t), heads.v2[t]) for t in heads.tiles]
        mixed = jnp.concatenate(mixed, axis=0) + wide_nn(pc, heads.vc2)
        total = jnp.where(heads.lane, sums[0], sums[1])
        out[...] = mixed / total
        lse[...] = jnp.where(heads.lane, peaks[0], peaks[1]) + jnp.log(total)

    return pl.pallas_call(
        body,
        compiler_params=ROOM,
        cost_estimate=cost(9.5),
        grid=(count, pairs),
        out_shape=[jax.ShapeDtypeStruct((rows_all, width), F32)] * 2,
        in_specs=[block(0), block(1), block(2), far_spec(0), far_spec(1)]
        + common
        + [pl.BlockSpec(memory_space=pl.ANY)] * carried,
        out_specs=[block(0), block(0)],
        input_output_aliases={10 + i: i for i in range(carried)},
    )(packed, packed, packed, far, far, *bias, spread, pool, same, *before)


def attention_backward(
    packed, far, bias, spread, pool, same, attended, lse, grad, seqs, local, which, before
):
    rows_all, triple = packed.shape
    width = triple // 3
    length = rows_all // seqs
    first, count, pair, pairs = which
    block, far_spec, fixed, common = attention_specs(length, width, first, pair)
    n4, n5 = length >> 4, length >> 5
    carried = len(before)

    def body(q, k, v, fk, fv, inner_bias, outer_bias, spread_ref, pool_ref, same_ref, *rest):
        o_ref, lse_ref, g_ref = rest[:3]
        dq_ref, dk_ref, dv_ref, f4, f5a, f5b = rest[3 + carried :]
        spread_m, pool_m, same_m = spread_ref[...], pool_ref[...], same_ref[...]
        heads = Heads(q[...] * 0.125, k[...], v[...], fk[0, 0], fv[0, 0], pool_m, local)
        lane = heads.lane
        s0, st = heads.scores(spread_m, same_m, inner_bias[0], outer_bias[0])
        logs = lse_ref[...]
        logs = (logs[:, 0:1], logs[:, 64:65])
        p0 = lanes2([jnp.exp(a - x) for a, x in zip(head_columns(s0), logs)])
        pc = lanes2([jnp.exp(a - x) for a, x in zip(head_columns(st), logs)])
        grad_rows = g_ref[...]
        g = split(grad_rows)
        product = grad_rows * o_ref[...]
        zero = jnp.zeros_like(product)
        deltas = [
            jnp.sum(jnp.where(lane, product, zero), axis=1, keepdims=True),
            jnp.sum(jnp.where(lane, zero, product), axis=1, keepdims=True),
        ]
        d0 = heads.inner(g, heads.v2)
        d0 = split(p0 * lanes2([a - x for a, x in zip(head_columns(d0), deltas)]))
        dt = wide_nt(g, heads.vc2)
        dt = split(pc * lanes2([a - x for a, x in zip(head_columns(dt), deltas)]))
        p0, pc = split(p0), split(pc)
        dv = [heads.one(tile_tn(rows(p0, t), rows(g, t))) for t in heads.tiles]
        dk = [heads.one(tile_tn(rows(d0, t), rows(heads.q, t))) for t in heads.tiles]
        dq = [wide_nn(rows(d0, t), heads.k2[t]) for t in heads.tiles]
        dvc = heads.one(wide_tn(pc, g))
        dsc = mm(spread_m, dt[0], 0, 0) + mm(spread_m, dt[1], 0, 0)
        dsc = split(dsc * lanes2((same_m, same_m)))
        dqc = wide_nn(dsc, heads.kc2)
        dkc = heads.one(wide_tn(dsc, heads.qc))
        near = lax.broadcasted_iota(jnp.int32, (length, 128), 0) < local
        high, low = split(
            jnp.concatenate([dqc, jnp.where(near, dkc, zero), jnp.where(near, dvc, zero)], axis=1)
        )
        back = mm(pool_m, lanes2((high, low)), 0, 0)
        back = back[:, :384] + back[:, 384:]
        dq_ref[...] = (jnp.concatenate(dq, axis=0) + back[:, :128]) * 0.125
        dk_ref[...] = jnp.concatenate(dk, axis=0) + back[:, 128:256]
        dv_ref[...] = jnp.concatenate(dv, axis=0) + back[:, 256:]
        for j, value in ((0, dkc), (1, dvc)):
            f4[0, j] = value[local : local + n4]
            f5a[0, j] = value[local + n4 : local + n4 + n5]
            f5b[0, j] = value[local + n4 + n5 :]

    far_out = lambda n: pl.BlockSpec((1, 2, n, 128), lambda s, h: (first + s, 0, 0, pair + h))
    return pl.pallas_call(
        body,
        compiler_params=ROOM,
        cost_estimate=cost(8),
        grid=(count, pairs),
        out_shape=[jax.ShapeDtypeStruct((rows_all, width), F32)] * 3
        + [jax.ShapeDtypeStruct((seqs, 2, n, width), F32) for n in (n4, n5, n5)],
        in_specs=[block(0), block(1), block(2), far_spec(0), far_spec(1)]
        + common
        + [block(0)] * 3
        + [pl.BlockSpec(memory_space=pl.ANY)] * carried,
        out_specs=[block(0)] * 3 + [far_out(n4), far_out(n5), far_out(n5)],
        input_output_aliases={13 + i: i for i in range(carried)},
    )(packed, packed, packed, far, far, *bias, spread, pool, same, attended, lse, grad, *before)


def middle_stage(tokens, attended, wh, wl):
    rows_all, width = tokens.shape

    def body(tok, att, wh_ref, wl_ref, middle, xhat, inv):
        x = tok[...] + mm3(split(att[...]), (wh_ref[...], wl_ref[...]), 1, 1)
        middle[...] = x
        centre = x - jnp.mean(x, axis=1, keepdims=True)
        scale = lax.rsqrt(jnp.mean(centre * centre, axis=1, keepdims=True) + EPSILON)
        xhat[...] = centre * scale
        inv[...] = jnp.broadcast_to(scale, inv.shape)

    return call(
        body,
        [((rows_all, width), F32), ((rows_all, width), F32), ((rows_all, 128), F32)],
        compiler_params=ROOM,
        cost_estimate=cost(4.3),
        in_specs=[whole()] * 4,
        out_specs=[whole()] * 3,
    )(tokens, attended, wh, wl)


def projection_stage(me, gathered, plan, width, hidden_width):
    rows, lanes = width // plan.dp, hidden_width // plan.fsdp
    out_lanes = width // plan.fsdp
    slots = gathered.arrays
    chunks = lanes // 128
    down_parts = [(k * rows, rows, 128 * k) for k in range(chunks)]
    out_parts = [(chunks * rows, rows, 0)]
    chunk = 512

    def body(me_ref, *rest):
        refs = rest[: len(slots)]
        dh, dl, oh, ol, full, full_out = rest[len(slots) :]
        me_d, me_f = me_ref[0], me_ref[1]
        step = pl.program_id(0)

        @pl.when(step == 0)
        def _():
            assemble(full_out, refs, gathered, me_d, me_f, rows, out_lanes, out_parts)
            w = split(full_out[...])
            oh[...] = w[0]
            ol[...] = w[1]
            assemble(full, refs, gathered, me_d, me_f, rows, lanes, down_parts)

        w = split(full[:, pl.ds(pl.multiple_of(step * chunk, chunk), chunk)])
        dh[...] = w[0]
        dl[...] = w[1]

    fixed = lambda shape: pl.BlockSpec(shape, lambda i: (0,) * len(shape))
    cols = pl.BlockSpec((width, chunk), lambda i: (0, i))
    return pl.pallas_call(
        body,
        compiler_params=ROOM,
        cost_estimate=cost(5),
        grid=(hidden_width // chunk,),
        out_shape=[jax.ShapeDtypeStruct((width, hidden_width), BF16)] * 2
        + [jax.ShapeDtypeStruct((width, width), BF16)] * 2,
        in_specs=[SMEM] + [fixed(x.shape) for x in slots],
        out_specs=[cols, cols, fixed((width, width)), fixed((width, width))],
        scratch_shapes=[pltpu.VMEM((width, hidden_width), F32), pltpu.VMEM((width, width), F32)],
    )(me, *slots)


def hidden_stage(me, xhat, ln, cot, dh, dl, gathered, plan):
    rows_all, width = xhat.shape
    hidden_width = dh.shape[1]
    rows, lanes = hidden_width // plan.dp, width // plan.fsdp
    slots = gathered.arrays
    chunk = 512
    steps = hidden_width // chunk
    root = float(np.sqrt(2.0 / np.pi))
    cubic = 0.044715 * root

    def body(me_ref, xhat_ref, ln_ref, cot_ref, d0, d1, *rest):
        refs = rest[: len(slots)]
        hh, hl, ph, plo, wh, wl, nth, ntl, cth, ctl, full, nh, nl, ch, cl = rest[len(slots) :]
        step = pl.program_id(0)

        @pl.when(step == 0)
        def _():
            assemble(full, refs, gathered, me_ref[0], me_ref[1], rows, lanes, [(0, rows, 0)])
            n = xhat_ref[...] * ln_ref[2:3, :] + ln_ref[3:4, :]
            c = cot_ref[...]
            for value, high, low in (
                (n, nh, nl),
                (c, ch, cl),
                (jnp.transpose(n), nth, ntl),
                (jnp.transpose(c), cth, ctl),
            ):
                halves = split(value)
                high[...] = halves[0]
                low[...] = halves[1]

        w = split(full[pl.ds(pl.multiple_of(step * chunk, chunk), chunk), :])
        wh[...] = w[0]
        wl[...] = w[1]
        v = mm3((nh[...], nl[...]), w, 1, 1)
        square = v * v
        half = 0.5 + 0.5 * jnp.tanh(v * (root + cubic * square))
        h = split(v * half)
        hh[...] = h[0]
        hl[...] = h[1]
        slope = half + (half - half * half) * (v * (2.0 * root + 6.0 * cubic * square))
        g = split(mm3((ch[...], cl[...]), (d0[...], d1[...]), 1, 0) * slope)
        ph[...] = g[0]
        plo[...] = g[1]

    fixed = lambda shape: pl.BlockSpec(shape, lambda i: (0,) * len(shape))
    cols = pl.BlockSpec((rows_all, chunk), lambda i: (0, i))
    down = pl.BlockSpec((width, chunk), lambda i: (0, i))
    act = fixed((rows_all, width))
    return pl.pallas_call(
        body,
        compiler_params=ROOM,
        cost_estimate=cost(15),
        grid=(steps,),
        out_shape=[jax.ShapeDtypeStruct((rows_all, hidden_width), BF16)] * 4
        + [jax.ShapeDtypeStruct((hidden_width, width), BF16)] * 2
        + [jax.ShapeDtypeStruct((width, rows_all), BF16)] * 4,
        in_specs=[SMEM, act, fixed((8, width)), act, down, down]
        + [fixed(x.shape) for x in slots],
        out_specs=[cols] * 4
        + [pl.BlockSpec((chunk, width), lambda i: (i, 0))] * 2
        + [fixed((width, rows_all))] * 4,
        scratch_shapes=[pltpu.VMEM((hidden_width, width), F32)]
        + [pltpu.VMEM((rows_all, width), BF16)] * 4,
    )(me, xhat, ln, cot, dh, dl, *slots)


def grad_down_stage(me, cth, ctl, hh, hl, plan, stream, core):
    width, rows_all = cth.shape
    hidden_width = hh.shape[1]
    rows, lanes = width // plan.dp, hidden_width // plan.fsdp

    def body(me_ref, c0, c1, h0, h1, out):
        jf = core + 2 * pl.program_id(0)
        res = mm3((c0[...], c1[...]), (h0[...], h1[...]), 1, 0)
        for d in range(plan.dp):
            jd = me_ref[0] ^ d
            for k in range(lanes // 128):
                value = res[d * rows : (d + 1) * rows, 128 * k : 128 * (k + 1)]
                stream.put(out, jd, jf, k * rows, value)

    cols = pl.BlockSpec((rows_all, lanes), lambda i, m: (0, m[1] ^ (core + 2 * i)))
    grid_spec = pltpu.PrefetchScalarGridSpec(
        num_scalar_prefetch=1,
        grid=(plan.fsdp // 2,),
        in_specs=[pl.BlockSpec((width, rows_all), lambda i, m: (0, 0))] * 2 + [cols, cols],
        out_specs=pl.BlockSpec(stream.shape(), lambda i, m: (0, 0, 0)),
    )
    return pl.pallas_call(
        body,
        compiler_params=ROOM,
        cost_estimate=cost(0.27),
        grid_spec=grid_spec,
        out_shape=jax.ShapeDtypeStruct(stream.shape(), F32),
    )(me, cth, ctl, hh, hl)


def half_lanes(ref, me_f, core, lanes):
    parts = []
    for y in range(2):
        start = pl.multiple_of((me_f ^ (core + 2 * y)) * lanes, 128)
        parts.append(ref[:, pl.ds(start, lanes)])
    return jnp.concatenate(parts, axis=1)


def half_rows(ref, me_f, core, count):
    parts = []
    for y in range(2):
        start = pl.multiple_of((me_f ^ (core + 2 * y)) * count, 128)
        parts.append(ref[pl.ds(start, count), :])
    return jnp.concatenate(parts, axis=0)


def grad_up_stage(me, nth, ntl, ph, plo, plan, stream, core):
    width, rows_all = nth.shape
    hidden_width = ph.shape[1]
    rows, lanes = hidden_width // plan.dp, width // plan.fsdp
    chunk = 512
    steps = hidden_width // chunk
    per = chunk // rows
    natural = rows % 128 == 0

    def body(me_ref, n0, n1, p0, p1, out):
        step = pl.program_id(0)
        n = (half_rows(n0, me_ref[1], core, lanes), half_rows(n1, me_ref[1], core, lanes))
        p = (p0[...], p1[...])
        res = mm3(n, p, 1, 0) if natural else mm3(p, n, 0, 1)
        for i in range(per):
            jd = (step * per + i) ^ me_ref[0]
            for y in range(2):
                if natural:
                    for k in range(rows // 128):
                        at = i * rows + 128 * k
                        value = res[y * lanes : (y + 1) * lanes, at : at + 128]
                        stream.put(out, jd, core + 2 * y, k * lanes, value)
                else:
                    value = res[i * rows : (i + 1) * rows, y * lanes : (y + 1) * lanes]
                    stream.put(out, jd, core + 2 * y, 0, value)

    fixed = lambda shape: pl.BlockSpec(shape, lambda i: (0,) * len(shape))
    cols = pl.BlockSpec((rows_all, chunk), lambda i: (0, i))
    return pl.pallas_call(
        body,
        compiler_params=ROOM,
        cost_estimate=cost(0.32),
        grid=(steps,),
        out_shape=jax.ShapeDtypeStruct(stream.shape(), F32),
        in_specs=[SMEM] + [fixed((width, rows_all))] * 2 + [cols, cols],
        out_specs=fixed(stream.shape()),
    )(me, nth, ntl, ph, plo)


def norm_back(e, gain, xhat, inv):
    u = e * gain
    mean_u = jnp.mean(u, axis=1, keepdims=True)
    mean_ux = jnp.mean(u * xhat, axis=1, keepdims=True)
    return inv * (u - mean_u - xhat * mean_ux)


def output_stage(middle, hh, hl, dh, dl):
    rows_all, width = middle.shape
    chunk = 512
    steps = hh.shape[1] // chunk

    def body(mid, h0, h1, d0, d1, out):
        @pl.when(pl.program_id(0) == 0)
        def _():
            out[...] = mid[...]

        out[...] += mm3((h0[...], h1[...]), (d0[...], d1[...]), 1, 1)

    cols = pl.BlockSpec((rows_all, chunk), lambda i: (0, i))
    act = pl.BlockSpec((rows_all, width), lambda i: (0, 0))
    return pl.pallas_call(
        body,
        compiler_params=ROOM,
        cost_estimate=cost(8),
        grid=(steps,),
        out_shape=jax.ShapeDtypeStruct((rows_all, width), F32),
        in_specs=[act, cols, cols] + [pl.BlockSpec((width, chunk), lambda i: (0, i))] * 2,
        out_specs=act,
    )(middle, hh, hl, dh, dl)


def middle_grad_stage(cot, xhat, inv, ln, ph, plo, uh, ul):
    rows_all, width = cot.shape
    chunk = 512
    steps = ph.shape[1] // chunk

    def body(cot_ref, xhat_ref, inv_ref, ln_ref, p0, p1, u0, u1, gm, gln, acc):
        step = pl.program_id(0)

        @pl.when(step == 0)
        def _():
            acc[...] = jnp.zeros_like(acc)

        acc[...] += mm3((p0[...], p1[...]), (u0[...], u1[...]), 1, 0)

        @pl.when(step == steps - 1)
        def _():
            e = acc[...]
            xh = xhat_ref[...]
            gm[...] = cot_ref[...] + norm_back(e, ln_ref[2:3, :], xh, inv_ref[:, 0:1])
            gln[0:1, :] = jnp.sum(e * xh, axis=0, keepdims=True)
            gln[1:2, :] = jnp.sum(e, axis=0, keepdims=True)

    fixed = lambda shape: pl.BlockSpec(shape, lambda i: (0,) * len(shape))
    cols = pl.BlockSpec((rows_all, chunk), lambda i: (0, i))
    act = fixed((rows_all, width))
    return pl.pallas_call(
        body,
        compiler_params=ROOM,
        cost_estimate=cost(8.5),
        grid=(steps,),
        out_shape=[
            jax.ShapeDtypeStruct((rows_all, width), F32),
            jax.ShapeDtypeStruct((8, width), F32),
        ],
        in_specs=[act, act, fixed((rows_all, 128)), fixed((8, width)), cols, cols]
        + [pl.BlockSpec((chunk, width), lambda i: (i, 0))] * 2,
        out_specs=[act, fixed((8, width))],
        scratch_shapes=[pltpu.VMEM((rows_all, width), F32)],
    )(cot, xhat, inv, ln, ph, plo, uh, ul)


def mixture_grad_stage(me, gm, attended, oh, ol, plan, stream):
    rows_all, width = gm.shape
    rows, lanes = width // plan.dp, width // plan.fsdp

    def body(me_ref, gm_ref, att, oh_ref, ol_ref, gmix, away, keep, full):
        g = split(gm_ref[...])
        gmix[...] = mm3(g, (oh_ref[...], ol_ref[...]), 1, 0)
        full[...] = att[...]
        for core in range(2):
            res = mm3(g, split(half_lanes(full, me_ref[1], core, lanes)), 0, 0)
            mine = away if core else keep
            for d in range(plan.dp):
                for y in range(2):
                    value = res[d * rows : (d + 1) * rows, y * lanes : (y + 1) * lanes]
                    stream.put(mine, d ^ me_ref[0], core + 2 * y, 0, value)

    return call(
        body,
        [((rows_all, width), F32), (stream.shape(), F32), (stream.shape(), F32)],
        [pltpu.VMEM((rows_all, width), F32)],
        compiler_params=ROOM,
        cost_estimate=cost(5),
        in_specs=[SMEM] + [whole()] * 4,
        out_specs=[whole()] * 3,
    )(me, gm, attended, oh, ol)


def packed_grad_stage(dq, dk, dv, g4, g5a, g5b, pool, seqs):
    rows_all, width = dq.shape
    length = rows_all // seqs

    def body(dq_r, dk_r, dv_r, g4_r, g5a_r, g5b_r, pool_r, gph, gpl, column):
        for j, ref in enumerate((dq_r, dk_r, dv_r)):
            total = None
            for s in range(seqs):
                rs = slice(s * length, (s + 1) * length)
                value = ref[rs, :]
                if j:
                    groups = jnp.concatenate(
                        [g4_r[s, j - 1], g5a_r[s, j - 1] + g5b_r[s, j - 1]], axis=0
                    )
                    value = value + mm2(pool_r[...], split(groups), 0, 0)
                part = jnp.sum(value, axis=0, keepdims=True)
                total = part if total is None else total + part
                h = split(value)
                gph[rs, j * width : (j + 1) * width] = h[0]
                gpl[rs, j * width : (j + 1) * width] = h[1]
            column[j * width : (j + 1) * width, :] = jnp.transpose(
                jnp.broadcast_to(total, (128, width))
            )

    return call(
        body,
        [((rows_all, 3 * width), BF16)] * 2 + [((3 * width, 128), F32)],
        compiler_params=ROOM,
        cost_estimate=cost(4.5),
        in_specs=[whole()] * 7,
        out_specs=[whole()] * 3,
    )(dq, dk, dv, g4, g5a, g5b, pool)


def input_grad_stage(gph, gpl, wqh, wql, xhat, inv, ln, gm):
    rows_all, width = gm.shape

    def body(gph_r, gpl_r, wh, wl, xhat_r, inv_r, ln_r, gm_r, gtok):
        e = mm3((gph_r[...], gpl_r[...]), (wh[...], wl[...]), 1, 0)
        gtok[...] = gm_r[...] + norm_back(e, ln_r[0:1, :], xhat_r[...], inv_r[:, 0:1])

    return call(
        body,
        [((rows_all, width), F32)],
        compiler_params=ROOM,
        cost_estimate=cost(7.4),
        in_specs=[whole()] * 8,
        out_specs=[whole()],
    )(gph, gpl, wqh, wql, xhat, inv, ln, gm)[0]


def grad_qkv_stage(me, gph, gpl, column, xhat, ln, wh, wl, plan, stream, core):
    rows_all, triple = gph.shape
    width = triple // 3
    rows, lanes = triple // plan.dp, width // plan.fsdp
    steps = 2
    block = triple // steps

    def body(me_ref, gph_r, gpl_r, col_r, xhat_r, ln_r, wh_r, wl_r, out, sums, nh, nl):
        me_f = me_ref[1]
        step = pl.program_id(0)
        pick = lambda ref: half_lanes(ref, me_f, core, lanes)

        @pl.when(step == 0)
        def _():
            n = split(pick(xhat_r))
            nh[...] = n[0]
            nl[...] = n[1]
            sums[...] = jnp.zeros_like(sums)

        params = pick(ln_r)
        res = mm3((gph_r[...], gpl_r[...]), (nh[...], nl[...]), 0, 0)
        w = pick(wh_r).astype(F32) + pick(wl_r).astype(F32)
        col = col_r[:, 0:1]
        parts = [jnp.sum(res * w, axis=0, keepdims=True), jnp.sum(w * col, axis=0, keepdims=True)]
        for y in range(2):
            at = pl.ds(pl.multiple_of((me_f ^ (core + 2 * y)) * lanes, 128), lanes)
            for i in range(2):
                sums[i : i + 1, at] += parts[i][:, y * lanes : (y + 1) * lanes]
        res = res * params[0:1, :] + col * params[1:2, :]
        for i in range(block // rows):
            jd = me_ref[0] ^ (step * (block // rows) + i)
            for y in range(2):
                value = res[i * rows : (i + 1) * rows, y * lanes : (y + 1) * lanes]
                stream.put(out, jd, core + 2 * y, 0, value)

    fixed = lambda shape: pl.BlockSpec(shape, lambda i: (0,) * len(shape))
    cols = pl.BlockSpec((rows_all, block), lambda i: (0, i))
    down = lambda n: pl.BlockSpec((block, n), lambda i: (i, 0))
    return pl.pallas_call(
        body,
        compiler_params=ROOM,
        cost_estimate=cost(0.25),
        grid=(steps,),
        out_shape=[
            jax.ShapeDtypeStruct(stream.shape(), F32),
            jax.ShapeDtypeStruct((8, width), F32),
        ],
        in_specs=[SMEM, cols, cols, down(128), fixed((rows_all, width)), fixed((8, width))]
        + [down(width)] * 2,
        out_specs=[fixed(stream.shape()), fixed((8, width))],
        scratch_shapes=[pltpu.VMEM((rows_all, 2 * lanes), BF16)] * 2,
    )(me, gph, gpl, column, xhat, ln, wh, wl)


def swap(x, mask, axis="fsdp"):
    size = lax.axis_size(axis)
    return lax.ppermute(x, axis, [(i, i ^ mask) for i in range(size)])


def local(
    tokens, segments, cotangent, ln1_gain, ln1_bias, w_qkv, w_out, ln2_gain, ln2_bias, w_up, w_down
):
    seqs, length, width = tokens.shape
    dp, fsdp = lax.axis_size("dp"), lax.axis_size("fsdp")
    plan = Plan(dp, fsdp)
    me_d = lax.axis_index("dp")
    me = jnp.stack([me_d, lax.axis_index("fsdp")]).astype(jnp.int32)
    rows_all = seqs * length
    hidden_width = w_down.shape[0] * fsdp

    spread, pool, same = pooling(length)
    layout, _ = level_layout(length)
    local_rows = [first for level, first, _ in layout if 2 * NR * (1 << level) > length][0]
    spread_c = jnp.asarray(spread, BF16)
    pool_c = jnp.asarray(pool, BF16)
    same_c = jnp.asarray(same, F32)
    far_pool = jnp.asarray(pool[local_rows : local_rows + (length >> 4) + (length >> 5)], BF16)

    share = width // dp
    norms = jnp.stack([ln1_gain, ln1_bias, ln2_gain, ln2_bias])
    placed = lax.dynamic_update_slice(jnp.zeros((4, width), F32), norms, (0, me_d * share))
    placed = placed.reshape(4, 4, 128).transpose(1, 0, 2).reshape(LN_ROWS, 128)
    rows_qkv, rows_d, rows_up = 3 * share, share, hidden_width // dp
    chunks = hidden_width // fsdp // 128
    down_piece = w_down.T.reshape(rows_d, chunks, 128).transpose(1, 0, 2).reshape(-1, 128)
    down_piece = jnp.concatenate([down_piece, w_out.T], axis=0)
    extra = [(name,) for name in plan.extra]
    qkv_piece = jnp.concatenate([placed, w_qkv.T], axis=0)
    up_piece = w_up.T
    qkv_piece = after(qkv_piece, me)
    qkv_in, down_in, up_in = (Gather(plan, p) for p in (qkv_piece, down_piece, up_piece))
    tok = tokens.reshape(rows_all, width)
    cot = cotangent.reshape(rows_all, width)
    attend = (spread_c, pool_c, same_c)

    near = swap(segments, 1)
    qkv_in.send([("z", "w")])
    for group in extra:
        qkv_in.stage([group])
    gate = qkv_in.came()
    qkv_in.join()
    qkv_in.cut(LN_ROWS + rows_qkv // 16 * 8)
    qkv_in.send([("x",), ("y",)], gate)
    down_in.send([("w",)], gate)
    for group in extra:
        down_in.stage([group])
    far_segments = swap(jnp.stack([segments, after(near, gate)]), 2)
    bias = score_bias(segments, near, far_segments[0], far_segments[1])
    qkv_in.stage([("y",), ("x",)], qkv_in.came())
    gate = (down_in.came(), far_segments)
    down_in.stage([("z",)], gate)
    up_in.send([("w",)], gate)
    for group in extra:
        up_in.stage([group])
    gate = (qkv_in.came(), down_in.came(), up_in.came(), bias)
    cores = qkv_in.share(True, gate) + qkv_in.share(False, gate)
    down_in.join()
    down_in.cut(down_piece.shape[0] // 16 * 8)
    down_in.send([("x",), ("y",)], cores)
    up_in.stage([("z",)], cores)
    packed, wqh, wql, xhat1, inv1, ln, s4, s5 = qkv_stage(
        me, after(tok, cores, bias), qkv_in, plan, far_pool, seqs
    )
    gate = (packed, down_in.came(), up_in.came())
    s4, s5 = after((s4, s5), gate)
    got = [swap(s4, 1), swap(s5, 2), swap(s5, 3)]
    far = jnp.concatenate(got, axis=2)
    down_in.stage([("y",), ("x",)], gate)
    cores = down_in.share(True, far)
    calls = [(s, 1, 0, width // 128) for s in range(seqs)]
    before = ()
    gate = far
    for index, which in enumerate(calls):
        packed_in = after(packed, gate, before)
        before = attention_forward(packed_in, far, bias, *attend, seqs, local_rows, which, before)
        if index == 0:
            gate = (before, down_in.came(), cores)
            cores = down_in.share(False, gate)
            up_in.join()
            up_in.cut(rows_up // 2 // 8 * 8)
            up_in.send([("x",), ("y",)], gate)
    attended, lse = before
    gate = (attended, up_in.came(), cores)
    up_in.stage([("y",), ("x",)], gate)
    dh, dl, oh, ol = projection_stage(after(me, gate), down_in, plan, width, hidden_width)
    cores = up_in.share(True, gate)
    middle, xhat2, inv2 = middle_stage(tok, attended, oh, ol)
    gate = (middle, up_in.came(), cores)
    cores = up_in.share(False, gate)
    hh, hl, ph, plo, uh, ul, nth, ntl, cth, ctl = hidden_stage(
        me, after(xhat2, cores), ln, cot, dh, dl, up_in, plan
    )

    single = [("x", "y"), ("z",), ("w",)] + extra
    double = [("x", "y"), ("z", "w")] + extra
    outer = [("z",), ("x",), ("w",)] + extra + [("y",)]
    down = Stream(plan, chunks * rows_d, outer)
    up = Stream(plan, rows_up, single)
    out = Stream(plan, rows_d, single)
    qkv = Stream(plan, rows_qkv, double)
    down_sum, up_sum, qkv_sum = Reduce(plan, outer), Reduce(plan, single), Reduce(plan, double)

    away = grad_down_stage(me, cth, ctl, hh, hl, plan, down, 1)
    cores = down_sum.begin(away)
    away = grad_up_stage(me, after(nth, away), ntl, ph, plo, plan, up, 1)
    cores += up_sum.begin(away)
    keep = grad_down_stage(me, after(cth, away), ctl, hh, hl, plan, down, 0)
    down_sum.keep(keep)
    keep = grad_up_stage(me, after(nth, keep), ntl, ph, plo, plan, up, 0)
    up_sum.keep(keep)
    sent = (down_sum.send(keep, cores), up_sum.send(keep, cores))
    gm, gln = middle_grad_stage(after(cot, sent), xhat2, inv2, ln, ph, plo, uh, ul)
    gmix, away_out, keep_out = mixture_grad_stage(me, gm, attended, oh, ol, plan, out)
    before = ()
    calls = [(s, 1, 0, width // 128) for s in range(seqs)]
    for which in calls:
        grad = after(gmix, sent, before)
        before = attention_backward(
            packed, far, bias, *attend, attended, lse, grad, seqs, local_rows, which, before
        )
    gate = (before, down_sum.last, up_sum.last)
    dq, dk, dv, f4, f5a, f5b = before
    f4, f5a, f5b = after((f4, f5a, f5b), gate)
    g4, g5a, g5b = swap(f4, 1), swap(f5a, 2), swap(f5b, 3)
    down_sum.send(gate)
    out_sum = Reduce(plan, single)
    out_cores = out_sum.begin(away_out, gate)
    out_sum.keep(keep_out)
    gph, gpl, column = packed_grad_stage(dq, dk, dv, g4, g5a, g5b, far_pool, seqs)
    away, sums_away = grad_qkv_stage(
        me, gph, gpl, column, xhat1, ln, wqh, wql, plan, qkv, 1
    )
    out_sum.send(gph, out_cores)
    got = qkv_sum.begin(away)
    keep, sums_keep = grad_qkv_stage(
        me, gph, gpl, column, after(xhat1, away), ln, wqh, wql, plan, qkv, 0
    )
    qkv_sum.keep(keep)
    sums = jnp.concatenate([(sums_away + sums_keep)[0:2], gln[0:2]], axis=0)
    sent = qkv_sum.send(got, out_sum.last, rider=sums.reshape(-1, 128))
    down_sum.send(sent)
    up_sum.absorb(out_sum, sent)
    up_sum.send()
    gtok = input_grad_stage(gph, gpl, wqh, wql, after(xhat1, sent), inv1, ln, gm)
    output = output_stage(after(middle, gtok), hh, hl, dh, dl)
    gate = (up_sum.last, down_sum.last, output)
    sent = qkv_sum.send(qkv_sum.last, gate)
    while qkv_sum.stages:
        sent = qkv_sum.send(qkv_sum.last)
    for total in (down_sum, up_sum):
        while total.stages:
            total.send(gate, sent)
    g_down, g_up = down_sum.total(), up_sum.total()
    g_up, g_out = g_up[:rows_up], g_up[rows_up:]
    if rows_up % 128 == 0:
        g_up = g_up.reshape(-1, width // fsdp, 128).transpose(1, 0, 2).reshape(-1, rows_up)
    else:
        g_up = g_up.T
    g_down = g_down.reshape(chunks, rows_d, 128).transpose(0, 2, 1).reshape(-1, rows_d)
    g_out = g_out.T
    qkv_sum.terms[-1] = after(qkv_sum.terms[-1], g_down, g_up, g_out)
    g_qkv = qkv_sum.total()
    g_qkv, sums = g_qkv[:rows_qkv], g_qkv[rows_qkv:]
    sums = (sums + plan.send(sums, ("c",))).reshape(4, width)
    mine = lax.dynamic_slice(sums, (0, me_d * share), (4, share))
    shape = tokens.shape
    return (
        output.reshape(shape),
        gtok.reshape(shape),
        mine[0],
        mine[1],
        g_qkv.T,
        g_out,
        mine[2],
        mine[3],
        g_up,
        g_down,
    )


def solution(mesh):
    weight = P("fsdp", "dp")
    rows = P("dp", "fsdp", None)
    vector = P("dp")
    return jax.shard_map(
        local,
        mesh=mesh,
        in_specs=(rows, P("dp", "fsdp"), rows, vector, vector, weight, weight, vector, vector, weight, weight),
        out_specs=(rows, rows, vector, vector, weight, weight, vector, vector, weight, weight),
        check_vma=False,
    )
```
